32 devices in a mesh: dp: 2 (over x), ctx: 16 (over z, y, core).
Axes of the slice: x: 2, y: 2, z: 4, core: 2. Of those that a mesh axis runs over, the one named last changes fastest.
Arguments:
- inputs: bfloat16 [2, 2048, 1024], P('dp', 'ctx'), may hold values from -6 to 6
- cotangent: bfloat16 [2, 2048, 1024], P('dp', 'ctx'), may hold values from -6 to 6
- block_ids: int32 [2, 2048], P('dp', 'ctx'), may hold values from 0 to 15, never falling along the last dimension, each value on 1 to 256 neighbouring positions
- ln1_gain: bfloat16 [1024], P(('dp', 'ctx')), may hold values from 0.5 to 1.5
- ln1_bias: bfloat16 [1024], P(('dp', 'ctx')), may hold values from -3 to 3
- w_qkv: bfloat16 [1024, 3072], P(('dp', 'ctx')), may hold values from -0.1875 to 0.1875
- b_qkv: bfloat16 [2048], P(('dp', 'ctx')), may hold values from -3 to 3
- w_out: bfloat16 [1024, 1024], P(('dp', 'ctx')), may hold values from -1.5 to 1.5
- b_out: bfloat16 [1024], P(('dp', 'ctx')), may hold values from -3 to 3
- ln2_gain: bfloat16 [1024], P(('dp', 'ctx')), may hold values from 0.5 to 1.5
- ln2_bias: bfloat16 [1024], P(('dp', 'ctx')), may hold values from -3 to 3
- w_fc: bfloat16 [1024, 4096], P(('dp', 'ctx')), may hold values from -0.1875 to 0.1875
- b_fc: bfloat16 [4096], P(('dp', 'ctx')), may hold values from -3 to 3
- w_proj: bfloat16 [4096, 1024], P(('dp', 'ctx')), may hold values from -0.09375 to 0.09375
- b_proj: bfloat16 [1024], P(('dp', 'ctx')), may hold values from -3 to 3
Outputs:
- output: bfloat16 [2, 2048, 1024], P('dp', 'ctx')
- input_grad: bfloat16 [2, 2048, 1024], P('dp', 'ctx')
- ln1_gain_grad: float32 [1024], P(('dp', 'ctx'))
- ln1_bias_grad: float32 [1024], P(('dp', 'ctx'))
- w_qkv_grad: float32 [1024, 3072], P(('dp', 'ctx'))
- b_qkv_grad: float32 [2048], P(('dp', 'ctx'))
- w_out_grad: float32 [1024, 1024], P(('dp', 'ctx'))
- b_out_grad: float32 [1024], P(('dp', 'ctx'))
- ln2_gain_grad: float32 [1024], P(('dp', 'ctx'))
- ln2_bias_grad: float32 [1024], P(('dp', 'ctx'))
- w_fc_grad: float32 [1024, 4096], P(('dp', 'ctx'))
- b_fc_grad: float32 [4096], P(('dp', 'ctx'))
- w_proj_grad: float32 [4096, 1024], P(('dp', 'ctx'))
- b_proj_grad: float32 [1024], P(('dp', 'ctx'))
The draws below stay inside these ranges and needn't reach their ends.
Inputs may be any that keep to these rules, and one draw needn't show every extreme that they name: `block_ids`: in each sequence the block numbers start at 0, never fall from one token to the next and rise in steps of one; each block has 1 to 256 tokens, and some block has exactly 256.
All inputs are finite; a program needn't handle non-finite values.
Results may differ from the reference program's by a relative error of at most 0.017.
Values may be sent and summed in bfloat16 or wider, within the bound.
A program may use at most 192 MiB of HBM per device.

```python
import math
import jax
import jax.numpy as jnp
import numpy as np
from jax import lax

D = 1024
HEADS = 16
HEAD_DIM = 64
FF = 4096
BLOCK_MOST = 256
LENGTH = 2048
SEQS = 2
BLOCKS = 16


def raised(values, own_key, source, target, shards_of, factor):
    owner, partner = [(jnp.arange(values.shape[position]) // (values.shape[position] // shards_of)).reshape([-1 if axis == position else 1 for axis in range(values.ndim)]) for position in (source, target)]
    chosen = jax.random.permutation(own_key, shards_of)[partner]
    strong = (owner == chosen) | (owner == (partner + shards_of // 2) % shards_of)
    return jnp.where(strong, factor * values, values)


def levels(stream_key, dims, shards, low, largest):
    loudness, own = 1.0, jax.random.fold_in(stream_key, 6)
    for axis_at, blocks in shards:
        draws = jnp.exp(jax.random.uniform(jax.random.fold_in(own, axis_at), (blocks,), jnp.float32, low / len(shards), largest / len(shards)))
        loudness = loudness * jnp.repeat(draws, dims[axis_at] // blocks).reshape([-1 if axis == axis_at else 1 for axis in range(len(dims))])
    return loudness


def profile(amount, total, bound, slope):
    portions = [(1 << 20) // math.isqrt(standing ** slope) + 1 for standing in range(2, amount + 1)]
    rest, holding = total - bound - (amount - 1), [1] * (amount - 1)
    while rest > 0:
        free = [i for i in range(amount - 1) if holding[i] < bound]
        pool, budget = sum([portions[i] for i in free]), rest
        for i in free:
            extra = min(bound - holding[i], max(1, budget * portions[i] // pool), rest)
            holding[i] = holding[i] + extra
            rest = rest - extra
    return np.array([bound] + holding)


def uneven(rng, amount, total, limit, skew):
    if amount == 2:
        one = jax.random.randint(rng, (), max(1, total - limit), min(limit, total - 1) + 1)
        return jnp.stack([one, total - one])
    tallies = jnp.asarray(profile(amount, total, limit, skew), jnp.int32)
    twos = (amount - 1) // 2
    donor, receiver = tallies[1:1 + 2 * twos:2], tallies[2:2 + 2 * twos:2]
    slack = jnp.minimum(donor - 1, limit - receiver)
    moved = jax.random.randint(jax.random.fold_in(rng, 1), (twos,), 0, 1 << 20) % (slack + 1)
    tallies = tallies.at[1:1 + 2 * twos:2].set(donor - moved).at[2:2 + 2 * twos:2].set(receiver + moved)
    return tallies[jax.random.permutation(jax.random.fold_in(rng, 2), amount)]


def noise(key, shape, deviation, bound, shards=(), dtype=jnp.bfloat16):
    array = jax.random.normal(key, shape, jnp.float32) * deviation
    if len(shards) > 0:
        array = levels(key, shape, shards, -0.22, 0.18) * array
    return jnp.clip(array, min=-bound, max=bound).astype(dtype)


def noise_with(key, dims, deviation, most, pieces, heavy, dtype=jnp.bfloat16):
    values = deviation * jax.random.normal(key, dims, jnp.float32)
    if pieces:
        values = values * levels(key, dims, pieces, -0.22, 0.18)
    return jnp.clip(raised(values, jax.random.fold_in(key, 3), *heavy), -most, most).astype(dtype)


def setup_inputs(seed: int = 0) -> dict:
    arg_keys = jax.random.split(jax.random.key(seed), 16)
    inputs = noise(arg_keys[0], (SEQS, LENGTH, D), 1.0, 6.0, ((0, 2), (1, 16)))
    cotangent = noise_with(arg_keys[1], (SEQS, LENGTH, D), 1.0, 6.0, ((0, 2), (1, 16)), (1, 2, 16, 2.0))
    block_ids = jax.vmap(lambda own: jnp.searchsorted(jnp.cumsum(uneven(own, BLOCKS, LENGTH, BLOCK_MOST, 0)), jnp.arange(LENGTH), side="right"))(jax.random.split(arg_keys[2], SEQS)).reshape((SEQS, LENGTH)).astype(jnp.int32)
    ln1_gain = jnp.clip(1.0 + 0.1 * jax.random.normal(arg_keys[3], (D,), jnp.float32), 0.5, 1.5).astype(jnp.bfloat16)
    ln1_bias = noise(arg_keys[4], (D,), 0.5, 3.0, ((0, 32),))
    w_qkv = noise(arg_keys[5], (D, 3 * D), D ** -0.5, 0.1875, ((0, 32),))
    b_qkv = noise(arg_keys[6], (2 * D,), 0.5, 3.0, ((0, 32),))
    w_out = noise(arg_keys[7], (D, D), (D // 64) ** -0.5, 1.5, ((0, 32),))
    b_out = noise(arg_keys[8], (D,), 0.5, 3.0, ((0, 32),))
    ln2_gain = jnp.clip(1.0 + 0.1 * jax.random.normal(arg_keys[9], (D,), jnp.float32), 0.5, 1.5).astype(jnp.bfloat16)
    ln2_bias = noise(arg_keys[10], (D,), 0.5, 3.0, ((0, 32),))
    w_fc = noise(arg_keys[11], (D, FF), D ** -0.5, 0.1875, ((0, 32),))
    b_fc = noise(arg_keys[12], (FF,), 0.5, 3.0, ((0, 32),))
    w_proj = noise(arg_keys[13], (FF, D), FF ** -0.5, 0.09375, ((0, 32),))
    b_proj = noise(arg_keys[14], (D,), 0.5, 3.0, ((0, 32),))
    return {"inputs": inputs, "cotangent": cotangent, "block_ids": block_ids, "ln1_gain": ln1_gain, "ln1_bias": ln1_bias, "w_qkv": w_qkv, "b_qkv": b_qkv, "w_out": w_out, "b_out": b_out, "ln2_gain": ln2_gain, "ln2_bias": ln2_bias, "w_fc": w_fc, "b_fc": b_fc, "w_proj": w_proj, "b_proj": b_proj}


HIGHEST_PRECISION = lax.Precision.HIGHEST
EPSILON = 1e-05

@jax.custom_vjp
def low(v):
    return lax.optimization_barrier(v.astype(jnp.bfloat16)).astype(jnp.float32)

@jax.custom_vjp
def low_back(v):
    return v

def low_keep(v):
    return (low(v), None)

def low_pass(kept, grad):
    return (grad,)

def back_keep(v):
    return (v, None)

def back_low(kept, grad):
    return (low(grad),)
low.defvjp(low_keep, low_pass)
low_back.defvjp(back_keep, back_low)

def norm_affine(rows, gain, shift):
    centred = rows - lax.optimization_barrier(jnp.mean(rows, axis=-1, keepdims=True))
    spread = lax.optimization_barrier(jnp.mean(centred * centred, axis=-1, keepdims=True))
    return centred * lax.rsqrt(spread + EPSILON) * gain + shift

def attend(queries, key_rows, value_rows, block_marks):
    length = queries.shape[0]
    block_span = min(512, length)
    block_count = length // block_span
    score_scale = 1.0 / math.sqrt(HEAD_DIM)

    def query_block(arguments):
        query_part, part_marks = arguments
        scores = low_back(jnp.einsum('qhd,khd->hqk', query_part, key_rows, precision=HIGHEST_PRECISION) * score_scale)
        allowed = block_marks[None, None, :] <= part_marks[None, :, None]
        exponent = jnp.where(allowed, jnp.exp(scores), 0.0)
        totals = lax.optimization_barrier(jnp.sum(exponent, axis=-1))
        summed = jnp.einsum('hqk,khd->qhd', low(exponent), value_rows, precision=HIGHEST_PRECISION)
        return low(low_back(summed) / jnp.transpose(totals)[:, :, None])
    attended = lax.map(jax.checkpoint(query_block), (queries.reshape(block_count, block_span, HEADS, HEAD_DIM), block_marks.reshape(block_count, block_span)))
    return attended.reshape(length, HEADS * HEAD_DIM)

def layer(residual, block_marks, ln1_gain, ln1_bias, w_qkv, b_qkv, w_out, b_out, ln2_gain, ln2_bias, w_fc, b_fc, w_proj, b_proj):
    first_normed = low(norm_affine(residual, ln1_gain, ln1_bias))
    bias_full = jnp.concatenate([b_qkv[:D], jnp.zeros((D,), jnp.float32), b_qkv[D:]])
    projected = low(low_back(jnp.dot(first_normed, w_qkv, precision=HIGHEST_PRECISION) + bias_full))
    length = residual.shape[0]
    queries = projected[:, :D].reshape(length, HEADS, HEAD_DIM)
    key_rows = projected[:, D:2 * D].reshape(length, HEADS, HEAD_DIM)
    value_rows = projected[:, 2 * D:].reshape(length, HEADS, HEAD_DIM)
    attended = attend(queries, key_rows, value_rows, block_marks)
    branch = low_back(jnp.dot(attended, w_out, precision=HIGHEST_PRECISION) + b_out)
    middle = residual + branch
    second_normed = low(norm_affine(middle, ln2_gain, ln2_bias))
    hidden = low_back(jnp.dot(second_normed, w_fc, precision=HIGHEST_PRECISION) + b_fc)
    active = low(jax.nn.gelu(hidden, approximate=True))
    return middle + low_back(jnp.dot(active, w_proj, precision=HIGHEST_PRECISION) + b_proj)

def reference(inputs, cotangent, block_ids, ln1_gain, ln1_bias, w_qkv, b_qkv, w_out, b_out, ln2_gain, ln2_bias, w_fc, b_fc, w_proj, b_proj):
    weight_list = tuple((tensor.astype(jnp.float32) for tensor in (ln1_gain, ln1_bias, w_qkv, b_qkv, w_out, b_out, ln2_gain, ln2_bias, w_fc, b_fc, w_proj, b_proj)))

    def per_sequence(running, sequence):
        residual, grad_out, block_marks = sequence

        def forward(residual_in, *params):
            return layer(residual_in, block_marks, *params)
        result, pullback = jax.vjp(forward, residual.astype(jnp.float32), *weight_list)
        gradients = pullback(grad_out.astype(jnp.float32))
        running = tuple((running_sum + gradient for running_sum, gradient in zip(running, gradients[1:])))
        return (running, (result.astype(jnp.bfloat16), gradients[0].astype(jnp.bfloat16)))
    initial = tuple((jnp.zeros_like(tensor) for tensor in weight_list))
    totals, (outputs, input_grads) = lax.scan(per_sequence, initial, (inputs, cotangent, block_ids))
    return (outputs, input_grads, totals[0], totals[1], totals[2], totals[3], totals[4], totals[5], totals[6], totals[7], totals[8], totals[9], totals[10], totals[11])
```

```python
import functools
import math

import jax
import jax.numpy as jnp
from jax import lax
from jax.experimental import pallas as pl
from jax.experimental.pallas import tpu as pltpu
from jax.sharding import PartitionSpec as P

HEADS = 16
EPSILON = 1e-05
QB = 256
F32, BF16 = jnp.float32, jnp.bfloat16
NT = (((1,), (1,)), ((), ()))
TN = (((0,), (0,)), ((), ()))


def attend_kernel(r, kc, a_ref, b_ref, idq_ref, idk_ref, o_ref, t_ref, acc, tot):
    part = lax.rem(lax.axis_index("ctx"), r) if r > 1 else 0
    length = b_ref.shape[0]

    def per_queries(lb, _):
        qs = pl.ds(pl.multiple_of(lb * QB, QB), QB)
        a = a_ref[qs, :] * 0.125
        idq = idq_ref[qs, :]
        acc[...] = jnp.zeros_like(acc)
        tot[...] = jnp.zeros_like(tot)

        def per_keys(kb, _):
            ks = pl.ds(pl.multiple_of(kb * kc, kc), kc)
            b = b_ref[ks, :]
            s = lax.dot_general(a, b, NT, preferred_element_type=F32)
            w = jnp.where(idk_ref[:, ks] <= idq, jnp.exp(s), 0.0)
            t = w[:, :128]
            for i in range(1, kc // 128):
                t = t + w[:, i * 128 : (i + 1) * 128]
            tot[...] += t
            acc[...] += jnp.dot(w.astype(BF16), b, preferred_element_type=F32)
            return 0

        reach = (lb * r + part + 2) * QB
        lax.fori_loop(0, jnp.minimum((reach + kc - 1) // kc, length // kc), per_keys, 0)
        t = jnp.sum(tot[...], axis=-1, keepdims=True)
        t_ref[qs, :] = t
        o_ref[qs, :] = acc[...] / t
        return 0

    lax.fori_loop(0, a_ref.shape[0] // QB, per_queries, 0)


def attend(r, a, b, idq, idk):
    rows = a.shape[0]
    return pl.pallas_call(
        functools.partial(attend_kernel, r, min(1024, b.shape[0])),
        out_shape=(jax.ShapeDtypeStruct((rows, 128), F32), jax.ShapeDtypeStruct((rows, 1), F32)),
        scratch_shapes=[pltpu.VMEM((QB, 128), F32), pltpu.VMEM((QB, 128), F32)],
        compiler_params=pltpu.CompilerParams(vmem_limit_bytes=48 << 20),
        name="attend",
    )(a, b, idq, idk)


def attend_back_kernel(r, kc, a_ref, b_ref, do_ref, ratio_ref, idq_ref, idk_ref, dq_ref, dkv_ref, acc):
    part = lax.rem(lax.axis_index("ctx"), r) if r > 1 else 0
    length = b_ref.shape[0]
    dkv_ref[...] = jnp.zeros_like(dkv_ref)

    def per_queries(lb, _):
        qs = pl.ds(pl.multiple_of(lb * QB, QB), QB)
        a = a_ref[qs, :]
        scaled = a * 0.125
        do = do_ref[qs, :]
        ado = jnp.concatenate([a, do], axis=0)
        idq = idq_ref[:, qs]
        ratio = ratio_ref[:, qs]
        acc[...] = jnp.zeros_like(acc)

        def per_keys(kb, _):
            ks = pl.ds(pl.multiple_of(kb * kc, kc), kc)
            b = b_ref[ks, :]
            s = lax.dot_general(b, scaled, NT, preferred_element_type=F32)
            w = jnp.where(idk_ref[ks, :] <= idq, jnp.exp(s), 0.0)
            p = lax.dot_general(b, do, NT, preferred_element_type=F32)
            g = (w * (p - ratio)).astype(BF16)
            gw = jnp.concatenate([g, w.astype(BF16)], axis=1)
            dkv_ref[ks, :] += jnp.dot(gw, ado, preferred_element_type=F32)
            acc[...] += lax.dot_general(g, b, TN, preferred_element_type=F32)
            return 0

        reach = (lb * r + part + 2) * QB
        lax.fori_loop(0, jnp.minimum((reach + kc - 1) // kc, length // kc), per_keys, 0)
        dq_ref[qs, :] = acc[...]
        return 0

    lax.fori_loop(0, a_ref.shape[0] // QB, per_queries, 0)


def attend_back(r, a, b, do, ratio, idq, idk):
    rows, length = a.shape[0], b.shape[0]
    return pl.pallas_call(
        functools.partial(attend_back_kernel, r, min(1024, length)),
        out_shape=(jax.ShapeDtypeStruct((rows, 128), F32), jax.ShapeDtypeStruct((length, 128), F32)),
        scratch_shapes=[pltpu.VMEM((QB, 128), F32)],
        compiler_params=pltpu.CompilerParams(vmem_limit_bytes=48 << 20),
        name="attend_back",
    )(a, b, do, ratio, idq, idk)


def normalize(rows):
    centred = rows - jnp.mean(rows, axis=-1, keepdims=True)
    rstd = lax.rsqrt(jnp.mean(centred * centred, axis=-1, keepdims=True) + EPSILON)
    return centred * rstd, rstd


def normalize_back(grad, normed, rstd):
    return rstd * (
        grad
        - jnp.mean(grad, axis=-1, keepdims=True)
        - normed * jnp.mean(grad * normed, axis=-1, keepdims=True)
    )


def gelu_both(u):
    c = math.sqrt(2.0 / math.pi)
    t = jnp.tanh(c * (u + 0.044715 * (u * u * u)))
    half = 0.5 * (1.0 + t)
    return u * half, half + 0.5 * u * (1.0 - t * t) * (c * (1.0 + 3.0 * 0.044715 * (u * u)))


def gather_ctx(v):
    return lax.all_gather(v, "ctx", axis=0, tiled=True)


def scatter_ctx(v):
    return lax.psum_scatter(v, "ctx", scatter_dimension=0, tiled=True).astype(F32)


def exchange_ctx(v):
    return lax.all_to_all(v, "ctx", 0, 0, tiled=True)


def dot(x, y, dims=(((1,), (0,)), ((), ()))):
    return lax.dot_general(x, y, dims, preferred_element_type=F32)


def local(n_dp, n, inputs, cotangent, block_ids, ln1_gain, ln1_bias, w_qkv, b_qkv, w_out, b_out, ln2_gain, ln2_bias, w_fc, b_fc, w_proj, b_proj):
    tokens, width = inputs.shape[1:]
    length = n * tokens
    rows = w_qkv.shape[0]
    units = w_proj.shape[0]
    r = n // HEADS
    hd = width // HEADS
    me = lax.axis_index("ctx")
    head, part = me // r, me % r

    small = jnp.concatenate([ln1_gain, ln1_bias, b_qkv, b_out, ln2_gain, ln2_bias, b_fc, b_proj])
    small = lax.all_gather(small, ("dp", "ctx"), axis=0).astype(F32)
    cuts, at = [], 0
    for v in (ln1_gain, ln1_bias, b_qkv, b_out, ln2_gain, ln2_bias, b_fc, b_proj):
        cuts.append(small[:, at : at + v.shape[0]])
        at += v.shape[0]
    g1, c1, bqv, bo, g2, c2, bf, bp = cuts
    g1, c1, bqv, bo, g2, c2, bp = (v.reshape(1, -1) for v in (g1, c1, bqv, bo, g2, c2, bp))
    bf = lax.dynamic_index_in_dim(bf.reshape(n_dp, n, units), me, 1, keepdims=False).reshape(1, -1)
    bqv = lax.dynamic_index_in_dim(bqv.reshape(2, HEADS, hd), head, 1, keepdims=False)
    zeros = jnp.zeros((hd,), F32)
    bias = jnp.concatenate([bqv[0], zeros, zeros, bqv[1]])[None]

    def spread(w):
        got = exchange_ctx(jnp.transpose(w, (1, 0, 2)))
        return lax.all_gather(got, "dp", axis=0, tiled=True).reshape(width, -1)

    wq = w_qkv.reshape(rows, 3, HEADS, 1, hd)
    wq = jnp.stack([wq[:, 0], jnp.zeros_like(wq[:, 0]), wq[:, 1], wq[:, 2]], axis=3)
    wq = jnp.broadcast_to(wq.reshape(rows, HEADS, 1, 4 * hd), (rows, HEADS, r, 4 * hd))
    wq = spread(wq.reshape(rows, n, 4 * hd))
    wf = spread(jnp.transpose(w_fc.reshape(rows, n_dp, n, units), (0, 2, 1, 3)).reshape(rows, n, n_dp * units))
    wp = lax.all_gather(w_proj, "dp", axis=0, tiled=True)
    wo = lax.all_gather(w_out, ("dp", "ctx"), axis=0, tiled=True)

    x_all = gather_ctx(inputs[0]).astype(F32)
    marks = gather_ctx(block_ids[0])
    normed, _ = normalize(x_all)
    first_low = (normed * g1 + c1).astype(BF16)
    qkv = (dot(first_low, wq) + bias).astype(BF16)
    a_all, b_all = qkv[:, : 2 * hd], qkv[:, 2 * hd :]

    def own_queries(v):
        if r == 1:
            return v
        split = v.reshape((length // QB // r, r, QB) + v.shape[1:])
        return lax.dynamic_index_in_dim(split, part, 1, keepdims=False).reshape((length // r,) + v.shape[1:])

    def all_queries(v):
        if r == 1:
            return v
        split = v.reshape((length // QB // r, 1, QB) + v.shape[1:])
        keep = (jnp.arange(r) == part).reshape((1, r, 1) + (1,) * (v.ndim - 1))
        return jnp.where(keep, split, 0).reshape((length,) + v.shape[1:])

    a, marks_q = own_queries(a_all), own_queries(marks)
    o, totals = attend(r, a, b_all, marks_q[:, None], marks[None])
    attended = o[:, hd:]
    low = all_queries(attended.astype(BF16))
    low = exchange_ctx(low.reshape(n, tokens, hd))
    low = low.reshape(HEADS, r, tokens, hd).sum(axis=1) if r > 1 else low
    attended_low = jnp.transpose(low, (1, 0, 2)).reshape(tokens, width)

    x = inputs[0].astype(F32)
    middle = x + dot(attended_low, wo) + bo
    n2, rstd2 = normalize(middle)
    second_low = gather_ctx((n2 * g2 + c2).astype(BF16))
    hidden = dot(second_low, wf) + bf
    active, slope = gelu_both(hidden)
    active_low = active.astype(BF16)
    output = middle + scatter_ctx(dot(active_low, wp).astype(BF16)) + bp

    dy_all = gather_ctx(cotangent[0])
    dy = cotangent[0].astype(F32)
    hidden_grad = slope * dot(dy_all, wp, NT)
    hidden_low = hidden_grad.astype(BF16)
    wp_grad = dot(active_low, dy_all, TN)
    wf_grad = dot(second_low, hidden_low, TN)
    bf_grad = jnp.sum(hidden_low.astype(F32), axis=0)
    second_grad = scatter_ctx(dot(hidden_low, wf, NT).astype(BF16))

    middle_grad = dy + normalize_back(second_grad * g2, n2, rstd2)
    branch_low = middle_grad.astype(BF16)
    wo_grad = dot(attended_low, branch_low, TN)
    attended_grad = dot(branch_low, wo, NT)
    sent = jnp.transpose(attended_grad.astype(BF16).reshape(tokens, HEADS, 1, hd), (1, 2, 0, 3))
    sent = jnp.broadcast_to(sent, (HEADS, r, tokens, hd)).reshape(n, tokens, hd)
    grad = own_queries(exchange_ctx(sent).reshape(length, hd)).astype(F32)
    ratio = jnp.sum(grad * attended, axis=-1, keepdims=True) / totals
    do = jnp.concatenate([jnp.zeros_like(grad), grad / totals], axis=1).astype(BF16)
    dq, dkv = attend_back(r, a, b_all, do, ratio.reshape(1, -1), marks_q[None], marks[:, None])
    dq = all_queries(dq[:, :hd]) * 0.125
    if r > 1:
        groups = [[h * r + i for i in range(r)] for h in range(HEADS)]
        dq, dkv = lax.psum((dq, dkv), "ctx", axis_index_groups=groups)
    mixed = jnp.concatenate([dq, jnp.zeros_like(dq), dkv[:, :hd] * 0.125, dkv[:, hd:]], axis=1).astype(BF16)
    if r > 1:
        mixed = jnp.where(part == 0, mixed, jnp.zeros_like(mixed))
    first_grad = scatter_ctx(dot(mixed, wq, NT).astype(BF16))
    wq_grad = dot(first_low, mixed, TN)
    mixed_sum = jnp.sum(mixed.astype(F32), axis=0)

    n1, rstd1 = normalize(x)
    input_grad = middle_grad + normalize_back(first_grad * g1, n1, rstd1)

    def collect(g):
        got = lax.psum_scatter(g.astype(BF16), "dp", scatter_dimension=0, tiled=True)
        return exchange_ctx(got.reshape(n, rows, -1)).astype(F32)

    wq_own = collect(wq_grad).reshape(HEADS, r, rows, 4, hd).sum(axis=1)
    wq_own = jnp.stack([wq_own[:, :, 0], wq_own[:, :, 2], wq_own[:, :, 3]], axis=1)
    wq_own = jnp.transpose(wq_own, (2, 1, 0, 3)).reshape(rows, 3 * width)
    wf_own = jnp.transpose(collect(wf_grad).reshape(n, rows, n_dp, units), (1, 2, 0, 3)).reshape(rows, -1)
    wp_own = lax.psum_scatter(wp_grad, "dp", scatter_dimension=0, tiled=True)
    wo_own = lax.psum_scatter(wo_grad.astype(BF16), ("dp", "ctx"), scatter_dimension=0, tiled=True).astype(F32)

    column = lambda v: jnp.sum(v, axis=0)
    hot = (jnp.arange(n) == me).astype(F32)[:, None]
    bqv_grad = jnp.stack([mixed_sum[:hd], mixed_sum[3 * hd :]])
    hot_head = (jnp.arange(HEADS) == head).astype(F32)[None, :, None]
    pieces = [
        column(first_grad * n1),
        column(first_grad),
        (hot_head * bqv_grad[:, None]).reshape(-1),
        column(branch_low.astype(F32)),
        column(second_grad * n2),
        column(second_grad),
        (hot[None] * bf_grad.reshape(n_dp, 1, units)).reshape(-1),
        column(dy),
    ]
    pieces = [v.reshape(n_dp * n, -1) for v in pieces]
    mine = lax.psum_scatter(jnp.concatenate(pieces, axis=1), ("dp", "ctx"), scatter_dimension=0, tiled=True)[0]
    outs, at = [], 0
    for v in pieces:
        outs.append(mine[at : at + v.shape[1]])
        at += v.shape[1]
    g1g, c1g, bqvg, bog, g2g, c2g, bfg, bpg = outs
    return (
        output.astype(BF16)[None], input_grad.astype(BF16)[None], g1g, c1g, wq_own, bqvg, wo_own, bog, g2g, c2g, wf_own, bfg, wp_own, bpg,
    )


def solution(mesh):
    both = ("dp", "ctx")
    act, vec, mat = P("dp", "ctx", None), P(both), P(both, None)
    return jax.shard_map(
        functools.partial(local, mesh.shape["dp"], mesh.shape["ctx"]),
        mesh=mesh,
        in_specs=(act, act, P("dp", "ctx"), vec, vec, mat, vec, mat, vec, vec, vec, mat, vec, mat, vec),
        out_specs=(act, act, vec, vec, mat, vec, mat, vec, vec, vec, mat, vec, mat, vec),
        check_vma=False,
    )
```

```python
import functools
import math

import jax
import jax.numpy as jnp
from jax import lax
from jax.experimental import pallas as pl
from jax.experimental.pallas import tpu as pltpu
from jax.sharding import PartitionSpec as P

HEADS = 16
EPSILON = 1e-05
QB = 256
F32, BF16 = jnp.float32, jnp.bfloat16
NT = (((1,), (1,)), ((), ()))
TN = (((0,), (0,)), ((), ()))
MESH = pl.DeviceIdType.MESH
DMA = pltpu.SemaphoreType.DMA


class Line:
    def __init__(self, n):
        self.n, self.ys = n, n // 8
        me = lax.axis_index("ctx")
        self.z, self.y, self.c = me // (2 * self.ys), me // 2 % self.ys, me % 2
        high = self.z // 2
        self.slots = [3 - 3 * high, 2 - high, self.z + 1 - 2 * (self.z % 2), self.z]
        self.inner = (self.z == 1) | (self.z == 2)
        self.outer = (self.z == 0) | (self.z == 3)
        self.side = (self.z + 1) // 2 % 2
        self.near = self.at(self.slots[2], self.y, self.c)
        self.far = self.at(self.z + 1 - 2 * high, self.y, self.c)
        self.core = self.at(self.z, self.y, 1 - self.c)

    def at(self, z, y, c):
        return {"ctx": (z * self.ys + y) * 2 + c}

    def others(self):
        return [(self.y + d) % self.ys for d in range(1, self.ys)]

    def greet(self):
        peers = [self.core, self.near] + [self.at(self.z, y, self.c) for y in self.others()]
        barrier = pltpu.get_barrier_semaphore()
        for peer in peers:
            pl.semaphore_signal(barrier, inc=1, device_id=peer, device_id_type=MESH)

        @pl.when(self.inner)
        def _():
            pl.semaphore_signal(barrier, inc=1, device_id=self.far, device_id_type=MESH)

        pl.semaphore_wait(barrier, len(peers) + self.side)


def remote(src, dst, send, recv, peer):
    return pltpu.make_async_remote_copy(src_ref=src, dst_ref=dst, send_sem=send, recv_sem=recv, device_id=peer, device_id_type=MESH)


class LineGather:
    def __init__(self, line, buf, sems):
        self.l, self.buf = line, buf
        self.zs, self.zr, self.ys, self.yr, self.ks, self.kr = sems

    @staticmethod
    def sems(n):
        ys = n // 8
        return [DMA((5,)), DMA((3,)), DMA((ys - 1, 4)), DMA((ys - 1, 4)), DMA((ys, 4)), DMA((ys, 4))]

    def move(self, z, y, c, send, recv, peer):
        ref = self.buf.at[z, y, c]
        return remote(ref, ref, send, recv, peer)

    def zcopy(self, i):
        l = self.l
        slot, peer, into = [(3, l.near, 0), (3, l.far, 1), (2, l.far, 2), (1, l.near, 1), (0, l.near, 2)][i]
        return self.move(l.slots[slot], l.y, l.c, self.zs.at[i], self.zr.at[into], peer)

    def ycopy(self, d, slot):
        l = self.l
        return self.move(l.slots[slot], l.y, l.c, self.ys.at[d, slot], self.yr.at[d, slot], l.at(l.z, l.others()[d], l.c))

    def kcopy(self, d, slot):
        l = self.l
        y = l.y if d == 0 else (l.y + l.ys - d) % l.ys
        return self.move(l.slots[slot], y, l.c, self.ks.at[d, slot], self.kr.at[d, slot], l.core)

    def spread(self, slot):
        for d in range(self.l.ys - 1):
            self.ycopy(d, slot).start()
        self.kcopy(0, slot).start()

    def start(self):
        self.zcopy(0).start()

        @pl.when(self.l.inner)
        def _():
            self.zcopy(1).start()

        self.spread(3)

    def z_step(self, r):
        self.zcopy((0, 3, 4)[r]).wait_recv()

        @pl.when(self.l.inner)
        def _():
            self.zcopy(2 + r).start()

        self.spread(2 - r)

    def y_step(self, slot):
        for d in range(self.l.ys - 1):
            self.ycopy(d, slot).wait_recv()
            self.kcopy(d + 1, slot).start()

    def run(self):
        self.start()
        for r in range(3):
            self.z_step(r)
            self.y_step(3 - r)
        self.y_step(0)

    def core_wait(self, slot):
        for d in range(self.l.ys):
            self.kcopy(d, slot).wait_recv()

    def finish(self):
        self.zcopy(0).wait_send()

        @pl.when(self.l.inner)
        def _():
            for i in range(1, 5):
                self.zcopy(i).wait_send()

        for slot in range(4):
            for d in range(self.l.ys - 1):
                self.ycopy(d, slot).wait_send()
            for d in range(self.l.ys):
                self.kcopy(d, slot).wait_send()


class LineScatter:
    def __init__(self, line, acc, kbuf, ybuf, zbuf, sems):
        self.l, self.acc, self.kbuf, self.ybuf, self.zbuf = line, acc, kbuf, ybuf, zbuf
        self.zs, self.zr, self.ys, self.yr, self.ks, self.kr = sems

    @staticmethod
    def sems(n):
        ys = n // 8
        return [DMA((3,)), DMA((2, 3)), DMA((ys - 1, 4)), DMA((ys - 1, 4)), DMA((ys, 4)), DMA((ys, 4))]

    @staticmethod
    def scratch(n, rows, cols):
        ys = n // 8
        return [pltpu.VMEM((4, ys, rows, cols), BF16), pltpu.VMEM((ys - 1, 4, rows, cols), BF16), pltpu.VMEM((2, 3, rows, cols), BF16)]

    def y_of(self, d):
        return self.l.y if d == 0 else self.l.others()[d - 1]

    def kcopy(self, d, slot):
        l = self.l
        z, y = l.slots[slot], self.y_of(d)
        return remote(self.acc.at[z, y, 1 - l.c], self.kbuf.at[z, y], self.ks.at[d, slot], self.kr.at[d, slot], l.core)

    def ycopy(self, d, slot):
        l = self.l
        z, y = l.slots[slot], self.y_of(d + 1)
        return remote(self.acc.at[z, y, l.c], self.ybuf.at[d, slot], self.ys.at[d, slot], self.yr.at[d, slot], l.at(l.z, y, l.c))

    def zcopy(self, slot):
        l = self.l
        return remote(self.acc.at[l.slots[slot], l.y, l.c], self.zbuf.at[l.side, slot], self.zs.at[slot], self.zr.at[l.side, slot], l.far if slot < 2 else l.near)

    def zwait(self, side, slot):
        buf = self.zbuf.at[side, slot]
        remote(buf, buf, self.zs.at[slot], self.zr.at[side, slot], self.l.near).wait_recv()
        return self.zbuf[side, slot].astype(F32)

    def own(self, slot):
        return (self.l.slots[slot], self.l.y, self.l.c)

    def core_start(self, slot):
        for d in range(self.l.ys - 1, -1, -1):
            self.kcopy(d, slot).start()

    def core_step(self, slot):
        l = self.l
        for d in list(range(1, l.ys)) + [0]:
            z, y = l.slots[slot], self.y_of(d)
            self.kcopy(d, slot).wait_recv()
            self.acc[z, y, l.c] = (self.acc[z, y, l.c].astype(F32) + self.kbuf[z, y].astype(F32)).astype(BF16)
            if d > 0:
                self.ycopy(d - 1, slot).start()

    def y_sum(self, slot):
        total = self.acc[self.own(slot)].astype(F32)
        for d in range(self.l.ys - 1):
            self.ycopy(d, slot).wait_recv()
            total = total + self.ybuf[d, slot].astype(F32)
        return total

    def z_step(self, slot):
        l, own = self.l, self.own(slot)
        total = self.y_sum(slot)
        self.acc[own] = total.astype(BF16)
        @pl.when(l.inner)
        def _():
            self.acc[own] = (self.acc[own].astype(F32) + self.zwait(*((0, slot) if slot < 2 else (1, 0)))).astype(BF16)

        self.zcopy(slot).start()

    def last(self, out):
        l = self.l
        out[...] = self.y_sum(3)

        @pl.when(l.inner)
        def _():
            out[...] += self.zwait(0, 2) + self.zwait(1, 1)

        @pl.when(l.outer)
        def _():
            out[...] += self.zwait(1, 2)

    def finish(self):
        for slot in range(4):
            for d in range(self.l.ys):
                self.kcopy(d, slot).wait_send()
            for d in range(self.l.ys - 1):
                self.ycopy(d, slot).wait_send()
        for slot in range(3):
            self.zcopy(slot).wait_send()


def line_gather_kernel(n, x_ref, o_ref, *sems):
    line = Line(n)
    g = LineGather(line, o_ref, sems)
    line.greet()
    o_ref[line.z, line.y, line.c] = x_ref[...]
    g.run()
    for slot in range(4):
        g.core_wait(slot)
    g.finish()


def line_gather(cid, n, x):
    out = pl.pallas_call(
        functools.partial(line_gather_kernel, n),
        out_shape=jax.ShapeDtypeStruct((4, n // 8, 2) + x.shape, x.dtype),
        in_specs=[pl.BlockSpec(memory_space=pltpu.VMEM)], out_specs=pl.BlockSpec(memory_space=pltpu.VMEM),
        scratch_shapes=LineGather.sems(n),
        compiler_params=pltpu.CompilerParams(collective_id=cid, has_side_effects=True, vmem_limit_bytes=56 << 20), name=f"line_gather{cid}")(x)
    return out.reshape((-1,) + x.shape[1:])


def line_scatter_kernel(n, v_ref, o_ref, acc, kbuf, ybuf, zbuf, *sems):
    line = Line(n)
    s = LineScatter(line, acc, kbuf, ybuf, zbuf, sems)
    acc[...] = v_ref[...]
    line.greet()
    for slot in range(4):
        s.core_start(slot)
    for slot in range(4):
        s.core_step(slot)
    for slot in range(3):
        s.z_step(slot)
    s.last(o_ref)
    s.finish()


def line_scatter(cid, n, v):
    rows, cols = v.shape[0] // n, v.shape[1]
    v = v.reshape((4, n // 8, 2, rows, cols))
    return pl.pallas_call(
        functools.partial(line_scatter_kernel, n),
        out_shape=jax.ShapeDtypeStruct((rows, cols), F32),
        in_specs=[pl.BlockSpec(memory_space=pltpu.VMEM)], out_specs=pl.BlockSpec(memory_space=pltpu.VMEM),
        scratch_shapes=[pltpu.VMEM(v.shape, BF16)] + LineScatter.scratch(n, rows, cols) + LineScatter.sems(n),
        compiler_params=pltpu.CompilerParams(collective_id=cid, has_side_effects=True, vmem_limit_bytes=56 << 20), name=f"line_scatter{cid}")(v)


def attend_kernel(r, kc, a_ref, b_ref, idq_ref, idk_ref, o_ref, t_ref, acc, tot):
    part = lax.rem(lax.axis_index("ctx"), r) if r > 1 else 0
    length = b_ref.shape[0]

    def per_queries(lb, _):
        qs = pl.ds(pl.multiple_of(lb * QB, QB), QB)
        a = a_ref[qs, :] * 0.125
        idq = idq_ref[qs, :]
        acc[...] = jnp.zeros_like(acc)
        tot[...] = jnp.zeros_like(tot)

        def per_keys(kb, _):
            ks = pl.ds(pl.multiple_of(kb * kc, kc), kc)
            b = b_ref[ks, :]
            s = lax.dot_general(a, b, NT, preferred_element_type=F32)
            w = jnp.where(idk_ref[:, ks] <= idq, jnp.exp(s), 0.0)
            t = w[:, :128]
            for i in range(1, kc // 128):
                t = t + w[:, i * 128 : (i + 1) * 128]
            tot[...] += t
            acc[...] += jnp.dot(w.astype(BF16), b, preferred_element_type=F32)
            return 0

        reach = (lb * r + part + 2) * QB
        lax.fori_loop(0, jnp.minimum((reach + kc - 1) // kc, length // kc), per_keys, 0)
        t = jnp.sum(tot[...], axis=-1, keepdims=True)
        t_ref[qs, :] = t
        o_ref[qs, :] = acc[...] / t
        return 0

    lax.fori_loop(0, a_ref.shape[0] // QB, per_queries, 0)


def attend(r, a, b, idq, idk):
    rows = a.shape[0]
    return pl.pallas_call(
        functools.partial(attend_kernel, r, min(1024, b.shape[0])),
        out_shape=(jax.ShapeDtypeStruct((rows, 128), F32), jax.ShapeDtypeStruct((rows, 1), F32)),
        scratch_shapes=[pltpu.VMEM((QB, 128), F32), pltpu.VMEM((QB, 128), F32)],
        compiler_params=pltpu.CompilerParams(vmem_limit_bytes=48 << 20),
        name="attend",
    )(a, b, idq, idk)


def attend_back_kernel(r, kc, a_ref, b_ref, do_ref, ratio_ref, idq_ref, idk_ref, dq_ref, dkv_ref, acc):
    part = lax.rem(lax.axis_index("ctx"), r) if r > 1 else 0
    length = b_ref.shape[0]
    dkv_ref[...] = jnp.zeros_like(dkv_ref)

    def per_queries(lb, _):
        qs = pl.ds(pl.multiple_of(lb * QB, QB), QB)
        a = a_ref[qs, :]
        scaled = a * 0.125
        do = do_ref[qs, :]
        ado = jnp.concatenate([a, do], axis=0)
        idq = idq_ref[:, qs]
        ratio = ratio_ref[:, qs]
        acc[...] = jnp.zeros_like(acc)

        def per_keys(kb, _):
            ks = pl.ds(pl.multiple_of(kb * kc, kc), kc)
            b = b_ref[ks, :]
            s = lax.dot_general(b, scaled, NT, preferred_element_type=F32)
            w = jnp.where(idk_ref[ks, :] <= idq, jnp.exp(s), 0.0)
            p = lax.dot_general(b, do, NT, preferred_element_type=F32)
            g = (w * (p - ratio)).astype(BF16)
            gw = jnp.concatenate([g, w.astype(BF16)], axis=1)
            dkv_ref[ks, :] += jnp.dot(gw, ado, preferred_element_type=F32)
            acc[...] += lax.dot_general(g, b, TN, preferred_element_type=F32)
            return 0

        reach = (lb * r + part + 2) * QB
        lax.fori_loop(0, jnp.minimum((reach + kc - 1) // kc, length // kc), per_keys, 0)
        dq_ref[qs, :] = acc[...]
        return 0

    lax.fori_loop(0, a_ref.shape[0] // QB, per_queries, 0)


def attend_back(r, a, b, do, ratio, idq, idk):
    rows, length = a.shape[0], b.shape[0]
    return pl.pallas_call(
        functools.partial(attend_back_kernel, r, min(1024, length)),
        out_shape=(jax.ShapeDtypeStruct((rows, 128), F32), jax.ShapeDtypeStruct((length, 128), F32)),
        scratch_shapes=[pltpu.VMEM((QB, 128), F32)],
        compiler_params=pltpu.CompilerParams(vmem_limit_bytes=48 << 20),
        name="attend_back",
    )(a, b, do, ratio, idq, idk)


def normalize(rows):
    centred = rows - jnp.mean(rows, axis=-1, keepdims=True)
    rstd = lax.rsqrt(jnp.mean(centred * centred, axis=-1, keepdims=True) + EPSILON)
    return centred * rstd, rstd


def normalize_back(grad, normed, rstd):
    return rstd * (
        grad
        - jnp.mean(grad, axis=-1, keepdims=True)
        - normed * jnp.mean(grad * normed, axis=-1, keepdims=True)
    )


def gelu_both(u):
    c = math.sqrt(2.0 / math.pi)
    t = jnp.tanh(c * (u + 0.044715 * (u * u * u)))
    half = 0.5 * (1.0 + t)
    return u * half, half + 0.5 * u * (1.0 - t * t) * (c * (1.0 + 3.0 * 0.044715 * (u * u)))


def exchange_ctx(v):
    return lax.all_to_all(v, "ctx", 0, 0, tiled=True)


def dot(x, y, dims=(((1,), (0,)), ((), ()))):
    return lax.dot_general(x, y, dims, preferred_element_type=F32)


def local(n_dp, n, inputs, cotangent, block_ids, ln1_gain, ln1_bias, w_qkv, b_qkv, w_out, b_out, ln2_gain, ln2_bias, w_fc, b_fc, w_proj, b_proj):
    tokens, width = inputs.shape[1:]
    length = n * tokens
    rows = w_qkv.shape[0]
    units = w_proj.shape[0]
    r = n // HEADS
    hd = width // HEADS
    me = lax.axis_index("ctx")
    head, part = me // r, me % r

    small = jnp.concatenate([ln1_gain, ln1_bias, b_qkv, b_out, ln2_gain, ln2_bias, b_fc, b_proj])
    small = lax.all_gather(small, ("dp", "ctx"), axis=0).astype(F32)
    cuts, at = [], 0
    for v in (ln1_gain, ln1_bias, b_qkv, b_out, ln2_gain, ln2_bias, b_fc, b_proj):
        cuts.append(small[:, at : at + v.shape[0]])
        at += v.shape[0]
    g1, c1, bqv, bo, g2, c2, bf, bp = cuts
    g1, c1, bqv, bo, g2, c2, bp = (v.reshape(1, -1) for v in (g1, c1, bqv, bo, g2, c2, bp))
    bf = lax.dynamic_index_in_dim(bf.reshape(n_dp, n, units), me, 1, keepdims=False).reshape(1, -1)
    bqv = lax.dynamic_index_in_dim(bqv.reshape(2, HEADS, hd), head, 1, keepdims=False)
    zeros = jnp.zeros((hd,), F32)
    bias = jnp.concatenate([bqv[0], zeros, zeros, bqv[1]])[None]

    def spread(w):
        got = exchange_ctx(jnp.transpose(w, (1, 0, 2)))
        return lax.all_gather(got, "dp", axis=0, tiled=True).reshape(width, -1)

    wq = w_qkv.reshape(rows, 3, HEADS, 1, hd)
    wq = jnp.stack([wq[:, 0], jnp.zeros_like(wq[:, 0]), wq[:, 1], wq[:, 2]], axis=3)
    wq = jnp.broadcast_to(wq.reshape(rows, HEADS, 1, 4 * hd), (rows, HEADS, r, 4 * hd))
    wq = spread(wq.reshape(rows, n, 4 * hd))
    wf = spread(jnp.transpose(w_fc.reshape(rows, n_dp, n, units), (0, 2, 1, 3)).reshape(rows, n, n_dp * units))
    wp = lax.all_gather(w_proj, "dp", axis=0, tiled=True)
    wo = lax.all_gather(w_out, ("dp", "ctx"), axis=0, tiled=True)

    x_all = line_gather(1, n, inputs[0]).astype(F32)
    marks = lax.all_gather(block_ids[0], "ctx", axis=0, tiled=True)
    normed, _ = normalize(x_all)
    first_low = (normed * g1 + c1).astype(BF16)
    qkv = (dot(first_low, wq) + bias).astype(BF16)
    a_all, b_all = qkv[:, : 2 * hd], qkv[:, 2 * hd :]

    def own_queries(v):
        if r == 1:
            return v
        split = v.reshape((length // QB // r, r, QB) + v.shape[1:])
        return lax.dynamic_index_in_dim(split, part, 1, keepdims=False).reshape((length // r,) + v.shape[1:])

    def all_queries(v):
        if r == 1:
            return v
        split = v.reshape((length // QB // r, 1, QB) + v.shape[1:])
        keep = (jnp.arange(r) == part).reshape((1, r, 1) + (1,) * (v.ndim - 1))
        return jnp.where(keep, split, 0).reshape((length,) + v.shape[1:])

    a, marks_q = own_queries(a_all), own_queries(marks)
    o, totals = attend(r, a, b_all, marks_q[:, None], marks[None])
    attended = o[:, hd:]
    low = all_queries(attended.astype(BF16))
    low = exchange_ctx(low.reshape(n, tokens, hd))
    low = low.reshape(HEADS, r, tokens, hd).sum(axis=1) if r > 1 else low
    attended_low = jnp.transpose(low, (1, 0, 2)).reshape(tokens, width)

    x = inputs[0].astype(F32)
    middle = x + dot(attended_low, wo) + bo
    n2, rstd2 = normalize(middle)
    second_low = line_gather(2, n, (n2 * g2 + c2).astype(BF16))
    hidden = dot(second_low, wf) + bf
    active, slope = gelu_both(hidden)
    active_low = active.astype(BF16)
    output = middle + line_scatter(3, n, dot(active_low, wp).astype(BF16)) + bp

    dy_all = line_gather(4, n, cotangent[0])
    dy = cotangent[0].astype(F32)
    hidden_grad = slope * dot(dy_all, wp, NT)
    hidden_low = hidden_grad.astype(BF16)
    wp_grad = dot(active_low, dy_all, TN)
    wf_grad = dot(second_low, hidden_low, TN)
    bf_grad = jnp.sum(hidden_low.astype(F32), axis=0)
    second_grad = line_scatter(5, n, dot(hidden_low, wf, NT).astype(BF16))

    middle_grad = dy + normalize_back(second_grad * g2, n2, rstd2)
    branch_low = middle_grad.astype(BF16)
    wo_grad = dot(attended_low, branch_low, TN)
    attended_grad = dot(branch_low, wo, NT)
    sent = jnp.transpose(attended_grad.astype(BF16).reshape(tokens, HEADS, 1, hd), (1, 2, 0, 3))
    sent = jnp.broadcast_to(sent, (HEADS, r, tokens, hd)).reshape(n, tokens, hd)
    grad = own_queries(exchange_ctx(sent).reshape(length, hd)).astype(F32)
    ratio = jnp.sum(grad * attended, axis=-1, keepdims=True) / totals
    do = jnp.concatenate([jnp.zeros_like(grad), grad / totals], axis=1).astype(BF16)
    dq, dkv = attend_back(r, a, b_all, do, ratio.reshape(1, -1), marks_q[None], marks[:, None])
    dq = all_queries(dq[:, :hd]) * 0.125
    if r > 1:
        groups = [[h * r + i for i in range(r)] for h in range(HEADS)]
        dq, dkv = lax.psum((dq, dkv), "ctx", axis_index_groups=groups)
    mixed = jnp.concatenate([dq, jnp.zeros_like(dq), dkv[:, :hd] * 0.125, dkv[:, hd:]], axis=1).astype(BF16)
    if r > 1:
        mixed = jnp.where(part == 0, mixed, jnp.zeros_like(mixed))
    first_grad = line_scatter(6, n, dot(mixed, wq, NT).astype(BF16))
    wq_grad = dot(first_low, mixed, TN)
    mixed_sum = jnp.sum(mixed.astype(F32), axis=0)

    n1, rstd1 = normalize(x)
    input_grad = middle_grad + normalize_back(first_grad * g1, n1, rstd1)

    def collect(g):
        got = lax.psum_scatter(g.astype(BF16), "dp", scatter_dimension=0, tiled=True)
        return exchange_ctx(got.reshape(n, rows, -1)).astype(F32)

    wq_own = collect(wq_grad).reshape(HEADS, r, rows, 4, hd).sum(axis=1)
    wq_own = jnp.stack([wq_own[:, :, 0], wq_own[:, :, 2], wq_own[:, :, 3]], axis=1)
    wq_own = jnp.transpose(wq_own, (2, 1, 0, 3)).reshape(rows, 3 * width)
    wf_own = jnp.transpose(collect(wf_grad).reshape(n, rows, n_dp, units), (1, 2, 0, 3)).reshape(rows, -1)
    wp_own = lax.psum_scatter(wp_grad, "dp", scatter_dimension=0, tiled=True)
    wo_own = lax.psum_scatter(wo_grad.astype(BF16), ("dp", "ctx"), scatter_dimension=0, tiled=True).astype(F32)

    column = lambda v: jnp.sum(v, axis=0)
    hot = (jnp.arange(n) == me).astype(F32)[:, None]
    bqv_grad = jnp.stack([mixed_sum[:hd], mixed_sum[3 * hd :]])
    hot_head = (jnp.arange(HEADS) == head).astype(F32)[None, :, None]
    pieces = [
        column(first_grad * n1),
        column(first_grad),
        (hot_head * bqv_grad[:, None]).reshape(-1),
        column(branch_low.astype(F32)),
        column(second_grad * n2),
        column(second_grad),
        (hot[None] * bf_grad.reshape(n_dp, 1, units)).reshape(-1),
        column(dy),
    ]
    pieces = [v.reshape(n_dp * n, -1) for v in pieces]
    mine = lax.psum_scatter(jnp.concatenate(pieces, axis=1), ("dp", "ctx"), scatter_dimension=0, tiled=True)[0]
    outs, at = [], 0
    for v in pieces:
        outs.append(mine[at : at + v.shape[1]])
        at += v.shape[1]
    g1g, c1g, bqvg, bog, g2g, c2g, bfg, bpg = outs
    return (
        output.astype(BF16)[None], input_grad.astype(BF16)[None], g1g, c1g, wq_own, bqvg, wo_own, bog, g2g, c2g, wf_own, bfg, wp_own, bpg,
    )


def solution(mesh):
    both = ("dp", "ctx")
    act, vec, mat = P("dp", "ctx", None), P(both), P(both, None)
    return jax.shard_map(
        functools.partial(local, mesh.shape["dp"], mesh.shape["ctx"]),
        mesh=mesh,
        in_specs=(act, act, P("dp", "ctx"), vec, vec, mat, vec, mat, vec, vec, vec, mat, vec, mat, vec),
        out_specs=(act, act, vec, vec, mat, vec, mat, vec, vec, vec, mat, vec, mat, vec),
        check_vma=False,
    )
```

```python
import functools
import math

import jax
import jax.numpy as jnp
from jax import lax
from jax.experimental import pallas as pl
from jax.experimental.pallas import tpu as pltpu
from jax.sharding import PartitionSpec as P

HEADS = 16
EPSILON = 1e-05
QB = 256
F32, BF16 = jnp.float32, jnp.bfloat16
NT = (((1,), (1,)), ((), ()))
TN = (((0,), (0,)), ((), ()))
MESH = pl.DeviceIdType.MESH
DMA = pltpu.SemaphoreType.DMA
VMEM_LIMIT = 60 << 20


def dot(x, y, dims=(((1,), (0,)), ((), ()))):
    return lax.dot_general(x, y, dims, preferred_element_type=F32)


def remote(src, dst, send, recv, peer):
    return pltpu.make_async_remote_copy(
        src_ref=src, dst_ref=dst, send_sem=send, recv_sem=recv, device_id=peer, device_id_type=MESH
    )


def greet(peers):
    barrier = pltpu.get_barrier_semaphore()
    for peer in peers:
        pl.semaphore_signal(barrier, inc=1, device_id=peer, device_id_type=MESH)
    pl.semaphore_wait(barrier, len(peers))


def greet_all(n_dp, n):
    barrier = pltpu.get_barrier_semaphore()
    flat = lax.axis_index("dp") * n + lax.axis_index("ctx")

    def signal(j, _):
        f = lax.rem(flat + j, n_dp * n)
        pl.semaphore_signal(barrier, inc=1, device_id={"dp": f // n, "ctx": f % n}, device_id_type=MESH)
        return 0

    lax.fori_loop(1, n_dp * n, signal, 0)
    pl.semaphore_wait(barrier, n_dp * n - 1)


class ToAll:
    def __init__(self, n_dp, n, block, into, sems, only_ctx=False):
        self.n, self.block, self.into, self.only = n, block, into, only_ctx
        self.send, self.recv = sems
        self.count = n if only_ctx else n_dp * n
        self.me = lax.axis_index("ctx") if only_ctx else lax.axis_index("dp") * n + lax.axis_index("ctx")

    def copy(self, j):
        f = lax.rem(self.me + j, self.count)
        peer = {"ctx": f} if self.only else {"dp": f // self.n, "ctx": f % self.n}
        return remote(self.block(f), self.into.at[self.me], self.send.at[j], self.recv.at[j], peer)

    def each(self, act):
        def step(j, _):
            act(self.copy(j))
            return 0

        lax.fori_loop(1, self.count, step, 0)

    def start(self):
        self.each(lambda c: c.start())

    def wait_recv(self):
        self.each(lambda c: c.wait_recv())

    def wait_send(self):
        self.each(lambda c: c.wait_send())


def own_bit(dim):
    axis, b = dim
    return lax.axis_index(axis) // (1 << b) % 2


def partner(dim):
    axis, b = dim
    return {axis: lax.axis_index(axis) + (1 - 2 * own_bit(dim)) * (1 << b)}


def cube_plan(n, rows):
    top = n.bit_length() - 2
    dims = [("dp", 0)] + [("ctx", b) for b in range(top - 1, 0, -1)] + [("ctx", 0)]
    links = len(dims) - 1
    size = -(-rows // (16 * links)) * 16
    cuts = [min(rows, size * i) for i in range(links)] + [rows]
    return dims, [(cuts[i], cuts[i + 1], [(i + j) % links for j in range(links)]) for i in range(links)], True


def all_plan(n_dp, n, rows):
    dims = [("dp", b) for b in range(n_dp.bit_length() - 2, -1, -1)] + [("ctx", b) for b in range(n.bit_length() - 2, -1, -1)]
    links = len(dims) - 1
    order = list(range(links))
    half = rows // 2
    return dims, [(0, half, order), (half, rows, order[2:] + order[:2])], False


class Pairwise:
    def __init__(self, plan, sems):
        self.dims, self.orders, self.core_first = plan
        self.links = len(self.dims) - 1
        self.link_send, self.link_recv, self.core_send, self.core_recv = sems
        self.mine = [own_bit(d) for d in self.dims]

    def index(self, links, core, tail=()):
        links = tuple(links)
        return ((core,) + links if self.core_first else links + (core,)) + tuple(tail)

    def peers(self):
        return [partner(d) for d in self.dims]


class Gather(Pairwise):
    def __init__(self, plan, buf, sems):
        super().__init__(plan, sems)
        self.buf = buf

    @staticmethod
    def sems(plan):
        links, parts = len(plan[0]) - 1, len(plan[1])
        return [DMA((parts, links))] * 2 + [DMA((parts * links + 1,))] * 2

    def own(self):
        return self.index(self.mine[:-1], self.mine[-1])

    def region(self, part, done, flip=None):
        lo, hi, _ = self.orders[part]
        where = [slice(None) if i in done else (1 - m if i == flip else m) for i, m in enumerate(self.mine[:-1])]
        return self.index(where, self.mine[-1], (pl.ds(lo, hi - lo),))

    def copy(self, where, send, recv, dim):
        return remote(self.buf.at[where], self.buf.at[where], send, recv, partner(self.dims[dim]))

    def link(self, part, k):
        order = self.orders[part][2]
        return self.copy(self.region(part, order[:k]), self.link_send.at[part, k], self.link_recv.at[part, k], order[k])

    def core(self, part, k):
        order = self.orders[part][2]
        at = part * self.links + k + 1
        return self.copy(self.region(part, order[:k], order[k]), self.core_send.at[at], self.core_recv.at[at], self.links)

    def core_own(self):
        return self.copy(self.own(), self.core_send.at[0], self.core_recv.at[0], self.links)

    def start(self):
        for part in range(len(self.orders)):
            self.link(part, 0).start()
        self.core_own().start()

    def step(self, k):
        for part in range(len(self.orders)):
            self.link(part, k).wait_recv()
            if k + 1 < self.links:
                self.link(part, k + 1).start()
            self.core(part, k).start()

    def core_wait(self):
        self.core_own().wait_recv()
        for part in range(len(self.orders)):
            for k in range(self.links):
                self.core(part, k).wait_recv()

    def finish(self):
        self.core_own().wait_send()
        for part in range(len(self.orders)):
            for k in range(self.links):
                self.link(part, k).wait_send()
                self.core(part, k).wait_send()


class Scatter(Pairwise):
    def __init__(self, plan, terms, bufs, sems):
        super().__init__(plan, sems)
        self.terms, self.run, self.bufs = terms, bufs[0], bufs[1:]

    @staticmethod
    def sems(plan):
        links, parts = len(plan[0]) - 1, len(plan[1])
        return [DMA((parts, links))] * 2 + [DMA((2,))] * 2

    @staticmethod
    def scratch(plan, rows, cols):
        links = len(plan[0]) - 1
        return [pltpu.VMEM((2,) * links + (rows, cols), BF16)] + [
            pltpu.VMEM((2,) * (links - 1 - k) + (rows, cols), BF16) for k in range(links)
        ]

    def core(self, half):
        where = (half,) + (slice(None),) * (self.links - 1)
        return remote(
            self.terms.at[self.index(where, 1 - self.mine[-1])], self.run.at[where],
            self.core_send.at[half], self.core_recv.at[half], partner(self.dims[-1]),
        )

    def where(self, part, k, flip):
        lo, hi, order = self.orders[part]
        order = order[::-1]
        d, gone = order[k], order[:k]
        at = []
        for i in range(self.links):
            if i == d:
                at.append(1 - self.mine[i] if flip else self.mine[i])
            else:
                at.append(self.mine[i] if i in gone else slice(None))
        return at, d, (pl.ds(lo, hi - lo),)

    def link(self, part, k):
        at, d, tail = self.where(part, k, True)
        return remote(
            self.run.at[tuple(at) + tail], self.bufs[k].at[(slice(None),) * (self.links - 1 - k) + tail],
            self.link_send.at[part, k], self.link_recv.at[part, k], partner(self.dims[d]),
        )

    def add_core(self, half):
        self.core(half).wait_recv()
        inner = self.links - 1
        for i in range(1 << inner):
            at = (half,) + tuple((i >> (inner - 1 - j)) & 1 for j in range(inner))
            own = self.terms[self.index(at, self.mine[-1])]
            self.run[at] = (self.run[at].astype(F32) + own.astype(F32)).astype(BF16)

    def start_links(self):
        for part in range(len(self.orders)):
            self.link(part, 0).start()

    def step(self, k, out=None):
        for part in range(len(self.orders)):
            at, _, tail = self.where(part, k, False)
            self.link(part, k).wait_recv()
            free = self.links - 1 - k
            for i in range(1 << free):
                idx = [(i >> (free - 1 - j)) & 1 for j in range(free)]
                rest = iter(idx)
                to = tuple(next(rest) if isinstance(v, slice) else v for v in at) + tail
                total = self.run[to].astype(F32) + self.bufs[k][tuple(idx) + tail].astype(F32)
                if k + 1 < self.links:
                    self.run[to] = total.astype(BF16)
                else:
                    out[tail[0], :] = total
            if k + 1 < self.links:
                self.link(part, k + 1).start()

    def finish(self):
        for half in range(2):
            self.core(half).wait_send()
        for part in range(len(self.orders)):
            for k in range(self.links):
                self.link(part, k).wait_send()


class Line:
    def __init__(self, n):
        self.n, self.ys = n, n // 8
        me = lax.axis_index("ctx")
        self.z, self.y, self.c = me // (2 * self.ys), me // 2 % self.ys, me % 2
        high = self.z // 2
        self.slots = [3 - 3 * high, 2 - high, self.z + 1 - 2 * (self.z % 2), self.z]
        self.inner = (self.z == 1) | (self.z == 2)
        self.outer = (self.z == 0) | (self.z == 3)
        self.side = (self.z + 1) // 2 % 2
        self.near = self.at(self.slots[2], self.y, self.c)
        self.far = self.at(self.z + 1 - 2 * high, self.y, self.c)
        self.core = self.at(self.z, self.y, 1 - self.c)

    def at(self, z, y, c):
        return {"ctx": (z * self.ys + y) * 2 + c}

    def others(self):
        return [(self.y + d) % self.ys for d in range(1, self.ys)]


class LineGather:
    def __init__(self, line, buf, sems):
        self.l, self.buf = line, buf
        self.zs, self.zr, self.ys, self.yr, self.ks, self.kr = sems

    @staticmethod
    def sems(n):
        ys = n // 8
        return [DMA((5,)), DMA((3,)), DMA((ys - 1, 4)), DMA((ys - 1, 4)), DMA((ys, 4)), DMA((ys, 4))]

    def move(self, z, y, c, send, recv, peer):
        ref = self.buf.at[z, y, c]
        return remote(ref, ref, send, recv, peer)

    def zcopy(self, i):
        l = self.l
        slot, peer, into = [(3, l.near, 0), (3, l.far, 1), (2, l.far, 2), (1, l.near, 1), (0, l.near, 2)][i]
        return self.move(l.slots[slot], l.y, l.c, self.zs.at[i], self.zr.at[into], peer)

    def ycopy(self, d, slot):
        l = self.l
        return self.move(l.slots[slot], l.y, l.c, self.ys.at[d, slot], self.yr.at[d, slot], l.at(l.z, l.others()[d], l.c))

    def kcopy(self, d, slot):
        l = self.l
        y = l.y if d == 0 else (l.y + l.ys - d) % l.ys
        return self.move(l.slots[slot], y, l.c, self.ks.at[d, slot], self.kr.at[d, slot], l.core)

    def spread(self, slot):
        for d in range(self.l.ys - 1):
            self.ycopy(d, slot).start()
        self.kcopy(0, slot).start()

    def start(self):
        self.zcopy(0).start()

        @pl.when(self.l.inner)
        def _():
            self.zcopy(1).start()

        self.spread(3)

    def z_step(self, r):
        self.zcopy((0, 3, 4)[r]).wait_recv()

        @pl.when(self.l.inner)
        def _():
            self.zcopy(2 + r).start()

        self.spread(2 - r)

    def y_step(self, slot):
        for d in range(self.l.ys - 1):
            self.ycopy(d, slot).wait_recv()
            self.kcopy(d + 1, slot).start()

    def run(self):
        self.start()
        for r in range(3):
            self.z_step(r)
            self.y_step(3 - r)
        self.y_step(0)

    def core_wait(self, slot):
        for d in range(self.l.ys):
            self.kcopy(d, slot).wait_recv()

    def finish(self):
        self.zcopy(0).wait_send()

        @pl.when(self.l.inner)
        def _():
            for i in range(1, 5):
                self.zcopy(i).wait_send()

        for slot in range(4):
            for d in range(self.l.ys - 1):
                self.ycopy(d, slot).wait_send()
            for d in range(self.l.ys):
                self.kcopy(d, slot).wait_send()


class LineScatter:
    def __init__(self, line, acc, kbuf, ybuf, zbuf, sems):
        self.l, self.acc, self.kbuf, self.ybuf, self.zbuf = line, acc, kbuf, ybuf, zbuf
        self.zs, self.zr, self.ys, self.yr, self.ks, self.kr = sems

    @staticmethod
    def sems(n):
        ys = n // 8
        return [DMA((3,)), DMA((2, 3)), DMA((ys - 1, 4)), DMA((ys - 1, 4)), DMA((ys, 4)), DMA((ys, 4))]

    @staticmethod
    def scratch(n, rows, cols):
        ys = n // 8
        return [pltpu.VMEM((4, ys, rows, cols), BF16), pltpu.VMEM((ys - 1, 4, rows, cols), BF16), pltpu.VMEM((2, 3, rows, cols), BF16)]

    def y_of(self, d):
        return self.l.y if d == 0 else self.l.others()[d - 1]

    def kcopy(self, d, slot):
        l = self.l
        z, y = l.slots[slot], self.y_of(d)
        return remote(self.acc.at[z, y, 1 - l.c], self.kbuf.at[z, y], self.ks.at[d, slot], self.kr.at[d, slot], l.core)

    def ycopy(self, d, slot):
        l = self.l
        z, y = l.slots[slot], self.y_of(d + 1)
        return remote(self.acc.at[z, y, l.c], self.ybuf.at[d, slot], self.ys.at[d, slot], self.yr.at[d, slot], l.at(l.z, y, l.c))

    def zcopy(self, slot):
        l = self.l
        return remote(self.acc.at[l.slots[slot], l.y, l.c], self.zbuf.at[l.side, slot], self.zs.at[slot], self.zr.at[l.side, slot], l.far if slot < 2 else l.near)

    def zwait(self, side, slot):
        buf = self.zbuf.at[side, slot]
        remote(buf, buf, self.zs.at[slot], self.zr.at[side, slot], self.l.near).wait_recv()
        return self.zbuf[side, slot].astype(F32)

    def own(self, slot):
        return (self.l.slots[slot], self.l.y, self.l.c)

    def core_start(self, slot):
        for d in range(self.l.ys - 1, -1, -1):
            self.kcopy(d, slot).start()

    def core_step(self, slot):
        l = self.l
        for d in list(range(1, l.ys)) + [0]:
            z, y = l.slots[slot], self.y_of(d)
            self.kcopy(d, slot).wait_recv()
            self.acc[z, y, l.c] = (self.acc[z, y, l.c].astype(F32) + self.kbuf[z, y].astype(F32)).astype(BF16)
            if d > 0:
                self.ycopy(d - 1, slot).start()

    def y_sum(self, slot):
        total = self.acc[self.own(slot)].astype(F32)
        for d in range(self.l.ys - 1):
            self.ycopy(d, slot).wait_recv()
            total = total + self.ybuf[d, slot].astype(F32)
        return total

    def z_step(self, slot):
        l, own = self.l, self.own(slot)
        total = self.y_sum(slot)
        self.acc[own] = total.astype(BF16)
        @pl.when(l.inner)
        def _():
            self.acc[own] = (self.acc[own].astype(F32) + self.zwait(*((0, slot) if slot < 2 else (1, 0)))).astype(BF16)

        self.zcopy(slot).start()

    def last(self, out):
        l = self.l
        out[...] = self.y_sum(3)

        @pl.when(l.inner)
        def _():
            out[...] += self.zwait(0, 2) + self.zwait(1, 1)

        @pl.when(l.outer)
        def _():
            out[...] += self.zwait(1, 2)

    def finish(self):
        for slot in range(4):
            for d in range(self.l.ys):
                self.kcopy(d, slot).wait_send()
            for d in range(self.l.ys - 1):
                self.ycopy(d, slot).wait_send()
        for slot in range(3):
            self.zcopy(slot).wait_send()


G1, C1, BQV, IDS, BO, G2, C2, BF, BP = range(9)


def put_ids(n, small_all, first, row, col):
    tokens = small_all.shape[2]
    for j in range(n):
        ids = small_all[first + j].astype(F32)[IDS : IDS + 1, :]
        row[:, j * tokens : (j + 1) * tokens] = ids
        col[j * tokens : (j + 1) * tokens, :] = jnp.transpose(jnp.broadcast_to(ids, (tokens, tokens)))[:, :1]


def half_row(tile_row, odd, high):
    lane = lax.broadcasted_iota(jnp.int32, tile_row.shape, 1)
    turned = pltpu.roll(tile_row, 64, 1)
    moved = jnp.where((odd == 1) == high, tile_row, turned)
    return jnp.where((lane >= 64) == high, moved, 0.0)


def normalize(rows):
    centred = rows - jnp.mean(rows, axis=-1, keepdims=True)
    rstd = lax.rsqrt(jnp.mean(centred * centred, axis=-1, keepdims=True) + EPSILON)
    return centred * rstd, rstd


def group_of(n, f):
    d, j = f // n, f % n
    return d % 2 * (n // 2) + j % (n // 2), d // 2 * 2 + j // (n // 2)


def group_peer(n, i, count):
    d, j = lax.axis_index("dp"), lax.axis_index("ctx")
    g = lax.rem(d // 2 * 2 + j // (n // 2) + i, count)
    return g, {"dp": g // 2 * 2 + d % 2, "ctx": g % 2 * (n // 2) + j % (n // 2)}


def front_kernel(n_dp, n, r, spread, cube, whole, *refs):
    refs = list(refs)
    take = lambda k: [refs.pop(0) for _ in range(k)]
    x_ref, small_ref, dy_ref = take(3)
    if spread:
        wqb, wfb, wpb, wob = take(4)
    else:
        (wq_all,) = take(1)
    small_all, first, a_ref, b_ref, o_ref, t_ref, att, dy_all = take(8)
    if spread:
        wq_all, wf_all, wp_all, wo_all = take(4)
    xbuf, prm, bqv, bias, idrow, idcol, packed, acc, tot = take(9)
    line_sems, small_sems, dy_sems, att_sems = take(6), take(2), take(4), take(2)
    if spread:
        wq_sems, wf_sems, wp_sems, wo_sems = take(2), take(2), take(2), take(4)

    tokens, width = x_ref.shape
    count = n_dp * n
    d, me = lax.axis_index("dp"), lax.axis_index("ctx")
    flat = d * n + me
    head, part = me // r, me % r
    line = Line(n)

    xg = LineGather(line, xbuf, line_sems)
    small = ToAll(n_dp, n, lambda f: small_ref, small_all, small_sems)
    dyg = Gather(cube, dy_all, dy_sems)
    xbuf[line.z, line.y, line.c] = x_ref[...]
    small_all[flat] = small_ref[...]
    dy_all[dyg.own()] = dy_ref[...]
    if spread:
        wq = ToAll(n_dp, n, lambda f: wqb.at[f % n], wq_all, wq_sems)
        wf = ToAll(n_dp, n, lambda f: wfb.at[group_of(n, f)[0]], wf_all, wf_sems)
        wog = Gather(whole, wo_all, wo_sems)
        rank, group = group_of(n, flat)
        wq_all[flat] = wqb[me]
        wf_all[flat] = wfb[rank]
        wp_all[group] = wpb[...]
        wo_all[wog.own()] = wob[...]
        wps = []
        for i in range(1, n_dp):
            _, peer = group_peer(n, i, n_dp)
            wps.append(remote(wpb, wp_all.at[group], wp_sems[0].at[i], wp_sems[1].at[i], peer))

    greet_all(n_dp, n)
    xg.start()
    small.start()
    if spread:
        wq.start()
    xg.z_step(0)
    if spread:
        for c in wps:
            c.start()
    xg.y_step(3)
    small.wait_recv()
    per = count * 128 // width
    for k in range(width // 128):
        tile = jnp.sum(small_all[k * per : (k + 1) * per].astype(F32), axis=0)
        prm[:, k * 128 : (k + 1) * 128] = tile[:8]
    per = count * 128 // (2 * width)
    for k in range(2 * width // 128):
        tile = jnp.sum(small_all[k * per : (k + 1) * per].astype(F32), axis=0)
        bqv[k : k + 1, :] = tile[BQV : BQV + 1]
    odd = head % 2
    bias[:, :128] = half_row(bqv[pl.ds(head // 2, 1), :], odd, False)
    bias[:, 128:] = half_row(bqv[pl.ds(width // 128 + head // 2, 1), :], odd, True)
    put_ids(n, small_all, d * n, idrow, idcol)
    if spread:
        wq.wait_recv()
    per_z = n // 4

    def project(slot):
        z = line.slots[slot]

        def one(i, _):
            rows = xbuf[z, i // 2, i % 2].astype(F32)
            normed, _ = normalize(rows)
            low = (normed * prm[G1 : G1 + 1, :] + prm[C1 : C1 + 1, :]).astype(BF16)
            at = pl.ds(pl.multiple_of((z * per_z + i) * tokens, tokens), tokens)
            first[at, :] = low
            return 0

        lax.fori_loop(0, per_z, one, 0)
        at = pl.ds(pl.multiple_of(z * per_z * tokens, per_z * tokens), per_z * tokens)
        qkv = (dot(first[at, :], wq_all[...].reshape(width, 256)) + bias[...]).astype(BF16)
        a_ref[at, :] = qkv[:, :128]
        b_ref[at, :] = qkv[:, 128:]

    xg.z_step(1)
    xg.y_step(2)
    xg.core_wait(3)
    project(3)
    xg.z_step(2)
    xg.y_step(1)
    xg.core_wait(2)
    project(2)
    xg.y_step(0)
    dyg.start()
    if spread:
        wf.start()
        wog.start()
    xg.core_wait(1)
    project(1)
    xg.core_wait(0)
    project(0)
    dyg.step(0)
    if spread:
        wog.step(0)

    length = b_ref.shape[0]
    kc = min(1024, length)
    half = tokens // 2
    if r > 1:
        packed[...] = jnp.zeros_like(packed)

    def per_queries(lb, _):
        gq = lb * r + part
        qs = pl.ds(pl.multiple_of(gq * QB, QB), QB)
        a = a_ref[qs, :] * 0.125
        ids = idcol[qs, :]
        acc[...] = jnp.zeros_like(acc)
        tot[...] = jnp.zeros_like(tot)

        def per_keys(kb, _):
            ks = pl.ds(pl.multiple_of(kb * kc, kc), kc)
            b = b_ref[ks, :]
            s = dot(a, b, NT)
            w = jnp.where(idrow[:, ks] <= ids, jnp.exp(s), 0.0)
            t = w[:, :128]
            for i in range(1, kc // 128):
                t = t + w[:, i * 128 : (i + 1) * 128]
            tot[...] += t
            acc[...] += dot(w.astype(BF16), b)
            return 0

        lax.fori_loop(0, jnp.minimum(((gq + 2) * QB + kc - 1) // kc, length // kc), per_keys, 0)
        t = jnp.sum(tot[...], axis=-1, keepdims=True)
        at = pl.ds(pl.multiple_of(lb * QB, QB), QB)
        t_ref[at, :] = t
        o = acc[...] / t
        o_ref[at, :] = o
        lane = lax.broadcasted_iota(jnp.int32, (half, 128), 1)
        for i in range(QB // tokens):
            lo, hi = o[i * tokens : i * tokens + half], o[i * tokens + half : (i + 1) * tokens]
            packed[gq * (QB // tokens) + i] = jnp.where(lane < 64, pltpu.roll(lo, 64, 1), hi).astype(BF16)
        return 0

    blocks = length // QB // r
    cuts = [0, blocks // 2, blocks * 3 // 4, blocks]
    for k in range(3):
        lax.fori_loop(cuts[k], cuts[k + 1], per_queries, 0)
        if k + 1 < min(3, dyg.links):
            dyg.step(k + 1)
            if spread:
                wog.step(k + 1)
    out = ToAll(n_dp, n, lambda f: packed.at[f], att, att_sems, True)
    att[me] = packed[me]
    out.start()
    for k in range(3, dyg.links):
        dyg.step(k)
    if spread:
        for k in range(3, wog.links):
            wog.step(k)
    out.wait_recv()
    dyg.core_wait()
    if spread:
        wf.wait_recv()
        for c in wps:
            c.wait_recv()
        wog.core_wait()
        for part_ in (wq, wf, wog):
            (part_.finish if part_ is wog else part_.wait_send)()
        for c in wps:
            c.wait_send()
    small.wait_send()
    out.wait_send()
    xg.finish()
    dyg.finish()


def front(n_dp, n, r, x, small, dy, weights, blocks):
    tokens, width = x.shape
    count, length = n_dp * n, n * tokens
    spread = weights is None
    cube = cube_plan(n, tokens)
    whole = all_plan(n_dp, n, 32)
    shape = jax.ShapeDtypeStruct
    outs = [
        shape((count, 16, 128), BF16), shape((length, width), BF16), shape((length, 128), BF16), shape((length, 128), BF16),
        shape((length // r, 128), F32), shape((length // r, 1), F32), shape((n, tokens // 2, 128), BF16),
        shape((2,) * len(cube[0]) + (tokens, width), BF16),
    ]
    sems = LineGather.sems(n) + [DMA((count,))] * 2 + Gather.sems(cube) + [DMA((n,))] * 2
    ins = [x, small, dy]
    if spread:
        wq, wf, wp, wo = blocks
        whole = all_plan(n_dp, n, wo.shape[0])
        outs += [
            shape((count,) + wq.shape[1:], BF16), shape((count,) + wf.shape[1:], BF16), shape((n_dp,) + wp.shape, BF16),
            shape((2,) * len(whole[0]) + wo.shape, BF16),
        ]
        sems += [DMA((count,))] * 4 + [DMA((n_dp,))] * 2 + Gather.sems(whole)
        ins += list(blocks)
    else:
        ins += [weights]
    vm = pl.BlockSpec(memory_space=pltpu.VMEM)
    return pl.pallas_call(
        functools.partial(front_kernel, n_dp, n, r, spread, cube, whole),
        out_shape=outs,
        in_specs=[vm] * len(ins),
        out_specs=[vm] * len(outs),
        scratch_shapes=[
            pltpu.VMEM((4, n // 8, 2, tokens, width), BF16), pltpu.VMEM((8, width), F32), pltpu.VMEM((2 * width // 128, 128), F32),
            pltpu.VMEM((1, 256), F32), pltpu.VMEM((1, length), F32), pltpu.VMEM((length, 1), F32),
            pltpu.VMEM((n, tokens // 2, 128), BF16), pltpu.VMEM((QB, 128), F32), pltpu.VMEM((QB, 128), F32),
        ] + sems,
        compiler_params=pltpu.CompilerParams(collective_id=1, has_side_effects=True, vmem_limit_bytes=VMEM_LIMIT),
        name="front",
    )(*ins)


def gelu_both(u):
    c = math.sqrt(2.0 / math.pi)
    t = jnp.tanh(c * (u + 0.044715 * (u * u * u)))
    half = 0.5 * (1.0 + t)
    return u * half, half + 0.5 * u * (1.0 - t * t) * (c * (1.0 + 3.0 * 0.044715 * (u * u)))


def ffn_kernel(plan, s_ref, dy_ref, wf_ref, wp_ref, bf_ref, sg_ref, out_ref, wp_grad, wf_grad, bf_grad, sbuf, grads, act, hid, acc, *rest):
    links = len(plan[0]) - 1
    bufs, rest = rest[: links + 1], rest[links + 1 :]
    g = Gather(plan, sbuf, rest[:4])
    s = Scatter(plan, acc, bufs, rest[4:])
    tokens, width = s_ref.shape
    quarter = (1 << (links - 1)) * tokens
    span = (1 << (links - 1),) + (tokens, width)
    sbuf[g.own()] = s_ref[...]
    greet(g.peers())
    g.start()
    core = g.mine[-1]

    def rows(c, a):
        return pl.ds(pl.multiple_of((2 * c + a) * quarter, quarter), quarter)

    inner = (slice(None),) * (links - 1)

    def grad_part(i):
        dy = dy_ref[(i // 2, i % 2) + inner].reshape(quarter, width)
        grads[rows(i // 2, i % 2), :] = dot(dy, wp_ref[...], NT)

    for k in range(links):
        grad_part(k)
        g.step(k)
    for k in range(links, 4):
        grad_part(k)
    g.core_wait()
    bf_grad[...] = jnp.zeros_like(bf_grad)

    def hidden_part(c, a):
        at = rows(c, a)
        low = sbuf[(c, a) + inner].reshape(quarter, width)
        active, slope = gelu_both(dot(low, wf_ref[...]) + bf_ref[...])
        act[at, :] = active.astype(BF16)
        h = (slope * grads[at, :]).astype(BF16)
        hid[at, :] = h
        bf_grad[...] += jnp.sum(h.astype(F32), axis=0, keepdims=True)
        acc[(c, a) + inner] = dot(h, wf_ref[...], NT).astype(BF16).reshape((2,) * (links - 1) + (tokens, width))

    for a in range(2):
        hidden_part(1 - core, a)
        s.core(a).start()
    for a in range(2):
        hidden_part(core, a)
        s.add_core(a)
    s.start_links()

    def weight_grads(k):
        at = slice(k * 256, (k + 1) * 256)
        low = sbuf[..., at].reshape(4 * quarter, 256)
        wf_grad[at, :] = jnp.transpose(dot(hid[...], low, TN)).astype(BF16)
        dy = dy_ref[..., at].reshape(4 * quarter, 256)
        wp_grad[:, at] = dot(act[...], dy, TN).astype(BF16)

    def out_part(i):
        at = rows(i // 2, i % 2)
        out_ref[(i // 2, i % 2) + inner] = dot(act[at, :], wp_ref[...]).astype(BF16).reshape((2,) * (links - 1) + (tokens, width))

    out_part(0)
    out_part(1)
    out_part(2)
    out_part(3)
    for k in range(links):
        s.step(k, sg_ref)
        if k < 2:
            weight_grads(2 * k)
            weight_grads(2 * k + 1)
    s.finish()
    g.finish()


def ffn(n, second_low, dy_all, wf, wp, bf):
    tokens, width = second_low.shape
    units = wf.shape[1]
    plan = cube_plan(n, tokens)
    block = (2,) * len(plan[0])
    length = n * tokens
    shape = jax.ShapeDtypeStruct
    vm = pl.BlockSpec(memory_space=pltpu.VMEM)
    return pl.pallas_call(
        functools.partial(ffn_kernel, plan),
        out_shape=[
            shape((tokens, width), F32), shape(block + (tokens, width), BF16), shape((units, width), BF16),
            shape((width, units), BF16), shape((1, units), F32),
        ],
        in_specs=[vm] * 5,
        out_specs=[vm] * 5,
        scratch_shapes=[
            pltpu.VMEM(block + (tokens, width), BF16), pltpu.VMEM((length, units), F32), pltpu.VMEM((length, units), BF16),
            pltpu.VMEM((length, units), BF16), pltpu.VMEM(block + (tokens, width), BF16),
        ] + Scatter.scratch(plan, tokens, width) + Gather.sems(plan) + Scatter.sems(plan),
        compiler_params=pltpu.CompilerParams(collective_id=2, has_side_effects=True, vmem_limit_bytes=VMEM_LIMIT),
        name="ffn",
    )(second_low, dy_all, wf, wp, bf)


def normalize_back(grad, normed, rstd):
    return rstd * (
        grad
        - jnp.mean(grad, axis=-1, keepdims=True)
        - normed * jnp.mean(grad * normed, axis=-1, keepdims=True)
    )


def back_kernel(n_dp, n, r, spread, cube, whole, *refs):
    refs = list(refs)
    take = lambda k: [refs.pop(0) for _ in range(k)]
    agb, a_ref, b_ref, o_ref, t_ref, small_all, wq_ref, first, part_out, x_ref, mg_ref, g1_ref, msgs = take(13)
    if spread:
        wfg, wpg, wog = take(3)
    out_ref, ig_ref, sums = take(3)
    if spread:
        wq_got, wf_got, wp_got, wo_own = take(4)
    else:
        (wq_sum,) = take(1)
    ag, idrow, idcol, mixed, dqacc, dkv, acc, kbuf, ybuf, zbuf, fg, got, msg, columns, column_sem = take(15)
    links = len(cube[0]) - 1
    out_bufs = take(links + 1)
    if r > 1:
        dkv_got = take(1)[0]
        pair_sems = take(2)
    ag_sems, line_sems, out_sems, msg_sems = take(2), take(6), take(4), take(2)
    if spread:
        wq_part, wq_sems, wf_sems, wp_sems = *take(1), take(2), take(2), take(2)
        wo_bufs = take(len(whole[0]))
        wo_sems = take(4)

    tokens, width = x_ref.shape
    length = b_ref.shape[0]
    count = n_dp * n
    d, me = lax.axis_index("dp"), lax.axis_index("ctx")
    flat = d * n + me
    head, part = me // r, me % r
    line = Line(n)
    kc = min(1024, length)
    half = tokens // 2

    grads = ToAll(n_dp, n, lambda f: agb.at[f], ag, ag_sems, True)
    outs = Scatter(cube, part_out, out_bufs, out_sems)
    ag[me] = agb[me]
    if spread:
        wf = ToAll(n_dp, n, lambda f: wfg.at[f], wf_got, wf_sems)
        wq = ToAll(n_dp, n, lambda f: wq_part.at[f], wq_got, wq_sems)
        wo = Scatter(whole, wog, wo_bufs, wo_sems)
        wf_got[flat] = wfg[flat]
        group = group_of(n, flat)[1]
        wp_got[group] = wpg[group]
        wps = []
        for i in range(1, n_dp):
            g, peer = group_peer(n, i, n_dp)
            wps.append(remote(wpg.at[g], wp_got.at[group], wp_sems[0].at[i], wp_sems[1].at[i], peer))
    greet_all(n_dp, n)
    grads.start()
    for h in range(2):
        outs.core(h).start()
    put_ids(n, small_all, d * n, idrow, idcol)
    dkv[...] = jnp.zeros_like(dkv)
    if r > 1:
        mixed[...] = jnp.zeros_like(mixed)
    for h in range(2):
        outs.add_core(h)
    grads.wait_recv()
    outs.start_links()
    if spread:
        for h in range(2):
            wo.core(h).start()
        for c in wps:
            c.start()

    def per_queries(lb, _):
        gq = lb * r + part
        qs = pl.ds(pl.multiple_of(gq * QB, QB), QB)
        at = pl.ds(pl.multiple_of(lb * QB, QB), QB)
        lane = lax.broadcasted_iota(jnp.int32, (half, 128), 1)
        pieces = []
        for i in range(QB // tokens):
            block = ag[gq * (QB // tokens) + i].astype(F32)
            pieces += [jnp.where(lane >= 64, pltpu.roll(block, 64, 1), 0.0), jnp.where(lane >= 64, block, 0.0)]
        grad = jnp.concatenate(pieces, axis=0)
        inverse = 1.0 / t_ref[at, :]
        upper = lax.broadcasted_iota(jnp.int32, (QB, 128), 1) >= 64
        ratio = jnp.sum(jnp.where(upper, grad * o_ref[at, :], 0.0), axis=-1, keepdims=True) * inverse
        ratio = jnp.transpose(jnp.broadcast_to(ratio, (QB, 128)))[:1, :]
        do = (grad * inverse).astype(BF16)
        a = a_ref[qs, :]
        scaled = a * 0.125
        ado = jnp.concatenate([a, do], axis=0)
        ids = idrow[:, qs]
        dqacc[...] = jnp.zeros_like(dqacc)

        def per_keys(kb, _):
            ks = pl.ds(pl.multiple_of(kb * kc, kc), kc)
            b = b_ref[ks, :]
            w = jnp.where(idcol[ks, :] <= ids, jnp.exp(dot(b, scaled, NT)), 0.0)
            g = (w * (dot(b, do, NT) - ratio)).astype(BF16)
            dkv[ks, :] += dot(jnp.concatenate([g, w.astype(BF16)], axis=1), ado)
            dqacc[...] += dot(g, b, TN)
            return 0

        lax.fori_loop(0, jnp.minimum(((gq + 2) * QB + kc - 1) // kc, length // kc), per_keys, 0)
        mixed[qs, :128] = jnp.where(upper, 0.0, dqacc[...] * 0.125).astype(BF16)
        return 0

    blocks = length // QB // r
    cuts = [0, blocks * 3 // 8, blocks * 5 // 8, blocks * 3 // 4, blocks]
    for k in range(4):
        lax.fori_loop(cuts[k], cuts[k + 1], per_queries, 0)
        if k < links:
            outs.step(k, out_ref)
        if k == 0 and spread:
            wf.start()
            for h in range(2):
                wo.add_core(h)
            wo.start_links()

    low = lax.broadcasted_iota(jnp.int32, (length, 128), 1) < 64
    total = dkv[...]
    if r > 1:
        both = remote(dkv, dkv_got, pair_sems[0], pair_sems[1], line.core)
        both.start()
        both.wait()
        total = jnp.where(part == 0, total + dkv_got[...], 0.0)
    mixed[:, 128:] = jnp.where(low, total * 0.125, total).astype(BF16)

    rs = LineScatter(line, acc, kbuf, ybuf, zbuf, line_sems)
    per_z = n // 4 * tokens

    def first_grad(slot):
        z = line.slots[slot]
        at = pl.ds(pl.multiple_of(z * per_z, per_z), per_z)
        acc[z] = dot(mixed[at, :], wq_ref[...], NT).astype(BF16).reshape(n // 8, 2, tokens, width)
        rs.core_start(slot)

    def fetch(k):
        return pltpu.make_async_copy(first.at[:, pl.ds(k * 256, 256)], columns, column_sem)

    fetch(0).start()
    first_grad(0)
    for slot in range(1, 4):
        first_grad(slot)
        rs.core_step(slot - 1)
    rs.core_step(3)
    column = jnp.sum(mixed[...].astype(F32), axis=0, keepdims=True)
    odd = head % 2
    q_row = half_row(column[:, :128], 0, False)
    q_row = jnp.where(odd == 1, pltpu.roll(q_row, 64, 1), q_row)
    v_row = half_row(column[:, 128:], 1, True)
    v_row = jnp.where(odd == 1, v_row, pltpu.roll(v_row, 64, 1))

    def wq_grad(k):
        at = slice(k * 256, (k + 1) * 256)
        fetch(k).wait()
        g = jnp.transpose(dot(mixed[...], columns[...], TN))
        if k < 3:
            fetch(k + 1).start()
        if spread:
            rows = width // count
            wq_part[256 // rows * k : 256 // rows * (k + 1)] = g.astype(BF16).reshape(256 // rows, rows, 256)
        else:
            wq_sum[at, :] = g

    for k in range(3):
        wq_grad(k)
        rs.z_step(k)
    wq_grad(3)
    if spread:
        wq_got[flat] = wq_part[flat]
        wq.start()
        for k in range(wo.links):
            wo.step(k, wo_own)
    rs.last(fg)

    x = x_ref[...].astype(F32)
    n1, rstd1 = normalize(x)
    grad = fg[...]
    gain = jnp.sum(grad * n1, axis=0, keepdims=True)
    shift = jnp.sum(grad, axis=0, keepdims=True)
    per = 128 * count // width

    for k in range(width // 128):
        rows = jnp.concatenate([gain[:, k * 128 : (k + 1) * 128], shift[:, k * 128 : (k + 1) * 128]], axis=0)

        def fill(i, _, k=k, rows=rows):
            msg[k * per + i, 0:2, :] = rows
            return 0

        lax.fori_loop(0, per, fill, 0)

    def rest(f, _):
        tile = f * 2 * width // count // 128
        bqv = jnp.where(tile == head // 2, q_row, 0.0) + jnp.where(tile == width // 128 + head // 2, v_row, 0.0)
        msg[f, 2:6, :] = msgs[f, 2:6, :]
        msg[f, 6:7, :] = bqv
        msg[f, 7:8, :] = msgs[f, 7:8, :]
        return 0

    lax.fori_loop(0, count, rest, 0)
    tell_all = ToAll(n_dp, n, lambda f: msg.at[f], got, msg_sems)
    tell_all.start()
    got[flat] = msg[flat]
    ig_ref[...] = (mg_ref[...] + normalize_back(grad * g1_ref[...], n1, rstd1)).astype(BF16)
    tell_all.wait_recv()
    sums[...] = jnp.sum(got[...], axis=0)
    tell_all.wait_send()
    if spread:
        wf.wait_recv()
        wq.wait_recv()
        for c in wps:
            c.wait()
        wf.wait_send()
        wq.wait_send()
        wo.finish()
    grads.wait_send()
    outs.finish()
    rs.finish()


def back(n_dp, n, r, agb, a, b, o, t, small_all, wq, first, part_out, x, mg, g1, msgs, grads):
    tokens, width = x.shape
    count, length = n_dp * n, n * tokens
    spread = grads is not None
    cube = cube_plan(n, tokens)
    whole = None
    shape = jax.ShapeDtypeStruct
    ins = [agb, a, b, o, t, small_all, wq, first, part_out, x, mg, g1, msgs]
    outs = [shape((tokens, width), F32), shape((tokens, width), BF16), shape((8, 128), F32)]
    scratch = [
        pltpu.VMEM((n, tokens // 2, 128), BF16), pltpu.VMEM((1, length), F32), pltpu.VMEM((length, 1), F32),
        pltpu.VMEM((length, 256), BF16), pltpu.VMEM((QB, 128), F32), pltpu.VMEM((length, 128), F32),
        pltpu.VMEM((4, n // 8, 2, tokens, width), BF16),
    ] + LineScatter.scratch(n, tokens, width) + [
        pltpu.VMEM((tokens, width), F32), pltpu.VMEM((count, 8, 128), F32), pltpu.VMEM((count, 8, 128), F32),
        pltpu.VMEM((length, 256), BF16), DMA,
    ] + Scatter.scratch(cube, tokens, width)
    if r > 1:
        scratch += [pltpu.VMEM((length, 128), F32), DMA, DMA]
    scratch += [DMA((n,))] * 2 + LineScatter.sems(n) + Scatter.sems(cube) + [DMA((count,))] * 2
    if spread:
        wfg, wpg, wog = grads
        rows = width // count
        whole = all_plan(n_dp, n, rows)
        ins += [wfg, wpg, wog]
        outs += [
            shape((count, rows, 256), BF16), shape(wfg.shape, BF16), shape(wpg.shape, BF16), shape((rows, width), F32),
        ]
        scratch += [pltpu.VMEM((count, rows, 256), BF16)] + [DMA((count,))] * 4 + [DMA((n_dp,))] * 2
        scratch += Scatter.scratch(whole, rows, width) + Scatter.sems(whole)
    else:
        outs += [shape((width, 256), F32)]
    vm = pl.BlockSpec(memory_space=pltpu.VMEM)
    return pl.pallas_call(
        functools.partial(back_kernel, n_dp, n, r, spread, cube, whole),
        out_shape=outs,
        in_specs=[pl.BlockSpec(memory_space=pl.ANY) if v is first else vm for v in ins],
        out_specs=[vm] * len(outs),
        scratch_shapes=scratch,
        compiler_params=pltpu.CompilerParams(collective_id=3, has_side_effects=True, vmem_limit_bytes=VMEM_LIMIT),
        name="back",
    )(*ins)


def place(v, flat):
    pieces = 128 // v.shape[0]
    return jnp.where(jnp.arange(128) // v.shape[0] == flat % pieces, jnp.tile(v, pieces), 0)


def local(n_dp, n, inputs, cotangent, block_ids, ln1_gain, ln1_bias, w_qkv, b_qkv, w_out, b_out, ln2_gain, ln2_bias, w_fc, b_fc, w_proj, b_proj):
    tokens, width = inputs.shape[1:]
    count = n_dp * n
    rows = w_qkv.shape[0]
    units = w_proj.shape[0]
    r = n // HEADS
    hd = width // HEADS
    d, me = lax.axis_index("dp"), lax.axis_index("ctx")
    flat = d * n + me
    head = me // r
    both = ("dp", "ctx")
    x, dy = inputs[0], cotangent[0]
    halves = (n_dp // 2, 2, 2, n // 2)

    small = [place(v, flat) for v in (ln1_gain, ln1_bias, b_qkv)] + [block_ids[0].astype(BF16)]
    small += [place(v, flat) for v in (b_out, ln2_gain, ln2_bias, b_fc, b_proj)]
    small = jnp.pad(jnp.stack(small), ((0, 16 - len(small)), (0, 0)))

    def heads_of(w):
        w = w.reshape(w.shape[0], 3, HEADS, 1, hd)
        w = jnp.stack([w[:, 0], jnp.zeros_like(w[:, 0]), w[:, 1], w[:, 2]], axis=3)
        return w.reshape(w.shape[0], HEADS, 4 * hd)

    spread = rows % 16 == 0
    if spread:
        wq = jnp.repeat(jnp.transpose(heads_of(w_qkv), (1, 0, 2)), r, axis=0)
        wf = jnp.transpose(w_fc.reshape((rows,) + halves + (units,)), (2, 4, 0, 1, 3, 5)).reshape(n, rows, n_dp * units)
        weights, blocks = None, (wq, wf, w_proj, w_out)
    else:
        full = lax.all_gather(w_qkv, both, axis=0, tiled=True)
        weights = lax.dynamic_index_in_dim(heads_of(full), head, 1, keepdims=False)
        blocks = None
        wf = lax.all_gather(w_fc, both, axis=0, tiled=True).reshape((width,) + halves + (units,))
        wf = lax.dynamic_index_in_dim(wf, d % 2, 2, keepdims=False)
        wf = lax.dynamic_index_in_dim(wf, me % (n // 2), 3, keepdims=False).reshape(width, n_dp * units)
        wp = lax.all_gather(w_proj, both, axis=0, tiled=True).reshape(halves + (units, width))
        wp = lax.dynamic_index_in_dim(wp, d % 2, 1, keepdims=False)
        wp = lax.dynamic_index_in_dim(wp, me % (n // 2), 2, keepdims=False).reshape(n_dp * units, width)
        wo = lax.all_gather(w_out, both, axis=0, tiled=True)

    got = front(n_dp, n, r, x, small, dy, weights, blocks)
    small_all, first, a, b, o, t, att, dy_all = got[:8]
    if spread:
        wq, wf, wp, wo = got[8:]
        wq, wf, wp, wo = wq.reshape(width, -1), wf.reshape(width, -1), wp.reshape(-1, width), wo.reshape(width, width)
    else:
        wq = weights

    def vector(row, size):
        tiles = small_all[:, row].astype(F32).reshape(-1, 128 // size, 128)
        return jnp.sum(tiles, axis=1).reshape(1, -1)

    g1, bo, g2, c2, bp = (vector(k, rows) for k in (G1, BO, G2, C2, BP))
    bf = vector(BF, units).reshape(halves + (units,))
    bf = lax.dynamic_index_in_dim(bf, d % 2, 1, keepdims=False)
    bf = lax.dynamic_index_in_dim(bf, me % (n // 2), 2, keepdims=False).reshape(1, -1)

    att = att.reshape(HEADS, r, tokens // 2, 2, hd)
    att = att[:, 0] if r == 1 else att.sum(axis=1)
    attended_low = jnp.transpose(att, (2, 1, 0, 3)).reshape(tokens, width)
    middle = x.astype(F32) + dot(attended_low, wo) + bo
    n2, rstd2 = normalize(middle)
    second_low = (n2 * g2 + c2).astype(BF16)

    second_grad, part_out, wp_grad, wf_grad, bf_grad = ffn(n, second_low, dy_all, wf, wp, bf)

    dy = dy.astype(F32)
    middle_grad = dy + normalize_back(second_grad * g2, n2, rstd2)
    branch_low = middle_grad.astype(BF16)
    wo_grad = dot(attended_low, branch_low, TN).astype(BF16)
    agb = dot(branch_low, wo, NT).astype(BF16).reshape(2, tokens // 2, HEADS, hd)
    agb = jnp.transpose(agb, (2, 1, 0, 3)).reshape(HEADS, tokens // 2, 2 * hd)
    agb = jnp.repeat(agb, r, axis=0)

    bf_full = bf_grad.reshape(n_dp // 2, 1, 2, 1, units)
    hot = (jnp.arange(2) == d % 2).reshape(1, 2, 1, 1, 1) & (jnp.arange(n // 2) == me % (n // 2)).reshape(1, 1, 1, -1, 1)
    lines = [jnp.sum(v, axis=0).reshape(count, -1) for v in (branch_low.astype(F32), second_grad * n2, second_grad, dy)]
    lines.append(jnp.where(hot, bf_full, 0.0).reshape(count, units))
    lines = [jnp.pad(v, ((0, 0), (0, 128 - v.shape[1]))) for v in lines]
    nothing = jnp.zeros((count, 128), F32)
    msgs = jnp.stack([nothing, nothing] + lines[:4] + [nothing, lines[4]], axis=1)

    if spread:
        whole = (2,) * (count.bit_length() - 1) + (rows, width)
        grads = (wf_grad.reshape(count, rows, -1), wp_grad.reshape(n_dp, units, width), wo_grad.reshape(whole))
    else:
        grads = None
    got = back(n_dp, n, r, agb, a, b, o, t, small_all, wq, first, part_out, x, middle_grad, g1, msgs, grads)
    out_sum, input_grad, sums = got[:3]
    output = (middle + out_sum + bp).astype(BF16)
    if spread:
        wq_own, wf_own, wp_own, wo_own = got[3:]
        wq_own = jnp.sum(wq_own.astype(F32).reshape(n_dp, HEADS, r, rows, 4, hd), axis=(0, 2))
        wq_own = jnp.stack([wq_own[:, :, 0], wq_own[:, :, 2], wq_own[:, :, 3]], axis=1)
        wq_own = jnp.transpose(wq_own, (2, 1, 0, 3)).reshape(rows, 3 * width)
        wf_own = jnp.sum(wf_own.astype(F32).reshape(halves + (rows, n_dp // 2, 2, units)), axis=(0, 2))
        wf_own = jnp.transpose(wf_own, (2, 3, 0, 4, 1, 5)).reshape(rows, -1)
        wp_own = jnp.sum(wp_own.astype(F32), axis=0)
    else:
        owned = lambda v: lax.psum_scatter(v, both, scatter_dimension=0, tiled=True)
        g = got[3].reshape(width, 4, 1, hd)
        g = jnp.stack([g[:, 0], g[:, 2], g[:, 3]], axis=1)
        wq_own = owned(jnp.where((jnp.arange(HEADS) == head).reshape(1, 1, -1, 1), g, 0.0).reshape(width, 3 * width))
        g = wf_grad.astype(F32).reshape(width, n_dp // 2, 1, 2, 1, units)
        wf_own = owned(jnp.where(hot[None], g, 0.0).reshape(width, -1))
        g = wp_grad.astype(F32).reshape(n_dp // 2, 1, 2, 1, units, width)
        wp_own = owned(jnp.where(hot[..., None], g, 0.0).reshape(-1, width))
        wo_own = owned(wo_grad.astype(F32))

    def cut(row, size):
        return lax.dynamic_slice(sums[row], (flat * size % 128,), (size,))

    g1g, c1g, bqvg = cut(0, rows), cut(1, rows), cut(6, 2 * rows)
    bog, g2g, c2g, bpg = (sums[k, :rows] for k in range(2, 6))
    bfg = sums[7, :units]
    return (
        output[None], input_grad[None], g1g, c1g, wq_own, bqvg, wo_own, bog, g2g, c2g, wf_own, bfg, wp_own, bpg,
    )


def solution(mesh):
    both = ("dp", "ctx")
    act, vec, mat = P("dp", "ctx", None), P(both), P(both, None)
    return jax.shard_map(
        functools.partial(local, mesh.shape["dp"], mesh.shape["ctx"]),
        mesh=mesh,
        in_specs=(act, act, P("dp", "ctx"), vec, vec, mat, vec, mat, vec, vec, vec, mat, vec, mat, vec),
        out_specs=(act, act, vec, vec, mat, vec, mat, vec, vec, vec, mat, vec, mat, vec),
        check_vma=False,
    )
```

```python
import functools
import math

import jax
import jax.numpy as jnp
from jax import lax
from jax.experimental import pallas as pl
from jax.experimental.pallas import tpu as pltpu
from jax.sharding import PartitionSpec as P

HEADS = 16
EPSILON = 1e-05
QB = 256
F32, BF16 = jnp.float32, jnp.bfloat16
NT = (((1,), (1,)), ((), ()))
TN = (((0,), (0,)), ((), ()))
MESH = pl.DeviceIdType.MESH
DMA = pltpu.SemaphoreType.DMA
VMEM_LIMIT = 60 << 20


def dot(x, y, dims=(((1,), (0,)), ((), ()))):
    return lax.dot_general(x, y, dims, preferred_element_type=F32)


def remote(src, dst, send, recv, peer):
    return pltpu.make_async_remote_copy(
        src_ref=src, dst_ref=dst, send_sem=send, recv_sem=recv, device_id=peer, device_id_type=MESH
    )


class Greet:
    def __init__(self, n_dp, n, peers=None):
        self.barrier = pltpu.get_barrier_semaphore()
        self.count = n_dp * n - 1 if peers is None else len(peers)
        for peer in peers or ():
            pl.semaphore_signal(self.barrier, inc=1, device_id=peer, device_id_type=MESH)
        if peers is None:
            flat = lax.axis_index("dp") * n + lax.axis_index("ctx")

            def signal(j, _):
                f = lax.rem(flat + j, n_dp * n)
                pl.semaphore_signal(self.barrier, inc=1, device_id={"dp": f // n, "ctx": f % n}, device_id_type=MESH)
                return 0

            lax.fori_loop(1, n_dp * n, signal, 0)

    def wait(self):
        pl.semaphore_wait(self.barrier, self.count)


class ToAll:
    def __init__(self, n_dp, n, block, into, sems, only_ctx=False):
        self.n, self.block, self.into, self.only = n, block, into, only_ctx
        self.send, self.recv = sems
        self.count = n if only_ctx else n_dp * n
        self.me = lax.axis_index("ctx") if only_ctx else lax.axis_index("dp") * n + lax.axis_index("ctx")

    def copy(self, j):
        f = lax.rem(self.me + j, self.count)
        peer = {"ctx": f} if self.only else {"dp": f // self.n, "ctx": f % self.n}
        return remote(self.block(f), self.into.at[self.me], self.send.at[j], self.recv.at[j], peer)

    def each(self, act):
        def step(j, _):
            act(self.copy(j))
            return 0

        lax.fori_loop(1, self.count, step, 0)

    def start(self):
        self.each(lambda c: c.start())

    def wait_recv(self):
        self.each(lambda c: c.wait_recv())

    def wait_send(self):
        self.each(lambda c: c.wait_send())


def own_bit(dim):
    axis, b = dim
    return lax.axis_index(axis) // (1 << b) % 2


def partner(dim):
    axis, b = dim
    return {axis: lax.axis_index(axis) + (1 - 2 * own_bit(dim)) * (1 << b)}


def cube_plan(n, rows):
    top = n.bit_length() - 2
    dims = [("dp", 0)] + [("ctx", b) for b in range(top - 1, 0, -1)] + [("ctx", 0)]
    links = len(dims) - 1
    size = -(-rows // (16 * links)) * 16
    cuts = [min(rows, size * i) for i in range(links)] + [rows]
    return dims, [(cuts[i], cuts[i + 1], [(i + j) % links for j in range(links)]) for i in range(links)], True


def all_plan(n_dp, n, rows):
    dims = [("dp", b) for b in range(n_dp.bit_length() - 2, -1, -1)] + [("ctx", b) for b in range(n.bit_length() - 2, -1, -1)]
    links, own = len(dims) - 1, n_dp.bit_length() - 1
    return dims, [(0, rows, list(range(own, links)) + list(range(own)))], False


class Pairwise:
    def __init__(self, plan, sems):
        self.dims, self.orders, self.core_first = plan
        self.links = len(self.dims) - 1
        self.link_send, self.link_recv, self.core_send, self.core_recv = sems
        self.mine = [own_bit(d) for d in self.dims]

    def index(self, links, core, tail=()):
        links = tuple(links)
        return ((core,) + links if self.core_first else links + (core,)) + tuple(tail)

    def peers(self):
        return [partner(d) for d in self.dims]


class Gather(Pairwise):
    def __init__(self, plan, buf, sems):
        super().__init__(plan, sems)
        self.buf = buf

    @staticmethod
    def sems(plan):
        links, parts = len(plan[0]) - 1, len(plan[1])
        return [DMA((parts, links))] * 2 + [DMA((parts * links + 1,))] * 2

    def own(self):
        return self.index(self.mine[:-1], self.mine[-1])

    def region(self, part, done, flip=None):
        lo, hi, _ = self.orders[part]
        where = [slice(None) if i in done else (1 - m if i == flip else m) for i, m in enumerate(self.mine[:-1])]
        return self.index(where, self.mine[-1], (pl.ds(lo, hi - lo),))

    def copy(self, where, send, recv, dim):
        return remote(self.buf.at[where], self.buf.at[where], send, recv, partner(self.dims[dim]))

    def link(self, part, k):
        order = self.orders[part][2]
        return self.copy(self.region(part, order[:k]), self.link_send.at[part, k], self.link_recv.at[part, k], order[k])

    def core(self, part, k):
        order = self.orders[part][2]
        at = part * self.links + k + 1
        return self.copy(self.region(part, order[:k], order[k]), self.core_send.at[at], self.core_recv.at[at], self.links)

    def core_own(self):
        return self.copy(self.own(), self.core_send.at[0], self.core_recv.at[0], self.links)

    def start(self):
        for part in range(len(self.orders)):
            self.link(part, 0).start()
        self.core_own().start()

    def step(self, k):
        for part in range(len(self.orders)):
            self.link(part, k).wait_recv()
            if k + 1 < self.links:
                self.link(part, k + 1).start()
            self.core(part, k).start()

    def core_wait(self):
        self.core_own().wait_recv()
        for part in range(len(self.orders)):
            for k in range(self.links):
                self.core(part, k).wait_recv()

    def finish(self):
        self.core_own().wait_send()
        for part in range(len(self.orders)):
            for k in range(self.links):
                self.link(part, k).wait_send()
                self.core(part, k).wait_send()


class Scatter(Pairwise):
    def __init__(self, plan, terms, bufs, sems, own=None):
        super().__init__(plan, sems)
        self.terms, self.run, self.bufs, self.own = terms, bufs[0], bufs[1:], own

    def fetch_own(self, sem):
        source = self.terms.at[self.index((slice(None),) * self.links, self.mine[-1])]
        return pltpu.make_async_copy(source, self.own, sem)

    @staticmethod
    def sems(plan):
        links, parts = len(plan[0]) - 1, len(plan[1])
        return [DMA((parts, links))] * 2 + [DMA((2,))] * 2

    @staticmethod
    def scratch(plan, rows, cols):
        links = len(plan[0]) - 1
        return [pltpu.VMEM((2,) * links + (rows, cols), BF16)] + [
            pltpu.VMEM((2,) * (links - 1 - k) + (rows, cols), BF16) for k in range(links)
        ]

    def core(self, half):
        where = (half,) + (slice(None),) * (self.links - 1)
        return remote(
            self.terms.at[self.index(where, 1 - self.mine[-1])], self.run.at[where],
            self.core_send.at[half], self.core_recv.at[half], partner(self.dims[-1]),
        )

    def where(self, part, k, flip):
        lo, hi, order = self.orders[part]
        order = order[::-1]
        d, gone = order[k], order[:k]
        at = []
        for i in range(self.links):
            if i == d:
                at.append(1 - self.mine[i] if flip else self.mine[i])
            else:
                at.append(self.mine[i] if i in gone else slice(None))
        return at, d, (pl.ds(lo, hi - lo),)

    def link(self, part, k):
        at, d, tail = self.where(part, k, True)
        return remote(
            self.run.at[tuple(at) + tail], self.bufs[k].at[(slice(None),) * (self.links - 1 - k) + tail],
            self.link_send.at[part, k], self.link_recv.at[part, k], partner(self.dims[d]),
        )

    def add_core(self, half):
        self.core(half).wait_recv()
        inner = self.links - 1
        for i in range(1 << inner):
            at = (half,) + tuple((i >> (inner - 1 - j)) & 1 for j in range(inner))
            own = self.terms[self.index(at, self.mine[-1])] if self.own is None else self.own[at]
            self.run[at] = (self.run[at].astype(F32) + own.astype(F32)).astype(BF16)

    def start_links(self):
        for part in range(len(self.orders)):
            self.link(part, 0).start()

    def step(self, k, out=None):
        for part in range(len(self.orders)):
            at, _, tail = self.where(part, k, False)
            self.link(part, k).wait_recv()
            free = self.links - 1 - k
            for i in range(1 << free):
                idx = [(i >> (free - 1 - j)) & 1 for j in range(free)]
                rest = iter(idx)
                to = tuple(next(rest) if isinstance(v, slice) else v for v in at) + tail
                total = self.run[to].astype(F32) + self.bufs[k][tuple(idx) + tail].astype(F32)
                if k + 1 < self.links:
                    self.run[to] = total.astype(BF16)
                else:
                    out[tail[0], :] = total
            if k + 1 < self.links:
                self.link(part, k + 1).start()

    def finish(self):
        for half in range(2):
            self.core(half).wait_send()
        for part in range(len(self.orders)):
            for k in range(self.links):
                self.link(part, k).wait_send()


class Line:
    def __init__(self, n):
        self.n, self.ys = n, n // 8
        me = lax.axis_index("ctx")
        self.z, self.y, self.c = me // (2 * self.ys), me // 2 % self.ys, me % 2
        high = self.z // 2
        self.slots = [3 - 3 * high, 2 - high, self.z + 1 - 2 * (self.z % 2), self.z]
        self.inner = (self.z == 1) | (self.z == 2)
        self.outer = (self.z == 0) | (self.z == 3)
        self.side = (self.z + 1) // 2 % 2
        self.near = self.at(self.slots[2], self.y, self.c)
        self.far = self.at(self.z + 1 - 2 * high, self.y, self.c)
        self.core = self.at(self.z, self.y, 1 - self.c)

    def at(self, z, y, c):
        return {"ctx": (z * self.ys + y) * 2 + c}

    def others(self):
        return [(self.y + d) % self.ys for d in range(1, self.ys)]


class LineGather:
    def __init__(self, line, buf, sems):
        self.l, self.buf = line, buf
        self.zs, self.zr, self.ys, self.yr, self.ks, self.kr = sems

    @staticmethod
    def sems(n):
        ys = n // 8
        return [DMA((5,)), DMA((3,)), DMA((ys - 1, 4)), DMA((ys - 1, 4)), DMA((ys, 4)), DMA((ys, 4))]

    def move(self, z, y, c, send, recv, peer):
        ref = self.buf.at[z, y, c]
        return remote(ref, ref, send, recv, peer)

    def zcopy(self, i):
        l = self.l
        slot, peer, into = [(3, l.near, 0), (3, l.far, 1), (2, l.far, 2), (1, l.near, 1), (0, l.near, 2)][i]
        return self.move(l.slots[slot], l.y, l.c, self.zs.at[i], self.zr.at[into], peer)

    def ycopy(self, d, slot):
        l = self.l
        return self.move(l.slots[slot], l.y, l.c, self.ys.at[d, slot], self.yr.at[d, slot], l.at(l.z, l.others()[d], l.c))

    def kcopy(self, d, slot):
        l = self.l
        y = l.y if d == 0 else (l.y + l.ys - d) % l.ys
        return self.move(l.slots[slot], y, l.c, self.ks.at[d, slot], self.kr.at[d, slot], l.core)

    def spread(self, slot):
        for d in range(self.l.ys - 1):
            self.ycopy(d, slot).start()
        self.kcopy(0, slot).start()

    def start(self):
        self.zcopy(0).start()

        @pl.when(self.l.inner)
        def _():
            self.zcopy(1).start()

        self.spread(3)

    def z_step(self, r):
        self.zcopy((0, 3, 4)[r]).wait_recv()

        @pl.when(self.l.inner)
        def _():
            self.zcopy(2 + r).start()

        self.spread(2 - r)

    def y_step(self, slot):
        for d in range(self.l.ys - 1):
            self.ycopy(d, slot).wait_recv()
            self.kcopy(d + 1, slot).start()

    def run(self):
        self.start()
        for r in range(3):
            self.z_step(r)
            self.y_step(3 - r)
        self.y_step(0)

    def core_wait(self, slot):
        for d in range(self.l.ys):
            self.kcopy(d, slot).wait_recv()

    def finish(self):
        self.zcopy(0).wait_send()

        @pl.when(self.l.inner)
        def _():
            for i in range(1, 5):
                self.zcopy(i).wait_send()

        for slot in range(4):
            for d in range(self.l.ys - 1):
                self.ycopy(d, slot).wait_send()
            for d in range(self.l.ys):
                self.kcopy(d, slot).wait_send()


class LineScatter:
    def __init__(self, line, acc, kbuf, ybuf, zbuf, sems):
        self.l, self.acc, self.kbuf, self.ybuf, self.zbuf = line, acc, kbuf, ybuf, zbuf
        self.zs, self.zr, self.ys, self.yr, self.ks, self.kr = sems

    @staticmethod
    def sems(n):
        ys = n // 8
        return [DMA((3,)), DMA((2, 3)), DMA((ys - 1, 4)), DMA((ys - 1, 4)), DMA((ys, 4)), DMA((ys, 4))]

    @staticmethod
    def scratch(n, rows, cols):
        ys = n // 8
        return [pltpu.VMEM((4, ys, rows, cols), BF16), pltpu.VMEM((ys - 1, 4, rows, cols), BF16), pltpu.VMEM((2, 3, rows, cols), BF16)]

    def y_of(self, d):
        return self.l.y if d == 0 else self.l.others()[d - 1]

    def kcopy(self, d, slot):
        l = self.l
        z, y = l.slots[slot], self.y_of(d)
        return remote(self.acc.at[z, y, 1 - l.c], self.kbuf.at[z, y], self.ks.at[d, slot], self.kr.at[d, slot], l.core)

    def ycopy(self, d, slot):
        l = self.l
        z, y = l.slots[slot], self.y_of(d + 1)
        return remote(self.acc.at[z, y, l.c], self.ybuf.at[d, slot], self.ys.at[d, slot], self.yr.at[d, slot], l.at(l.z, y, l.c))

    def zcopy(self, slot):
        l = self.l
        return remote(self.acc.at[l.slots[slot], l.y, l.c], self.zbuf.at[l.side, slot], self.zs.at[slot], self.zr.at[l.side, slot], l.far if slot < 2 else l.near)

    def zwait(self, side, slot):
        buf = self.zbuf.at[side, slot]
        remote(buf, buf, self.zs.at[slot], self.zr.at[side, slot], self.l.near).wait_recv()
        return self.zbuf[side, slot].astype(F32)

    def own(self, slot):
        return (self.l.slots[slot], self.l.y, self.l.c)

    def core_start(self, slot):
        for d in range(self.l.ys - 1, -1, -1):
            self.kcopy(d, slot).start()

    def core_step(self, slot):
        l = self.l
        for d in list(range(1, l.ys)) + [0]:
            z, y = l.slots[slot], self.y_of(d)
            self.kcopy(d, slot).wait_recv()
            self.acc[z, y, l.c] = (self.acc[z, y, l.c].astype(F32) + self.kbuf[z, y].astype(F32)).astype(BF16)
            if d > 0:
                self.ycopy(d - 1, slot).start()

    def y_sum(self, slot):
        total = self.acc[self.own(slot)].astype(F32)
        for d in range(self.l.ys - 1):
            self.ycopy(d, slot).wait_recv()
            total = total + self.ybuf[d, slot].astype(F32)
        return total

    def z_step(self, slot):
        l, own = self.l, self.own(slot)
        total = self.y_sum(slot)
        self.acc[own] = total.astype(BF16)
        @pl.when(l.inner)
        def _():
            self.acc[own] = (self.acc[own].astype(F32) + self.zwait(*((0, slot) if slot < 2 else (1, 0)))).astype(BF16)

        self.zcopy(slot).start()

    def last(self, out):
        l = self.l
        out[...] = self.y_sum(3)

        @pl.when(l.inner)
        def _():
            out[...] += self.zwait(0, 2) + self.zwait(1, 1)

        @pl.when(l.outer)
        def _():
            out[...] += self.zwait(1, 2)

    def finish(self):
        for slot in range(4):
            for d in range(self.l.ys):
                self.kcopy(d, slot).wait_send()
            for d in range(self.l.ys - 1):
                self.ycopy(d, slot).wait_send()
        for slot in range(3):
            self.zcopy(slot).wait_send()


G1, C1, BQV, IDS, BO, G2, C2, BF, BP = range(9)


def put_ids(n, small_all, first, row, col):
    tokens = small_all.shape[2]
    for j in range(n):
        ids = small_all[first + j].astype(F32)[IDS : IDS + 1, :]
        row[:, j * tokens : (j + 1) * tokens] = ids
        col[j * tokens : (j + 1) * tokens, :] = jnp.transpose(jnp.broadcast_to(ids, (tokens, tokens)))[:, :1]


def half_row(tile_row, odd, high):
    lane = lax.broadcasted_iota(jnp.int32, tile_row.shape, 1)
    turned = pltpu.roll(tile_row, 64, 1)
    moved = jnp.where((odd == 1) == high, tile_row, turned)
    return jnp.where((lane >= 64) == high, moved, 0.0)


def normalize(rows):
    centred = rows - jnp.mean(rows, axis=-1, keepdims=True)
    rstd = lax.rsqrt(jnp.mean(centred * centred, axis=-1, keepdims=True) + EPSILON)
    return centred * rstd, rstd


def group_of(n, f):
    d, j = f // n, f % n
    return d % 2 * (n // 2) + j % (n // 2), d // 2 * 2 + j // (n // 2)


def group_peer(n, i, count):
    d, j = lax.axis_index("dp"), lax.axis_index("ctx")
    g = lax.rem(d // 2 * 2 + j // (n // 2) + i, count)
    return g, {"dp": g // 2 * 2 + d % 2, "ctx": g % 2 * (n // 2) + j % (n // 2)}


def front_kernel(n_dp, n, r, spread, cube, whole, *refs):
    refs = list(refs)
    take = lambda k: [refs.pop(0) for _ in range(k)]
    x_ref, small_ref, dy_ref = take(3)
    if spread:
        wqb, wfb, wob = take(3)
    else:
        (wq_all,) = take(1)
    small_all, first_out, a_ref, b_ref, o_ref, att, dy_all = take(7)
    if spread:
        wq_all, wf_all, wo_all = take(3)
    xbuf, first, prm, bqv, bias, idrow, idcol, packed, acc, tot, own_sems, first_sems = take(12)
    line_sems, small_sems, dy_sems, att_sems = take(6), take(2), take(4), take(2)
    if spread:
        wq_sems, wf_sems, wo_sems = take(4), take(2), take(4)

    tokens, width = x_ref.shape
    count = n_dp * n
    d, me = lax.axis_index("dp"), lax.axis_index("ctx")
    flat = d * n + me
    head, part = me // r, me % r
    line = Line(n)
    hello = Greet(n_dp, n)

    xg = LineGather(line, xbuf, line_sems)
    small = ToAll(n_dp, n, lambda f: small_ref, small_all, small_sems)
    dyg = Gather(cube, dy_all, dy_sems)
    own_copies = [pltpu.make_async_copy(dy_ref, dy_all.at[dyg.own()], own_sems.at[0])]
    if spread:
        wq = ToAll(n_dp, n, lambda f: wqb.at[f], wq_all.at[d], wq_sems[:2], True)
        wf = ToAll(n_dp, n, lambda f: wfb.at[group_of(n, f)[0]], wf_all, wf_sems)
        wog = Gather(whole, wo_all, wo_sems)
        own_copies.append(pltpu.make_async_copy(wfb.at[group_of(n, flat)[0]], wf_all.at[flat], own_sems.at[1]))
        own_copies.append(pltpu.make_async_copy(wob, wo_all.at[wog.own()], own_sems.at[2]))
        dps = []
        for i in range(1, n_dp):
            dps.append(remote(wq_all.at[d], wq_all.at[d], wq_sems[2].at[i], wq_sems[3].at[i], {"dp": (d + i) % n_dp}))
    for c in own_copies:
        c.start()
    xbuf[line.z, line.y, line.c] = x_ref[...]
    small_all[flat] = small_ref[...]
    if spread:
        wq_all[d, me] = wqb[me]
    hello.wait()
    xg.start()
    small.start()
    if spread:
        wq.start()
    for c in own_copies:
        c.wait()
    if spread:
        wog.start()
    xg.z_step(0)
    xg.y_step(3)
    if spread:
        wq.wait_recv()
        for c in dps:
            c.start()
    small.wait_recv()
    per = count * 128 // width
    for k in range(width // 128):
        tile = jnp.sum(small_all[k * per : (k + 1) * per].astype(F32), axis=0)
        prm[:, k * 128 : (k + 1) * 128] = tile[:8]
    per = count * 128 // (2 * width)
    for k in range(2 * width // 128):
        tile = jnp.sum(small_all[k * per : (k + 1) * per].astype(F32), axis=0)
        bqv[k : k + 1, :] = tile[BQV : BQV + 1]
    odd = head % 2
    bias[:, :128] = half_row(bqv[pl.ds(head // 2, 1), :], odd, False)
    bias[:, 128:] = half_row(bqv[pl.ds(width // 128 + head // 2, 1), :], odd, True)
    put_ids(n, small_all, d * n, idrow, idcol)
    per_z = n // 4

    def plane(slot):
        return pl.ds(pl.multiple_of(line.slots[slot] * per_z * tokens, per_z * tokens), per_z * tokens)

    def save(slot):
        return pltpu.make_async_copy(first.at[plane(slot)], first_out.at[plane(slot)], first_sems.at[slot])

    def project(slot):
        z = line.slots[slot]

        def one(i, _):
            normed, _ = normalize(xbuf[z, i // 2, i % 2].astype(F32))
            low = (normed * prm[G1 : G1 + 1, :] + prm[C1 : C1 + 1, :]).astype(BF16)
            first[pl.ds(pl.multiple_of((z * per_z + i) * tokens, tokens), tokens), :] = low
            return 0

        lax.fori_loop(0, per_z, one, 0)
        at = plane(slot)
        weights = wq_all[...].reshape(width, 256) if spread else wq_all[...]
        qkv = (dot(first[at, :], weights) + bias[...]).astype(BF16)
        a_ref[at, :] = qkv[:, :128]
        b_ref[at, :] = qkv[:, 128:]
        save(slot).start()

    xg.z_step(1)
    xg.y_step(2)
    if spread:
        wog.step(0)
        for c in dps:
            c.wait_recv()
    xg.core_wait(3)
    project(3)
    xg.z_step(2)
    xg.y_step(1)
    if spread:
        wog.step(1)
    xg.core_wait(2)
    project(2)
    xg.y_step(0)
    dyg.start()
    if spread:
        wf.start()
        wog.step(2)
    xg.core_wait(1)
    project(1)
    xg.core_wait(0)
    project(0)
    dyg.step(0)

    length = b_ref.shape[0]
    kc = min(1024, length)
    half = tokens // 2
    if r > 1:
        packed[...] = jnp.zeros_like(packed)

    def per_queries(lb, _):
        gq = lb * r + part
        qs = pl.ds(pl.multiple_of(gq * QB, QB), QB)
        a = a_ref[qs, :] * 0.125
        ids = idcol[qs, :]
        acc[...] = jnp.zeros_like(acc)
        tot[...] = jnp.zeros_like(tot)

        def per_keys(kb, _):
            ks = pl.ds(pl.multiple_of(kb * kc, kc), kc)
            b = b_ref[ks, :]
            s = dot(a, b, NT)
            w = jnp.where(idrow[:, ks] <= ids, jnp.exp(s), 0.0)
            t = w[:, :128]
            for i in range(1, kc // 128):
                t = t + w[:, i * 128 : (i + 1) * 128]
            tot[...] += t
            acc[...] += dot(w.astype(BF16), b)
            return 0

        lax.fori_loop(0, jnp.minimum(((gq + 2) * QB + kc - 1) // kc, length // kc), per_keys, 0)
        t = jnp.sum(tot[...], axis=-1, keepdims=True)
        o = acc[...] / t
        lane = lax.broadcasted_iota(jnp.int32, (QB, 128), 1)
        o_ref[pl.ds(pl.multiple_of(lb * QB, QB), QB), :] = jnp.where(lane < 64, t, o)
        lane = lax.broadcasted_iota(jnp.int32, (half, 128), 1)
        for i in range(QB // tokens):
            lo, hi = o[i * tokens : i * tokens + half], o[i * tokens + half : (i + 1) * tokens]
            packed[gq * (QB // tokens) + i] = jnp.where(lane < 64, pltpu.roll(lo, 64, 1), hi).astype(BF16)
        return 0

    blocks = length // QB // r
    cuts = [0, blocks // 2, blocks * 3 // 4, blocks]
    for k in range(3):
        lax.fori_loop(cuts[k], cuts[k + 1], per_queries, 0)
        if k + 1 < dyg.links:
            dyg.step(k + 1)
        if k == 0 and spread:
            for i in range(3, wog.links):
                wog.step(i)
    out = ToAll(n_dp, n, lambda f: packed.at[f], att, att_sems, True)
    att[me] = packed[me]
    out.start()
    for k in range(3, dyg.links):
        dyg.step(k)
    out.wait_recv()
    dyg.core_wait()
    if spread:
        wf.wait_recv()
        wog.core_wait()
        wq.wait_send()
        wf.wait_send()
        wog.finish()
        for c in dps:
            c.wait_send()
    for slot in range(4):
        save(slot).wait()
    small.wait_send()
    out.wait_send()
    xg.finish()
    dyg.finish()


def front(n_dp, n, r, x, small, dy, weights, blocks):
    tokens, width = x.shape
    count, length = n_dp * n, n * tokens
    spread = weights is None
    cube, whole = cube_plan(n, tokens), None
    shape = jax.ShapeDtypeStruct
    vm, hbm = pl.BlockSpec(memory_space=pltpu.VMEM), pl.BlockSpec(memory_space=pl.ANY)
    outs = [
        (shape((count, 16, 128), BF16), vm), (shape((length, width), BF16), hbm), (shape((length, 128), BF16), vm),
        (shape((length, 128), BF16), vm), (shape((length // r, 128), F32), vm), (shape((n, tokens // 2, 128), BF16), vm),
        (shape((2,) * len(cube[0]) + (tokens, width), BF16), hbm),
    ]
    sems = LineGather.sems(n) + [DMA((count,))] * 2 + Gather.sems(cube) + [DMA((n,))] * 2
    ins = [x, small, dy]
    if spread:
        wq, wf, wo = blocks
        whole = all_plan(n_dp, n, wo.shape[0])
        outs += [
            (shape((n_dp, n) + wq.shape[1:], BF16), vm), (shape((count,) + wf.shape[1:], BF16), hbm),
            (shape((2,) * len(whole[0]) + wo.shape, BF16), hbm),
        ]
        sems += [DMA((n,))] * 2 + [DMA((n_dp,))] * 2 + [DMA((count,))] * 2 + Gather.sems(whole)
        ins += list(blocks)
    else:
        ins += [weights]
    return pl.pallas_call(
        functools.partial(front_kernel, n_dp, n, r, spread, cube, whole),
        out_shape=[o for o, _ in outs],
        in_specs=[vm] * len(ins),
        out_specs=[s for _, s in outs],
        scratch_shapes=[
            pltpu.VMEM((4, n // 8, 2, tokens, width), BF16), pltpu.VMEM((length, width), BF16), pltpu.VMEM((8, width), F32),
            pltpu.VMEM((2 * width // 128, 128), F32), pltpu.VMEM((1, 256), F32), pltpu.VMEM((1, length), F32),
            pltpu.VMEM((length, 1), F32), pltpu.VMEM((n, tokens // 2, 128), BF16), pltpu.VMEM((QB, 128), F32),
            pltpu.VMEM((QB, 128), F32), DMA((3,)), DMA((4,)),
        ] + sems,
        compiler_params=pltpu.CompilerParams(collective_id=1, has_side_effects=True, vmem_limit_bytes=VMEM_LIMIT),
        name="front",
    )(*ins)


def gelu_both(u):
    c = math.sqrt(2.0 / math.pi)
    t = jnp.tanh(c * (u + 0.044715 * (u * u * u)))
    half = 0.5 * (1.0 + t)
    return u * half, half + 0.5 * u * (1.0 - t * t) * (c * (1.0 + 3.0 * 0.044715 * (u * u)))


def normalize_back(grad, normed, rstd):
    return rstd * (
        grad
        - jnp.mean(grad, axis=-1, keepdims=True)
        - normed * jnp.mean(grad * normed, axis=-1, keepdims=True)
    )


def ffn_kernel(n_dp, n, r, spread, plan, *refs):
    refs = list(refs)
    take = lambda k: [refs.pop(0) for _ in range(k)]
    att, x_ref, dy_own, dy_hbm, wo_ref, wf_ref, wp_in, bf_ref, par_ref = take(9)
    middle_ref, mg_ref, low_ref, branch_ref, agb, sums_ref, out_hbm, wp_grad, wf_grad, bf_grad = take(10)
    links = len(plan[0]) - 1
    sbuf, dy_ref, grads, act, hid, acc, out_ref, sg, copy_sems, out_sems = take(10)
    bufs, gather_sems, scatter_sems = take(links + 1), take(4), take(4)
    g = Gather(plan, sbuf, gather_sems)
    s = Scatter(plan, acc, bufs, scatter_sems)
    peers = g.peers()
    if spread:
        wp_ref, wp_send, wp_recv = take(3)
        for i in range(1, n_dp):
            peers.append(group_peer(n, i, n_dp)[1])
    hello = Greet(n_dp, n, peers)
    if spread:
        group = group_of(n, lax.axis_index("dp") * n + lax.axis_index("ctx"))[1]
        units = wp_in.shape[0]
        wps = [
            remote(wp_in, wp_ref.at[pl.ds(group * units, units)], wp_send.at[i], wp_recv.at[i], peers[len(peers) - n_dp + i])
            for i in range(1, n_dp)
        ]
        wp_ref[pl.ds(pl.multiple_of(group * units, units), units), :] = wp_in[...]
    else:
        wp_ref = wp_in
    dy_copy = pltpu.make_async_copy(dy_hbm, dy_ref, copy_sems)
    dy_copy.start()
    tokens, width = x_ref.shape
    half = tokens // 2
    quarter = (1 << (links - 1)) * tokens
    inner = (slice(None),) * (links - 1)
    core = g.mine[-1]

    lane = lax.broadcasted_iota(jnp.int32, (half, 128), 1)

    def block(h):
        total = att[h * r].astype(F32)
        for i in range(1, r):
            total = total + att[h * r + i].astype(F32)
        return total

    for h in range(0, HEADS, 2):
        b0, b1 = block(h), block(h + 1)
        at = slice(h * 64, h * 64 + 128)
        low_ref[:half, at] = jnp.where(lane < 64, b0, pltpu.roll(b1, 64, 1)).astype(BF16)
        low_ref[half:, at] = jnp.where(lane < 64, pltpu.roll(b0, 64, 1), b1).astype(BF16)
    middle = x_ref[...].astype(F32) + dot(low_ref[...], wo_ref[...]) + par_ref[0:1, :]
    middle_ref[...] = middle
    n2, _ = normalize(middle)
    sbuf[g.own()] = (n2 * par_ref[1:2, :] + par_ref[2:3, :]).astype(BF16)
    hello.wait()
    g.start()
    if spread:
        for c in wps:
            c.start()
    dy_copy.wait()
    if spread:
        for c in wps:
            c.wait_recv()

    def rows(c, a):
        return pl.ds(pl.multiple_of((2 * c + a) * quarter, quarter), quarter)

    def grad_part(i):
        dy = dy_ref[(i // 2, i % 2) + inner].reshape(quarter, width)
        grads[rows(i // 2, i % 2), :] = dot(dy, wp_ref[...], NT)

    for k in range(links):
        g.step(k)
        if k == 1:
            for i in range(4):
                grad_part(i)
    g.core_wait()
    bf_grad[...] = jnp.zeros_like(bf_grad)

    def hidden_part(c, a):
        at = rows(c, a)
        low = sbuf[(c, a) + inner].reshape(quarter, width)
        active, slope = gelu_both(dot(low, wf_ref[...]) + bf_ref[...])
        act[at, :] = active.astype(BF16)
        h = (slope * grads[at, :]).astype(BF16)
        hid[at, :] = h
        bf_grad[...] += jnp.sum(h.astype(F32), axis=0, keepdims=True)
        acc[(c, a) + inner] = dot(h, wf_ref[...], NT).astype(BF16).reshape((2,) * (links - 1) + (tokens, width))

    for a in range(2):
        hidden_part(1 - core, a)
        s.core(a).start()
    for a in range(2):
        hidden_part(core, a)
        s.add_core(a)
    s.start_links()

    def weight_grads(k):
        at = slice(k * 256, (k + 1) * 256)
        low = sbuf[..., at].reshape(4 * quarter, 256)
        wf_grad[at, :] = jnp.transpose(dot(hid[...], low, TN)).astype(BF16)
        dy = dy_ref[..., at].reshape(4 * quarter, 256)
        wp_grad[:, at] = dot(act[...], dy, TN).astype(BF16)

    def out_part(i):
        at = (i // 2, i % 2) + inner
        if i >= out_ref.shape[0]:
            out_copy(i - out_ref.shape[0]).wait()
        terms = dot(act[rows(i // 2, i % 2), :], wp_ref[...]).astype(BF16)
        out_ref[i % out_ref.shape[0]] = terms.reshape((2,) * (links - 1) + (tokens, width))
        out_copy(i).start()

    def out_copy(i):
        slot = i % out_ref.shape[0]
        return pltpu.make_async_copy(out_ref.at[slot], out_hbm.at[(i // 2, i % 2) + inner], out_sems.at[slot])

    for i in range(4):
        out_part(i)
    for k in range(links):
        s.step(k, sg)
        if k < 2:
            weight_grads(2 * k)
            weight_grads(2 * k + 1)

    second_grad = sg[...]
    dy = dy_own[...].astype(F32)
    n2, rstd2 = normalize(middle_ref[...])
    mg = dy + normalize_back(second_grad * par_ref[1:2, :], n2, rstd2)
    mg_ref[...] = mg
    branch = mg.astype(BF16)
    branch_ref[...] = branch
    grad = dot(branch, wo_ref[...], NT)
    for h in range(0, HEADS, 2):
        lo, hi = grad[:half, h * 64 : h * 64 + 128], grad[half:, h * 64 : h * 64 + 128]
        b0 = jnp.where(lane < 64, lo, pltpu.roll(hi, 64, 1)).astype(BF16)
        b1 = jnp.where(lane < 64, pltpu.roll(lo, 64, 1), hi).astype(BF16)
        for i in range(r):
            agb[h * r + i] = b0
            agb[(h + 1) * r + i] = b1
    column = lambda v: jnp.sum(v, axis=0, keepdims=True)
    sums_ref[0:1, :] = column(branch.astype(F32))
    sums_ref[1:2, :] = column(second_grad * n2)
    sums_ref[2:3, :] = column(second_grad)
    sums_ref[3:4, :] = column(dy)
    for i in range(4 - out_ref.shape[0], 4):
        out_copy(i).wait()
    if spread:
        for c in wps:
            c.wait_send()
    s.finish()
    g.finish()


def ffn(n_dp, n, r, spread, att, x, dy, dy_all, wo, wf, wp, bf, params):
    tokens, width = x.shape
    units = wf.shape[1]
    plan = cube_plan(n, tokens)
    block = (2,) * len(plan[0])
    length = n * tokens
    shape = jax.ShapeDtypeStruct
    vm, hbm = pl.BlockSpec(memory_space=pltpu.VMEM), pl.BlockSpec(memory_space=pl.ANY)
    extra = [pltpu.VMEM((units, width), BF16), DMA((n_dp,)), DMA((n_dp,))] if spread else []
    return pl.pallas_call(
        functools.partial(ffn_kernel, n_dp, n, r, spread, plan),
        out_shape=[
            shape((tokens, width), F32), shape((tokens, width), F32), shape((tokens, width), BF16), shape((tokens, width), BF16),
            shape((n, tokens // 2, 128), BF16), shape((4, width), F32), shape(block + (tokens, width), BF16),
            shape((units, width), BF16), shape((width, units), BF16), shape((1, units), F32),
        ],
        in_specs=[vm, vm, vm, hbm, vm, vm, vm, vm, vm],
        out_specs=[vm, vm, vm, vm, vm, vm, hbm, vm, vm, vm],
        scratch_shapes=[
            pltpu.VMEM(block + (tokens, width), BF16), pltpu.VMEM(block + (tokens, width), BF16), pltpu.VMEM((length, units), F32),
            pltpu.VMEM((length, units), BF16), pltpu.VMEM((length, units), BF16), pltpu.VMEM(block + (tokens, width), BF16),
            pltpu.VMEM((2,) + block[2:] + (tokens, width), BF16), pltpu.VMEM((tokens, width), F32), DMA, DMA((2,)),
        ] + Scatter.scratch(plan, tokens, width) + Gather.sems(plan) + Scatter.sems(plan) + extra,
        compiler_params=pltpu.CompilerParams(collective_id=2, has_side_effects=True, vmem_limit_bytes=VMEM_LIMIT),
        name="ffn",
    )(att, x, dy, dy_all, wo, wf, wp, bf, params)


def back_kernel(n_dp, n, r, spread, cube, whole, *refs):
    refs = list(refs)
    take = lambda k: [refs.pop(0) for _ in range(k)]
    agb, a_ref, b_ref, o_ref, small_all, wq_ref, first, part_out, x_ref, mid_ref, mg_ref, par_ref, sums_in, bf_grad = take(14)
    if spread:
        low_ref, branch_ref, wfg, wpg = take(4)
    out_ref, ig_ref, sums = take(3)
    if spread:
        wq_got, wf_got, wp_got, wo_own = take(4)
    else:
        (wq_sum,) = take(1)
    ag, idrow, idcol, mixed, dqacc, dkv, acc, kbuf, ybuf, zbuf, fg, got, msg, columns, column_sem, own_out, own_sem, osum = take(18)
    links = len(cube[0]) - 1
    out_bufs = take(links + 1)
    if r > 1:
        (dkv_got,) = take(1)
        pair_sems = take(2)
    ag_sems, line_sems, out_sems, msg_sems = take(2), take(6), take(4), take(2)
    if spread:
        wq_part, wq_mine, wq_else, wo_part = take(4)
        wq_sems, wf_sems, wp_sems = take(4), take(2), take(2)
        wo_bufs = take(len(whole[0]))
        wo_sems = take(4)

    tokens, width = x_ref.shape
    length = b_ref.shape[0]
    count = n_dp * n
    d, me = lax.axis_index("dp"), lax.axis_index("ctx")
    flat = d * n + me
    head, part = me // r, me % r
    line = Line(n)
    hello = Greet(n_dp, n)
    kc = min(1024, length)
    half = tokens // 2

    grads = ToAll(n_dp, n, lambda f: agb.at[f], ag, ag_sems, True)
    outs = Scatter(cube, part_out, out_bufs, out_sems, own_out)
    own_copy = outs.fetch_own(own_sem)
    own_copy.start()
    ag[me] = agb[me]
    if spread:
        wf = ToAll(n_dp, n, lambda f: wfg.at[f], wf_got, wf_sems)
        wq = ToAll(n_dp, n, lambda f: wq_mine.at[f], wq_got, wq_sems[:2], True)
        wo = Scatter(whole, wo_part, wo_bufs, wo_sems)
        wf_got[flat] = wfg[flat]
        rank, group = group_of(n, flat)
        wp_got[group] = wpg[group]
        wps, dps = [], []
        for i in range(1, n_dp):
            g, peer = group_peer(n, i, n_dp)
            wps.append(remote(wpg.at[g], wp_got.at[group], wp_sems[0].at[i], wp_sems[1].at[i], peer))
            dps.append(remote(wq_part.at[(d + i) % n_dp], wq_else.at[i], wq_sems[2].at[i], wq_sems[3].at[i], {"dp": (d + i) % n_dp}))
    else:
        rank, group = group_of(n, flat)
    dkv[...] = jnp.zeros_like(dkv)
    if r > 1:
        mixed[...] = jnp.zeros_like(mixed)
    hello.wait()
    grads.start()
    for h in range(2):
        outs.core(h).start()
    if spread:
        for c in wps:
            c.start()
    put_ids(n, small_all, d * n, idrow, idcol)
    if spread:
        rows = width // count
        for k in range(width // 256):
            terms = dot(low_ref[:, k * 256 : (k + 1) * 256], branch_ref[...], TN).astype(BF16)
            for i in range(256 // rows):
                f = k * (256 // rows) + i
                bits = tuple((f >> b) & 1 for b in range(len(whole[0]) - 1, -1, -1))
                wo_part[bits] = terms[i * rows : (i + 1) * rows]
        for h in range(2):
            wo.core(h).start()
    own_copy.wait()
    for h in range(2):
        outs.add_core(h)
    outs.start_links()
    grads.wait_recv()
    if spread:
        wf.start()

    def per_queries(lb, _):
        gq = lb * r + part
        qs = pl.ds(pl.multiple_of(gq * QB, QB), QB)
        at = pl.ds(pl.multiple_of(lb * QB, QB), QB)
        lane = lax.broadcasted_iota(jnp.int32, (half, 128), 1)
        pieces = []
        for i in range(QB // tokens):
            block = ag[gq * (QB // tokens) + i].astype(F32)
            pieces += [jnp.where(lane >= 64, pltpu.roll(block, 64, 1), 0.0), jnp.where(lane >= 64, block, 0.0)]
        grad = jnp.concatenate(pieces, axis=0)
        o = o_ref[at, :]
        inverse = 1.0 / o[:, :1]
        upper = lax.broadcasted_iota(jnp.int32, (QB, 128), 1) >= 64
        ratio = jnp.sum(jnp.where(upper, grad * o, 0.0), axis=-1, keepdims=True) * inverse
        ratio = jnp.transpose(jnp.broadcast_to(ratio, (QB, 128)))[:1, :]
        do = (grad * inverse).astype(BF16)
        a = a_ref[qs, :]
        scaled = a * 0.125
        ado = jnp.concatenate([a, do], axis=0)
        ids = idrow[:, qs]
        dqacc[...] = jnp.zeros_like(dqacc)

        def per_keys(kb, _):
            ks = pl.ds(pl.multiple_of(kb * kc, kc), kc)
            b = b_ref[ks, :]
            w = jnp.where(idcol[ks, :] <= ids, jnp.exp(dot(b, scaled, NT)), 0.0)
            g = (w * (dot(b, do, NT) - ratio)).astype(BF16)
            dkv[ks, :] += dot(jnp.concatenate([g, w.astype(BF16)], axis=1), ado)
            dqacc[...] += dot(g, b, TN)
            return 0

        lax.fori_loop(0, jnp.minimum(((gq + 2) * QB + kc - 1) // kc, length // kc), per_keys, 0)
        mixed[qs, :128] = jnp.where(upper, 0.0, dqacc[...] * 0.125).astype(BF16)
        return 0

    blocks = length // QB // r
    cuts = [0, blocks // 2, blocks * 3 // 4, blocks]
    for k in range(3):
        lax.fori_loop(cuts[k], cuts[k + 1], per_queries, 0)
        if k + 1 < links:
            outs.step(k, osum)
    if spread:
        for h in range(2):
            wo.add_core(h)

    def fetch(k):
        return pltpu.make_async_copy(first.at[:, pl.ds(pl.multiple_of(k * 256, 256), 256)], columns, column_sem)

    turns = [((d + 1) * (width // 256 // n_dp) + i) % (width // 256) if spread else i for i in range(width // 256)]
    fetch(turns[0]).start()
    low = lax.broadcasted_iota(jnp.int32, (length, 128), 1) < 64
    total = dkv[...]
    if r > 1:
        both = remote(dkv, dkv_got, pair_sems[0], pair_sems[1], line.core)
        both.start()
        both.wait()
        total = jnp.where(part == 0, total + dkv_got[...], 0.0)
    mixed[:, 128:] = jnp.where(low, total * 0.125, total).astype(BF16)

    rs = LineScatter(line, acc, kbuf, ybuf, zbuf, line_sems)
    per_z = n // 4 * tokens

    def first_grad(slot):
        z = line.slots[slot]
        at = pl.ds(pl.multiple_of(z * per_z, per_z), per_z)
        acc[z] = dot(mixed[at, :], wq_ref[...], NT).astype(BF16).reshape(n // 8, 2, tokens, width)
        rs.core_start(slot)

    first_grad(0)
    for slot in range(1, 4):
        first_grad(slot)
        rs.core_step(slot - 1)
    rs.core_step(3)
    for k in range(min(2, links - 1), links):
        outs.step(k, osum)
    if spread:
        wo.start_links()

    def wq_grad(i):
        k = turns[i]
        fetch(k).wait()
        g = jnp.transpose(dot(mixed[...], columns[...], TN))
        if i + 1 < len(turns):
            fetch(turns[i + 1]).start()
        if spread:
            per = n_dp * 256 // width
            q = 256 // rows
            at = k * q
            wq_part[at // n, pl.ds(at % n, q)] = g.astype(BF16).reshape(q, rows, 256)
        else:
            wq_sum[pl.ds(pl.multiple_of(k * 256, 256), 256), :] = g

    ahead = len(turns) - len(turns) // n_dp if spread else 2
    for i in range(ahead):
        wq_grad(i)
    if spread:
        for c in dps:
            c.start()
    rs.z_step(0)
    for i in range(ahead, len(turns)):
        wq_grad(i)
    rs.z_step(1)
    if spread:
        total = wq_part[d].astype(F32)
        for i, c in enumerate(dps):
            c.wait_recv()
            total = total + wq_else[i + 1].astype(F32)
        wq_mine[...] = total.astype(BF16)
        wq_got[me] = wq_mine[me]
        wq.start()
        wo.step(0, wo_own)
    column = jnp.sum(mixed[...].astype(F32), axis=0, keepdims=True)
    odd = head % 2
    q_row = half_row(column[:, :128], 0, False)
    q_row = jnp.where(odd == 1, pltpu.roll(q_row, 64, 1), q_row)
    v_row = half_row(column[:, 128:], 1, True)
    v_row = jnp.where(odd == 1, v_row, pltpu.roll(v_row, 64, 1))
    rs.z_step(2)
    out_ref[...] = (mid_ref[...] + osum[...] + par_ref[1:2, :]).astype(BF16)
    n1, rstd1 = normalize(x_ref[...].astype(F32))
    if spread:
        wo.step(1, wo_own)

    wide = bf_grad.shape[1] // 128

    def prepare(f, _):
        tile = f * 2 * width // count // 128
        bqv = jnp.where(tile == head // 2, q_row, 0.0) + jnp.where(tile == width // 128 + head // 2, v_row, 0.0)
        msg[f, 6:7, :] = bqv
        same = group_of(n, f)[0] == rank
        for i in range(wide):
            msg[f, 7 + i : 8 + i, :] = jnp.where(same, bf_grad[:, i * 128 : (i + 1) * 128], 0.0)
        return 0

    msg[...] = jnp.zeros_like(msg)
    lax.fori_loop(0, count, prepare, 0)
    rs.last(fg)

    grad = fg[...]
    gain = jnp.sum(grad * n1, axis=0, keepdims=True)
    shift = jnp.sum(grad, axis=0, keepdims=True)
    per = 128 * count // width
    for k in range(width // 128):
        at = slice(k * 128, (k + 1) * 128)
        lines = jnp.concatenate([gain[:, at], shift[:, at], sums_in[:, at]], axis=0)

        def fill(i, _, k=k, lines=lines):
            msg[k * per + i, 0:6, :] = lines
            return 0

        lax.fori_loop(0, per, fill, 0)
    tell = ToAll(n_dp, n, lambda f: msg.at[f], got, msg_sems)
    tell.start()
    got[flat] = msg[flat]
    ig_ref[...] = (mg_ref[...] + normalize_back(grad * par_ref[0:1, :], n1, rstd1)).astype(BF16)
    if spread:
        for k in range(2, wo.links):
            wo.step(k, wo_own)
        wf.wait_recv()
        wq.wait_recv()
        for c in wps:
            c.wait()
    tell.wait_recv()
    sums[...] = jnp.sum(got[...], axis=0)
    tell.wait_send()
    if spread:
        wf.wait_send()
        wq.wait_send()
        for c in dps:
            c.wait_send()
        wo.finish()
    grads.wait_send()
    outs.finish()
    rs.finish()


def back(n_dp, n, r, agb, a, b, o, small_all, wq, first, part_out, x, middle, mg, params, sums4, bf_grad, grads):
    tokens, width = x.shape
    count, length = n_dp * n, n * tokens
    spread = grads is not None
    cube = cube_plan(n, tokens)
    links = len(cube[0]) - 1
    whole = None
    shape = jax.ShapeDtypeStruct
    ins = [agb, a, b, o, small_all, wq, first, part_out, x, middle, mg, params, sums4, bf_grad]
    outs = [shape((tokens, width), BF16), shape((tokens, width), BF16), shape((16, 128), F32)]
    scratch = [
        pltpu.VMEM((n, tokens // 2, 128), BF16), pltpu.VMEM((1, length), F32), pltpu.VMEM((length, 1), F32),
        pltpu.VMEM((length, 256), BF16), pltpu.VMEM((QB, 128), F32), pltpu.VMEM((length, 128), F32),
        pltpu.VMEM((4, n // 8, 2, tokens, width), BF16),
    ] + LineScatter.scratch(n, tokens, width) + [
        pltpu.VMEM((tokens, width), F32), pltpu.VMEM((count, 16, 128), F32), pltpu.VMEM((count, 16, 128), F32),
        pltpu.VMEM((length, 256), BF16), DMA, pltpu.VMEM((2,) * links + (tokens, width), BF16), DMA,
        pltpu.VMEM((tokens, width), F32),
    ] + Scatter.scratch(cube, tokens, width)
    if r > 1:
        scratch += [pltpu.VMEM((length, 128), F32), DMA, DMA]
    scratch += [DMA((n,))] * 2 + LineScatter.sems(n) + Scatter.sems(cube) + [DMA((count,))] * 2
    if spread:
        low, branch, wfg, wpg = grads
        rows = width // count
        whole = all_plan(n_dp, n, rows)
        ins += [low, branch, wfg, wpg]
        outs += [shape((n, rows, 256), BF16), shape(wfg.shape, BF16), shape(wpg.shape, BF16), shape((rows, width), F32)]
        scratch += [
            pltpu.VMEM((n_dp, n, rows, 256), BF16), pltpu.VMEM((n, rows, 256), BF16), pltpu.VMEM((n_dp, n, rows, 256), BF16),
            pltpu.VMEM((2,) * len(whole[0]) + (rows, width), BF16),
        ]
        scratch += [DMA((n,))] * 2 + [DMA((n_dp,))] * 2 + [DMA((count,))] * 2 + [DMA((n_dp,))] * 2
        scratch += Scatter.scratch(whole, rows, width) + Scatter.sems(whole)
    else:
        outs += [shape((width, 256), F32)]
    vm, hbm = pl.BlockSpec(memory_space=pltpu.VMEM), pl.BlockSpec(memory_space=pl.ANY)
    return pl.pallas_call(
        functools.partial(back_kernel, n_dp, n, r, spread, cube, whole),
        out_shape=outs,
        in_specs=[hbm if v is first or v is part_out else vm for v in ins],
        out_specs=[vm] * len(outs),
        scratch_shapes=scratch,
        compiler_params=pltpu.CompilerParams(collective_id=3, has_side_effects=True, vmem_limit_bytes=VMEM_LIMIT),
        name="back",
    )(*ins)


def place(v, flat):
    pieces = 128 // v.shape[0]
    return jnp.where(jnp.arange(128) // v.shape[0] == flat % pieces, jnp.tile(v, pieces), 0)


def local(n_dp, n, inputs, cotangent, block_ids, ln1_gain, ln1_bias, w_qkv, b_qkv, w_out, b_out, ln2_gain, ln2_bias, w_fc, b_fc, w_proj, b_proj):
    tokens, width = inputs.shape[1:]
    count = n_dp * n
    rows = w_qkv.shape[0]
    units = w_proj.shape[0]
    r = n // HEADS
    hd = width // HEADS
    d, me = lax.axis_index("dp"), lax.axis_index("ctx")
    flat = d * n + me
    head = me // r
    both = ("dp", "ctx")
    x, dy = inputs[0], cotangent[0]
    halves = (n_dp // 2, 2, 2, n // 2)

    small = [place(v, flat) for v in (ln1_gain, ln1_bias, b_qkv)] + [block_ids[0].astype(BF16)]
    small += [place(v, flat) for v in (b_out, ln2_gain, ln2_bias, b_fc, b_proj)]
    small = jnp.pad(jnp.stack(small), ((0, 16 - len(small)), (0, 0)))

    def heads_of(w):
        w = w.reshape(w.shape[0], 3, HEADS, 1, hd)
        w = jnp.stack([w[:, 0], jnp.zeros_like(w[:, 0]), w[:, 1], w[:, 2]], axis=3)
        return w.reshape(w.shape[0], HEADS, 4 * hd)

    spread = rows % 16 == 0
    if spread:
        wq = jnp.repeat(jnp.transpose(heads_of(w_qkv), (1, 0, 2)), r, axis=0)
        wf = jnp.transpose(w_fc.reshape((rows,) + halves + (units,)), (2, 4, 0, 1, 3, 5)).reshape(n, rows, n_dp * units)
        weights, blocks = None, (wq, wf, w_out)
    else:
        full = lax.all_gather(w_qkv, both, axis=0, tiled=True)
        weights = lax.dynamic_index_in_dim(heads_of(full), head, 1, keepdims=False)
        blocks = None
        wf = lax.all_gather(w_fc, both, axis=0, tiled=True).reshape((width,) + halves + (units,))
        wf = lax.dynamic_index_in_dim(wf, d % 2, 2, keepdims=False)
        wf = lax.dynamic_index_in_dim(wf, me % (n // 2), 3, keepdims=False).reshape(width, n_dp * units)
        wp = lax.all_gather(w_proj, both, axis=0, tiled=True).reshape(halves + (units, width))
        wp = lax.dynamic_index_in_dim(wp, d % 2, 1, keepdims=False)
        wp = lax.dynamic_index_in_dim(wp, me % (n // 2), 2, keepdims=False).reshape(n_dp * units, width)
        wo = lax.all_gather(w_out, both, axis=0, tiled=True)

    got = front(n_dp, n, r, x, small, dy, weights, blocks)
    small_all, first, a, b, o, att, dy_all = got[:7]
    if spread:
        wq, wf, wo = (v.reshape(width, -1) for v in got[7:])
        wp = w_proj
    else:
        wq = weights

    def vector(row, size):
        tiles = small_all[:, row].astype(F32).reshape(-1, 128 // size, 128)
        return jnp.sum(tiles, axis=1).reshape(1, -1)

    params = jnp.concatenate([vector(k, rows) for k in (BO, G2, C2, G1, BP)])
    bf = vector(BF, units).reshape(halves + (units,))
    bf = lax.dynamic_index_in_dim(bf, d % 2, 1, keepdims=False)
    bf = lax.dynamic_index_in_dim(bf, me % (n // 2), 2, keepdims=False).reshape(1, -1)

    got = ffn(n_dp, n, r, spread, att, x, dy, dy_all, wo, wf, wp, bf, params[:3])
    middle, middle_grad, low, branch, agb, sums4, part_out, wp_grad, wf_grad, bf_grad = got
    if spread:
        grads = (low, branch, wf_grad.reshape(count, rows, -1), wp_grad.reshape(n_dp, units, width))
    else:
        grads = None
    got = back(n_dp, n, r, agb, a, b, o, small_all, wq, first, part_out, x, middle, middle_grad, params[3:], sums4, bf_grad, grads)
    output, input_grad, sums = got[:3]
    if spread:
        wq_own, wf_own, wp_own, wo_own = got[3:]
        wq_own = jnp.sum(wq_own.astype(F32).reshape(HEADS, r, rows, 4, hd), axis=1)
        wq_own = jnp.stack([wq_own[:, :, 0], wq_own[:, :, 2], wq_own[:, :, 3]], axis=1)
        wq_own = jnp.transpose(wq_own, (2, 1, 0, 3)).reshape(rows, 3 * width)
        wf_own = jnp.sum(wf_own.astype(F32).reshape(halves + (rows, n_dp // 2, 2, units)), axis=(0, 2))
        wf_own = jnp.transpose(wf_own, (2, 3, 0, 4, 1, 5)).reshape(rows, -1)
        wp_own = jnp.sum(wp_own.astype(F32), axis=0)
    else:
        owned = lambda v: lax.psum_scatter(v, both, scatter_dimension=0, tiled=True)
        hot = (jnp.arange(2) == d % 2).reshape(1, 2, 1, 1, 1) & (jnp.arange(n // 2) == me % (n // 2)).reshape(1, 1, 1, -1, 1)
        g = got[3].reshape(width, 4, 1, hd)
        g = jnp.stack([g[:, 0], g[:, 2], g[:, 3]], axis=1)
        wq_own = owned(jnp.where((jnp.arange(HEADS) == head).reshape(1, 1, -1, 1), g, 0.0).reshape(width, 3 * width))
        g = wf_grad.astype(F32).reshape(width, n_dp // 2, 1, 2, 1, units)
        wf_own = owned(jnp.where(hot[None], g, 0.0).reshape(width, -1))
        g = wp_grad.astype(F32).reshape(n_dp // 2, 1, 2, 1, units, width)
        wp_own = owned(jnp.where(hot[..., None], g, 0.0).reshape(-1, width))
        wo_own = owned(dot(low, branch, TN))

    def cut(row, size):
        return lax.dynamic_slice(sums[row], (flat * size % 128,), (size,))

    g1g, c1g, bqvg = cut(0, rows), cut(1, rows), cut(6, 2 * rows)
    bog, g2g, c2g, bpg = (cut(k, rows) for k in range(2, 6))
    group = d // 2 * 2 + me // (n // 2)
    bfg = lax.dynamic_slice(sums[7 : 7 + n_dp * units // 128].reshape(-1), (group * units,), (units,))
    return (
        output[None], input_grad[None], g1g, c1g, wq_own, bqvg, wo_own, bog, g2g, c2g, wf_own, bfg, wp_own, bpg,
    )


def solution(mesh):
    both = ("dp", "ctx")
    act, vec, mat = P("dp", "ctx", None), P(both), P(both, None)
    return jax.shard_map(
        functools.partial(local, mesh.shape["dp"], mesh.shape["ctx"]),
        mesh=mesh,
        in_specs=(act, act, P("dp", "ctx"), vec, vec, mat, vec, mat, vec, vec, vec, mat, vec, mat, vec),
        out_specs=(act, act, vec, vec, mat, vec, mat, vec, vec, vec, mat, vec, mat, vec),
        check_vma=False,
    )
```

```python
import functools
import math

import jax
import jax.numpy as jnp
from jax import lax
from jax.experimental import pallas as pl
from jax.experimental.pallas import tpu as pltpu
from jax.sharding import PartitionSpec as P

HEADS = 16
EPSILON = 1e-05
QB = 256
F32, BF16 = jnp.float32, jnp.bfloat16
NT = (((1,), (1,)), ((), ()))
TN = (((0,), (0,)), ((), ()))
MESH = pl.DeviceIdType.MESH
DMA = pltpu.SemaphoreType.DMA
VMEM_LIMIT = 60 << 20


def dot(x, y, dims=(((1,), (0,)), ((), ()))):
    return lax.dot_general(x, y, dims, preferred_element_type=F32)


def remote(src, dst, send, recv, peer):
    return pltpu.make_async_remote_copy(
        src_ref=src, dst_ref=dst, send_sem=send, recv_sem=recv, device_id=peer, device_id_type=MESH
    )


class Greet:
    def __init__(self, n_dp, n, peers=None):
        self.barrier = pltpu.get_barrier_semaphore()
        self.count = n_dp * n - 1 if peers is None else len(peers)
        for peer in peers or ():
            pl.semaphore_signal(self.barrier, inc=1, device_id=peer, device_id_type=MESH)
        if peers is None:
            flat = lax.axis_index("dp") * n + lax.axis_index("ctx")

            def signal(j, _):
                f = lax.rem(flat + j, n_dp * n)
                pl.semaphore_signal(self.barrier, inc=1, device_id={"dp": f // n, "ctx": f % n}, device_id_type=MESH)
                return 0

            lax.fori_loop(1, n_dp * n, signal, 0)

    def wait(self):
        pl.semaphore_wait(self.barrier, self.count)


class ToAll:
    def __init__(self, n_dp, n, block, into, sems, only_ctx=False):
        self.n, self.block, self.into, self.only = n, block, into, only_ctx
        self.send, self.recv = sems
        self.count = n if only_ctx else n_dp * n
        self.me = lax.axis_index("ctx") if only_ctx else lax.axis_index("dp") * n + lax.axis_index("ctx")

    def copy(self, j):
        f = lax.rem(self.me + j, self.count)
        peer = {"ctx": f} if self.only else {"dp": f // self.n, "ctx": f % self.n}
        return remote(self.block(f), self.into.at[self.me], self.send.at[j], self.recv.at[j], peer)

    def each(self, act):
        def step(j, _):
            act(self.copy(j))
            return 0

        lax.fori_loop(1, self.count, step, 0)

    def start(self):
        self.each(lambda c: c.start())

    def wait_recv(self):
        self.each(lambda c: c.wait_recv())

    def wait_send(self):
        self.each(lambda c: c.wait_send())


def own_bit(dim):
    axis, b = dim
    return lax.axis_index(axis) // (1 << b) % 2


def partner(dim):
    axis, b = dim
    return {axis: lax.axis_index(axis) + (1 - 2 * own_bit(dim)) * (1 << b)}


def cube_plan(n, rows):
    top = n.bit_length() - 2
    dims = [("dp", 0)] + [("ctx", b) for b in range(top - 1, 0, -1)] + [("ctx", 0)]
    links = len(dims) - 1
    size = -(-rows // (16 * links)) * 16
    cuts = [min(rows, size * i) for i in range(links)] + [rows]
    return dims, [(cuts[i], cuts[i + 1], [(i + j) % links for j in range(links)]) for i in range(links)], True


def all_plan(n_dp, n, rows):
    dims = [("dp", b) for b in range(n_dp.bit_length() - 2, -1, -1)] + [("ctx", b) for b in range(n.bit_length() - 2, -1, -1)]
    links, own = len(dims) - 1, n_dp.bit_length() - 1
    return dims, [(0, rows, list(range(own, links)) + list(range(own)))], False


class Pairwise:
    def __init__(self, plan, sems):
        self.dims, self.orders, self.core_first = plan
        self.links = len(self.dims) - 1
        self.link_send, self.link_recv, self.core_send, self.core_recv = sems
        self.mine = [own_bit(d) for d in self.dims]

    def index(self, links, core, tail=()):
        links = tuple(links)
        return ((core,) + links if self.core_first else links + (core,)) + tuple(tail)

    def peers(self):
        return [partner(d) for d in self.dims]


class Gather(Pairwise):
    def __init__(self, plan, buf, sems):
        super().__init__(plan, sems)
        self.buf = buf

    @staticmethod
    def sems(plan):
        links, parts = len(plan[0]) - 1, len(plan[1])
        return [DMA((parts, links))] * 2 + [DMA((parts * links + 1,))] * 2

    def own(self):
        return self.index(self.mine[:-1], self.mine[-1])

    def region(self, part, done, flip=None):
        lo, hi, _ = self.orders[part]
        where = [slice(None) if i in done else (1 - m if i == flip else m) for i, m in enumerate(self.mine[:-1])]
        return self.index(where, self.mine[-1], (pl.ds(lo, hi - lo),))

    def copy(self, where, send, recv, dim):
        return remote(self.buf.at[where], self.buf.at[where], send, recv, partner(self.dims[dim]))

    def link(self, part, k):
        order = self.orders[part][2]
        return self.copy(self.region(part, order[:k]), self.link_send.at[part, k], self.link_recv.at[part, k], order[k])

    def core(self, part, k):
        order = self.orders[part][2]
        at = part * self.links + k + 1
        return self.copy(self.region(part, order[:k], order[k]), self.core_send.at[at], self.core_recv.at[at], self.links)

    def core_own(self):
        return self.copy(self.own(), self.core_send.at[0], self.core_recv.at[0], self.links)

    def start(self):
        for part in range(len(self.orders)):
            self.link(part, 0).start()
        self.core_own().start()

    def step(self, k):
        for part in range(len(self.orders)):
            self.link(part, k).wait_recv()
            if k + 1 < self.links:
                self.link(part, k + 1).start()
            self.core(part, k).start()

    def core_wait(self):
        self.core_own().wait_recv()
        for part in range(len(self.orders)):
            for k in range(self.links):
                self.core(part, k).wait_recv()

    def finish(self):
        self.core_own().wait_send()
        for part in range(len(self.orders)):
            for k in range(self.links):
                self.link(part, k).wait_send()
                self.core(part, k).wait_send()


class Scatter(Pairwise):
    def __init__(self, plan, terms, bufs, sems, own=None):
        super().__init__(plan, sems)
        self.terms, self.run, self.bufs, self.own = terms, bufs[0], bufs[1:], own

    def fetch_own(self, sem):
        source = self.terms.at[self.index((slice(None),) * self.links, self.mine[-1])]
        return pltpu.make_async_copy(source, self.own, sem)

    @staticmethod
    def sems(plan):
        links, parts = len(plan[0]) - 1, len(plan[1])
        return [DMA((parts, links))] * 2 + [DMA((2,))] * 2

    @staticmethod
    def scratch(plan, rows, cols):
        links = len(plan[0]) - 1
        return [pltpu.VMEM((2,) * links + (rows, cols), BF16)] + [
            pltpu.VMEM((2,) * (links - 1 - k) + (rows, cols), BF16) for k in range(links)
        ]

    def core(self, half):
        where = (half,) + (slice(None),) * (self.links - 1)
        return remote(
            self.terms.at[self.index(where, 1 - self.mine[-1])], self.run.at[where],
            self.core_send.at[half], self.core_recv.at[half], partner(self.dims[-1]),
        )

    def where(self, part, k, flip):
        lo, hi, order = self.orders[part]
        order = order[::-1]
        d, gone = order[k], order[:k]
        at = []
        for i in range(self.links):
            if i == d:
                at.append(1 - self.mine[i] if flip else self.mine[i])
            else:
                at.append(self.mine[i] if i in gone else slice(None))
        return at, d, (pl.ds(lo, hi - lo),)

    def link(self, part, k):
        at, d, tail = self.where(part, k, True)
        return remote(
            self.run.at[tuple(at) + tail], self.bufs[k].at[(slice(None),) * (self.links - 1 - k) + tail],
            self.link_send.at[part, k], self.link_recv.at[part, k], partner(self.dims[d]),
        )

    def add_core(self, half):
        self.core(half).wait_recv()
        inner = self.links - 1
        for i in range(1 << inner):
            at = (half,) + tuple((i >> (inner - 1 - j)) & 1 for j in range(inner))
            own = self.terms[self.index(at, self.mine[-1])] if self.own is None else self.own[at]
            self.run[at] = (self.run[at].astype(F32) + own.astype(F32)).astype(BF16)

    def start_links(self):
        for part in range(len(self.orders)):
            self.link(part, 0).start()

    def step(self, k, out=None):
        for part in range(len(self.orders)):
            at, _, tail = self.where(part, k, False)
            self.link(part, k).wait_recv()
            free = self.links - 1 - k
            for i in range(1 << free):
                idx = [(i >> (free - 1 - j)) & 1 for j in range(free)]
                rest = iter(idx)
                to = tuple(next(rest) if isinstance(v, slice) else v for v in at) + tail
                total = self.run[to].astype(F32) + self.bufs[k][tuple(idx) + tail].astype(F32)
                if k + 1 < self.links:
                    self.run[to] = total.astype(BF16)
                else:
                    out[tail[0], :] = total
            if k + 1 < self.links:
                self.link(part, k + 1).start()

    def finish(self):
        for half in range(2):
            self.core(half).wait_send()
        for part in range(len(self.orders)):
            for k in range(self.links):
                self.link(part, k).wait_send()


class Line:
    def __init__(self, n):
        self.n, self.ys = n, n // 8
        me = lax.axis_index("ctx")
        self.z, self.y, self.c = me // (2 * self.ys), me // 2 % self.ys, me % 2
        high = self.z // 2
        self.slots = [3 - 3 * high, 2 - high, self.z + 1 - 2 * (self.z % 2), self.z]
        self.inner = (self.z == 1) | (self.z == 2)
        self.outer = (self.z == 0) | (self.z == 3)
        self.side = (self.z + 1) // 2 % 2
        self.near = self.at(self.slots[2], self.y, self.c)
        self.far = self.at(self.z + 1 - 2 * high, self.y, self.c)
        self.core = self.at(self.z, self.y, 1 - self.c)

    def at(self, z, y, c):
        return {"ctx": (z * self.ys + y) * 2 + c}

    def others(self):
        return [(self.y + d) % self.ys for d in range(1, self.ys)]


class LineGather:
    def __init__(self, line, buf, sems):
        self.l, self.buf = line, buf
        self.zs, self.zr, self.ys, self.yr, self.ks, self.kr = sems

    @staticmethod
    def sems(n):
        ys = n // 8
        return [DMA((5,)), DMA((3,)), DMA((ys - 1, 4)), DMA((ys - 1, 4)), DMA((ys, 4)), DMA((ys, 4))]

    def move(self, z, y, c, send, recv, peer):
        ref = self.buf.at[z, y, c]
        return remote(ref, ref, send, recv, peer)

    def zcopy(self, i):
        l = self.l
        slot, peer, into = [(3, l.near, 0), (3, l.far, 1), (2, l.far, 2), (1, l.near, 1), (0, l.near, 2)][i]
        return self.move(l.slots[slot], l.y, l.c, self.zs.at[i], self.zr.at[into], peer)

    def ycopy(self, d, slot):
        l = self.l
        return self.move(l.slots[slot], l.y, l.c, self.ys.at[d, slot], self.yr.at[d, slot], l.at(l.z, l.others()[d], l.c))

    def kcopy(self, d, slot):
        l = self.l
        y = l.y if d == 0 else (l.y + l.ys - d) % l.ys
        return self.move(l.slots[slot], y, l.c, self.ks.at[d, slot], self.kr.at[d, slot], l.core)

    def spread(self, slot):
        for d in range(self.l.ys - 1):
            self.ycopy(d, slot).start()
        self.kcopy(0, slot).start()

    def start(self):
        self.zcopy(0).start()

        @pl.when(self.l.inner)
        def _():
            self.zcopy(1).start()

        self.spread(3)

    def z_step(self, r):
        self.zcopy((0, 3, 4)[r]).wait_recv()

        @pl.when(self.l.inner)
        def _():
            self.zcopy(2 + r).start()

        self.spread(2 - r)

    def y_step(self, slot):
        for d in range(self.l.ys - 1):
            self.ycopy(d, slot).wait_recv()
            self.kcopy(d + 1, slot).start()

    def run(self):
        self.start()
        for r in range(3):
            self.z_step(r)
            self.y_step(3 - r)
        self.y_step(0)

    def core_wait(self, slot):
        for d in range(self.l.ys):
            self.kcopy(d, slot).wait_recv()

    def finish(self):
        self.zcopy(0).wait_send()

        @pl.when(self.l.inner)
        def _():
            for i in range(1, 5):
                self.zcopy(i).wait_send()

        for slot in range(4):
            for d in range(self.l.ys - 1):
                self.ycopy(d, slot).wait_send()
            for d in range(self.l.ys):
                self.kcopy(d, slot).wait_send()


class LineScatter:
    def __init__(self, line, acc, kbuf, ybuf, zbuf, sems):
        self.l, self.acc, self.kbuf, self.ybuf, self.zbuf = line, acc, kbuf, ybuf, zbuf
        self.zs, self.zr, self.ys, self.yr, self.ks, self.kr = sems

    @staticmethod
    def sems(n):
        ys = n // 8
        return [DMA((3,)), DMA((2, 3)), DMA((ys - 1, 4)), DMA((ys - 1, 4)), DMA((ys, 4)), DMA((ys, 4))]

    @staticmethod
    def scratch(n, rows, cols):
        ys = n // 8
        return [pltpu.VMEM((4, ys, rows, cols), BF16), pltpu.VMEM((ys - 1, 4, rows, cols), BF16), pltpu.VMEM((2, 3, rows, cols), BF16)]

    def y_of(self, d):
        return self.l.y if d == 0 else self.l.others()[d - 1]

    def kcopy(self, d, slot):
        l = self.l
        z, y = l.slots[slot], self.y_of(d)
        return remote(self.acc.at[z, y, 1 - l.c], self.kbuf.at[z, y], self.ks.at[d, slot], self.kr.at[d, slot], l.core)

    def ycopy(self, d, slot):
        l = self.l
        z, y = l.slots[slot], self.y_of(d + 1)
        return remote(self.acc.at[z, y, l.c], self.ybuf.at[d, slot], self.ys.at[d, slot], self.yr.at[d, slot], l.at(l.z, y, l.c))

    def zcopy(self, slot):
        l = self.l
        return remote(self.acc.at[l.slots[slot], l.y, l.c], self.zbuf.at[l.side, slot], self.zs.at[slot], self.zr.at[l.side, slot], l.far if slot < 2 else l.near)

    def zwait(self, side, slot):
        buf = self.zbuf.at[side, slot]
        remote(buf, buf, self.zs.at[slot], self.zr.at[side, slot], self.l.near).wait_recv()
        return self.zbuf[side, slot].astype(F32)

    def own(self, slot):
        return (self.l.slots[slot], self.l.y, self.l.c)

    def core_start(self, slot):
        for d in range(self.l.ys - 1, -1, -1):
            self.kcopy(d, slot).start()

    def core_step(self, slot):
        l = self.l
        for d in list(range(1, l.ys)) + [0]:
            z, y = l.slots[slot], self.y_of(d)
            self.kcopy(d, slot).wait_recv()
            self.acc[z, y, l.c] = (self.acc[z, y, l.c].astype(F32) + self.kbuf[z, y].astype(F32)).astype(BF16)
            if d > 0:
                self.ycopy(d - 1, slot).start()

    def y_sum(self, slot):
        total = self.acc[self.own(slot)].astype(F32)
        for d in range(self.l.ys - 1):
            self.ycopy(d, slot).wait_recv()
            total = total + self.ybuf[d, slot].astype(F32)
        return total

    def z_step(self, slot):
        l, own = self.l, self.own(slot)
        total = self.y_sum(slot)
        self.acc[own] = total.astype(BF16)
        @pl.when(l.inner)
        def _():
            self.acc[own] = (self.acc[own].astype(F32) + self.zwait(*((0, slot) if slot < 2 else (1, 0)))).astype(BF16)

        self.zcopy(slot).start()

    def last(self, out):
        l = self.l
        out[...] = self.y_sum(3)

        @pl.when(l.inner)
        def _():
            out[...] += self.zwait(0, 2) + self.zwait(1, 1)

        @pl.when(l.outer)
        def _():
            out[...] += self.zwait(1, 2)

    def finish(self):
        for slot in range(4):
            for d in range(self.l.ys):
                self.kcopy(d, slot).wait_send()
            for d in range(self.l.ys - 1):
                self.ycopy(d, slot).wait_send()
        for slot in range(3):
            self.zcopy(slot).wait_send()


G1, C1, BQV, IDS, BO, G2, C2, BF, BP = range(9)


def put_ids(n, small_all, first, row, col):
    tokens = small_all.shape[2]
    for j in range(n):
        ids = small_all[first + j].astype(F32)[IDS : IDS + 1, :]
        row[:, j * tokens : (j + 1) * tokens] = ids
        col[j * tokens : (j + 1) * tokens, :] = jnp.transpose(jnp.broadcast_to(ids, (tokens, tokens)))[:, :1]


def half_row(tile_row, odd, high):
    lane = lax.broadcasted_iota(jnp.int32, tile_row.shape, 1)
    turned = pltpu.roll(tile_row, 64, 1)
    moved = jnp.where((odd == 1) == high, tile_row, turned)
    return jnp.where((lane >= 64) == high, moved, 0.0)


def normalize(rows):
    centred = rows - jnp.mean(rows, axis=-1, keepdims=True)
    rstd = lax.rsqrt(jnp.mean(centred * centred, axis=-1, keepdims=True) + EPSILON)
    return centred * rstd, rstd


def group_of(n, f):
    d, j = f // n, f % n
    return d % 2 * (n // 2) + j % (n // 2), d // 2 * 2 + j // (n // 2)


def group_peer(n, i, count):
    d, j = lax.axis_index("dp"), lax.axis_index("ctx")
    g = lax.rem(d // 2 * 2 + j // (n // 2) + i, count)
    return g, {"dp": g // 2 * 2 + d % 2, "ctx": g % 2 * (n // 2) + j % (n // 2)}


def put_small(pieces, tile, small_ref):
    tile[...] = jnp.zeros_like(tile)
    for k, piece in enumerate(pieces):
        tile[k : k + 1, : piece.shape[1]] = piece[...].astype(F32)
    small_ref[...] = tile[...].astype(BF16)


def put_params(count, width, small_all, prm, bqv):
    for size, ref in ((width // count, prm), (2 * width // count, bqv)):
        per = 128 // size
        for k in range(count // per):
            tile = small_all[k * per].astype(F32)
            for i in range(1, per):
                tile = tile + pltpu.roll(small_all[k * per + i].astype(F32), i * size, 1)
            if ref is prm:
                prm[:, k * 128 : (k + 1) * 128] = tile
            else:
                bqv[k : k + 1, :] = tile[BQV : BQV + 1]


def front_kernel(n_dp, n, r, cube, *refs):
    refs = list(refs)
    take = lambda k: [refs.pop(0) for _ in range(k)]
    x_ref, pieces, dy_ref = refs.pop(0), take(9), refs.pop(0)
    (wq_all,) = take(1)
    small_all, first_out, a_ref, b_ref, o_ref, att, dy_all = take(7)
    xbuf, first, prm, bqv, bias, idrow, idcol, packed, acc, tot, own_sems, first_sems, tile, small_ref = take(14)
    line_sems, small_sems, dy_sems, att_sems = take(6), take(2), take(4), take(2)
    tokens, width = x_ref.shape
    count = n_dp * n
    d, me = lax.axis_index("dp"), lax.axis_index("ctx")
    flat = d * n + me
    head, part = me // r, me % r
    line = Line(n)
    hello = Greet(n_dp, n)

    xg = LineGather(line, xbuf, line_sems)
    small = ToAll(n_dp, n, lambda f: small_ref, small_all, small_sems)
    dyg = Gather(cube, dy_all, dy_sems)
    own_copies = [pltpu.make_async_copy(dy_ref, dy_all.at[dyg.own()], own_sems.at[0])]
    for c in own_copies:
        c.start()
    xbuf[line.z, line.y, line.c] = x_ref[...]
    put_small(pieces, tile, small_ref)
    small_all[flat] = small_ref[...]
    hello.wait()
    xg.start()
    small.start()
    for c in own_copies:
        c.wait()
    xg.z_step(0)
    xg.y_step(3)
    small.wait_recv()
    put_params(count, width, small_all, prm, bqv)
    odd = head % 2
    bias[:, :128] = half_row(bqv[pl.ds(head // 2, 1), :], odd, False)
    bias[:, 128:] = half_row(bqv[pl.ds(width // 128 + head // 2, 1), :], odd, True)
    put_ids(n, small_all, d * n, idrow, idcol)
    per_z = n // 4

    def plane(slot):
        return pl.ds(pl.multiple_of(line.slots[slot] * per_z * tokens, per_z * tokens), per_z * tokens)

    def save(slot):
        return pltpu.make_async_copy(first.at[plane(slot)], first_out.at[plane(slot)], first_sems.at[slot])

    def project(slot):
        z = line.slots[slot]

        def one(i, _):
            normed, _ = normalize(xbuf[z, i // 2, i % 2].astype(F32))
            low = (normed * prm[G1 : G1 + 1, :] + prm[C1 : C1 + 1, :]).astype(BF16)
            first[pl.ds(pl.multiple_of((z * per_z + i) * tokens, tokens), tokens), :] = low
            return 0

        lax.fori_loop(0, per_z, one, 0)
        at = plane(slot)
        weights = wq_all[...]
        qkv = (dot(first[at, :], weights) + bias[...]).astype(BF16)
        a_ref[at, :] = qkv[:, :128]
        b_ref[at, :] = qkv[:, 128:]
        save(slot).start()

    xg.z_step(1)
    xg.y_step(2)
    xg.core_wait(3)
    project(3)
    xg.z_step(2)
    xg.y_step(1)
    xg.core_wait(2)
    project(2)
    xg.y_step(0)
    dyg.start()
    xg.core_wait(1)
    project(1)
    xg.core_wait(0)
    project(0)
    dyg.step(0)

    length = b_ref.shape[0]
    kc = min(1024, length)
    half = tokens // 2
    if r > 1:
        packed[...] = jnp.zeros_like(packed)

    def per_queries(lb, _):
        gq = lb * r + part
        qs = pl.ds(pl.multiple_of(gq * QB, QB), QB)
        a = a_ref[qs, :] * 0.125
        ids = idcol[qs, :]
        acc[...] = jnp.zeros_like(acc)
        tot[...] = jnp.zeros_like(tot)

        def per_keys(kb, _):
            ks = pl.ds(pl.multiple_of(kb * kc, kc), kc)
            b = b_ref[ks, :]
            s = dot(a, b, NT)
            w = jnp.where(idrow[:, ks] <= ids, jnp.exp(s), 0.0)
            t = w[:, :128]
            for i in range(1, kc // 128):
                t = t + w[:, i * 128 : (i + 1) * 128]
            tot[...] += t
            acc[...] += dot(w.astype(BF16), b)
            return 0

        lax.fori_loop(0, jnp.minimum(((gq + 2) * QB + kc - 1) // kc, length // kc), per_keys, 0)
        t = jnp.sum(tot[...], axis=-1, keepdims=True)
        o = acc[...] / t
        lane = lax.broadcasted_iota(jnp.int32, (QB, 128), 1)
        o_ref[pl.ds(pl.multiple_of(lb * QB, QB), QB), :] = jnp.where(lane < 64, t, o)
        lane = lax.broadcasted_iota(jnp.int32, (half, 128), 1)
        for i in range(QB // tokens):
            lo, hi = o[i * tokens : i * tokens + half], o[i * tokens + half : (i + 1) * tokens]
            packed[gq * (QB // tokens) + i] = jnp.where(lane < 64, pltpu.roll(lo, 64, 1), hi).astype(BF16)
        return 0

    blocks = length // QB // r
    cuts = [0, blocks // 2, blocks * 3 // 4, blocks]
    for k in range(3):
        lax.fori_loop(cuts[k], cuts[k + 1], per_queries, 0)
        if k + 1 < dyg.links:
            dyg.step(k + 1)
    out = ToAll(n_dp, n, lambda f: packed.at[f], att, att_sems, True)
    att[me] = packed[me]
    out.start()
    for k in range(3, dyg.links):
        dyg.step(k)
    out.wait_recv()
    dyg.core_wait()
    for slot in range(4):
        save(slot).wait()
    small.wait_send()
    out.wait_send()
    xg.finish()
    dyg.finish()


def front(n_dp, n, r, x, small, dy, weights):
    tokens, width = x.shape
    count, length = n_dp * n, n * tokens
    cube = cube_plan(n, tokens)
    shape = jax.ShapeDtypeStruct
    vm, hbm = pl.BlockSpec(memory_space=pltpu.VMEM), pl.BlockSpec(memory_space=pl.ANY)
    outs = [
        (shape((count, 16, 128), BF16), vm), (shape((length, width), BF16), hbm), (shape((length, 128), BF16), vm),
        (shape((length, 128), BF16), vm), (shape((length // r, 128), F32), vm), (shape((n, tokens // 2, 128), BF16), vm),
        (shape((2,) * len(cube[0]) + (tokens, width), BF16), hbm),
    ]
    sems = LineGather.sems(n) + [DMA((count,))] * 2 + Gather.sems(cube) + [DMA((n,))] * 2
    ins = [x, *small, dy]
    ins += [weights]
    return pl.pallas_call(
        functools.partial(front_kernel, n_dp, n, r, cube),
        out_shape=[o for o, _ in outs],
        in_specs=[vm] * len(ins),
        out_specs=[s for _, s in outs],
        scratch_shapes=[
            pltpu.VMEM((4, n // 8, 2, tokens, width), BF16), pltpu.VMEM((length, width), BF16), pltpu.VMEM((16, width), F32),
            pltpu.VMEM((2 * width // 128, 128), F32), pltpu.VMEM((1, 256), F32), pltpu.VMEM((1, length), F32),
            pltpu.VMEM((length, 1), F32), pltpu.VMEM((n, tokens // 2, 128), BF16), pltpu.VMEM((QB, 128), F32),
            pltpu.VMEM((QB, 128), F32), DMA((3,)), DMA((4,)),
            pltpu.VMEM((16, 128), F32), pltpu.VMEM((16, 128), BF16),
        ] + sems,
        compiler_params=pltpu.CompilerParams(collective_id=1, has_side_effects=True, vmem_limit_bytes=VMEM_LIMIT),
        name="front",
    )(*ins)


def gelu_both(u):
    c = math.sqrt(2.0 / math.pi)
    t = jnp.tanh(c * (u + 0.044715 * (u * u * u)))
    half = 0.5 * (1.0 + t)
    return u * half, half + 0.5 * u * (1.0 - t * t) * (c * (1.0 + 3.0 * 0.044715 * (u * u)))


def normalize_back(grad, normed, rstd):
    return rstd * (
        grad
        - jnp.mean(grad, axis=-1, keepdims=True)
        - normed * jnp.mean(grad * normed, axis=-1, keepdims=True)
    )


def ffn_kernel(n, r, plan, *refs):
    refs = list(refs)
    take = lambda k: [refs.pop(0) for _ in range(k)]
    att, x_ref, dy_own, dy_hbm, wo_ref, wf_ref, wp_in, bf_ref, par_ref = take(9)
    middle_ref, mg_ref, low_ref, branch_ref, agb, sums_ref, out_hbm, wp_grad, wf_grad, bf_grad = take(10)
    links = len(plan[0]) - 1
    sbuf, dy_ref, grads, act, hid, acc, out_ref, sg, copy_sems, out_sems = take(10)
    bufs, gather_sems, scatter_sems = take(links + 1), take(4), take(4)
    g = Gather(plan, sbuf, gather_sems)
    s = Scatter(plan, acc, bufs, scatter_sems)
    peers = g.peers()
    hello = Greet(1, n, peers)
    wp_ref = wp_in
    dy_copy = pltpu.make_async_copy(dy_hbm, dy_ref, copy_sems)
    dy_copy.start()
    tokens, width = x_ref.shape
    half = tokens // 2
    quarter = (1 << (links - 1)) * tokens
    inner = (slice(None),) * (links - 1)
    core = g.mine[-1]

    lane = lax.broadcasted_iota(jnp.int32, (half, 128), 1)

    def block(h):
        total = att[h * r].astype(F32)
        for i in range(1, r):
            total = total + att[h * r + i].astype(F32)
        return total

    for h in range(0, HEADS, 2):
        b0, b1 = block(h), block(h + 1)
        at = slice(h * 64, h * 64 + 128)
        low_ref[:half, at] = jnp.where(lane < 64, b0, pltpu.roll(b1, 64, 1)).astype(BF16)
        low_ref[half:, at] = jnp.where(lane < 64, pltpu.roll(b0, 64, 1), b1).astype(BF16)
    middle = x_ref[...].astype(F32) + dot(low_ref[...], wo_ref[...]) + par_ref[0:1, :]
    middle_ref[...] = middle
    n2, _ = normalize(middle)
    sbuf[g.own()] = (n2 * par_ref[1:2, :] + par_ref[2:3, :]).astype(BF16)
    hello.wait()
    g.start()
    dy_copy.wait()
    def rows(c, a):
        return pl.ds(pl.multiple_of((2 * c + a) * quarter, quarter), quarter)

    def grad_part(i):
        dy = dy_ref[(i // 2, i % 2) + inner].reshape(quarter, width)
        grads[rows(i // 2, i % 2), :] = dot(dy, wp_ref[...], NT)

    for k in range(links):
        g.step(k)
        if k == 1:
            for i in range(4):
                grad_part(i)
    g.core_wait()
    bf_grad[...] = jnp.zeros_like(bf_grad)

    def hidden_part(c, a):
        at = rows(c, a)
        low = sbuf[(c, a) + inner].reshape(quarter, width)
        active, slope = gelu_both(dot(low, wf_ref[...]) + bf_ref[...])
        act[at, :] = active.astype(BF16)
        h = (slope * grads[at, :]).astype(BF16)
        hid[at, :] = h
        bf_grad[...] += jnp.sum(h.astype(F32), axis=0, keepdims=True)
        acc[(c, a) + inner] = dot(h, wf_ref[...], NT).astype(BF16).reshape((2,) * (links - 1) + (tokens, width))

    for a in range(2):
        hidden_part(1 - core, a)
        s.core(a).start()
    for a in range(2):
        hidden_part(core, a)
        s.add_core(a)
    s.start_links()

    def weight_grads(k):
        at = slice(k * 256, (k + 1) * 256)
        low = sbuf[..., at].reshape(4 * quarter, 256)
        wf_grad[at, :] = jnp.transpose(dot(hid[...], low, TN)).astype(BF16)
        dy = dy_ref[..., at].reshape(4 * quarter, 256)
        wp_grad[:, at] = dot(act[...], dy, TN).astype(BF16)

    def out_part(i):
        at = (i // 2, i % 2) + inner
        if i >= out_ref.shape[0]:
            out_copy(i - out_ref.shape[0]).wait()
        terms = dot(act[rows(i // 2, i % 2), :], wp_ref[...]).astype(BF16)
        out_ref[i % out_ref.shape[0]] = terms.reshape((2,) * (links - 1) + (tokens, width))
        out_copy(i).start()

    def out_copy(i):
        slot = i % out_ref.shape[0]
        return pltpu.make_async_copy(out_ref.at[slot], out_hbm.at[(i // 2, i % 2) + inner], out_sems.at[slot])

    for i in range(4):
        out_part(i)
    for k in range(links):
        s.step(k, sg)
        if k < 2:
            weight_grads(2 * k)
            weight_grads(2 * k + 1)

    second_grad = sg[...]
    dy = dy_own[...].astype(F32)
    n2, rstd2 = normalize(middle_ref[...])
    mg = dy + normalize_back(second_grad * par_ref[1:2, :], n2, rstd2)
    mg_ref[...] = mg
    branch = mg.astype(BF16)
    branch_ref[...] = branch
    grad = dot(branch, wo_ref[...], NT)
    for h in range(0, HEADS, 2):
        lo, hi = grad[:half, h * 64 : h * 64 + 128], grad[half:, h * 64 : h * 64 + 128]
        b0 = jnp.where(lane < 64, lo, pltpu.roll(hi, 64, 1)).astype(BF16)
        b1 = jnp.where(lane < 64, pltpu.roll(lo, 64, 1), hi).astype(BF16)
        for i in range(r):
            agb[h * r + i] = b0
            agb[(h + 1) * r + i] = b1
    column = lambda v: jnp.sum(v, axis=0, keepdims=True)
    sums_ref[0:1, :] = column(branch.astype(F32))
    sums_ref[1:2, :] = column(second_grad * n2)
    sums_ref[2:3, :] = column(second_grad)
    sums_ref[3:4, :] = column(dy)
    for i in range(4 - out_ref.shape[0], 4):
        out_copy(i).wait()
    s.finish()
    g.finish()


def ffn(n, r, att, x, dy, dy_all, wo, wf, wp, bf, params):
    tokens, width = x.shape
    units = wf.shape[1]
    plan = cube_plan(n, tokens)
    block = (2,) * len(plan[0])
    length = n * tokens
    shape = jax.ShapeDtypeStruct
    vm, hbm = pl.BlockSpec(memory_space=pltpu.VMEM), pl.BlockSpec(memory_space=pl.ANY)
    return pl.pallas_call(
        functools.partial(ffn_kernel, n, r, plan),
        out_shape=[
            shape((tokens, width), F32), shape((tokens, width), F32), shape((tokens, width), BF16), shape((tokens, width), BF16),
            shape((n, tokens // 2, 128), BF16), shape((4, width), F32), shape(block + (tokens, width), BF16),
            shape((units, width), BF16), shape((width, units), BF16), shape((1, units), F32),
        ],
        in_specs=[vm, vm, vm, hbm, vm, vm, vm, vm, vm],
        out_specs=[vm, vm, vm, vm, vm, vm, hbm, vm, vm, vm],
        scratch_shapes=[
            pltpu.VMEM(block + (tokens, width), BF16), pltpu.VMEM(block + (tokens, width), BF16), pltpu.VMEM((length, units), F32),
            pltpu.VMEM((length, units), BF16), pltpu.VMEM((length, units), BF16), pltpu.VMEM(block + (tokens, width), BF16),
            pltpu.VMEM((2,) + block[2:] + (tokens, width), BF16), pltpu.VMEM((tokens, width), F32), DMA, DMA((2,)),
        ] + Scatter.scratch(plan, tokens, width) + Gather.sems(plan) + Scatter.sems(plan),
        compiler_params=pltpu.CompilerParams(collective_id=2, has_side_effects=True, vmem_limit_bytes=VMEM_LIMIT),
        name="ffn",
    )(att, x, dy, dy_all, wo, wf, wp, bf, params)


def project_rows(rows, prm):
    normed, _ = normalize(rows.astype(F32))
    return (normed * prm[G1 : G1 + 1, :] + prm[C1 : C1 + 1, :]).astype(BF16)


def lead_kernel(n_dp, n, cube, whole, *refs):
    refs = list(refs)
    take = lambda k: [refs.pop(0) for _ in range(k)]
    x_ref, pieces, (dy_own, w_qkv, w_fc, w_proj, w_out) = refs.pop(0), take(9), take(5)
    small_all, first_out, a_ref, b_ref, o_ref, wq_all, par_ref = take(7)
    middle_ref, mg_ref, low_ref, branch_ref, agb, sums_ref, out_hbm, wp_grad, wf_grad, bf_grad = take(10)
    xbuf, first, prm, bqv, bias, bf_row, idrow, idcol, packed, acc, tot, att, wqb, wfb = take(14)
    wf_all, wo_all, wp_ref, dy_ref, sbuf, grads, act, hid, terms, out_ref, sg = take(11)
    first_sems, out_sems, tile, small_ref = take(4)
    links = len(cube[0]) - 1
    bufs = take(links + 1)
    line_sems, small_sems, dy_sems, att_sems, wq_sems, wf_sems, wo_sems = take(6), take(2), take(4), take(2), take(4), take(2), take(4)
    wp_sems, gather_sems, scatter_sems = take(2), take(4), take(4)

    tokens, width = x_ref.shape
    length = n * tokens
    rows, units = w_fc.shape[0], w_proj.shape[0]
    count = n_dp * n
    d, me = lax.axis_index("dp"), lax.axis_index("ctx")
    flat = d * n + me
    rank, group = group_of(n, flat)
    line = Line(n)
    hello = Greet(n_dp, n)

    xg = LineGather(line, xbuf, line_sems)
    small = ToAll(n_dp, n, lambda f: small_ref, small_all, small_sems)
    wq = ToAll(n_dp, n, lambda f: wqb.at[f], wq_all.at[d], wq_sems[:2], True)
    wf = ToAll(n_dp, n, lambda f: wfb.at[group_of(n, f)[0]], wf_all, wf_sems)
    dyg = Gather(cube, dy_ref, dy_sems)
    wog = Gather(whole, wo_all, wo_sems)
    out = ToAll(n_dp, n, lambda f: packed.at[f], att, att_sems, True)
    g = Gather(cube, sbuf, gather_sems)
    s = Scatter(cube, terms, bufs, scatter_sems)
    dps, wps = [], []
    for i in range(1, n_dp):
        dps.append(remote(wq_all.at[d], wq_all.at[d], wq_sems[2].at[i], wq_sems[3].at[i], {"dp": (d + i) % n_dp}))
        to = wp_ref.at[pl.ds(pl.multiple_of(group * units, units), units)]
        wps.append(remote(w_proj, to, wp_sems[0].at[i], wp_sems[1].at[i], group_peer(n, i, n_dp)[1]))

    low = lax.broadcasted_iota(jnp.int32, (rows, 128), 1) < 64
    for h in range(0, HEADS, 2):
        q, k, v = (w_qkv[:, p * width + h * 64 : p * width + h * 64 + 128].astype(F32) for p in range(3))
        turn = lambda t: pltpu.roll(t, 64, 1)
        wqb[h, :, :128] = jnp.where(low, q, 0.0).astype(BF16)
        wqb[h, :, 128:] = jnp.where(low, k, turn(v)).astype(BF16)
        wqb[h + 1, :, :128] = jnp.where(low, turn(q), 0.0).astype(BF16)
        wqb[h + 1, :, 128:] = jnp.where(low, turn(k), v).astype(BF16)
    xbuf[line.z, line.y, line.c] = x_ref[...]
    put_small(pieces, tile, small_ref)
    small_all[flat] = small_ref[...]
    wq_all[d, me] = wqb[me]
    wo_all[wog.own()] = w_out[...]
    hello.wait()
    xg.start()
    small.start()
    wq.start()
    wog.start()
    for m in range(n):
        for i in range(n_dp):
            at = ((i // 2 * 2 + m // (n // 2)) * n + i % 2 * (n // 2) + m % (n // 2)) * units
            wfb[m, :, i * units : (i + 1) * units] = w_fc[:, at : at + units]
    dy_ref[dyg.own()] = dy_own[...]
    wf_all[flat] = wfb[rank]
    wp_ref[pl.ds(pl.multiple_of(group * units, units), units), :] = w_proj[...]
    xg.z_step(0)
    xg.y_step(3)
    wq.wait_recv()
    for c in dps:
        c.start()
    small.wait_recv()
    put_params(count, width, small_all, prm, bqv)
    odd = me % 2
    bias[:, :128] = half_row(bqv[pl.ds(me // 2, 1), :], odd, False)
    bias[:, 128:] = half_row(bqv[pl.ds(width // 128 + me // 2, 1), :], odd, True)
    for i in range(n_dp):
        owner = (i // 2 * 2 + d % 2) * n + i % 2 * (n // 2) + me % (n // 2)
        bf_row[:, i * units : (i + 1) * units] = small_all[owner].astype(F32)[BF : BF + 1, :units]
    par_ref[0:1, :] = prm[G1 : G1 + 1, :]
    par_ref[1:2, :] = prm[BP : BP + 1, :]
    put_ids(n, small_all, d * n, idrow, idcol)
    per_z = n // 4

    def plane(slot):
        return pl.ds(pl.multiple_of(line.slots[slot] * per_z * tokens, per_z * tokens), per_z * tokens)

    def save(slot):
        return pltpu.make_async_copy(first.at[plane(slot)], first_out.at[plane(slot)], first_sems.at[slot])

    def project(slot):
        z = line.slots[slot]

        def one(i, _):
            at = pl.ds(pl.multiple_of((z * per_z + i) * tokens, tokens), tokens)
            first[at, :] = project_rows(xbuf[z, i // 2, i % 2], prm)
            return 0

        lax.fori_loop(0, per_z, one, 0)
        at = plane(slot)
        qkv = (dot(first[at, :], wq_all[...].reshape(width, 256)) + bias[...]).astype(BF16)
        a_ref[at, :] = qkv[:, :128]
        b_ref[at, :] = qkv[:, 128:]
        save(slot).start()

    xg.z_step(1)
    xg.y_step(2)
    wog.step(0)
    for c in dps:
        c.wait_recv()
    xg.core_wait(3)
    project(3)
    xg.z_step(2)
    xg.y_step(1)
    wog.step(1)
    xg.core_wait(2)
    project(2)
    xg.y_step(0)
    dyg.start()
    for c in wps:
        c.start()
    wf.start()
    wog.step(2)
    xg.core_wait(1)
    project(1)
    xg.core_wait(0)
    project(0)
    dyg.step(0)

    kc = min(1024, length)
    half = tokens // 2
    lane = lax.broadcasted_iota(jnp.int32, (half, 128), 1)

    def per_queries(gq, _):
        qs = pl.ds(pl.multiple_of(gq * QB, QB), QB)
        a = a_ref[qs, :] * 0.125
        ids = idcol[qs, :]
        acc[...] = jnp.zeros_like(acc)
        tot[...] = jnp.zeros_like(tot)

        def per_keys(kb, _):
            ks = pl.ds(pl.multiple_of(kb * kc, kc), kc)
            b = b_ref[ks, :]
            w = jnp.where(idrow[:, ks] <= ids, jnp.exp(dot(a, b, NT)), 0.0)
            t = w[:, :128]
            for i in range(1, kc // 128):
                t = t + w[:, i * 128 : (i + 1) * 128]
            tot[...] += t
            acc[...] += dot(w.astype(BF16), b)
            return 0

        lax.fori_loop(0, jnp.minimum(((gq + 2) * QB + kc - 1) // kc, length // kc), per_keys, 0)
        t = jnp.sum(tot[...], axis=-1, keepdims=True)
        o = acc[...] / t
        o_ref[qs, :] = jnp.where(lax.broadcasted_iota(jnp.int32, (QB, 128), 1) < 64, t, o)
        for i in range(QB // tokens):
            lo, hi = o[i * tokens : i * tokens + half], o[i * tokens + half : (i + 1) * tokens]
            packed[gq * (QB // tokens) + i] = jnp.where(lane < 64, pltpu.roll(lo, 64, 1), hi).astype(BF16)
        return 0

    blocks = length // QB
    lax.fori_loop(0, blocks // 2, per_queries, 0)
    dyg.step(1)
    wog.step(3)
    lax.fori_loop(blocks // 2, blocks, per_queries, 0)
    att[me] = packed[me]
    out.start()
    for k in range(4, wog.links):
        wog.step(k)
    wog.core_wait()
    out.wait_recv()

    for h in range(0, HEADS, 2):
        b0, b1 = att[h].astype(F32), att[h + 1].astype(F32)
        at = slice(h * 64, h * 64 + 128)
        low_ref[:half, at] = jnp.where(lane < 64, b0, pltpu.roll(b1, 64, 1)).astype(BF16)
        low_ref[half:, at] = jnp.where(lane < 64, pltpu.roll(b0, 64, 1), b1).astype(BF16)
    middle = x_ref[...].astype(F32) + dot(low_ref[...], wo_all[...].reshape(width, width)) + prm[BO : BO + 1, :]
    middle_ref[...] = middle
    n2, _ = normalize(middle)
    sbuf[g.own()] = (n2 * prm[G2 : G2 + 1, :] + prm[C2 : C2 + 1, :]).astype(BF16)
    g.start()
    for k in range(2, links):
        dyg.step(k)
    for c in wps:
        c.wait_recv()
    dyg.core_wait()

    quarter = (1 << (links - 1)) * tokens
    inner = (slice(None),) * (links - 1)
    block = (2,) * (links - 1) + (tokens, width)
    core = g.mine[-1]

    def span(c, a):
        return pl.ds(pl.multiple_of((2 * c + a) * quarter, quarter), quarter)

    def grad_part(i):
        dy = dy_ref[(i // 2, i % 2) + inner].reshape(quarter, width)
        grads[span(i // 2, i % 2), :] = dot(dy, wp_ref[...], NT)

    for k in range(links):
        grad_part(k)
        g.step(k)
    for k in range(links, 4):
        grad_part(k)
    wf.wait_recv()
    g.core_wait()
    bf_grad[...] = jnp.zeros_like(bf_grad)

    def hidden_part(c, a):
        at = span(c, a)
        weights = wf_all[...].reshape(width, -1)
        active, slope = gelu_both(dot(sbuf[(c, a) + inner].reshape(quarter, width), weights) + bf_row[...])
        act[at, :] = active.astype(BF16)
        h = (slope * grads[at, :]).astype(BF16)
        hid[at, :] = h
        bf_grad[...] += jnp.sum(h.astype(F32), axis=0, keepdims=True)
        terms[(c, a) + inner] = dot(h, weights, NT).astype(BF16).reshape(block)

    for a in range(2):
        hidden_part(1 - core, a)
        s.core(a).start()
    for a in range(2):
        hidden_part(core, a)
        s.add_core(a)
    s.start_links()

    def weight_grads(k):
        at = slice(k * 256, (k + 1) * 256)
        low = sbuf[..., at].reshape(4 * quarter, 256)
        wf_grad[at, :] = jnp.transpose(dot(hid[...], low, TN)).astype(BF16)
        wp_grad[:, at] = dot(act[...], dy_ref[..., at].reshape(4 * quarter, 256), TN).astype(BF16)

    def out_copy(i):
        return pltpu.make_async_copy(out_ref.at[i % 2], out_hbm.at[(i // 2, i % 2) + inner], out_sems.at[i % 2])

    for i in range(4):
        if i >= 2:
            out_copy(i - 2).wait()
        out_ref[i % 2] = dot(act[span(i // 2, i % 2), :], wp_ref[...]).astype(BF16).reshape(block)
        out_copy(i).start()
    for k in range(links):
        s.step(k, sg)
        if k < 2:
            weight_grads(2 * k)
            weight_grads(2 * k + 1)

    second_grad = sg[...]
    dy = dy_own[...].astype(F32)
    n2, rstd2 = normalize(middle_ref[...])
    mg = dy + normalize_back(second_grad * prm[G2 : G2 + 1, :], n2, rstd2)
    mg_ref[...] = mg
    branch = mg.astype(BF16)
    branch_ref[...] = branch
    grad = dot(branch, wo_all[...].reshape(width, width), NT)
    for h in range(0, HEADS, 2):
        lo, hi = grad[:half, h * 64 : h * 64 + 128], grad[half:, h * 64 : h * 64 + 128]
        agb[h] = jnp.where(lane < 64, lo, pltpu.roll(hi, 64, 1)).astype(BF16)
        agb[h + 1] = jnp.where(lane < 64, pltpu.roll(lo, 64, 1), hi).astype(BF16)
    column = lambda v: jnp.sum(v, axis=0, keepdims=True)
    sums_ref[0:1, :] = column(branch.astype(F32))
    sums_ref[1:2, :] = column(second_grad * n2)
    sums_ref[2:3, :] = column(second_grad)
    sums_ref[3:4, :] = column(dy)
    for i in (2, 3):
        out_copy(i).wait()
    for slot in range(4):
        save(slot).wait()
    for c in (wq, wf, small, out):
        c.wait_send()
    for c in dps + wps:
        c.wait_send()
    for c in (xg, wog, dyg, g, s):
        c.finish()


def lead(n_dp, n, x, small, dy, w_qkv, w_fc, w_proj, w_out):
    tokens, width = x.shape
    count, length = n_dp * n, n * tokens
    rows, units = w_fc.shape[0], n_dp * w_proj.shape[0]
    cube, whole = cube_plan(n, tokens), all_plan(n_dp, n, rows)
    block = (2,) * len(cube[0]) + (tokens, width)
    shape = jax.ShapeDtypeStruct
    vm, hbm = pl.BlockSpec(memory_space=pltpu.VMEM), pl.BlockSpec(memory_space=pl.ANY)
    outs = [
        (shape((count, 16, 128), BF16), vm), (shape((length, width), BF16), hbm), (shape((length, 128), BF16), vm),
        (shape((length, 128), BF16), vm), (shape((length, 128), F32), vm), (shape((n_dp, n, rows, 256), BF16), vm),
        (shape((2, width), F32), vm), (shape((tokens, width), F32), vm), (shape((tokens, width), F32), vm),
        (shape((tokens, width), BF16), vm), (shape((tokens, width), BF16), vm), (shape((n, tokens // 2, 128), BF16), vm),
        (shape((4, width), F32), vm), (shape(block, BF16), hbm), (shape((units, width), BF16), vm),
        (shape((width, units), BF16), vm), (shape((1, units), F32), vm),
    ]
    return pl.pallas_call(
        functools.partial(lead_kernel, n_dp, n, cube, whole),
        out_shape=[o for o, _ in outs],
        in_specs=[vm] * 15,
        out_specs=[s for _, s in outs],
        scratch_shapes=[
            pltpu.VMEM((4, n // 8, 2, tokens, width), BF16), pltpu.VMEM((length, width), BF16), pltpu.VMEM((16, width), F32),
            pltpu.VMEM((2 * width // 128, 128), F32), pltpu.VMEM((1, 256), F32), pltpu.VMEM((1, units), F32),
            pltpu.VMEM((1, length), F32), pltpu.VMEM((length, 1), F32), pltpu.VMEM((n, tokens // 2, 128), BF16),
            pltpu.VMEM((QB, 128), F32), pltpu.VMEM((QB, 128), F32), pltpu.VMEM((n, tokens // 2, 128), BF16),
            pltpu.VMEM((n, rows, 256), BF16), pltpu.VMEM((n, rows, units), BF16),
            pltpu.VMEM((count, rows, units), BF16), pltpu.VMEM((2,) * len(whole[0]) + (rows, width), BF16),
            pltpu.VMEM((units, width), BF16), pltpu.VMEM(block, BF16), pltpu.VMEM(block, BF16),
            pltpu.VMEM((length, units), F32), pltpu.VMEM((length, units), BF16), pltpu.VMEM((length, units), BF16),
            pltpu.VMEM(block, BF16), pltpu.VMEM((2,) + block[2:], BF16), pltpu.VMEM((tokens, width), F32), DMA((4,)), DMA((2,)),
            pltpu.VMEM((16, 128), F32), pltpu.VMEM((16, 128), BF16),
        ] + Scatter.scratch(cube, tokens, width) + LineGather.sems(n) + [DMA((count,))] * 2 + Gather.sems(cube) + [DMA((n,))] * 2
        + [DMA((n,))] * 2 + [DMA((n_dp,))] * 2 + [DMA((count,))] * 2 + Gather.sems(whole) + [DMA((n_dp,))] * 2
        + Gather.sems(cube) + Scatter.sems(cube),
        compiler_params=pltpu.CompilerParams(collective_id=1, has_side_effects=True, vmem_limit_bytes=VMEM_LIMIT),
        name="lead",
    )(x, *small, dy, w_qkv, w_fc, w_proj, w_out)


def back_kernel(n_dp, n, r, spread, cube, whole, *refs):
    refs = list(refs)
    take = lambda k: [refs.pop(0) for _ in range(k)]
    agb, a_ref, b_ref, o_ref, small_all, wq_ref, first, part_out, x_ref, mid_ref, mg_ref, par_ref, sums_in, bf_grad = take(14)
    if spread:
        low_ref, branch_ref, wfg, wpg = take(4)
    out_ref, ig_ref, sums = take(3)
    if spread:
        wq_got, wf_got, wp_got, wo_own = take(4)
    else:
        (wq_sum,) = take(1)
    ag, idrow, idcol, mixed, dqacc, dkv, acc, kbuf, ybuf, zbuf, fg, got, msg, columns, column_sem, own_out, own_sem, osum = take(18)
    links = len(cube[0]) - 1
    out_bufs = take(links + 1)
    if r > 1:
        (dkv_got,) = take(1)
        pair_sems = take(2)
    ag_sems, line_sems, out_sems, msg_sems = take(2), take(6), take(4), take(2)
    if spread:
        wq_part, wq_mine, wq_else, wo_part = take(4)
        wq_sems, wf_sems, wp_sems = take(4), take(2), take(2)
        wo_bufs = take(len(whole[0]))
        wo_sems = take(4)

    tokens, width = x_ref.shape
    length = b_ref.shape[0]
    count = n_dp * n
    d, me = lax.axis_index("dp"), lax.axis_index("ctx")
    flat = d * n + me
    head, part = me // r, me % r
    line = Line(n)
    hello = Greet(n_dp, n)
    kc = min(1024, length)
    half = tokens // 2

    grads = ToAll(n_dp, n, lambda f: agb.at[f], ag, ag_sems, True)
    outs = Scatter(cube, part_out, out_bufs, out_sems, own_out)
    own_copy = outs.fetch_own(own_sem)
    own_copy.start()
    ag[me] = agb[me]
    if spread:
        wf = ToAll(n_dp, n, lambda f: wfg.at[f], wf_got, wf_sems)
        wq = ToAll(n_dp, n, lambda f: wq_mine.at[f], wq_got, wq_sems[:2], True)
        wo = Scatter(whole, wo_part, wo_bufs, wo_sems)
        wf_got[flat] = wfg[flat]
        rank, group = group_of(n, flat)
        wp_got[group] = wpg[group]
        wps, dps = [], []
        for i in range(1, n_dp):
            g, peer = group_peer(n, i, n_dp)
            wps.append(remote(wpg.at[g], wp_got.at[group], wp_sems[0].at[i], wp_sems[1].at[i], peer))
            dps.append(remote(wq_part.at[(d + i) % n_dp], wq_else.at[i], wq_sems[2].at[i], wq_sems[3].at[i], {"dp": (d + i) % n_dp}))
    else:
        rank, group = group_of(n, flat)
    dkv[...] = jnp.zeros_like(dkv)
    if r > 1:
        mixed[...] = jnp.zeros_like(mixed)
    hello.wait()
    grads.start()
    for h in range(2):
        outs.core(h).start()
    if spread:
        for c in wps:
            c.start()
    put_ids(n, small_all, d * n, idrow, idcol)
    if spread:
        rows = width // count
        for k in range(width // 256):
            terms = dot(low_ref[:, k * 256 : (k + 1) * 256], branch_ref[...], TN).astype(BF16)
            for i in range(256 // rows):
                f = k * (256 // rows) + i
                bits = tuple((f >> b) & 1 for b in range(len(whole[0]) - 1, -1, -1))
                wo_part[bits] = terms[i * rows : (i + 1) * rows]
        for h in range(2):
            wo.core(h).start()
    own_copy.wait()
    for h in range(2):
        outs.add_core(h)
    outs.start_links()
    grads.wait_recv()
    if spread:
        wf.start()

    def per_queries(lb, _):
        gq = lb * r + part
        qs = pl.ds(pl.multiple_of(gq * QB, QB), QB)
        at = pl.ds(pl.multiple_of(lb * QB, QB), QB)
        lane = lax.broadcasted_iota(jnp.int32, (half, 128), 1)
        pieces = []
        for i in range(QB // tokens):
            block = ag[gq * (QB // tokens) + i].astype(F32)
            pieces += [jnp.where(lane >= 64, pltpu.roll(block, 64, 1), 0.0), jnp.where(lane >= 64, block, 0.0)]
        grad = jnp.concatenate(pieces, axis=0)
        o = o_ref[at, :]
        inverse = 1.0 / o[:, :1]
        upper = lax.broadcasted_iota(jnp.int32, (QB, 128), 1) >= 64
        ratio = jnp.sum(jnp.where(upper, grad * o, 0.0), axis=-1, keepdims=True) * inverse
        ratio = jnp.transpose(jnp.broadcast_to(ratio, (QB, 128)))[:1, :]
        do = (grad * inverse).astype(BF16)
        a = a_ref[qs, :]
        scaled = a * 0.125
        ado = jnp.concatenate([a, do], axis=0)
        ids = idrow[:, qs]
        dqacc[...] = jnp.zeros_like(dqacc)

        def per_keys(kb, _):
            ks = pl.ds(pl.multiple_of(kb * kc, kc), kc)
            b = b_ref[ks, :]
            w = jnp.where(idcol[ks, :] <= ids, jnp.exp(dot(b, scaled, NT)), 0.0)
            g = (w * (dot(b, do, NT) - ratio)).astype(BF16)
            dkv[ks, :] += dot(jnp.concatenate([g, w.astype(BF16)], axis=1), ado)
            dqacc[...] += dot(g, b, TN)
            return 0

        lax.fori_loop(0, jnp.minimum(((gq + 2) * QB + kc - 1) // kc, length // kc), per_keys, 0)
        mixed[qs, :128] = jnp.where(upper, 0.0, dqacc[...] * 0.125).astype(BF16)
        return 0

    blocks = length // QB // r
    cuts = [0, blocks // 2, blocks * 3 // 4, blocks]
    for k in range(3):
        lax.fori_loop(cuts[k], cuts[k + 1], per_queries, 0)
        if k + 1 < links:
            outs.step(k, osum)
    if spread:
        for h in range(2):
            wo.add_core(h)

    def fetch(k):
        return pltpu.make_async_copy(first.at[:, pl.ds(pl.multiple_of(k * 256, 256), 256)], columns, column_sem)

    turns = [((d + 1) * (width // 256 // n_dp) + i) % (width // 256) if spread else i for i in range(width // 256)]
    fetch(turns[0]).start()
    low = lax.broadcasted_iota(jnp.int32, (length, 128), 1) < 64
    total = dkv[...]
    if r > 1:
        both = remote(dkv, dkv_got, pair_sems[0], pair_sems[1], line.core)
        both.start()
        both.wait()
        total = jnp.where(part == 0, total + dkv_got[...], 0.0)
    mixed[:, 128:] = jnp.where(low, total * 0.125, total).astype(BF16)

    rs = LineScatter(line, acc, kbuf, ybuf, zbuf, line_sems)
    per_z = n // 4 * tokens

    def first_grad(slot):
        z = line.slots[slot]
        at = pl.ds(pl.multiple_of(z * per_z, per_z), per_z)
        acc[z] = dot(mixed[at, :], wq_ref[...], NT).astype(BF16).reshape(n // 8, 2, tokens, width)
        rs.core_start(slot)

    first_grad(0)
    for slot in range(1, 4):
        first_grad(slot)
        rs.core_step(slot - 1)
    rs.core_step(3)
    for k in range(min(2, links - 1), links):
        outs.step(k, osum)
    if spread:
        wo.start_links()

    def wq_grad(i):
        k = turns[i]
        fetch(k).wait()
        g = jnp.transpose(dot(mixed[...], columns[...], TN))
        if i + 1 < len(turns):
            fetch(turns[i + 1]).start()
        if spread:
            per = n_dp * 256 // width
            q = 256 // rows
            at = k * q
            wq_part[at // n, pl.ds(at % n, q)] = g.astype(BF16).reshape(q, rows, 256)
        else:
            wq_sum[pl.ds(pl.multiple_of(k * 256, 256), 256), :] = g

    ahead = len(turns) - len(turns) // n_dp if spread else 2
    for i in range(ahead):
        wq_grad(i)
    if spread:
        for c in dps:
            c.start()
    rs.z_step(0)
    for i in range(ahead, len(turns)):
        wq_grad(i)
    rs.z_step(1)
    if spread:
        total = wq_part[d].astype(F32)
        for i, c in enumerate(dps):
            c.wait_recv()
            total = total + wq_else[i + 1].astype(F32)
        wq_mine[...] = total.astype(BF16)
        wq_got[me] = wq_mine[me]
        wq.start()
        wo.step(0, wo_own)
    column = jnp.sum(mixed[...].astype(F32), axis=0, keepdims=True)
    odd = head % 2
    q_row = half_row(column[:, :128], 0, False)
    q_row = jnp.where(odd == 1, pltpu.roll(q_row, 64, 1), q_row)
    v_row = half_row(column[:, 128:], 1, True)
    v_row = jnp.where(odd == 1, v_row, pltpu.roll(v_row, 64, 1))
    rs.z_step(2)
    out_ref[...] = (mid_ref[...] + osum[...] + par_ref[1:2, :]).astype(BF16)
    n1, rstd1 = normalize(x_ref[...].astype(F32))
    if spread:
        wo.step(1, wo_own)

    wide = bf_grad.shape[1] // 128

    def prepare(f, _):
        tile = f * 2 * width // count // 128
        bqv = jnp.where(tile == head // 2, q_row, 0.0) + jnp.where(tile == width // 128 + head // 2, v_row, 0.0)
        msg[f, 6:7, :] = bqv
        same = group_of(n, f)[0] == rank
        for i in range(wide):
            msg[f, 7 + i : 8 + i, :] = jnp.where(same, bf_grad[:, i * 128 : (i + 1) * 128], 0.0)
        return 0

    msg[...] = jnp.zeros_like(msg)
    lax.fori_loop(0, count, prepare, 0)
    rs.last(fg)

    grad = fg[...]
    gain = jnp.sum(grad * n1, axis=0, keepdims=True)
    shift = jnp.sum(grad, axis=0, keepdims=True)
    per = 128 * count // width
    for k in range(width // 128):
        at = slice(k * 128, (k + 1) * 128)
        lines = jnp.concatenate([gain[:, at], shift[:, at], sums_in[:, at]], axis=0)

        def fill(i, _, k=k, lines=lines):
            msg[k * per + i, 0:6, :] = lines
            return 0

        lax.fori_loop(0, per, fill, 0)
    tell = ToAll(n_dp, n, lambda f: msg.at[f], got, msg_sems)
    tell.start()
    got[flat] = msg[flat]
    ig_ref[...] = (mg_ref[...] + normalize_back(grad * par_ref[0:1, :], n1, rstd1)).astype(BF16)
    if spread:
        for k in range(2, wo.links):
            wo.step(k, wo_own)
        wf.wait_recv()
        wq.wait_recv()
        for c in wps:
            c.wait()
    tell.wait_recv()
    sums[...] = jnp.sum(got[...], axis=0)
    tell.wait_send()
    if spread:
        wf.wait_send()
        wq.wait_send()
        for c in dps:
            c.wait_send()
        wo.finish()
    grads.wait_send()
    outs.finish()
    rs.finish()


def back(n_dp, n, r, agb, a, b, o, small_all, wq, first, part_out, x, middle, mg, params, sums4, bf_grad, grads):
    tokens, width = x.shape
    count, length = n_dp * n, n * tokens
    spread = grads is not None
    cube = cube_plan(n, tokens)
    links = len(cube[0]) - 1
    whole = None
    shape = jax.ShapeDtypeStruct
    ins = [agb, a, b, o, small_all, wq, first, part_out, x, middle, mg, params, sums4, bf_grad]
    outs = [shape((tokens, width), BF16), shape((tokens, width), BF16), shape((16, 128), F32)]
    scratch = [
        pltpu.VMEM((n, tokens // 2, 128), BF16), pltpu.VMEM((1, length), F32), pltpu.VMEM((length, 1), F32),
        pltpu.VMEM((length, 256), BF16), pltpu.VMEM((QB, 128), F32), pltpu.VMEM((length, 128), F32),
        pltpu.VMEM((4, n // 8, 2, tokens, width), BF16),
    ] + LineScatter.scratch(n, tokens, width) + [
        pltpu.VMEM((tokens, width), F32), pltpu.VMEM((count, 16, 128), F32), pltpu.VMEM((count, 16, 128), F32),
        pltpu.VMEM((length, 256), BF16), DMA, pltpu.VMEM((2,) * links + (tokens, width), BF16), DMA,
        pltpu.VMEM((tokens, width), F32),
    ] + Scatter.scratch(cube, tokens, width)
    if r > 1:
        scratch += [pltpu.VMEM((length, 128), F32), DMA, DMA]
    scratch += [DMA((n,))] * 2 + LineScatter.sems(n) + Scatter.sems(cube) + [DMA((count,))] * 2
    if spread:
        low, branch, wfg, wpg = grads
        rows = width // count
        whole = all_plan(n_dp, n, rows)
        ins += [low, branch, wfg, wpg]
        outs += [shape((n, rows, 256), BF16), shape(wfg.shape, BF16), shape(wpg.shape, BF16), shape((rows, width), F32)]
        scratch += [
            pltpu.VMEM((n_dp, n, rows, 256), BF16), pltpu.VMEM((n, rows, 256), BF16), pltpu.VMEM((n_dp, n, rows, 256), BF16),
            pltpu.VMEM((2,) * len(whole[0]) + (rows, width), BF16),
        ]
        scratch += [DMA((n,))] * 2 + [DMA((n_dp,))] * 2 + [DMA((count,))] * 2 + [DMA((n_dp,))] * 2
        scratch += Scatter.scratch(whole, rows, width) + Scatter.sems(whole)
    else:
        outs += [shape((width, 256), F32)]
    vm, hbm = pl.BlockSpec(memory_space=pltpu.VMEM), pl.BlockSpec(memory_space=pl.ANY)
    return pl.pallas_call(
        functools.partial(back_kernel, n_dp, n, r, spread, cube, whole),
        out_shape=outs,
        in_specs=[hbm if v is first or v is part_out else vm for v in ins],
        out_specs=[vm] * len(outs),
        scratch_shapes=scratch,
        compiler_params=pltpu.CompilerParams(collective_id=3, has_side_effects=True, vmem_limit_bytes=VMEM_LIMIT),
        name="back",
    )(*ins)


def own_sums(n_dp, n, piece, sums):
    flat = lax.axis_index("dp") * n + lax.axis_index("ctx")
    wide = pltpu.roll(sums, (128 - flat * piece % 128) % 128, 1)
    return wide, pltpu.roll(sums, (128 - flat * 2 * piece % 128) % 128, 1)[6:7]


def finish_kernel(n_dp, n, out_in, ig_in, sums, wq_got, wf_got, wp_got, wo_in, *outs):
    out, ig, g1, c1, wq_own, bqv, wo_own, bo, g2, c2, wf_own, bf, wp_own, bp = outs
    count = n_dp * n
    rows, width = wo_in.shape
    units = wp_got.shape[1]
    out[0] = out_in[...]
    ig[0] = ig_in[...]
    wo_own[...] = wo_in[...]
    wp_own[...] = jnp.sum(wp_got[...].astype(F32), axis=0)
    for f in range(count):
        m, g = group_of(n, f)
        total = 0.0
        for i in range(n_dp):
            source = (i // 2 * 2 + m // (n // 2)) * n + i % 2 * (n // 2) + m % (n // 2)
            total = total + wf_got[source, :, g * units : (g + 1) * units].astype(F32)
        wf_own[:, f * units : (f + 1) * units] = total
    lower = lax.broadcasted_iota(jnp.int32, (rows, 128), 1) < 64
    turn = lambda t: pltpu.roll(t, 64, 1)
    for h in range(0, HEADS, 2):
        (q0, e0), (q1, e1) = ((wq_got[i, :, :128].astype(F32), wq_got[i, :, 128:].astype(F32)) for i in (h, h + 1))
        for p, v in enumerate((jnp.where(lower, q0, turn(q1)), jnp.where(lower, e0, turn(e1)), jnp.where(lower, turn(e0), e1))):
            wq_own[:, p * width + h * 64 : p * width + h * 64 + 128] = v
    wide, double = own_sums(n_dp, n, rows, sums[...])
    for i, ref in enumerate((g1, c1, bo, g2, c2, bp)):
        ref[...] = wide[i : i + 1, :rows]
    bqv[...] = double[:, : 2 * rows]
    group = group_of(n, lax.axis_index("dp") * n + lax.axis_index("ctx"))[1]
    bf[...] = sums[pl.ds(7 + group, 1), :]


def finish(n_dp, n, out, ig, sums, wq_got, wf_got, wp_got, wo):
    rows, width = wo.shape
    units = wp_got.shape[1]
    shape = jax.ShapeDtypeStruct
    row = shape((1, rows), F32)
    vm = pl.BlockSpec(memory_space=pltpu.VMEM)
    got = pl.pallas_call(
        functools.partial(finish_kernel, n_dp, n),
        out_shape=[
            shape((1,) + out.shape, BF16), shape((1,) + ig.shape, BF16), row, row, shape((rows, 3 * width), F32),
            shape((1, 2 * rows), F32), shape((rows, width), F32), row, row, row, shape((rows, n_dp * n * units), F32),
            shape((1, units), F32), shape((units, width), F32), row,
        ],
        in_specs=[vm] * 7,
        out_specs=[vm] * 14,
        compiler_params=pltpu.CompilerParams(vmem_limit_bytes=VMEM_LIMIT),
        name="finish",
    )(out, ig, sums, wq_got, wf_got, wp_got, wo)
    return tuple(v.reshape(-1) if v.shape[0] == 1 and v.ndim == 2 else v for v in got)


def local(n_dp, n, inputs, cotangent, block_ids, ln1_gain, ln1_bias, w_qkv, b_qkv, w_out, b_out, ln2_gain, ln2_bias, w_fc, b_fc, w_proj, b_proj):
    tokens, width = inputs.shape[1:]
    count = n_dp * n
    rows = w_qkv.shape[0]
    units = w_proj.shape[0]
    r = n // HEADS
    hd = width // HEADS
    d, me = lax.axis_index("dp"), lax.axis_index("ctx")
    flat = d * n + me
    head = me // r
    both = ("dp", "ctx")
    x, dy = inputs[0], cotangent[0]
    halves = (n_dp // 2, 2, 2, n // 2)

    small = (ln1_gain, ln1_bias, b_qkv, block_ids[0], b_out, ln2_gain, ln2_bias, b_fc, b_proj)
    small = [v.reshape(1, -1) for v in small]

    def heads_of(w):
        w = w.reshape(w.shape[0], 3, HEADS, 1, hd)
        w = jnp.stack([w[:, 0], jnp.zeros_like(w[:, 0]), w[:, 1], w[:, 2]], axis=3)
        return w.reshape(w.shape[0], HEADS, 4 * hd)

    spread = rows % 16 == 0 and units == 128 and r == 1
    if spread:
        got = lead(n_dp, n, x, small, dy, w_qkv, w_fc, w_proj, w_out)
        small_all, first, a, b, o, wq, params = got[:7]
        middle, middle_grad, low, branch, agb, sums4, part_out, wp_grad, wf_grad, bf_grad = got[7:]
        wq = wq.reshape(width, -1)
        grads = (low, branch, wf_grad.reshape(count, rows, -1), wp_grad.reshape(n_dp, units, width))
    else:
        full = lax.all_gather(w_qkv, both, axis=0, tiled=True)
        wq = lax.dynamic_index_in_dim(heads_of(full), head, 1, keepdims=False)
        wf = lax.all_gather(w_fc, both, axis=0, tiled=True).reshape((width,) + halves + (units,))
        wf = lax.dynamic_index_in_dim(wf, d % 2, 2, keepdims=False)
        wf = lax.dynamic_index_in_dim(wf, me % (n // 2), 3, keepdims=False).reshape(width, n_dp * units)
        wp = lax.all_gather(w_proj, both, axis=0, tiled=True).reshape(halves + (units, width))
        wp = lax.dynamic_index_in_dim(wp, d % 2, 1, keepdims=False)
        wp = lax.dynamic_index_in_dim(wp, me % (n // 2), 2, keepdims=False).reshape(n_dp * units, width)
        wo = lax.all_gather(w_out, both, axis=0, tiled=True)
        small_all, first, a, b, o, att, dy_all = front(n_dp, n, r, x, small, dy, wq)

        def vector(row, size):
            return small_all[:, row, :size].astype(F32).reshape(1, -1)

        params = jnp.concatenate([vector(k, rows) for k in (BO, G2, C2, G1, BP)])
        bf = vector(BF, units).reshape(halves + (units,))
        bf = lax.dynamic_index_in_dim(bf, d % 2, 1, keepdims=False)
        bf = lax.dynamic_index_in_dim(bf, me % (n // 2), 2, keepdims=False).reshape(1, -1)
        got = ffn(n, r, att, x, dy, dy_all, wo, wf, wp, bf, params[:3])
        middle, middle_grad, low, branch, agb, sums4, part_out, wp_grad, wf_grad, bf_grad = got
        params, grads = params[3:], None
    got = back(n_dp, n, r, agb, a, b, o, small_all, wq, first, part_out, x, middle, middle_grad, params, sums4, bf_grad, grads)
    if spread:
        return finish(n_dp, n, *got)
    output, input_grad, sums = got[:3]
    owned = lambda v: lax.psum_scatter(v, both, scatter_dimension=0, tiled=True)
    hot = (jnp.arange(2) == d % 2).reshape(1, 2, 1, 1, 1) & (jnp.arange(n // 2) == me % (n // 2)).reshape(1, 1, 1, -1, 1)
    g = got[3].reshape(width, 4, 1, hd)
    g = jnp.stack([g[:, 0], g[:, 2], g[:, 3]], axis=1)
    wq_own = owned(jnp.where((jnp.arange(HEADS) == head).reshape(1, 1, -1, 1), g, 0.0).reshape(width, 3 * width))
    g = wf_grad.astype(F32).reshape(width, n_dp // 2, 1, 2, 1, units)
    wf_own = owned(jnp.where(hot[None], g, 0.0).reshape(width, -1))
    g = wp_grad.astype(F32).reshape(n_dp // 2, 1, 2, 1, units, width)
    wp_own = owned(jnp.where(hot[..., None], g, 0.0).reshape(-1, width))
    wo_own = owned(dot(low, branch, TN))

    cut = lambda k, size: lax.dynamic_slice(sums[k], (flat * size % 128,), (size,))
    g1g, c1g, bog, g2g, c2g, bpg = (cut(k, rows) for k in range(6))
    bqvg = cut(6, 2 * rows)
    group = d // 2 * 2 + me // (n // 2)
    bfg = lax.dynamic_slice(sums[7 : 7 + n_dp * units // 128].reshape(-1), (group * units,), (units,))
    return (
    output[None], input_grad[None], g1g, c1g, wq_own, bqvg, wo_own, bog, g2g, c2g, wf_own, bfg, wp_own, bpg,
    )


def solution(mesh):
    both = ("dp", "ctx")
    act, vec, mat = P("dp", "ctx", None), P(both), P(both, None)
    return jax.shard_map(
    functools.partial(local, mesh.shape["dp"], mesh.shape["ctx"]),
    mesh=mesh,
    in_specs=(act, act, P("dp", "ctx"), vec, vec, mat, vec, mat, vec, vec, vec, mat, vec, mat, vec),
    out_specs=(act, act, vec, vec, mat, vec, mat, vec, vec, vec, mat, vec, mat, vec),
    check_vma=False,
    )
```

```python
import functools
import math

import jax
import jax.numpy as jnp
from jax import lax
from jax.experimental import pallas as pl
from jax.experimental.pallas import tpu as pltpu
from jax.sharding import PartitionSpec as P

HEADS = 16
EPSILON = 1e-05
QB = 256
F32, BF16 = jnp.float32, jnp.bfloat16
NT = (((1,), (1,)), ((), ()))
TN = (((0,), (0,)), ((), ()))
MESH = pl.DeviceIdType.MESH
DMA = pltpu.SemaphoreType.DMA
VMEM_LIMIT = 60 << 20
VMEM_MOST = 63 << 20


def dot(x, y, dims=(((1,), (0,)), ((), ()))):
    return lax.dot_general(x, y, dims, preferred_element_type=F32)


def remote(src, dst, send, recv, peer):
    return pltpu.make_async_remote_copy(
        src_ref=src, dst_ref=dst, send_sem=send, recv_sem=recv, device_id=peer, device_id_type=MESH
    )


class Greet:
    def __init__(self, n_dp, n, peers=None):
        self.barrier = pltpu.get_barrier_semaphore()
        self.count = n_dp * n - 1 if peers is None else len(peers)
        for peer in peers or ():
            pl.semaphore_signal(self.barrier, inc=1, device_id=peer, device_id_type=MESH)
        if peers is None:
            flat = lax.axis_index("dp") * n + lax.axis_index("ctx")

            def signal(j, _):
                f = lax.rem(flat + j, n_dp * n)
                pl.semaphore_signal(self.barrier, inc=1, device_id={"dp": f // n, "ctx": f % n}, device_id_type=MESH)
                return 0

            lax.fori_loop(1, n_dp * n, signal, 0)

    def wait(self):
        pl.semaphore_wait(self.barrier, self.count)


class ToAll:
    def __init__(self, n_dp, n, block, into, sems, only_ctx=False):
        self.n, self.block, self.into, self.only = n, block, into, only_ctx
        self.send, self.recv = sems
        self.count = n if only_ctx else n_dp * n
        self.me = lax.axis_index("ctx") if only_ctx else lax.axis_index("dp") * n + lax.axis_index("ctx")

    def copy(self, j):
        f = lax.rem(self.me + j, self.count)
        peer = {"ctx": f} if self.only else {"dp": f // self.n, "ctx": f % self.n}
        return remote(self.block(f), self.into.at[self.me], self.send.at[j], self.recv.at[j], peer)

    def each(self, act):
        def step(j, _):
            act(self.copy(j))
            return 0

        lax.fori_loop(1, self.count, step, 0)

    def start(self):
        self.each(lambda c: c.start())

    def wait_recv(self):
        self.each(lambda c: c.wait_recv())

    def wait_send(self):
        self.each(lambda c: c.wait_send())


def own_bit(dim):
    axis, b = dim
    return lax.axis_index(axis) // (1 << b) % 2


def partner(dim):
    axis, b = dim
    return {axis: lax.axis_index(axis) + (1 - 2 * own_bit(dim)) * (1 << b)}


def cube_plan(n, rows):
    top = n.bit_length() - 2
    dims = [("dp", 0)] + [("ctx", b) for b in range(top - 1, 0, -1)] + [("ctx", 0)]
    links = len(dims) - 1
    size = -(-rows // (16 * links)) * 16
    cuts = [min(rows, size * i) for i in range(links)] + [rows]
    return dims, [(cuts[i], cuts[i + 1], [(i + j) % links for j in range(links)]) for i in range(links)], True


def all_plan(n_dp, n, rows):
    dims = [("dp", b) for b in range(n_dp.bit_length() - 2, -1, -1)] + [("ctx", b) for b in range(n.bit_length() - 2, -1, -1)]
    links, own = len(dims) - 1, n_dp.bit_length() - 1
    return dims, [(0, rows, list(range(own, links)) + list(range(own)))], False


class Pairwise:
    def __init__(self, plan, sems):
        self.dims, self.orders, self.core_first = plan
        self.links = len(self.dims) - 1
        self.link_send, self.link_recv, self.core_send, self.core_recv = sems
        self.mine = [own_bit(d) for d in self.dims]

    def index(self, links, core, tail=()):
        links = tuple(links)
        return ((core,) + links if self.core_first else links + (core,)) + tuple(tail)

    def peers(self):
        return [partner(d) for d in self.dims]


class Gather(Pairwise):
    def __init__(self, plan, buf, sems):
        super().__init__(plan, sems)
        self.buf = buf

    @staticmethod
    def sems(plan):
        links, parts = len(plan[0]) - 1, len(plan[1])
        return [DMA((parts, links))] * 2 + [DMA((parts * links + 1,))] * 2

    def own(self):
        return self.index(self.mine[:-1], self.mine[-1])

    def region(self, part, done, flip=None):
        lo, hi, _ = self.orders[part]
        where = [slice(None) if i in done else (1 - m if i == flip else m) for i, m in enumerate(self.mine[:-1])]
        return self.index(where, self.mine[-1], (pl.ds(lo, hi - lo),))

    def copy(self, where, send, recv, dim):
        return remote(self.buf.at[where], self.buf.at[where], send, recv, partner(self.dims[dim]))

    def link(self, part, k):
        order = self.orders[part][2]
        return self.copy(self.region(part, order[:k]), self.link_send.at[part, k], self.link_recv.at[part, k], order[k])

    def core(self, part, k):
        order = self.orders[part][2]
        at = part * self.links + k + 1
        return self.copy(self.region(part, order[:k], order[k]), self.core_send.at[at], self.core_recv.at[at], self.links)

    def core_own(self):
        return self.copy(self.own(), self.core_send.at[0], self.core_recv.at[0], self.links)

    def start(self):
        for part in range(len(self.orders)):
            self.link(part, 0).start()
        self.core_own().start()

    def step(self, k):
        for part in range(len(self.orders)):
            self.link(part, k).wait_recv()
            if k + 1 < self.links:
                self.link(part, k + 1).start()
            self.core(part, k).start()

    def core_wait(self):
        self.core_own().wait_recv()
        for part in range(len(self.orders)):
            for k in range(self.links):
                self.core(part, k).wait_recv()

    def finish(self):
        self.core_own().wait_send()
        for part in range(len(self.orders)):
            for k in range(self.links):
                self.link(part, k).wait_send()
                self.core(part, k).wait_send()


class Scatter(Pairwise):
    def __init__(self, plan, terms, bufs, sems, own=None):
        super().__init__(plan, sems)
        self.terms, self.run, self.bufs, self.own = terms, bufs[0], bufs[1:], own

    def fetch_own(self, sem):
        source = self.terms.at[self.index((slice(None),) * self.links, self.mine[-1])]
        return pltpu.make_async_copy(source, self.own, sem)

    @staticmethod
    def sems(plan):
        links, parts = len(plan[0]) - 1, len(plan[1])
        return [DMA((parts, links))] * 2 + [DMA((2,))] * 2

    @staticmethod
    def scratch(plan, rows, cols):
        links = len(plan[0]) - 1
        return [pltpu.VMEM((2,) * links + (rows, cols), BF16)] + [
            pltpu.VMEM((2,) * (links - 1 - k) + (rows, cols), BF16) for k in range(links)
        ]

    def core(self, half):
        where = (half,) + (slice(None),) * (self.links - 1)
        return remote(
            self.terms.at[self.index(where, 1 - self.mine[-1])], self.run.at[where],
            self.core_send.at[half], self.core_recv.at[half], partner(self.dims[-1]),
        )

    def where(self, part, k, flip):
        lo, hi, order = self.orders[part]
        order = order[::-1]
        d, gone = order[k], order[:k]
        at = []
        for i in range(self.links):
            if i == d:
                at.append(1 - self.mine[i] if flip else self.mine[i])
            else:
                at.append(self.mine[i] if i in gone else slice(None))
        return at, d, (pl.ds(lo, hi - lo),)

    def link(self, part, k):
        at, d, tail = self.where(part, k, True)
        return remote(
            self.run.at[tuple(at) + tail], self.bufs[k].at[(slice(None),) * (self.links - 1 - k) + tail],
            self.link_send.at[part, k], self.link_recv.at[part, k], partner(self.dims[d]),
        )

    def add_core(self, half):
        self.core(half).wait_recv()
        inner = self.links - 1
        for i in range(1 << inner):
            at = (half,) + tuple((i >> (inner - 1 - j)) & 1 for j in range(inner))
            own = self.terms[self.index(at, self.mine[-1])] if self.own is None else self.own[at]
            self.run[at] = (self.run[at].astype(F32) + own.astype(F32)).astype(BF16)

    def start_links(self):
        for part in range(len(self.orders)):
            self.link(part, 0).start()

    def step(self, k, out=None):
        for part in range(len(self.orders)):
            at, _, tail = self.where(part, k, False)
            self.link(part, k).wait_recv()
            free = self.links - 1 - k
            for i in range(1 << free):
                idx = [(i >> (free - 1 - j)) & 1 for j in range(free)]
                rest = iter(idx)
                to = tuple(next(rest) if isinstance(v, slice) else v for v in at) + tail
                total = self.run[to].astype(F32) + self.bufs[k][tuple(idx) + tail].astype(F32)
                if k + 1 < self.links:
                    self.run[to] = total.astype(BF16)
                else:
                    out[tail[0], :] = total
            if k + 1 < self.links:
                self.link(part, k + 1).start()

    def core_sent(self):
        for half in range(2):
            self.core(half).wait_send()

    def links_sent(self):
        for part in range(len(self.orders)):
            for k in range(self.links):
                self.link(part, k).wait_send()

    def finish(self):
        self.core_sent()
        self.links_sent()


class Line:
    def __init__(self, n):
        self.n, self.ys = n, n // 8
        me = lax.axis_index("ctx")
        self.z, self.y, self.c = me // (2 * self.ys), me // 2 % self.ys, me % 2
        high = self.z // 2
        self.slots = [3 - 3 * high, 2 - high, self.z + 1 - 2 * (self.z % 2), self.z]
        self.inner = (self.z == 1) | (self.z == 2)
        self.outer = (self.z == 0) | (self.z == 3)
        self.side = (self.z + 1) // 2 % 2
        self.near = self.at(self.slots[2], self.y, self.c)
        self.far = self.at(self.z + 1 - 2 * high, self.y, self.c)
        self.core = self.at(self.z, self.y, 1 - self.c)

    def at(self, z, y, c):
        return {"ctx": (z * self.ys + y) * 2 + c}

    def others(self):
        return [(self.y + d) % self.ys for d in range(1, self.ys)]


class LineGather:
    def __init__(self, line, buf, sems):
        self.l, self.buf = line, buf
        self.zs, self.zr, self.ys, self.yr, self.ks, self.kr = sems

    @staticmethod
    def sems(n):
        ys = n // 8
        return [DMA((5,)), DMA((3,)), DMA((ys - 1, 4)), DMA((ys - 1, 4)), DMA((ys, 4)), DMA((ys, 4))]

    def move(self, z, y, c, send, recv, peer):
        ref = self.buf.at[z, y, c]
        return remote(ref, ref, send, recv, peer)

    def zcopy(self, i):
        l = self.l
        slot, peer, into = [(3, l.near, 0), (3, l.far, 1), (2, l.far, 2), (1, l.near, 1), (0, l.near, 2)][i]
        return self.move(l.slots[slot], l.y, l.c, self.zs.at[i], self.zr.at[into], peer)

    def ycopy(self, d, slot):
        l = self.l
        return self.move(l.slots[slot], l.y, l.c, self.ys.at[d, slot], self.yr.at[d, slot], l.at(l.z, l.others()[d], l.c))

    def kcopy(self, d, slot):
        l = self.l
        y = l.y if d == 0 else (l.y + l.ys - d) % l.ys
        return self.move(l.slots[slot], y, l.c, self.ks.at[d, slot], self.kr.at[d, slot], l.core)

    def spread(self, slot):
        for d in range(self.l.ys - 1):
            self.ycopy(d, slot).start()
        self.kcopy(0, slot).start()

    def start(self):
        self.zcopy(0).start()

        @pl.when(self.l.inner)
        def _():
            self.zcopy(1).start()

        self.spread(3)

    def z_step(self, r):
        self.zcopy((0, 3, 4)[r]).wait_recv()

        @pl.when(self.l.inner)
        def _():
            self.zcopy(2 + r).start()

        self.spread(2 - r)

    def y_step(self, slot):
        for d in range(self.l.ys - 1):
            self.ycopy(d, slot).wait_recv()
            self.kcopy(d + 1, slot).start()

    def run(self):
        self.start()
        for r in range(3):
            self.z_step(r)
            self.y_step(3 - r)
        self.y_step(0)

    def core_wait(self, slot):
        for d in range(self.l.ys):
            self.kcopy(d, slot).wait_recv()

    def finish(self):
        self.zcopy(0).wait_send()

        @pl.when(self.l.inner)
        def _():
            for i in range(1, 5):
                self.zcopy(i).wait_send()

        for slot in range(4):
            for d in range(self.l.ys - 1):
                self.ycopy(d, slot).wait_send()
            for d in range(self.l.ys):
                self.kcopy(d, slot).wait_send()


class LineScatter:
    def __init__(self, line, acc, kbuf, ybuf, zbuf, sems):
        self.l, self.acc, self.kbuf, self.ybuf, self.zbuf = line, acc, kbuf, ybuf, zbuf
        self.zs, self.zr, self.ys, self.yr, self.ks, self.kr = sems

    @staticmethod
    def sems(n):
        ys = n // 8
        return [DMA((3,)), DMA((2, 3)), DMA((ys - 1, 4)), DMA((ys - 1, 4)), DMA((ys, 4)), DMA((ys, 4))]

    @staticmethod
    def scratch(n, rows, cols):
        ys = n // 8
        return [pltpu.VMEM((4, ys, rows, cols), BF16), pltpu.VMEM((ys - 1, 4, rows, cols), BF16), pltpu.VMEM((2, 3, rows, cols), BF16)]

    def y_of(self, d):
        return self.l.y if d == 0 else self.l.others()[d - 1]

    def kcopy(self, d, slot):
        l = self.l
        z, y = l.slots[slot], self.y_of(d)
        return remote(self.acc.at[z, y, 1 - l.c], self.kbuf.at[z, y], self.ks.at[d, slot], self.kr.at[d, slot], l.core)

    def ycopy(self, d, slot):
        l = self.l
        z, y = l.slots[slot], self.y_of(d + 1)
        return remote(self.acc.at[z, y, l.c], self.ybuf.at[d, slot], self.ys.at[d, slot], self.yr.at[d, slot], l.at(l.z, y, l.c))

    def zcopy(self, slot):
        l = self.l
        return remote(self.acc.at[l.slots[slot], l.y, l.c], self.zbuf.at[l.side, slot], self.zs.at[slot], self.zr.at[l.side, slot], l.far if slot < 2 else l.near)

    def zwait(self, side, slot):
        buf = self.zbuf.at[side, slot]
        remote(buf, buf, self.zs.at[slot], self.zr.at[side, slot], self.l.near).wait_recv()
        return self.zbuf[side, slot].astype(F32)

    def own(self, slot):
        return (self.l.slots[slot], self.l.y, self.l.c)

    def core_start(self, slot):
        for d in range(self.l.ys - 1, -1, -1):
            self.kcopy(d, slot).start()

    def core_step(self, slot):
        l = self.l
        for d in list(range(1, l.ys)) + [0]:
            z, y = l.slots[slot], self.y_of(d)
            self.kcopy(d, slot).wait_recv()
            self.acc[z, y, l.c] = (self.acc[z, y, l.c].astype(F32) + self.kbuf[z, y].astype(F32)).astype(BF16)
            if d > 0:
                self.ycopy(d - 1, slot).start()

    def y_sum(self, slot):
        total = self.acc[self.own(slot)].astype(F32)
        for d in range(self.l.ys - 1):
            self.ycopy(d, slot).wait_recv()
            total = total + self.ybuf[d, slot].astype(F32)
        return total

    def z_step(self, slot):
        l, own = self.l, self.own(slot)
        total = self.y_sum(slot)
        self.acc[own] = total.astype(BF16)
        @pl.when(l.inner)
        def _():
            self.acc[own] = (self.acc[own].astype(F32) + self.zwait(*((0, slot) if slot < 2 else (1, 0)))).astype(BF16)

        self.zcopy(slot).start()

    def last(self, out):
        l = self.l
        out[...] = self.y_sum(3)

        @pl.when(l.inner)
        def _():
            out[...] += self.zwait(0, 2) + self.zwait(1, 1)

        @pl.when(l.outer)
        def _():
            out[...] += self.zwait(1, 2)

    def finish(self):
        for slot in range(4):
            for d in range(self.l.ys):
                self.kcopy(d, slot).wait_send()
            for d in range(self.l.ys - 1):
                self.ycopy(d, slot).wait_send()
        for slot in range(3):
            self.zcopy(slot).wait_send()


G1, C1, BQV, IDS, BO, G2, C2, BF, BP = range(9)


def put_ids(n, small_all, first, row, col):
    tokens = small_all.shape[2]
    for j in range(n):
        ids = small_all[first + j].astype(F32)[IDS : IDS + 1, :]
        row[:, j * tokens : (j + 1) * tokens] = ids
        col[j * tokens : (j + 1) * tokens, :] = jnp.transpose(jnp.broadcast_to(ids, (tokens, tokens)))[:, :1]


def half_row(tile_row, odd, high):
    lane = lax.broadcasted_iota(jnp.int32, tile_row.shape, 1)
    turned = pltpu.roll(tile_row, 64, 1)
    moved = jnp.where((odd == 1) == high, tile_row, turned)
    return jnp.where((lane >= 64) == high, moved, 0.0)


def normalize(rows):
    centred = rows - jnp.mean(rows, axis=-1, keepdims=True)
    rstd = lax.rsqrt(jnp.mean(centred * centred, axis=-1, keepdims=True) + EPSILON)
    return centred * rstd, rstd


def group_of(n, f):
    d, j = f // n, f % n
    return d % 2 * (n // 2) + j % (n // 2), d // 2 * 2 + j // (n // 2)


def group_peer(n, i, count):
    d, j = lax.axis_index("dp"), lax.axis_index("ctx")
    g = lax.rem(d // 2 * 2 + j // (n // 2) + i, count)
    return g, {"dp": g // 2 * 2 + d % 2, "ctx": g % 2 * (n // 2) + j % (n // 2)}


def put_small(pieces, tile, small_ref):
    tile[...] = jnp.zeros_like(tile)
    for k, piece in enumerate(pieces):
        tile[k : k + 1, : piece.shape[1]] = piece[...].astype(F32)
    small_ref[...] = tile[...].astype(BF16)


def put_params(count, width, small_all, prm, bqv):
    for size, ref in ((width // count, prm), (2 * width // count, bqv)):
        per = 128 // size
        for k in range(count // per):
            tile = small_all[k * per].astype(F32)
            for i in range(1, per):
                tile = tile + pltpu.roll(small_all[k * per + i].astype(F32), i * size, 1)
            if ref is prm:
                prm[:, k * 128 : (k + 1) * 128] = tile
            else:
                bqv[k : k + 1, :] = tile[BQV : BQV + 1]


def front_kernel(n_dp, n, r, cube, *refs):
    refs = list(refs)
    take = lambda k: [refs.pop(0) for _ in range(k)]
    x_ref, pieces, dy_ref = refs.pop(0), take(9), refs.pop(0)
    (wq_all,) = take(1)
    small_all, first_out, a_ref, b_ref, o_ref, att, dy_all = take(7)
    xbuf, first, prm, bqv, bias, idrow, idcol, packed, acc, tot, own_sems, first_sems, tile, small_ref = take(14)
    line_sems, small_sems, dy_sems, att_sems = take(6), take(2), take(4), take(2)
    tokens, width = x_ref.shape
    count = n_dp * n
    d, me = lax.axis_index("dp"), lax.axis_index("ctx")
    flat = d * n + me
    head, part = me // r, me % r
    line = Line(n)
    hello = Greet(n_dp, n)

    xg = LineGather(line, xbuf, line_sems)
    small = ToAll(n_dp, n, lambda f: small_ref, small_all, small_sems)
    dyg = Gather(cube, dy_all, dy_sems)
    own_copies = [pltpu.make_async_copy(dy_ref, dy_all.at[dyg.own()], own_sems.at[0])]
    for c in own_copies:
        c.start()
    xbuf[line.z, line.y, line.c] = x_ref[...]
    put_small(pieces, tile, small_ref)
    small_all[flat] = small_ref[...]
    hello.wait()
    xg.start()
    small.start()
    for c in own_copies:
        c.wait()
    xg.z_step(0)
    xg.y_step(3)
    small.wait_recv()
    put_params(count, width, small_all, prm, bqv)
    odd = head % 2
    bias[:, :128] = half_row(bqv[pl.ds(head // 2, 1), :], odd, False)
    bias[:, 128:] = half_row(bqv[pl.ds(width // 128 + head // 2, 1), :], odd, True)
    put_ids(n, small_all, d * n, idrow, idcol)
    per_z = n // 4

    def plane(slot):
        return pl.ds(pl.multiple_of(line.slots[slot] * per_z * tokens, per_z * tokens), per_z * tokens)

    def save(slot):
        return pltpu.make_async_copy(first.at[plane(slot)], first_out.at[plane(slot)], first_sems.at[slot])

    def project(slot):
        z = line.slots[slot]

        def one(i, _):
            normed, _ = normalize(xbuf[z, i // 2, i % 2].astype(F32))
            low = (normed * prm[G1 : G1 + 1, :] + prm[C1 : C1 + 1, :]).astype(BF16)
            first[pl.ds(pl.multiple_of((z * per_z + i) * tokens, tokens), tokens), :] = low
            return 0

        lax.fori_loop(0, per_z, one, 0)
        at = plane(slot)
        weights = wq_all[...]
        qkv = (dot(first[at, :], weights) + bias[...]).astype(BF16)
        a_ref[at, :] = qkv[:, :128]
        b_ref[at, :] = qkv[:, 128:]
        save(slot).start()

    xg.z_step(1)
    xg.y_step(2)
    xg.core_wait(3)
    project(3)
    xg.z_step(2)
    xg.y_step(1)
    xg.core_wait(2)
    project(2)
    xg.y_step(0)
    dyg.start()
    xg.core_wait(1)
    project(1)
    xg.core_wait(0)
    project(0)
    dyg.step(0)

    length = b_ref.shape[0]
    kc = min(1024, length)
    half = tokens // 2
    if r > 1:
        packed[...] = jnp.zeros_like(packed)

    def per_queries(lb, _):
        gq = lb * r + part
        qs = pl.ds(pl.multiple_of(gq * QB, QB), QB)
        a = a_ref[qs, :] * 0.125
        ids = idcol[qs, :]
        acc[...] = jnp.zeros_like(acc)
        tot[...] = jnp.zeros_like(tot)

        def per_keys(kb, _):
            ks = pl.ds(pl.multiple_of(kb * kc, kc), kc)
            b = b_ref[ks, :]
            s = dot(a, b, NT)
            w = jnp.where(idrow[:, ks] <= ids, jnp.exp(s), 0.0)
            t = w[:, :128]
            for i in range(1, kc // 128):
                t = t + w[:, i * 128 : (i + 1) * 128]
            tot[...] += t
            acc[...] += dot(w.astype(BF16), b)
            return 0

        lax.fori_loop(0, jnp.minimum(((gq + 2) * QB + kc - 1) // kc, length // kc), per_keys, 0)
        t = jnp.sum(tot[...], axis=-1, keepdims=True)
        o = acc[...] / t
        lane = lax.broadcasted_iota(jnp.int32, (QB, 128), 1)
        o_ref[pl.ds(pl.multiple_of(lb * QB, QB), QB), :] = jnp.where(lane < 64, t, o)
        lane = lax.broadcasted_iota(jnp.int32, (half, 128), 1)
        for i in range(QB // tokens):
            lo, hi = o[i * tokens : i * tokens + half], o[i * tokens + half : (i + 1) * tokens]
            packed[gq * (QB // tokens) + i] = jnp.where(lane < 64, pltpu.roll(lo, 64, 1), hi).astype(BF16)
        return 0

    blocks = length // QB // r
    cuts = [0, blocks // 2, blocks * 3 // 4, blocks]
    for k in range(3):
        lax.fori_loop(cuts[k], cuts[k + 1], per_queries, 0)
        if k + 1 < dyg.links:
            dyg.step(k + 1)
    out = ToAll(n_dp, n, lambda f: packed.at[f], att, att_sems, True)
    att[me] = packed[me]
    out.start()
    for k in range(3, dyg.links):
        dyg.step(k)
    out.wait_recv()
    dyg.core_wait()
    for slot in range(4):
        save(slot).wait()
    small.wait_send()
    out.wait_send()
    xg.finish()
    dyg.finish()


def front(n_dp, n, r, x, small, dy, weights):
    tokens, width = x.shape
    count, length = n_dp * n, n * tokens
    cube = cube_plan(n, tokens)
    shape = jax.ShapeDtypeStruct
    vm, hbm = pl.BlockSpec(memory_space=pltpu.VMEM), pl.BlockSpec(memory_space=pl.ANY)
    outs = [
        (shape((count, 16, 128), BF16), vm), (shape((length, width), BF16), hbm), (shape((length, 128), BF16), vm),
        (shape((length, 128), BF16), vm), (shape((length // r, 128), F32), vm), (shape((n, tokens // 2, 128), BF16), vm),
        (shape((2,) * len(cube[0]) + (tokens, width), BF16), hbm),
    ]
    sems = LineGather.sems(n) + [DMA((count,))] * 2 + Gather.sems(cube) + [DMA((n,))] * 2
    ins = [x, *small, dy]
    ins += [weights]
    return pl.pallas_call(
        functools.partial(front_kernel, n_dp, n, r, cube),
        out_shape=[o for o, _ in outs],
        in_specs=[vm] * len(ins),
        out_specs=[s for _, s in outs],
        scratch_shapes=[
            pltpu.VMEM((4, n // 8, 2, tokens, width), BF16), pltpu.VMEM((length, width), BF16), pltpu.VMEM((16, width), F32),
            pltpu.VMEM((2 * width // 128, 128), F32), pltpu.VMEM((1, 256), F32), pltpu.VMEM((1, length), F32),
            pltpu.VMEM((length, 1), F32), pltpu.VMEM((n, tokens // 2, 128), BF16), pltpu.VMEM((QB, 128), F32),
            pltpu.VMEM((QB, 128), F32), DMA((3,)), DMA((4,)),
            pltpu.VMEM((16, 128), F32), pltpu.VMEM((16, 128), BF16),
        ] + sems,
        compiler_params=pltpu.CompilerParams(collective_id=1, has_side_effects=True, vmem_limit_bytes=VMEM_LIMIT),
        name="front",
    )(*ins)


def gelu_both(u):
    c = math.sqrt(2.0 / math.pi)
    t = jnp.tanh(c * (u + 0.044715 * (u * u * u)))
    half = 0.5 * (1.0 + t)
    return u * half, half + 0.5 * u * (1.0 - t * t) * (c * (1.0 + 3.0 * 0.044715 * (u * u)))


def normalize_back(grad, normed, rstd):
    return rstd * (
        grad
        - jnp.mean(grad, axis=-1, keepdims=True)
        - normed * jnp.mean(grad * normed, axis=-1, keepdims=True)
    )


def ffn_kernel(n, r, plan, *refs):
    refs = list(refs)
    take = lambda k: [refs.pop(0) for _ in range(k)]
    att, x_ref, dy_own, dy_hbm, wo_ref, wf_ref, wp_in, bf_ref, par_ref = take(9)
    middle_ref, mg_ref, low_ref, branch_ref, agb, sums_ref, out_hbm, wp_grad, wf_grad, bf_grad = take(10)
    links = len(plan[0]) - 1
    sbuf, dy_ref, grads, act, hid, acc, out_ref, sg, copy_sems, out_sems = take(10)
    bufs, gather_sems, scatter_sems = take(links + 1), take(4), take(4)
    g = Gather(plan, sbuf, gather_sems)
    s = Scatter(plan, acc, bufs, scatter_sems)
    peers = g.peers()
    hello = Greet(1, n, peers)
    wp_ref = wp_in
    dy_copy = pltpu.make_async_copy(dy_hbm, dy_ref, copy_sems)
    dy_copy.start()
    tokens, width = x_ref.shape
    half = tokens // 2
    quarter = (1 << (links - 1)) * tokens
    inner = (slice(None),) * (links - 1)
    core = g.mine[-1]

    lane = lax.broadcasted_iota(jnp.int32, (half, 128), 1)

    def block(h):
        total = att[h * r].astype(F32)
        for i in range(1, r):
            total = total + att[h * r + i].astype(F32)
        return total

    for h in range(0, HEADS, 2):
        b0, b1 = block(h), block(h + 1)
        at = slice(h * 64, h * 64 + 128)
        low_ref[:half, at] = jnp.where(lane < 64, b0, pltpu.roll(b1, 64, 1)).astype(BF16)
        low_ref[half:, at] = jnp.where(lane < 64, pltpu.roll(b0, 64, 1), b1).astype(BF16)
    middle = x_ref[...].astype(F32) + dot(low_ref[...], wo_ref[...]) + par_ref[0:1, :]
    middle_ref[...] = middle
    n2, _ = normalize(middle)
    sbuf[g.own()] = (n2 * par_ref[1:2, :] + par_ref[2:3, :]).astype(BF16)
    hello.wait()
    g.start()
    dy_copy.wait()
    def rows(c, a):
        return pl.ds(pl.multiple_of((2 * c + a) * quarter, quarter), quarter)

    def grad_part(i):
        dy = dy_ref[(i // 2, i % 2) + inner].reshape(quarter, width)
        grads[rows(i // 2, i % 2), :] = dot(dy, wp_ref[...], NT)

    for k in range(links):
        g.step(k)
        if k == 1:
            for i in range(4):
                grad_part(i)
    g.core_wait()
    bf_grad[...] = jnp.zeros_like(bf_grad)

    def hidden_part(c, a):
        at = rows(c, a)
        low = sbuf[(c, a) + inner].reshape(quarter, width)
        active, slope = gelu_both(dot(low, wf_ref[...]) + bf_ref[...])
        act[at, :] = active.astype(BF16)
        h = (slope * grads[at, :]).astype(BF16)
        hid[at, :] = h
        bf_grad[...] += jnp.sum(h.astype(F32), axis=0, keepdims=True)
        acc[(c, a) + inner] = dot(h, wf_ref[...], NT).astype(BF16).reshape((2,) * (links - 1) + (tokens, width))

    for a in range(2):
        hidden_part(1 - core, a)
        s.core(a).start()
    for a in range(2):
        hidden_part(core, a)
        s.add_core(a)
    s.start_links()

    def weight_grads(k):
        at = slice(k * 256, (k + 1) * 256)
        low = sbuf[..., at].reshape(4 * quarter, 256)
        wf_grad[at, :] = jnp.transpose(dot(hid[...], low, TN)).astype(BF16)
        dy = dy_ref[..., at].reshape(4 * quarter, 256)
        wp_grad[:, at] = dot(act[...], dy, TN).astype(BF16)

    def out_part(i):
        at = (i // 2, i % 2) + inner
        if i >= out_ref.shape[0]:
            out_copy(i - out_ref.shape[0]).wait()
        terms = dot(act[rows(i // 2, i % 2), :], wp_ref[...]).astype(BF16)
        out_ref[i % out_ref.shape[0]] = terms.reshape((2,) * (links - 1) + (tokens, width))
        out_copy(i).start()

    def out_copy(i):
        slot = i % out_ref.shape[0]
        return pltpu.make_async_copy(out_ref.at[slot], out_hbm.at[(i // 2, i % 2) + inner], out_sems.at[slot])

    for i in range(4):
        out_part(i)
    for k in range(links):
        s.step(k, sg)
        if k < 2:
            weight_grads(2 * k)
            weight_grads(2 * k + 1)

    second_grad = sg[...]
    dy = dy_own[...].astype(F32)
    n2, rstd2 = normalize(middle_ref[...])
    mg = dy + normalize_back(second_grad * par_ref[1:2, :], n2, rstd2)
    mg_ref[...] = mg
    branch = mg.astype(BF16)
    branch_ref[...] = branch
    grad = dot(branch, wo_ref[...], NT)
    for h in range(0, HEADS, 2):
        lo, hi = grad[:half, h * 64 : h * 64 + 128], grad[half:, h * 64 : h * 64 + 128]
        b0 = jnp.where(lane < 64, lo, pltpu.roll(hi, 64, 1)).astype(BF16)
        b1 = jnp.where(lane < 64, pltpu.roll(lo, 64, 1), hi).astype(BF16)
        for i in range(r):
            agb[h * r + i] = b0
            agb[(h + 1) * r + i] = b1
    column = lambda v: jnp.sum(v, axis=0, keepdims=True)
    sums_ref[0:1, :] = column(branch.astype(F32))
    sums_ref[1:2, :] = column(second_grad * n2)
    sums_ref[2:3, :] = column(second_grad)
    sums_ref[3:4, :] = column(dy)
    for i in range(4 - out_ref.shape[0], 4):
        out_copy(i).wait()
    s.finish()
    g.finish()


def ffn(n, r, att, x, dy, dy_all, wo, wf, wp, bf, params):
    tokens, width = x.shape
    units = wf.shape[1]
    plan = cube_plan(n, tokens)
    block = (2,) * len(plan[0])
    length = n * tokens
    shape = jax.ShapeDtypeStruct
    vm, hbm = pl.BlockSpec(memory_space=pltpu.VMEM), pl.BlockSpec(memory_space=pl.ANY)
    return pl.pallas_call(
        functools.partial(ffn_kernel, n, r, plan),
        out_shape=[
            shape((tokens, width), F32), shape((tokens, width), F32), shape((tokens, width), BF16), shape((tokens, width), BF16),
            shape((n, tokens // 2, 128), BF16), shape((4, width), F32), shape(block + (tokens, width), BF16),
            shape((units, width), BF16), shape((width, units), BF16), shape((1, units), F32),
        ],
        in_specs=[vm, vm, vm, hbm, vm, vm, vm, vm, vm],
        out_specs=[vm, vm, vm, vm, vm, vm, hbm, vm, vm, vm],
        scratch_shapes=[
            pltpu.VMEM(block + (tokens, width), BF16), pltpu.VMEM(block + (tokens, width), BF16), pltpu.VMEM((length, units), F32),
            pltpu.VMEM((length, units), BF16), pltpu.VMEM((length, units), BF16), pltpu.VMEM(block + (tokens, width), BF16),
            pltpu.VMEM((2,) + block[2:] + (tokens, width), BF16), pltpu.VMEM((tokens, width), F32), DMA, DMA((2,)),
        ] + Scatter.scratch(plan, tokens, width) + Gather.sems(plan) + Scatter.sems(plan),
        compiler_params=pltpu.CompilerParams(collective_id=2, has_side_effects=True, vmem_limit_bytes=VMEM_LIMIT),
        name="ffn",
    )(att, x, dy, dy_all, wo, wf, wp, bf, params)


def project_rows(rows, prm):
    normed, _ = normalize(rows.astype(F32))
    return (normed * prm[G1 : G1 + 1, :] + prm[C1 : C1 + 1, :]).astype(BF16)


def layer_kernel(n_dp, n, cube, whole, *refs):
    refs = list(refs)
    take = lambda k: [refs.pop(0) for _ in range(k)]
    x_ref, pieces, (dy_own, w_qkv, w_fc, w_proj, w_out) = refs.pop(0), take(9), take(5)
    out_ref, ig_ref, sums, wq_got, wf_got, wp_got, wo_own = take(7)
    small_all, a_ref, b_ref, o_ref, wq_all, middle_ref, mg_ref, low_ref, branch_ref, agb, wp_grad, wf_grad, bf_grad = take(13)
    xbuf, first, prm, bqv, bias, bf_row, idrow, idcol, packed, acc, tot, att, wqb, wfb = take(14)
    wf_all, wo_all, wp_ref, dy_ref, sbuf, grads, act, hid, terms, sg, osum, tile, small_ref, sums_ref = take(14)
    ag, kbuf, ybuf, zbuf, got, msg, wq_part, wq_mine, wq_else = take(9)
    links = len(cube[0]) - 1
    bufs, out_bufs = take(links + 1), take(links + 1)
    wo_bufs = take(len(whole[0]))
    line_sems, small_sems, dy_sems, att_sems, wq_sems, wf_sems, wo_sems = take(6), take(2), take(4), take(2), take(4), take(2), take(4)
    wp_sems, gather_sems, scatter_sems = take(2), take(4), take(4)
    ag_sems, back_sems, outs_sems, msg_sems = take(2), take(6), take(4), take(2)
    wqg_sems, wfg_sems, wpg_sems, wog_sems = take(4), take(2), take(2), take(4)

    tokens, width = x_ref.shape
    length = n * tokens
    rows, units = w_fc.shape[0], w_proj.shape[0]
    count = n_dp * n
    d, me = lax.axis_index("dp"), lax.axis_index("ctx")
    flat = d * n + me
    rank, group = group_of(n, flat)
    line = Line(n)
    hello = Greet(n_dp, n)

    xg = LineGather(line, xbuf, line_sems)
    small = ToAll(n_dp, n, lambda f: small_ref, small_all, small_sems)
    wq = ToAll(n_dp, n, lambda f: wqb.at[f], wq_all.at[d], wq_sems[:2], True)
    wf = ToAll(n_dp, n, lambda f: wfb.at[group_of(n, f)[0]], wf_all, wf_sems)
    dyg = Gather(cube, dy_ref, dy_sems)
    wog = Gather(whole, wo_all, wo_sems)
    out = ToAll(n_dp, n, lambda f: packed.at[f], att, att_sems, True)
    g = Gather(cube, sbuf, gather_sems)
    s = Scatter(cube, terms, bufs, scatter_sems)
    dps, wps = [], []
    for i in range(1, n_dp):
        dps.append(remote(wq_all.at[d], wq_all.at[d], wq_sems[2].at[i], wq_sems[3].at[i], {"dp": (d + i) % n_dp}))
        to = wp_ref.at[pl.ds(pl.multiple_of(group * units, units), units)]
        wps.append(remote(w_proj, to, wp_sems[0].at[i], wp_sems[1].at[i], group_peer(n, i, n_dp)[1]))

    low = lax.broadcasted_iota(jnp.int32, (rows, 128), 1) < 64
    for h in range(0, HEADS, 2):
        q, k, v = (w_qkv[:, p * width + h * 64 : p * width + h * 64 + 128].astype(F32) for p in range(3))
        turn = lambda t: pltpu.roll(t, 64, 1)
        wqb[h, :, :128] = jnp.where(low, q, 0.0).astype(BF16)
        wqb[h, :, 128:] = jnp.where(low, k, turn(v)).astype(BF16)
        wqb[h + 1, :, :128] = jnp.where(low, turn(q), 0.0).astype(BF16)
        wqb[h + 1, :, 128:] = jnp.where(low, turn(k), v).astype(BF16)
    xbuf[line.z, line.y, line.c] = x_ref[...]
    put_small(pieces, tile, small_ref)
    small_all[flat] = small_ref[...]
    wq_all[d, me] = wqb[me]
    wo_all[wog.own()] = w_out[...]
    hello.wait()
    xg.start()
    small.start()
    wq.start()
    wog.start()
    for m in range(n):
        for i in range(n_dp):
            at = ((i // 2 * 2 + m // (n // 2)) * n + i % 2 * (n // 2) + m % (n // 2)) * units
            wfb[m, :, i * units : (i + 1) * units] = w_fc[:, at : at + units]
    dy_ref[dyg.own()] = dy_own[...]
    wf_all[flat] = wfb[rank]
    wp_ref[pl.ds(pl.multiple_of(group * units, units), units), :] = w_proj[...]
    xg.z_step(0)
    xg.y_step(3)
    wq.wait_recv()
    for c in dps:
        c.start()
    small.wait_recv()
    put_params(count, width, small_all, prm, bqv)
    odd = me % 2
    bias[:, :128] = half_row(bqv[pl.ds(me // 2, 1), :], odd, False)
    bias[:, 128:] = half_row(bqv[pl.ds(width // 128 + me // 2, 1), :], odd, True)
    for i in range(n_dp):
        owner = (i // 2 * 2 + d % 2) * n + i % 2 * (n // 2) + me % (n // 2)
        bf_row[:, i * units : (i + 1) * units] = small_all[owner].astype(F32)[BF : BF + 1, :units]
    put_ids(n, small_all, d * n, idrow, idcol)
    per_z = n // 4

    def plane(slot):
        return pl.ds(pl.multiple_of(line.slots[slot] * per_z * tokens, per_z * tokens), per_z * tokens)

    def project(slot):
        z = line.slots[slot]

        def one(i, _):
            at = pl.ds(pl.multiple_of((z * per_z + i) * tokens, tokens), tokens)
            first[at, :] = project_rows(xbuf[z, i // 2, i % 2], prm)
            return 0

        lax.fori_loop(0, per_z, one, 0)
        at = plane(slot)
        qkv = (dot(first[at, :], wq_all[...].reshape(width, 256)) + bias[...]).astype(BF16)
        a_ref[at, :] = qkv[:, :128]
        b_ref[at, :] = qkv[:, 128:]

    xg.z_step(1)
    xg.y_step(2)
    wog.step(0)
    for c in dps:
        c.wait_recv()
    xg.core_wait(3)
    project(3)
    xg.z_step(2)
    xg.y_step(1)
    wog.step(1)
    xg.core_wait(2)
    project(2)
    xg.y_step(0)
    dyg.start()
    for c in wps:
        c.start()
    wf.start()
    wog.step(2)
    xg.core_wait(1)
    project(1)
    xg.core_wait(0)
    project(0)
    dyg.step(0)

    kc = min(1024, length)
    half = tokens // 2
    lane = lax.broadcasted_iota(jnp.int32, (half, 128), 1)

    def per_queries(gq, _):
        qs = pl.ds(pl.multiple_of(gq * QB, QB), QB)
        a = a_ref[qs, :] * 0.125
        ids = idcol[qs, :]
        acc[...] = jnp.zeros_like(acc)
        tot[...] = jnp.zeros_like(tot)

        def per_keys(kb, _):
            ks = pl.ds(pl.multiple_of(kb * kc, kc), kc)
            b = b_ref[ks, :]
            w = jnp.where(idrow[:, ks] <= ids, jnp.exp(dot(a, b, NT)), 0.0)
            t = w[:, :128]
            for i in range(1, kc // 128):
                t = t + w[:, i * 128 : (i + 1) * 128]
            tot[...] += t
            acc[...] += dot(w.astype(BF16), b)
            return 0

        lax.fori_loop(0, jnp.minimum(((gq + 2) * QB + kc - 1) // kc, length // kc), per_keys, 0)
        t = jnp.sum(tot[...], axis=-1, keepdims=True)
        o = acc[...] / t
        o_ref[qs, :] = jnp.where(lax.broadcasted_iota(jnp.int32, (QB, 128), 1) < 64, t, o)
        for i in range(QB // tokens):
            lo, hi = o[i * tokens : i * tokens + half], o[i * tokens + half : (i + 1) * tokens]
            packed[gq * (QB // tokens) + i] = jnp.where(lane < 64, pltpu.roll(lo, 64, 1), hi).astype(BF16)
        return 0

    blocks = length // QB
    lax.fori_loop(0, blocks // 2, per_queries, 0)
    dyg.step(1)
    wog.step(3)
    lax.fori_loop(blocks // 2, blocks, per_queries, 0)
    att[me] = packed[me]
    out.start()
    for k in range(4, wog.links):
        wog.step(k)
    wog.core_wait()
    out.wait_recv()

    for h in range(0, HEADS, 2):
        b0, b1 = att[h].astype(F32), att[h + 1].astype(F32)
        at = slice(h * 64, h * 64 + 128)
        low_ref[:half, at] = jnp.where(lane < 64, b0, pltpu.roll(b1, 64, 1)).astype(BF16)
        low_ref[half:, at] = jnp.where(lane < 64, pltpu.roll(b0, 64, 1), b1).astype(BF16)
    middle = x_ref[...].astype(F32) + dot(low_ref[...], wo_all[...].reshape(width, width)) + prm[BO : BO + 1, :]
    middle_ref[...] = middle
    n2, _ = normalize(middle)
    sbuf[g.own()] = (n2 * prm[G2 : G2 + 1, :] + prm[C2 : C2 + 1, :]).astype(BF16)
    g.start()
    for k in range(2, links):
        dyg.step(k)
    for c in wps:
        c.wait_recv()
    dyg.core_wait()

    quarter = (1 << (links - 1)) * tokens
    inner = (slice(None),) * (links - 1)
    block = (2,) * (links - 1) + (tokens, width)
    core = g.mine[-1]

    def span(c, a):
        return pl.ds(pl.multiple_of((2 * c + a) * quarter, quarter), quarter)

    def grad_part(i):
        dy = dy_ref[(i // 2, i % 2) + inner].reshape(quarter, width)
        grads[span(i // 2, i % 2), :] = dot(dy, wp_ref[...], NT)

    for k in range(links):
        grad_part(k)
        g.step(k)
    for k in range(links, 4):
        grad_part(k)
    wf.wait_recv()
    g.core_wait()
    bf_grad[...] = jnp.zeros_like(bf_grad)

    def hidden_part(c, a):
        at = span(c, a)
        weights = wf_all[...].reshape(width, -1)
        active, slope = gelu_both(dot(sbuf[(c, a) + inner].reshape(quarter, width), weights) + bf_row[...])
        act[at, :] = active.astype(BF16)
        h = (slope * grads[at, :]).astype(BF16)
        hid[at, :] = h
        bf_grad[...] += jnp.sum(h.astype(F32), axis=0, keepdims=True)
        terms[(c, a) + inner] = dot(h, weights, NT).astype(BF16).reshape(block)

    for a in range(2):
        hidden_part(1 - core, a)
        s.core(a).start()
    for a in range(2):
        hidden_part(core, a)
        s.add_core(a)
    s.start_links()

    def weight_grads(k):
        at = slice(k * 256, (k + 1) * 256)
        low = sbuf[..., at].reshape(4 * quarter, 256)
        wf_grad[at, :] = jnp.transpose(dot(hid[...], low, TN)).astype(BF16)
        wp_grad[:, at] = dot(act[...], dy_ref[..., at].reshape(4 * quarter, 256), TN).astype(BF16)

    outs = Scatter(cube, terms, out_bufs, outs_sems)
    s.core_sent()
    for i in range(4):
        terms[(i // 2, i % 2) + inner] = dot(act[span(i // 2, i % 2), :], wp_ref[...]).astype(BF16).reshape(block)
    for h in range(2):
        outs.core(h).start()
    for k in range(links):
        s.step(k, sg)
        if k < 2:
            weight_grads(2 * k)
            weight_grads(2 * k + 1)

    second_grad = sg[...]
    dy = dy_own[...].astype(F32)
    n2, rstd2 = normalize(middle_ref[...])
    mg = dy + normalize_back(second_grad * prm[G2 : G2 + 1, :], n2, rstd2)
    mg_ref[...] = mg
    branch = mg.astype(BF16)
    branch_ref[...] = branch
    grad = dot(branch, wo_all[...].reshape(width, width), NT)
    for h in range(0, HEADS, 2):
        lo, hi = grad[:half, h * 64 : h * 64 + 128], grad[half:, h * 64 : h * 64 + 128]
        agb[h] = jnp.where(lane < 64, lo, pltpu.roll(hi, 64, 1)).astype(BF16)
        agb[h + 1] = jnp.where(lane < 64, pltpu.roll(lo, 64, 1), hi).astype(BF16)
    heads = ToAll(n_dp, n, lambda f: agb.at[f], ag, ag_sems, True)
    heads.start()
    ag[me] = agb[me]
    column = lambda v: jnp.sum(v, axis=0, keepdims=True)
    sums_ref[0:1, :] = column(branch.astype(F32))
    sums_ref[1:2, :] = column(second_grad * n2)
    sums_ref[2:3, :] = column(second_grad)
    sums_ref[3:4, :] = column(dy)

    block_of = lambda ref, f, size: ref.at[pl.ds(pl.multiple_of(f * size, size), size)]
    wfs = ToAll(n_dp, n, lambda f: block_of(wf_grad, f, rows), wf_got, wfg_sems)
    wqs = ToAll(n_dp, n, lambda f: wq_mine.at[f], wq_got, wqg_sems[:2], True)
    wo = Scatter(whole, wo_all, wo_bufs, wog_sems)
    wf_got[flat] = block_of(wf_grad, flat, rows)[...]
    wp_got[group] = block_of(wp_grad, group, units)[...]
    wpgs, dpgs = [], []
    for i in range(1, n_dp):
        to, peer = group_peer(n, i, n_dp)
        wpgs.append(remote(block_of(wp_grad, to, units), wp_got.at[group], wpg_sems[0].at[i], wpg_sems[1].at[i], peer))
        other = (d + i) % n_dp
        dpgs.append(remote(wq_part.at[other], wq_else.at[i], wqg_sems[2].at[i], wqg_sems[3].at[i], {"dp": other}))
    for c in wpgs:
        c.start()
    for h in range(2):
        outs.add_core(h)
    heads.wait_recv()
    outs.start_links()
    wfs.start()
    wog.finish()
    for k in range(width // 256):
        part = dot(low_ref[:, k * 256 : (k + 1) * 256], branch, TN).astype(BF16)
        for i in range(256 // rows):
            f = k * (256 // rows) + i
            wo_all[tuple((f >> b) & 1 for b in range(len(whole[0]) - 1, -1, -1))] = part[i * rows : (i + 1) * rows]
    for h in range(2):
        wo.core(h).start()
    mixed, dkv = act, grads
    dkv[:, :128] = jnp.zeros((length, 128), F32)

    def per_queries_back(gq, _):
        qs = pl.ds(pl.multiple_of(gq * QB, QB), QB)
        pieces = []
        for i in range(QB // tokens):
            t = ag[gq * (QB // tokens) + i].astype(F32)
            pieces += [jnp.where(lane >= 64, pltpu.roll(t, 64, 1), 0.0), jnp.where(lane >= 64, t, 0.0)]
        grad = jnp.concatenate(pieces, axis=0)
        o = o_ref[qs, :]
        inverse = 1.0 / o[:, :1]
        upper = lax.broadcasted_iota(jnp.int32, (QB, 128), 1) >= 64
        ratio = jnp.sum(jnp.where(upper, grad * o, 0.0), axis=-1, keepdims=True) * inverse
        ratio = jnp.transpose(jnp.broadcast_to(ratio, (QB, 128)))[:1, :]
        do = (grad * inverse).astype(BF16)
        a = a_ref[qs, :]
        scaled = a * 0.125
        ado = jnp.concatenate([a, do], axis=0)
        ids = idrow[:, qs]
        acc[...] = jnp.zeros_like(acc)

        def per_keys(kb, _):
            ks = pl.ds(pl.multiple_of(kb * kc, kc), kc)
            b = b_ref[ks, :]
            w = jnp.where(idcol[ks, :] <= ids, jnp.exp(dot(b, scaled, NT)), 0.0)
            t = (w * (dot(b, do, NT) - ratio)).astype(BF16)
            dkv[ks, :128] += dot(jnp.concatenate([t, w.astype(BF16)], axis=1), ado)
            acc[...] += dot(t, b, TN)
            return 0

        lax.fori_loop(0, jnp.minimum(((gq + 2) * QB + kc - 1) // kc, length // kc), per_keys, 0)
        mixed[qs, :128] = jnp.where(upper, 0.0, acc[...] * 0.125).astype(BF16)
        return 0

    cuts = [0, blocks // 2, blocks * 3 // 4, blocks]
    for k in range(3):
        lax.fori_loop(cuts[k], cuts[k + 1], per_queries_back, 0)
        if k + 1 < links:
            outs.step(k, osum)
    for h in range(2):
        wo.add_core(h)
    total = dkv[:, :128]
    lower = lax.broadcasted_iota(jnp.int32, (length, 128), 1) < 64
    mixed[:, 128:] = jnp.where(lower, total * 0.125, total).astype(BF16)

    xg.finish()
    rs = LineScatter(line, xbuf, kbuf, ybuf, zbuf, back_sems)

    def first_grad(slot):
        part = dot(mixed[plane(slot), :], wq_all[...].reshape(width, 256), NT).astype(BF16)
        xbuf[line.slots[slot]] = part.reshape(n // 8, 2, tokens, width)
        rs.core_start(slot)

    first_grad(0)
    for slot in range(1, 4):
        first_grad(slot)
        rs.core_step(slot - 1)
    rs.core_step(3)
    for k in range(min(2, links - 1), links):
        outs.step(k, osum)
    wo.start_links()

    def wq_grad(i):
        k = ((d + 1) * (width // 256 // n_dp) + i) % (width // 256)
        part = jnp.transpose(dot(mixed[...], first[:, pl.ds(pl.multiple_of(k * 256, 256), 256)], TN))
        q = 256 // rows
        wq_part[k * q // n, pl.ds(k * q % n, q)] = part.astype(BF16).reshape(q, rows, 256)

    turns = width // 256
    ahead = turns - turns // n_dp
    for i in range(ahead):
        wq_grad(i)
    for c in dpgs:
        c.start()
    rs.z_step(0)
    for i in range(ahead, turns):
        wq_grad(i)
    rs.z_step(1)
    total = wq_part[d].astype(F32)
    for i, c in enumerate(dpgs):
        c.wait_recv()
        total = total + wq_else[i + 1].astype(F32)
    wq_mine[...] = total.astype(BF16)
    wq_got[me] = wq_mine[me]
    wqs.start()
    wo.step(0, wo_own)
    total = jnp.sum(mixed[...].astype(F32), axis=0, keepdims=True)
    q_row = half_row(total[:, :128], 0, False)
    q_row = jnp.where(odd == 1, pltpu.roll(q_row, 64, 1), q_row)
    v_row = half_row(total[:, 128:], 1, True)
    v_row = jnp.where(odd == 1, v_row, pltpu.roll(v_row, 64, 1))
    rs.z_step(2)
    out_ref[...] = (middle_ref[...] + osum[...] + prm[BP : BP + 1, :]).astype(BF16)
    n1, rstd1 = normalize(x_ref[...].astype(F32))
    wo.step(1, wo_own)

    def prepare(f, _):
        at = f * 2 * width // count // 128
        msg[f, 6:7, :] = jnp.where(at == me // 2, q_row, 0.0) + jnp.where(at == width // 128 + me // 2, v_row, 0.0)
        same = group_of(n, f)[0] == rank
        for i in range(bf_grad.shape[1] // 128):
            msg[f, 7 + i : 8 + i, :] = jnp.where(same, bf_grad[:, i * 128 : (i + 1) * 128], 0.0)
        return 0

    msg[...] = jnp.zeros_like(msg)
    lax.fori_loop(0, count, prepare, 0)
    rs.last(sg)

    grad = sg[...]
    gain, shift = column(grad * n1), column(grad)
    per = 128 * count // width
    for k in range(width // 128):
        at = slice(k * 128, (k + 1) * 128)
        lines = jnp.concatenate([gain[:, at], shift[:, at], sums_ref[:, at]], axis=0)
        for i in range(per):
            msg[k * per + i, 0:6, :] = lines
    tell = ToAll(n_dp, n, lambda f: msg.at[f], got, msg_sems)
    tell.start()
    got[flat] = msg[flat]
    ig_ref[...] = (mg_ref[...] + normalize_back(grad * prm[G1 : G1 + 1, :], n1, rstd1)).astype(BF16)
    for k in range(2, wo.links):
        wo.step(k, wo_own)
    wfs.wait_recv()
    wqs.wait_recv()
    for c in wpgs:
        c.wait_recv()
    tell.wait_recv()
    sums[...] = jnp.sum(got[...], axis=0)
    for c in (wq, wf, small, out, heads, wfs, wqs, tell):
        c.wait_send()
    for c in dps + wps + wpgs + dpgs:
        c.wait_send()
    s.links_sent()
    for c in (dyg, g, outs, wo, rs):
        c.finish()


def layer(n_dp, n, x, small, dy, w_qkv, w_fc, w_proj, w_out):
    tokens, width = x.shape
    count, length = n_dp * n, n * tokens
    rows, own = w_fc.shape[0], w_proj.shape[0]
    units = n_dp * own
    cube, whole = cube_plan(n, tokens), all_plan(n_dp, n, rows)
    block = (2,) * len(cube[0]) + (tokens, width)
    shape, v = jax.ShapeDtypeStruct, pltpu.VMEM
    vm = pl.BlockSpec(memory_space=pltpu.VMEM)
    outs = [
        shape((tokens, width), BF16), shape((tokens, width), BF16), shape((16, 128), F32), shape((n, rows, 256), BF16),
        shape((count, rows, units), BF16), shape((n_dp, own, width), BF16), shape((rows, width), F32),
    ]
    heads = (n, tokens // 2, 128)
    all_sems = [DMA((count,))] * 2
    weight_sems = [DMA((n,))] * 2 + [DMA((n_dp,))] * 2
    return pl.pallas_call(
        functools.partial(layer_kernel, n_dp, n, cube, whole),
        out_shape=outs,
        in_specs=[vm] * 15,
        out_specs=[vm] * len(outs),
        scratch_shapes=[
            v((count, 16, 128), BF16), v((length, 128), BF16), v((length, 128), BF16), v((length, 128), F32),
            v((n_dp, n, rows, 256), BF16), v((tokens, width), F32), v((tokens, width), F32), v((tokens, width), BF16),
            v((tokens, width), BF16), v(heads, BF16), v((units, width), BF16), v((width, units), BF16), v((1, units), F32),
            v((4, n // 8, 2, tokens, width), BF16), v((length, width), BF16), v((16, width), F32), v((2 * width // 128, 128), F32),
            v((1, 256), F32), v((1, units), F32), v((1, length), F32), v((length, 1), F32), v(heads, BF16), v((QB, 128), F32),
            v((QB, 128), F32), v(heads, BF16), v((n, rows, 256), BF16), v((n, rows, units), BF16),
            v((count, rows, units), BF16), v((2,) * len(whole[0]) + (rows, width), BF16), v((units, width), BF16), v(block, BF16),
            v(block, BF16), v((length, units), F32), v((length, units), BF16), v((length, units), BF16), v(block, BF16),
            v((tokens, width), F32), v((tokens, width), F32), v((16, 128), F32), v((16, 128), BF16), v((4, width), F32),
            v(heads, BF16),
        ] + LineScatter.scratch(n, tokens, width) + [
            v((count, 16, 128), F32), v((count, 16, 128), F32), v((n_dp, n, rows, 256), BF16), v((n, rows, 256), BF16),
            v((n_dp, n, rows, 256), BF16),
        ] + Scatter.scratch(cube, tokens, width) * 2 + Scatter.scratch(whole, rows, width)
        + LineGather.sems(n) + all_sems + Gather.sems(cube) + [DMA((n,))] * 2 + weight_sems + all_sems + Gather.sems(whole)
        + [DMA((n_dp,))] * 2 + Gather.sems(cube) + Scatter.sems(cube)
        + [DMA((n,))] * 2 + LineScatter.sems(n) + Scatter.sems(cube) + all_sems
        + weight_sems + all_sems + [DMA((n_dp,))] * 2 + Scatter.sems(whole),
        compiler_params=pltpu.CompilerParams(collective_id=4, has_side_effects=True, vmem_limit_bytes=VMEM_MOST),
        name="layer",
    )(x, *small, dy, w_qkv, w_fc, w_proj, w_out)


def back_kernel(n_dp, n, r, spread, cube, whole, *refs):
    refs = list(refs)
    take = lambda k: [refs.pop(0) for _ in range(k)]
    agb, a_ref, b_ref, o_ref, small_all, wq_ref, first, part_out, x_ref, mid_ref, mg_ref, par_ref, sums_in, bf_grad = take(14)
    if spread:
        low_ref, branch_ref, wfg, wpg = take(4)
    out_ref, ig_ref, sums = take(3)
    if spread:
        wq_got, wf_got, wp_got, wo_own = take(4)
    else:
        (wq_sum,) = take(1)
    ag, idrow, idcol, mixed, dqacc, dkv, acc, kbuf, ybuf, zbuf, fg, got, msg, columns, column_sem, own_out, own_sem, osum = take(18)
    links = len(cube[0]) - 1
    out_bufs = take(links + 1)
    if r > 1:
        (dkv_got,) = take(1)
        pair_sems = take(2)
    ag_sems, line_sems, out_sems, msg_sems = take(2), take(6), take(4), take(2)
    if spread:
        wq_part, wq_mine, wq_else, wo_part = take(4)
        wq_sems, wf_sems, wp_sems = take(4), take(2), take(2)
        wo_bufs = take(len(whole[0]))
        wo_sems = take(4)

    tokens, width = x_ref.shape
    length = b_ref.shape[0]
    count = n_dp * n
    d, me = lax.axis_index("dp"), lax.axis_index("ctx")
    flat = d * n + me
    head, part = me // r, me % r
    line = Line(n)
    hello = Greet(n_dp, n)
    kc = min(1024, length)
    half = tokens // 2

    grads = ToAll(n_dp, n, lambda f: agb.at[f], ag, ag_sems, True)
    outs = Scatter(cube, part_out, out_bufs, out_sems, own_out)
    own_copy = outs.fetch_own(own_sem)
    own_copy.start()
    ag[me] = agb[me]
    if spread:
        wf = ToAll(n_dp, n, lambda f: wfg.at[f], wf_got, wf_sems)
        wq = ToAll(n_dp, n, lambda f: wq_mine.at[f], wq_got, wq_sems[:2], True)
        wo = Scatter(whole, wo_part, wo_bufs, wo_sems)
        wf_got[flat] = wfg[flat]
        rank, group = group_of(n, flat)
        wp_got[group] = wpg[group]
        wps, dps = [], []
        for i in range(1, n_dp):
            g, peer = group_peer(n, i, n_dp)
            wps.append(remote(wpg.at[g], wp_got.at[group], wp_sems[0].at[i], wp_sems[1].at[i], peer))
            dps.append(remote(wq_part.at[(d + i) % n_dp], wq_else.at[i], wq_sems[2].at[i], wq_sems[3].at[i], {"dp": (d + i) % n_dp}))
    else:
        rank, group = group_of(n, flat)
    dkv[...] = jnp.zeros_like(dkv)
    if r > 1:
        mixed[...] = jnp.zeros_like(mixed)
    hello.wait()
    grads.start()
    for h in range(2):
        outs.core(h).start()
    if spread:
        for c in wps:
            c.start()
    put_ids(n, small_all, d * n, idrow, idcol)
    if spread:
        rows = width // count
        for k in range(width // 256):
            terms = dot(low_ref[:, k * 256 : (k + 1) * 256], branch_ref[...], TN).astype(BF16)
            for i in range(256 // rows):
                f = k * (256 // rows) + i
                bits = tuple((f >> b) & 1 for b in range(len(whole[0]) - 1, -1, -1))
                wo_part[bits] = terms[i * rows : (i + 1) * rows]
        for h in range(2):
            wo.core(h).start()
    own_copy.wait()
    for h in range(2):
        outs.add_core(h)
    outs.start_links()
    grads.wait_recv()
    if spread:
        wf.start()

    def per_queries(lb, _):
        gq = lb * r + part
        qs = pl.ds(pl.multiple_of(gq * QB, QB), QB)
        at = pl.ds(pl.multiple_of(lb * QB, QB), QB)
        lane = lax.broadcasted_iota(jnp.int32, (half, 128), 1)
        pieces = []
        for i in range(QB // tokens):
            block = ag[gq * (QB // tokens) + i].astype(F32)
            pieces += [jnp.where(lane >= 64, pltpu.roll(block, 64, 1), 0.0), jnp.where(lane >= 64, block, 0.0)]
        grad = jnp.concatenate(pieces, axis=0)
        o = o_ref[at, :]
        inverse = 1.0 / o[:, :1]
        upper = lax.broadcasted_iota(jnp.int32, (QB, 128), 1) >= 64
        ratio = jnp.sum(jnp.where(upper, grad * o, 0.0), axis=-1, keepdims=True) * inverse
        ratio = jnp.transpose(jnp.broadcast_to(ratio, (QB, 128)))[:1, :]
        do = (grad * inverse).astype(BF16)
        a = a_ref[qs, :]
        scaled = a * 0.125
        ado = jnp.concatenate([a, do], axis=0)
        ids = idrow[:, qs]
        dqacc[...] = jnp.zeros_like(dqacc)

        def per_keys(kb, _):
            ks = pl.ds(pl.multiple_of(kb * kc, kc), kc)
            b = b_ref[ks, :]
            w = jnp.where(idcol[ks, :] <= ids, jnp.exp(dot(b, scaled, NT)), 0.0)
            g = (w * (dot(b, do, NT) - ratio)).astype(BF16)
            dkv[ks, :] += dot(jnp.concatenate([g, w.astype(BF16)], axis=1), ado)
            dqacc[...] += dot(g, b, TN)
            return 0

        lax.fori_loop(0, jnp.minimum(((gq + 2) * QB + kc - 1) // kc, length // kc), per_keys, 0)
        mixed[qs, :128] = jnp.where(upper, 0.0, dqacc[...] * 0.125).astype(BF16)
        return 0

    blocks = length // QB // r
    cuts = [0, blocks // 2, blocks * 3 // 4, blocks]
    for k in range(3):
        lax.fori_loop(cuts[k], cuts[k + 1], per_queries, 0)
        if k + 1 < links:
            outs.step(k, osum)
    if spread:
        for h in range(2):
            wo.add_core(h)

    def fetch(k):
        return pltpu.make_async_copy(first.at[:, pl.ds(pl.multiple_of(k * 256, 256), 256)], columns, column_sem)

    turns = [((d + 1) * (width // 256 // n_dp) + i) % (width // 256) if spread else i for i in range(width // 256)]
    fetch(turns[0]).start()
    low = lax.broadcasted_iota(jnp.int32, (length, 128), 1) < 64
    total = dkv[...]
    if r > 1:
        both = remote(dkv, dkv_got, pair_sems[0], pair_sems[1], line.core)
        both.start()
        both.wait()
        total = jnp.where(part == 0, total + dkv_got[...], 0.0)
    mixed[:, 128:] = jnp.where(low, total * 0.125, total).astype(BF16)

    rs = LineScatter(line, acc, kbuf, ybuf, zbuf, line_sems)
    per_z = n // 4 * tokens

    def first_grad(slot):
        z = line.slots[slot]
        at = pl.ds(pl.multiple_of(z * per_z, per_z), per_z)
        acc[z] = dot(mixed[at, :], wq_ref[...], NT).astype(BF16).reshape(n // 8, 2, tokens, width)
        rs.core_start(slot)

    first_grad(0)
    for slot in range(1, 4):
        first_grad(slot)
        rs.core_step(slot - 1)
    rs.core_step(3)
    for k in range(min(2, links - 1), links):
        outs.step(k, osum)
    if spread:
        wo.start_links()

    def wq_grad(i):
        k = turns[i]
        fetch(k).wait()
        g = jnp.transpose(dot(mixed[...], columns[...], TN))
        if i + 1 < len(turns):
            fetch(turns[i + 1]).start()
        if spread:
            per = n_dp * 256 // width
            q = 256 // rows
            at = k * q
            wq_part[at // n, pl.ds(at % n, q)] = g.astype(BF16).reshape(q, rows, 256)
        else:
            wq_sum[pl.ds(pl.multiple_of(k * 256, 256), 256), :] = g

    ahead = len(turns) - len(turns) // n_dp if spread else 2
    for i in range(ahead):
        wq_grad(i)
    if spread:
        for c in dps:
            c.start()
    rs.z_step(0)
    for i in range(ahead, len(turns)):
        wq_grad(i)
    rs.z_step(1)
    if spread:
        total = wq_part[d].astype(F32)
        for i, c in enumerate(dps):
            c.wait_recv()
            total = total + wq_else[i + 1].astype(F32)
        wq_mine[...] = total.astype(BF16)
        wq_got[me] = wq_mine[me]
        wq.start()
        wo.step(0, wo_own)
    column = jnp.sum(mixed[...].astype(F32), axis=0, keepdims=True)
    odd = head % 2
    q_row = half_row(column[:, :128], 0, False)
    q_row = jnp.where(odd == 1, pltpu.roll(q_row, 64, 1), q_row)
    v_row = half_row(column[:, 128:], 1, True)
    v_row = jnp.where(odd == 1, v_row, pltpu.roll(v_row, 64, 1))
    rs.z_step(2)
    out_ref[...] = (mid_ref[...] + osum[...] + par_ref[1:2, :]).astype(BF16)
    n1, rstd1 = normalize(x_ref[...].astype(F32))
    if spread:
        wo.step(1, wo_own)

    wide = bf_grad.shape[1] // 128

    def prepare(f, _):
        tile = f * 2 * width // count // 128
        bqv = jnp.where(tile == head // 2, q_row, 0.0) + jnp.where(tile == width // 128 + head // 2, v_row, 0.0)
        msg[f, 6:7, :] = bqv
        same = group_of(n, f)[0] == rank
        for i in range(wide):
            msg[f, 7 + i : 8 + i, :] = jnp.where(same, bf_grad[:, i * 128 : (i + 1) * 128], 0.0)
        return 0

    msg[...] = jnp.zeros_like(msg)
    lax.fori_loop(0, count, prepare, 0)
    rs.last(fg)

    grad = fg[...]
    gain = jnp.sum(grad * n1, axis=0, keepdims=True)
    shift = jnp.sum(grad, axis=0, keepdims=True)
    per = 128 * count // width
    for k in range(width // 128):
        at = slice(k * 128, (k + 1) * 128)
        lines = jnp.concatenate([gain[:, at], shift[:, at], sums_in[:, at]], axis=0)

        def fill(i, _, k=k, lines=lines):
            msg[k * per + i, 0:6, :] = lines
            return 0

        lax.fori_loop(0, per, fill, 0)
    tell = ToAll(n_dp, n, lambda f: msg.at[f], got, msg_sems)
    tell.start()
    got[flat] = msg[flat]
    ig_ref[...] = (mg_ref[...] + normalize_back(grad * par_ref[0:1, :], n1, rstd1)).astype(BF16)
    if spread:
        for k in range(2, wo.links):
            wo.step(k, wo_own)
        wf.wait_recv()
        wq.wait_recv()
        for c in wps:
            c.wait()
    tell.wait_recv()
    sums[...] = jnp.sum(got[...], axis=0)
    tell.wait_send()
    if spread:
        wf.wait_send()
        wq.wait_send()
        for c in dps:
            c.wait_send()
        wo.finish()
    grads.wait_send()
    outs.finish()
    rs.finish()


def back(n_dp, n, r, agb, a, b, o, small_all, wq, first, part_out, x, middle, mg, params, sums4, bf_grad, grads):
    tokens, width = x.shape
    count, length = n_dp * n, n * tokens
    spread = grads is not None
    cube = cube_plan(n, tokens)
    links = len(cube[0]) - 1
    whole = None
    shape = jax.ShapeDtypeStruct
    ins = [agb, a, b, o, small_all, wq, first, part_out, x, middle, mg, params, sums4, bf_grad]
    outs = [shape((tokens, width), BF16), shape((tokens, width), BF16), shape((16, 128), F32)]
    scratch = [
        pltpu.VMEM((n, tokens // 2, 128), BF16), pltpu.VMEM((1, length), F32), pltpu.VMEM((length, 1), F32),
        pltpu.VMEM((length, 256), BF16), pltpu.VMEM((QB, 128), F32), pltpu.VMEM((length, 128), F32),
        pltpu.VMEM((4, n // 8, 2, tokens, width), BF16),
    ] + LineScatter.scratch(n, tokens, width) + [
        pltpu.VMEM((tokens, width), F32), pltpu.VMEM((count, 16, 128), F32), pltpu.VMEM((count, 16, 128), F32),
        pltpu.VMEM((length, 256), BF16), DMA, pltpu.VMEM((2,) * links + (tokens, width), BF16), DMA,
        pltpu.VMEM((tokens, width), F32),
    ] + Scatter.scratch(cube, tokens, width)
    if r > 1:
        scratch += [pltpu.VMEM((length, 128), F32), DMA, DMA]
    scratch += [DMA((n,))] * 2 + LineScatter.sems(n) + Scatter.sems(cube) + [DMA((count,))] * 2
    if spread:
        low, branch, wfg, wpg = grads
        rows = width // count
        whole = all_plan(n_dp, n, rows)
        ins += [low, branch, wfg, wpg]
        outs += [shape((n, rows, 256), BF16), shape(wfg.shape, BF16), shape(wpg.shape, BF16), shape((rows, width), F32)]
        scratch += [
            pltpu.VMEM((n_dp, n, rows, 256), BF16), pltpu.VMEM((n, rows, 256), BF16), pltpu.VMEM((n_dp, n, rows, 256), BF16),
            pltpu.VMEM((2,) * len(whole[0]) + (rows, width), BF16),
        ]
        scratch += [DMA((n,))] * 2 + [DMA((n_dp,))] * 2 + [DMA((count,))] * 2 + [DMA((n_dp,))] * 2
        scratch += Scatter.scratch(whole, rows, width) + Scatter.sems(whole)
    else:
        outs += [shape((width, 256), F32)]
    vm, hbm = pl.BlockSpec(memory_space=pltpu.VMEM), pl.BlockSpec(memory_space=pl.ANY)
    return pl.pallas_call(
        functools.partial(back_kernel, n_dp, n, r, spread, cube, whole),
        out_shape=outs,
        in_specs=[hbm if v is first or v is part_out else vm for v in ins],
        out_specs=[vm] * len(outs),
        scratch_shapes=scratch,
        compiler_params=pltpu.CompilerParams(collective_id=3, has_side_effects=True, vmem_limit_bytes=VMEM_LIMIT),
        name="back",
    )(*ins)


def own_sums(n_dp, n, piece, sums):
    flat = lax.axis_index("dp") * n + lax.axis_index("ctx")
    wide = pltpu.roll(sums, (128 - flat * piece % 128) % 128, 1)
    return wide, pltpu.roll(sums, (128 - flat * 2 * piece % 128) % 128, 1)[6:7]


def finish_kernel(n_dp, n, out_in, ig_in, sums, wq_got, wf_got, wp_got, wo_in, *outs):
    out, ig, g1, c1, wq_own, bqv, wo_own, bo, g2, c2, wf_own, bf, wp_own, bp = outs
    count = n_dp * n
    rows, width = wo_in.shape
    units = wp_got.shape[1]
    out[0] = out_in[...]
    ig[0] = ig_in[...]
    wo_own[...] = wo_in[...]
    wp_own[...] = jnp.sum(wp_got[...].astype(F32), axis=0)
    for f in range(count):
        m, g = group_of(n, f)
        total = 0.0
        for i in range(n_dp):
            source = (i // 2 * 2 + m // (n // 2)) * n + i % 2 * (n // 2) + m % (n // 2)
            total = total + wf_got[source, :, g * units : (g + 1) * units].astype(F32)
        wf_own[:, f * units : (f + 1) * units] = total
    lower = lax.broadcasted_iota(jnp.int32, (rows, 128), 1) < 64
    turn = lambda t: pltpu.roll(t, 64, 1)
    for h in range(0, HEADS, 2):
        (q0, e0), (q1, e1) = ((wq_got[i, :, :128].astype(F32), wq_got[i, :, 128:].astype(F32)) for i in (h, h + 1))
        for p, v in enumerate((jnp.where(lower, q0, turn(q1)), jnp.where(lower, e0, turn(e1)), jnp.where(lower, turn(e0), e1))):
            wq_own[:, p * width + h * 64 : p * width + h * 64 + 128] = v
    wide, double = own_sums(n_dp, n, rows, sums[...])
    for i, ref in enumerate((g1, c1, bo, g2, c2, bp)):
        ref[...] = wide[i : i + 1, :rows]
    bqv[...] = double[:, : 2 * rows]
    group = group_of(n, lax.axis_index("dp") * n + lax.axis_index("ctx"))[1]
    bf[...] = sums[pl.ds(7 + group, 1), :]


def finish(n_dp, n, out, ig, sums, wq_got, wf_got, wp_got, wo):
    rows, width = wo.shape
    units = wp_got.shape[1]
    shape = jax.ShapeDtypeStruct
    row = shape((1, rows), F32)
    vm = pl.BlockSpec(memory_space=pltpu.VMEM)
    got = pl.pallas_call(
        functools.partial(finish_kernel, n_dp, n),
        out_shape=[
            shape((1,) + out.shape, BF16), shape((1,) + ig.shape, BF16), row, row, shape((rows, 3 * width), F32),
            shape((1, 2 * rows), F32), shape((rows, width), F32), row, row, row, shape((rows, n_dp * n * units), F32),
            shape((1, units), F32), shape((units, width), F32), row,
        ],
        in_specs=[vm] * 7,
        out_specs=[vm] * 14,
        compiler_params=pltpu.CompilerParams(vmem_limit_bytes=VMEM_LIMIT),
        name="finish",
    )(out, ig, sums, wq_got, wf_got, wp_got, wo)
    return tuple(v.reshape(-1) if v.shape[0] == 1 and v.ndim == 2 else v for v in got)


def local(n_dp, n, inputs, cotangent, block_ids, ln1_gain, ln1_bias, w_qkv, b_qkv, w_out, b_out, ln2_gain, ln2_bias, w_fc, b_fc, w_proj, b_proj):
    tokens, width = inputs.shape[1:]
    count = n_dp * n
    rows = w_qkv.shape[0]
    units = w_proj.shape[0]
    r = n // HEADS
    hd = width // HEADS
    d, me = lax.axis_index("dp"), lax.axis_index("ctx")
    flat = d * n + me
    head = me // r
    both = ("dp", "ctx")
    x, dy = inputs[0], cotangent[0]
    halves = (n_dp // 2, 2, 2, n // 2)

    small = (ln1_gain, ln1_bias, b_qkv, block_ids[0], b_out, ln2_gain, ln2_bias, b_fc, b_proj)
    small = [v.reshape(1, -1) for v in small]

    def heads_of(w):
        w = w.reshape(w.shape[0], 3, HEADS, 1, hd)
        w = jnp.stack([w[:, 0], jnp.zeros_like(w[:, 0]), w[:, 1], w[:, 2]], axis=3)
        return w.reshape(w.shape[0], HEADS, 4 * hd)

    spread = rows % 16 == 0 and units == 128 and r == 1
    if spread:
        return finish(n_dp, n, *layer(n_dp, n, x, small, dy, w_qkv, w_fc, w_proj, w_out))
    full = lax.all_gather(w_qkv, both, axis=0, tiled=True)
    wq = lax.dynamic_index_in_dim(heads_of(full), head, 1, keepdims=False)
    wf = lax.all_gather(w_fc, both, axis=0, tiled=True).reshape((width,) + halves + (units,))
    wf = lax.dynamic_index_in_dim(wf, d % 2, 2, keepdims=False)
    wf = lax.dynamic_index_in_dim(wf, me % (n // 2), 3, keepdims=False).reshape(width, n_dp * units)
    wp = lax.all_gather(w_proj, both, axis=0, tiled=True).reshape(halves + (units, width))
    wp = lax.dynamic_index_in_dim(wp, d % 2, 1, keepdims=False)
    wp = lax.dynamic_index_in_dim(wp, me % (n // 2), 2, keepdims=False).reshape(n_dp * units, width)
    wo = lax.all_gather(w_out, both, axis=0, tiled=True)
    small_all, first, a, b, o, att, dy_all = front(n_dp, n, r, x, small, dy, wq)

    def vector(row, size):
        return small_all[:, row, :size].astype(F32).reshape(1, -1)

    params = jnp.concatenate([vector(k, rows) for k in (BO, G2, C2, G1, BP)])
    bf = vector(BF, units).reshape(halves + (units,))
    bf = lax.dynamic_index_in_dim(bf, d % 2, 1, keepdims=False)
    bf = lax.dynamic_index_in_dim(bf, me % (n // 2), 2, keepdims=False).reshape(1, -1)
    got = ffn(n, r, att, x, dy, dy_all, wo, wf, wp, bf, params[:3])
    middle, middle_grad, low, branch, agb, sums4, part_out, wp_grad, wf_grad, bf_grad = got
    got = back(n_dp, n, r, agb, a, b, o, small_all, wq, first, part_out, x, middle, middle_grad, params[3:], sums4, bf_grad, None)
    output, input_grad, sums = got[:3]
    owned = lambda v: lax.psum_scatter(v, both, scatter_dimension=0, tiled=True)
    hot = (jnp.arange(2) == d % 2).reshape(1, 2, 1, 1, 1) & (jnp.arange(n // 2) == me % (n // 2)).reshape(1, 1, 1, -1, 1)
    g = got[3].reshape(width, 4, 1, hd)
    g = jnp.stack([g[:, 0], g[:, 2], g[:, 3]], axis=1)
    wq_own = owned(jnp.where((jnp.arange(HEADS) == head).reshape(1, 1, -1, 1), g, 0.0).reshape(width, 3 * width))
    g = wf_grad.astype(F32).reshape(width, n_dp // 2, 1, 2, 1, units)
    wf_own = owned(jnp.where(hot[None], g, 0.0).reshape(width, -1))
    g = wp_grad.astype(F32).reshape(n_dp // 2, 1, 2, 1, units, width)
    wp_own = owned(jnp.where(hot[..., None], g, 0.0).reshape(-1, width))
    wo_own = owned(dot(low, branch, TN))

    cut = lambda k, size: lax.dynamic_slice(sums[k], (flat * size % 128,), (size,))
    g1g, c1g, bog, g2g, c2g, bpg = (cut(k, rows) for k in range(6))
    bqvg = cut(6, 2 * rows)
    group = d // 2 * 2 + me // (n // 2)
    bfg = lax.dynamic_slice(sums[7 : 7 + n_dp * units // 128].reshape(-1), (group * units,), (units,))
    return (
    output[None], input_grad[None], g1g, c1g, wq_own, bqvg, wo_own, bog, g2g, c2g, wf_own, bfg, wp_own, bpg,
    )


def solution(mesh):
    both = ("dp", "ctx")
    act, vec, mat = P("dp", "ctx", None), P(both), P(both, None)
    return jax.shard_map(
    functools.partial(local, mesh.shape["dp"], mesh.shape["ctx"]),
    mesh=mesh,
    in_specs=(act, act, P("dp", "ctx"), vec, vec, mat, vec, mat, vec, vec, vec, mat, vec, mat, vec),
    out_specs=(act, act, vec, vec, mat, vec, mat, vec, vec, vec, mat, vec, mat, vec),
    check_vma=False,
    )
```

```python
import functools
import math

import jax
import jax.numpy as jnp
from jax import lax
from jax.experimental import pallas as pl
from jax.experimental.pallas import tpu as pltpu
from jax.sharding import PartitionSpec as P

HEADS = 16
EPSILON = 1e-05
QB = 256
F32, BF16 = jnp.float32, jnp.bfloat16
NT = (((1,), (1,)), ((), ()))
TN = (((0,), (0,)), ((), ()))
MESH = pl.DeviceIdType.MESH
DMA = pltpu.SemaphoreType.DMA
VMEM_LIMIT = 60 << 20
VMEM_MOST = 63 << 20


def dot(x, y, dims=(((1,), (0,)), ((), ()))):
    return lax.dot_general(x, y, dims, preferred_element_type=F32)


def remote(src, dst, send, recv, peer):
    return pltpu.make_async_remote_copy(
        src_ref=src, dst_ref=dst, send_sem=send, recv_sem=recv, device_id=peer, device_id_type=MESH
    )


class Greet:
    def __init__(self, n_dp, n, peers=None):
        self.barrier = pltpu.get_barrier_semaphore()
        self.count = n_dp * n - 1 if peers is None else len(peers)
        for peer in peers or ():
            pl.semaphore_signal(self.barrier, inc=1, device_id=peer, device_id_type=MESH)
        if peers is None:
            flat = lax.axis_index("dp") * n + lax.axis_index("ctx")

            def signal(j, _):
                f = lax.rem(flat + j, n_dp * n)
                pl.semaphore_signal(self.barrier, inc=1, device_id={"dp": f // n, "ctx": f % n}, device_id_type=MESH)
                return 0

            lax.fori_loop(1, n_dp * n, signal, 0)

    def wait(self):
        pl.semaphore_wait(self.barrier, self.count)


class ToAll:
    def __init__(self, n_dp, n, block, into, sems, only_ctx=False):
        self.n, self.block, self.into, self.only = n, block, into, only_ctx
        self.send, self.recv = sems
        self.count = n if only_ctx else n_dp * n
        self.me = lax.axis_index("ctx") if only_ctx else lax.axis_index("dp") * n + lax.axis_index("ctx")

    def copy(self, j):
        f = lax.rem(self.me + j, self.count)
        peer = {"ctx": f} if self.only else {"dp": f // self.n, "ctx": f % self.n}
        return remote(self.block(f), self.into.at[self.me], self.send.at[j], self.recv.at[j], peer)

    def each(self, act):
        def step(j, _):
            act(self.copy(j))
            return 0

        lax.fori_loop(1, self.count, step, 0)

    def start(self):
        self.each(lambda c: c.start())

    def wait_recv(self):
        self.each(lambda c: c.wait_recv())

    def wait_send(self):
        self.each(lambda c: c.wait_send())


def own_bit(dim):
    axis, b = dim
    return lax.axis_index(axis) // (1 << b) % 2


def partner(dim):
    axis, b = dim
    return {axis: lax.axis_index(axis) + (1 - 2 * own_bit(dim)) * (1 << b)}


def cube_plan(n, rows):
    top = n.bit_length() - 2
    dims = [("dp", 0)] + [("ctx", b) for b in range(top - 1, 0, -1)] + [("ctx", 0)]
    links = len(dims) - 1
    size = -(-rows // (16 * links)) * 16
    cuts = [min(rows, size * i) for i in range(links)] + [rows]
    return dims, [(cuts[i], cuts[i + 1], [(i + j) % links for j in range(links)]) for i in range(links)], True


def all_plan(n_dp, n, rows):
    dims = [("dp", b) for b in range(n_dp.bit_length() - 2, -1, -1)] + [("ctx", b) for b in range(n.bit_length() - 2, -1, -1)]
    links, own = len(dims) - 1, n_dp.bit_length() - 1
    return dims, [(0, rows, list(range(own, links)) + list(range(own)))], False


class Pairwise:
    def __init__(self, plan, sems):
        self.dims, self.orders, self.core_first = plan
        self.links = len(self.dims) - 1
        self.link_send, self.link_recv, self.core_send, self.core_recv = sems
        self.mine = [own_bit(d) for d in self.dims]

    def index(self, links, core, tail=()):
        links = tuple(links)
        return ((core,) + links if self.core_first else links + (core,)) + tuple(tail)

    def peers(self):
        return [partner(d) for d in self.dims]


class Gather(Pairwise):
    def __init__(self, plan, buf, sems):
        super().__init__(plan, sems)
        self.buf = buf

    @staticmethod
    def sems(plan):
        links, parts = len(plan[0]) - 1, len(plan[1])
        return [DMA((parts, links))] * 2 + [DMA((parts * links + 1,))] * 2

    def own(self):
        return self.index(self.mine[:-1], self.mine[-1])

    def region(self, part, done, flip=None):
        lo, hi, _ = self.orders[part]
        where = [slice(None) if i in done else (1 - m if i == flip else m) for i, m in enumerate(self.mine[:-1])]
        return self.index(where, self.mine[-1], (pl.ds(lo, hi - lo),))

    def copy(self, where, send, recv, dim):
        return remote(self.buf.at[where], self.buf.at[where], send, recv, partner(self.dims[dim]))

    def link(self, part, k):
        order = self.orders[part][2]
        return self.copy(self.region(part, order[:k]), self.link_send.at[part, k], self.link_recv.at[part, k], order[k])

    def core(self, part, k):
        order = self.orders[part][2]
        at = part * self.links + k + 1
        return self.copy(self.region(part, order[:k], order[k]), self.core_send.at[at], self.core_recv.at[at], self.links)

    def core_own(self):
        return self.copy(self.own(), self.core_send.at[0], self.core_recv.at[0], self.links)

    def start(self):
        for part in range(len(self.orders)):
            self.link(part, 0).start()
        self.core_own().start()

    def step(self, k):
        for part in range(len(self.orders)):
            self.link(part, k).wait_recv()
            if k + 1 < self.links:
                self.link(part, k + 1).start()
            self.core(part, k).start()

    def core_wait(self):
        self.core_own().wait_recv()
        for part in range(len(self.orders)):
            for k in range(self.links):
                self.core(part, k).wait_recv()

    def finish(self):
        self.core_own().wait_send()
        for part in range(len(self.orders)):
            for k in range(self.links):
                self.link(part, k).wait_send()
                self.core(part, k).wait_send()


class Scatter(Pairwise):
    def __init__(self, plan, terms, bufs, sems, own=None):
        super().__init__(plan, sems)
        self.terms, self.run, self.bufs, self.own = terms, bufs[0], bufs[1:], own

    def fetch_own(self, sem):
        source = self.terms.at[self.index((slice(None),) * self.links, self.mine[-1])]
        return pltpu.make_async_copy(source, self.own, sem)

    @staticmethod
    def sems(plan):
        links, parts = len(plan[0]) - 1, len(plan[1])
        return [DMA((parts, links))] * 2 + [DMA((2,))] * 2

    @staticmethod
    def scratch(plan, rows, cols):
        links = len(plan[0]) - 1
        return [pltpu.VMEM((2,) * links + (rows, cols), BF16)] + [
            pltpu.VMEM((2,) * (links - 1 - k) + (rows, cols), BF16) for k in range(links)
        ]

    def core(self, half):
        where = (half,) + (slice(None),) * (self.links - 1)
        return remote(
            self.terms.at[self.index(where, 1 - self.mine[-1])], self.run.at[where],
            self.core_send.at[half], self.core_recv.at[half], partner(self.dims[-1]),
        )

    def where(self, part, k, flip):
        lo, hi, order = self.orders[part]
        order = order[::-1]
        d, gone = order[k], order[:k]
        at = []
        for i in range(self.links):
            if i == d:
                at.append(1 - self.mine[i] if flip else self.mine[i])
            else:
                at.append(self.mine[i] if i in gone else slice(None))
        return at, d, (pl.ds(lo, hi - lo),)

    def link(self, part, k):
        at, d, tail = self.where(part, k, True)
        return remote(
            self.run.at[tuple(at) + tail], self.bufs[k].at[(slice(None),) * (self.links - 1 - k) + tail],
            self.link_send.at[part, k], self.link_recv.at[part, k], partner(self.dims[d]),
        )

    def add_core(self, half):
        self.core(half).wait_recv()
        inner = self.links - 1
        for i in range(1 << inner):
            at = (half,) + tuple((i >> (inner - 1 - j)) & 1 for j in range(inner))
            own = self.terms[self.index(at, self.mine[-1])] if self.own is None else self.own[at]
            self.run[at] = (self.run[at].astype(F32) + own.astype(F32)).astype(BF16)

    def start_links(self):
        for part in range(len(self.orders)):
            self.link(part, 0).start()

    def step(self, k, out=None):
        for part in range(len(self.orders)):
            at, _, tail = self.where(part, k, False)
            self.link(part, k).wait_recv()
            free = self.links - 1 - k
            for i in range(1 << free):
                idx = [(i >> (free - 1 - j)) & 1 for j in range(free)]
                rest = iter(idx)
                to = tuple(next(rest) if isinstance(v, slice) else v for v in at) + tail
                total = self.run[to].astype(F32) + self.bufs[k][tuple(idx) + tail].astype(F32)
                if k + 1 < self.links:
                    self.run[to] = total.astype(BF16)
                else:
                    out[tail[0], :] = total
            if k + 1 < self.links:
                self.link(part, k + 1).start()

    def core_sent(self):
        for half in range(2):
            self.core(half).wait_send()

    def links_sent(self):
        for part in range(len(self.orders)):
            for k in range(self.links):
                self.link(part, k).wait_send()

    def finish(self):
        self.core_sent()
        self.links_sent()


class Line:
    def __init__(self, n):
        self.n, self.ys = n, n // 8
        me = lax.axis_index("ctx")
        self.z, self.y, self.c = me // (2 * self.ys), me // 2 % self.ys, me % 2
        high = self.z // 2
        self.slots = [3 - 3 * high, 2 - high, self.z + 1 - 2 * (self.z % 2), self.z]
        self.inner = (self.z == 1) | (self.z == 2)
        self.outer = (self.z == 0) | (self.z == 3)
        self.side = (self.z + 1) // 2 % 2
        self.near = self.at(self.slots[2], self.y, self.c)
        self.far = self.at(self.z + 1 - 2 * high, self.y, self.c)
        self.core = self.at(self.z, self.y, 1 - self.c)

    def at(self, z, y, c):
        return {"ctx": (z * self.ys + y) * 2 + c}

    def others(self):
        return [(self.y + d) % self.ys for d in range(1, self.ys)]


class LineGather:
    def __init__(self, line, buf, sems):
        self.l, self.buf = line, buf
        self.zs, self.zr, self.ys, self.yr, self.ks, self.kr = sems

    @staticmethod
    def sems(n):
        ys = n // 8
        return [DMA((5,)), DMA((3,)), DMA((ys - 1, 4)), DMA((ys - 1, 4)), DMA((ys, 4)), DMA((ys, 4))]

    def move(self, z, y, c, send, recv, peer):
        ref = self.buf.at[z, y, c]
        return remote(ref, ref, send, recv, peer)

    def zcopy(self, i):
        l = self.l
        slot, peer, into = [(3, l.near, 0), (3, l.far, 1), (2, l.far, 2), (1, l.near, 1), (0, l.near, 2)][i]
        return self.move(l.slots[slot], l.y, l.c, self.zs.at[i], self.zr.at[into], peer)

    def ycopy(self, d, slot):
        l = self.l
        return self.move(l.slots[slot], l.y, l.c, self.ys.at[d, slot], self.yr.at[d, slot], l.at(l.z, l.others()[d], l.c))

    def kcopy(self, d, slot):
        l = self.l
        y = l.y if d == 0 else (l.y + l.ys - d) % l.ys
        return self.move(l.slots[slot], y, l.c, self.ks.at[d, slot], self.kr.at[d, slot], l.core)

    def spread(self, slot):
        for d in range(self.l.ys - 1):
            self.ycopy(d, slot).start()
        self.kcopy(0, slot).start()

    def start(self):
        self.zcopy(0).start()

        @pl.when(self.l.inner)
        def _():
            self.zcopy(1).start()

        self.spread(3)

    def z_step(self, r):
        self.zcopy((0, 3, 4)[r]).wait_recv()

        @pl.when(self.l.inner)
        def _():
            self.zcopy(2 + r).start()

        self.spread(2 - r)

    def y_step(self, slot):
        for d in range(self.l.ys - 1):
            self.ycopy(d, slot).wait_recv()
            self.kcopy(d + 1, slot).start()

    def run(self):
        self.start()
        for r in range(3):
            self.z_step(r)
            self.y_step(3 - r)
        self.y_step(0)

    def core_wait(self, slot):
        for d in range(self.l.ys):
            self.kcopy(d, slot).wait_recv()

    def finish(self):
        self.zcopy(0).wait_send()

        @pl.when(self.l.inner)
        def _():
            for i in range(1, 5):
                self.zcopy(i).wait_send()

        for slot in range(4):
            for d in range(self.l.ys - 1):
                self.ycopy(d, slot).wait_send()
            for d in range(self.l.ys):
                self.kcopy(d, slot).wait_send()


class LineScatter:
    def __init__(self, line, acc, kbuf, ybuf, zbuf, sems):
        self.l, self.acc, self.kbuf, self.ybuf, self.zbuf = line, acc, kbuf, ybuf, zbuf
        self.zs, self.zr, self.ys, self.yr, self.ks, self.kr = sems

    @staticmethod
    def sems(n):
        ys = n // 8
        return [DMA((3,)), DMA((2, 3)), DMA((ys - 1, 4)), DMA((ys - 1, 4)), DMA((ys, 4)), DMA((ys, 4))]

    @staticmethod
    def scratch(n, rows, cols):
        ys = n // 8
        return [pltpu.VMEM((4, ys, rows, cols), BF16), pltpu.VMEM((ys - 1, 4, rows, cols), BF16), pltpu.VMEM((2, 3, rows, cols), BF16)]

    def y_of(self, d):
        return self.l.y if d == 0 else self.l.others()[d - 1]

    def kcopy(self, d, slot):
        l = self.l
        z, y = l.slots[slot], self.y_of(d)
        return remote(self.acc.at[z, y, 1 - l.c], self.kbuf.at[z, y], self.ks.at[d, slot], self.kr.at[d, slot], l.core)

    def ycopy(self, d, slot):
        l = self.l
        z, y = l.slots[slot], self.y_of(d + 1)
        return remote(self.acc.at[z, y, l.c], self.ybuf.at[d, slot], self.ys.at[d, slot], self.yr.at[d, slot], l.at(l.z, y, l.c))

    def zcopy(self, slot):
        l = self.l
        return remote(self.acc.at[l.slots[slot], l.y, l.c], self.zbuf.at[l.side, slot], self.zs.at[slot], self.zr.at[l.side, slot], l.far if slot < 2 else l.near)

    def zwait(self, side, slot):
        buf = self.zbuf.at[side, slot]
        remote(buf, buf, self.zs.at[slot], self.zr.at[side, slot], self.l.near).wait_recv()
        return self.zbuf[side, slot].astype(F32)

    def own(self, slot):
        return (self.l.slots[slot], self.l.y, self.l.c)

    def core_start(self, slot):
        for d in range(self.l.ys - 1, -1, -1):
            self.kcopy(d, slot).start()

    def core_step(self, slot):
        l = self.l
        for d in list(range(1, l.ys)) + [0]:
            z, y = l.slots[slot], self.y_of(d)
            self.kcopy(d, slot).wait_recv()
            self.acc[z, y, l.c] = (self.acc[z, y, l.c].astype(F32) + self.kbuf[z, y].astype(F32)).astype(BF16)
            if d > 0:
                self.ycopy(d - 1, slot).start()

    def y_sum(self, slot):
        total = self.acc[self.own(slot)].astype(F32)
        for d in range(self.l.ys - 1):
            self.ycopy(d, slot).wait_recv()
            total = total + self.ybuf[d, slot].astype(F32)
        return total

    def z_step(self, slot):
        l, own = self.l, self.own(slot)
        total = self.y_sum(slot)
        self.acc[own] = total.astype(BF16)
        @pl.when(l.inner)
        def _():
            self.acc[own] = (self.acc[own].astype(F32) + self.zwait(*((0, slot) if slot < 2 else (1, 0)))).astype(BF16)

        self.zcopy(slot).start()

    def last(self, out):
        l = self.l
        out[...] = self.y_sum(3)

        @pl.when(l.inner)
        def _():
            out[...] += self.zwait(0, 2) + self.zwait(1, 1)

        @pl.when(l.outer)
        def _():
            out[...] += self.zwait(1, 2)

    def finish(self):
        for slot in range(4):
            for d in range(self.l.ys):
                self.kcopy(d, slot).wait_send()
            for d in range(self.l.ys - 1):
                self.ycopy(d, slot).wait_send()
        for slot in range(3):
            self.zcopy(slot).wait_send()


G1, C1, BQV, IDS, BO, G2, C2, BF, BP = range(9)


def put_ids(n, small_all, first, row, col):
    tokens = small_all.shape[2]
    for j in range(n):
        ids = small_all[first + j].astype(F32)[IDS : IDS + 1, :]
        row[:, j * tokens : (j + 1) * tokens] = ids
        col[j * tokens : (j + 1) * tokens, :] = jnp.transpose(jnp.broadcast_to(ids, (tokens, tokens)))[:, :1]


def half_row(tile_row, odd, high):
    lane = lax.broadcasted_iota(jnp.int32, tile_row.shape, 1)
    turned = pltpu.roll(tile_row, 64, 1)
    moved = jnp.where((odd == 1) == high, tile_row, turned)
    return jnp.where((lane >= 64) == high, moved, 0.0)


def normalize(rows):
    centred = rows - jnp.mean(rows, axis=-1, keepdims=True)
    rstd = lax.rsqrt(jnp.mean(centred * centred, axis=-1, keepdims=True) + EPSILON)
    return centred * rstd, rstd


def group_of(n, f):
    d, j = f // n, f % n
    return d % 2 * (n // 2) + j % (n // 2), d // 2 * 2 + j // (n // 2)


def group_peer(n, i, count):
    d, j = lax.axis_index("dp"), lax.axis_index("ctx")
    g = lax.rem(d // 2 * 2 + j // (n // 2) + i, count)
    return g, {"dp": g // 2 * 2 + d % 2, "ctx": g % 2 * (n // 2) + j % (n // 2)}


def put_small(pieces, tile, small_ref):
    tile[...] = jnp.zeros_like(tile)
    for k, piece in enumerate(pieces):
        tile[k : k + 1, : piece.shape[1]] = piece[...].astype(F32)
    small_ref[...] = tile[...].astype(BF16)


def put_params(count, width, small_all, prm, bqv):
    for size, ref in ((width // count, prm), (2 * width // count, bqv)):
        per = 128 // size
        for k in range(count // per):
            tile = small_all[k * per].astype(F32)
            for i in range(1, per):
                tile = tile + pltpu.roll(small_all[k * per + i].astype(F32), i * size, 1)
            if ref is prm:
                prm[:, k * 128 : (k + 1) * 128] = tile
            else:
                bqv[k : k + 1, :] = tile[BQV : BQV + 1]


def front_kernel(n_dp, n, r, cube, *refs):
    refs = list(refs)
    take = lambda k: [refs.pop(0) for _ in range(k)]
    x_ref, pieces, dy_ref = refs.pop(0), take(9), refs.pop(0)
    (wq_all,) = take(1)
    small_all, first_out, a_ref, b_ref, o_ref, att, dy_all = take(7)
    xbuf, first, prm, bqv, bias, idrow, idcol, packed, acc, tot, own_sems, first_sems, tile, small_ref = take(14)
    line_sems, small_sems, dy_sems, att_sems = take(6), take(2), take(4), take(2)
    tokens, width = x_ref.shape
    count = n_dp * n
    d, me = lax.axis_index("dp"), lax.axis_index("ctx")
    flat = d * n + me
    head, part = me // r, me % r
    line = Line(n)
    hello = Greet(n_dp, n)

    xg = LineGather(line, xbuf, line_sems)
    small = ToAll(n_dp, n, lambda f: small_ref, small_all, small_sems)
    dyg = Gather(cube, dy_all, dy_sems)
    own_copies = [pltpu.make_async_copy(dy_ref, dy_all.at[dyg.own()], own_sems.at[0])]
    for c in own_copies:
        c.start()
    xbuf[line.z, line.y, line.c] = x_ref[...]
    put_small(pieces, tile, small_ref)
    small_all[flat] = small_ref[...]
    hello.wait()
    xg.start()
    small.start()
    for c in own_copies:
        c.wait()
    xg.z_step(0)
    xg.y_step(3)
    small.wait_recv()
    put_params(count, width, small_all, prm, bqv)
    odd = head % 2
    bias[:, :128] = half_row(bqv[pl.ds(head // 2, 1), :], odd, False)
    bias[:, 128:] = half_row(bqv[pl.ds(width // 128 + head // 2, 1), :], odd, True)
    put_ids(n, small_all, d * n, idrow, idcol)
    per_z = n // 4

    def plane(slot):
        return pl.ds(pl.multiple_of(line.slots[slot] * per_z * tokens, per_z * tokens), per_z * tokens)

    def save(slot):
        return pltpu.make_async_copy(first.at[plane(slot)], first_out.at[plane(slot)], first_sems.at[slot])

    def project(slot):
        z = line.slots[slot]

        def one(i, _):
            normed, _ = normalize(xbuf[z, i // 2, i % 2].astype(F32))
            low = (normed * prm[G1 : G1 + 1, :] + prm[C1 : C1 + 1, :]).astype(BF16)
            first[pl.ds(pl.multiple_of((z * per_z + i) * tokens, tokens), tokens), :] = low
            return 0

        lax.fori_loop(0, per_z, one, 0)
        at = plane(slot)
        weights = wq_all[...]
        qkv = (dot(first[at, :], weights) + bias[...]).astype(BF16)
        a_ref[at, :] = qkv[:, :128]
        b_ref[at, :] = qkv[:, 128:]
        save(slot).start()

    xg.z_step(1)
    xg.y_step(2)
    xg.core_wait(3)
    project(3)
    xg.z_step(2)
    xg.y_step(1)
    xg.core_wait(2)
    project(2)
    xg.y_step(0)
    dyg.start()
    xg.core_wait(1)
    project(1)
    xg.core_wait(0)
    project(0)
    dyg.step(0)

    length = b_ref.shape[0]
    kc = min(1024, length)
    half = tokens // 2
    if r > 1:
        packed[...] = jnp.zeros_like(packed)

    def per_queries(lb, _):
        gq = lb * r + part
        qs = pl.ds(pl.multiple_of(gq * QB, QB), QB)
        a = a_ref[qs, :] * 0.125
        ids = idcol[qs, :]
        acc[...] = jnp.zeros_like(acc)
        tot[...] = jnp.zeros_like(tot)

        def per_keys(kb, _):
            ks = pl.ds(pl.multiple_of(kb * kc, kc), kc)
            b = b_ref[ks, :]
            s = dot(a, b, NT)
            w = jnp.where(idrow[:, ks] <= ids, jnp.exp(s), 0.0)
            t = w[:, :128]
            for i in range(1, kc // 128):
                t = t + w[:, i * 128 : (i + 1) * 128]
            tot[...] += t
            acc[...] += dot(w.astype(BF16), b)
            return 0

        lax.fori_loop(0, jnp.minimum(((gq + 2) * QB + kc - 1) // kc, length // kc), per_keys, 0)
        t = jnp.sum(tot[...], axis=-1, keepdims=True)
        o = acc[...] / t
        lane = lax.broadcasted_iota(jnp.int32, (QB, 128), 1)
        o_ref[pl.ds(pl.multiple_of(lb * QB, QB), QB), :] = jnp.where(lane < 64, t, o)
        lane = lax.broadcasted_iota(jnp.int32, (half, 128), 1)
        for i in range(QB // tokens):
            lo, hi = o[i * tokens : i * tokens + half], o[i * tokens + half : (i + 1) * tokens]
            packed[gq * (QB // tokens) + i] = jnp.where(lane < 64, pltpu.roll(lo, 64, 1), hi).astype(BF16)
        return 0

    blocks = length // QB // r
    cuts = [0, blocks // 2, blocks * 3 // 4, blocks]
    for k in range(3):
        lax.fori_loop(cuts[k], cuts[k + 1], per_queries, 0)
        if k + 1 < dyg.links:
            dyg.step(k + 1)
    out = ToAll(n_dp, n, lambda f: packed.at[f], att, att_sems, True)
    att[me] = packed[me]
    out.start()
    for k in range(3, dyg.links):
        dyg.step(k)
    out.wait_recv()
    dyg.core_wait()
    for slot in range(4):
        save(slot).wait()
    small.wait_send()
    out.wait_send()
    xg.finish()
    dyg.finish()


def front(n_dp, n, r, x, small, dy, weights):
    tokens, width = x.shape
    count, length = n_dp * n, n * tokens
    cube = cube_plan(n, tokens)
    shape = jax.ShapeDtypeStruct
    vm, hbm = pl.BlockSpec(memory_space=pltpu.VMEM), pl.BlockSpec(memory_space=pl.ANY)
    outs = [
        (shape((count, 16, 128), BF16), vm), (shape((length, width), BF16), hbm), (shape((length, 128), BF16), vm),
        (shape((length, 128), BF16), vm), (shape((length // r, 128), F32), vm), (shape((n, tokens // 2, 128), BF16), vm),
        (shape((2,) * len(cube[0]) + (tokens, width), BF16), hbm),
    ]
    sems = LineGather.sems(n) + [DMA((count,))] * 2 + Gather.sems(cube) + [DMA((n,))] * 2
    ins = [x, *small, dy]
    ins += [weights]
    return pl.pallas_call(
        functools.partial(front_kernel, n_dp, n, r, cube),
        out_shape=[o for o, _ in outs],
        in_specs=[vm] * len(ins),
        out_specs=[s for _, s in outs],
        scratch_shapes=[
            pltpu.VMEM((4, n // 8, 2, tokens, width), BF16), pltpu.VMEM((length, width), BF16), pltpu.VMEM((16, width), F32),
            pltpu.VMEM((2 * width // 128, 128), F32), pltpu.VMEM((1, 256), F32), pltpu.VMEM((1, length), F32),
            pltpu.VMEM((length, 1), F32), pltpu.VMEM((n, tokens // 2, 128), BF16), pltpu.VMEM((QB, 128), F32),
            pltpu.VMEM((QB, 128), F32), DMA((3,)), DMA((4,)),
            pltpu.VMEM((16, 128), F32), pltpu.VMEM((16, 128), BF16),
        ] + sems,
        compiler_params=pltpu.CompilerParams(collective_id=1, has_side_effects=True, vmem_limit_bytes=VMEM_LIMIT),
        name="front",
    )(*ins)


def gelu_both(u):
    c = math.sqrt(2.0 / math.pi)
    t = jnp.tanh(c * (u + 0.044715 * (u * u * u)))
    half = 0.5 * (1.0 + t)
    return u * half, half + 0.5 * u * (1.0 - t * t) * (c * (1.0 + 3.0 * 0.044715 * (u * u)))


def normalize_back(grad, normed, rstd):
    return rstd * (
        grad
        - jnp.mean(grad, axis=-1, keepdims=True)
        - normed * jnp.mean(grad * normed, axis=-1, keepdims=True)
    )


def ffn_kernel(n, r, plan, *refs):
    refs = list(refs)
    take = lambda k: [refs.pop(0) for _ in range(k)]
    att, x_ref, dy_own, dy_hbm, wo_ref, wf_ref, wp_in, bf_ref, par_ref = take(9)
    middle_ref, mg_ref, low_ref, branch_ref, agb, sums_ref, out_hbm, wp_grad, wf_grad, bf_grad = take(10)
    links = len(plan[0]) - 1
    sbuf, dy_ref, grads, act, hid, acc, out_ref, sg, copy_sems, out_sems = take(10)
    bufs, gather_sems, scatter_sems = take(links + 1), take(4), take(4)
    g = Gather(plan, sbuf, gather_sems)
    s = Scatter(plan, acc, bufs, scatter_sems)
    peers = g.peers()
    hello = Greet(1, n, peers)
    wp_ref = wp_in
    dy_copy = pltpu.make_async_copy(dy_hbm, dy_ref, copy_sems)
    dy_copy.start()
    tokens, width = x_ref.shape
    half = tokens // 2
    quarter = (1 << (links - 1)) * tokens
    inner = (slice(None),) * (links - 1)
    core = g.mine[-1]

    lane = lax.broadcasted_iota(jnp.int32, (half, 128), 1)

    def block(h):
        total = att[h * r].astype(F32)
        for i in range(1, r):
            total = total + att[h * r + i].astype(F32)
        return total

    for h in range(0, HEADS, 2):
        b0, b1 = block(h), block(h + 1)
        at = slice(h * 64, h * 64 + 128)
        low_ref[:half, at] = jnp.where(lane < 64, b0, pltpu.roll(b1, 64, 1)).astype(BF16)
        low_ref[half:, at] = jnp.where(lane < 64, pltpu.roll(b0, 64, 1), b1).astype(BF16)
    middle = x_ref[...].astype(F32) + dot(low_ref[...], wo_ref[...]) + par_ref[0:1, :]
    middle_ref[...] = middle
    n2, _ = normalize(middle)
    sbuf[g.own()] = (n2 * par_ref[1:2, :] + par_ref[2:3, :]).astype(BF16)
    hello.wait()
    g.start()
    dy_copy.wait()
    def rows(c, a):
        return pl.ds(pl.multiple_of((2 * c + a) * quarter, quarter), quarter)

    def grad_part(i):
        dy = dy_ref[(i // 2, i % 2) + inner].reshape(quarter, width)
        grads[rows(i // 2, i % 2), :] = dot(dy, wp_ref[...], NT)

    for k in range(links):
        g.step(k)
        if k == 1:
            for i in range(4):
                grad_part(i)
    g.core_wait()
    bf_grad[...] = jnp.zeros_like(bf_grad)

    def hidden_part(c, a):
        at = rows(c, a)
        low = sbuf[(c, a) + inner].reshape(quarter, width)
        active, slope = gelu_both(dot(low, wf_ref[...]) + bf_ref[...])
        act[at, :] = active.astype(BF16)
        h = (slope * grads[at, :]).astype(BF16)
        hid[at, :] = h
        bf_grad[...] += jnp.sum(h.astype(F32), axis=0, keepdims=True)
        acc[(c, a) + inner] = dot(h, wf_ref[...], NT).astype(BF16).reshape((2,) * (links - 1) + (tokens, width))

    for a in range(2):
        hidden_part(1 - core, a)
        s.core(a).start()
    for a in range(2):
        hidden_part(core, a)
        s.add_core(a)
    s.start_links()

    def weight_grads(k):
        at = slice(k * 256, (k + 1) * 256)
        low = sbuf[..., at].reshape(4 * quarter, 256)
        wf_grad[at, :] = jnp.transpose(dot(hid[...], low, TN)).astype(BF16)
        dy = dy_ref[..., at].reshape(4 * quarter, 256)
        wp_grad[:, at] = dot(act[...], dy, TN).astype(BF16)

    def out_part(i):
        at = (i // 2, i % 2) + inner
        if i >= out_ref.shape[0]:
            out_copy(i - out_ref.shape[0]).wait()
        terms = dot(act[rows(i // 2, i % 2), :], wp_ref[...]).astype(BF16)
        out_ref[i % out_ref.shape[0]] = terms.reshape((2,) * (links - 1) + (tokens, width))
        out_copy(i).start()

    def out_copy(i):
        slot = i % out_ref.shape[0]
        return pltpu.make_async_copy(out_ref.at[slot], out_hbm.at[(i // 2, i % 2) + inner], out_sems.at[slot])

    for i in range(4):
        out_part(i)
    for k in range(links):
        s.step(k, sg)
        if k < 2:
            weight_grads(2 * k)
            weight_grads(2 * k + 1)

    second_grad = sg[...]
    dy = dy_own[...].astype(F32)
    n2, rstd2 = normalize(middle_ref[...])
    mg = dy + normalize_back(second_grad * par_ref[1:2, :], n2, rstd2)
    mg_ref[...] = mg
    branch = mg.astype(BF16)
    branch_ref[...] = branch
    grad = dot(branch, wo_ref[...], NT)
    for h in range(0, HEADS, 2):
        lo, hi = grad[:half, h * 64 : h * 64 + 128], grad[half:, h * 64 : h * 64 + 128]
        b0 = jnp.where(lane < 64, lo, pltpu.roll(hi, 64, 1)).astype(BF16)
        b1 = jnp.where(lane < 64, pltpu.roll(lo, 64, 1), hi).astype(BF16)
        for i in range(r):
            agb[h * r + i] = b0
            agb[(h + 1) * r + i] = b1
    column = lambda v: jnp.sum(v, axis=0, keepdims=True)
    sums_ref[0:1, :] = column(branch.astype(F32))
    sums_ref[1:2, :] = column(second_grad * n2)
    sums_ref[2:3, :] = column(second_grad)
    sums_ref[3:4, :] = column(dy)
    for i in range(4 - out_ref.shape[0], 4):
        out_copy(i).wait()
    s.finish()
    g.finish()


def ffn(n, r, att, x, dy, dy_all, wo, wf, wp, bf, params):
    tokens, width = x.shape
    units = wf.shape[1]
    plan = cube_plan(n, tokens)
    block = (2,) * len(plan[0])
    length = n * tokens
    shape = jax.ShapeDtypeStruct
    vm, hbm = pl.BlockSpec(memory_space=pltpu.VMEM), pl.BlockSpec(memory_space=pl.ANY)
    return pl.pallas_call(
        functools.partial(ffn_kernel, n, r, plan),
        out_shape=[
            shape((tokens, width), F32), shape((tokens, width), F32), shape((tokens, width), BF16), shape((tokens, width), BF16),
            shape((n, tokens // 2, 128), BF16), shape((4, width), F32), shape(block + (tokens, width), BF16),
            shape((units, width), BF16), shape((width, units), BF16), shape((1, units), F32),
        ],
        in_specs=[vm, vm, vm, hbm, vm, vm, vm, vm, vm],
        out_specs=[vm, vm, vm, vm, vm, vm, hbm, vm, vm, vm],
        scratch_shapes=[
            pltpu.VMEM(block + (tokens, width), BF16), pltpu.VMEM(block + (tokens, width), BF16), pltpu.VMEM((length, units), F32),
            pltpu.VMEM((length, units), BF16), pltpu.VMEM((length, units), BF16), pltpu.VMEM(block + (tokens, width), BF16),
            pltpu.VMEM((2,) + block[2:] + (tokens, width), BF16), pltpu.VMEM((tokens, width), F32), DMA, DMA((2,)),
        ] + Scatter.scratch(plan, tokens, width) + Gather.sems(plan) + Scatter.sems(plan),
        compiler_params=pltpu.CompilerParams(collective_id=2, has_side_effects=True, vmem_limit_bytes=VMEM_LIMIT),
        name="ffn",
    )(att, x, dy, dy_all, wo, wf, wp, bf, params)


def project_rows(rows, prm):
    normed, _ = normalize(rows.astype(F32))
    return (normed * prm[G1 : G1 + 1, :] + prm[C1 : C1 + 1, :]).astype(BF16)


def layer_kernel(n_dp, n, cube, whole, *refs):
    refs = list(refs)
    take = lambda k: [refs.pop(0) for _ in range(k)]
    x_ref, pieces, (dy_own, w_qkv, w_fc, w_proj, w_out) = refs.pop(0), take(9), take(5)
    out_ref, ig_ref, sums, wq_got, wf_got, wp_got, wo_own = take(7)
    small_all, a_ref, b_ref, o_ref, wq_all, middle_ref, mg_ref, low_ref, branch_ref, agb, wp_grad, wf_grad, bf_grad = take(13)
    xbuf, first, prm, bqv, bias, bf_row, idrow, idcol, packed, acc, tot, att, wqb, wfb = take(14)
    wf_all, wo_all, wp_ref, dy_ref, sbuf, grads, act, hid, terms, sg, osum, tile, small_ref, sums_ref = take(14)
    ag, kbuf, ybuf, zbuf, got, msg, wq_part, wq_mine, wq_else = take(9)
    links = len(cube[0]) - 1
    bufs, out_bufs = take(links + 1), take(links + 1)
    wo_bufs = take(len(whole[0]))
    line_sems, small_sems, dy_sems, att_sems, wq_sems, wf_sems, wo_sems = take(6), take(2), take(4), take(2), take(4), take(2), take(4)
    wp_sems, gather_sems, scatter_sems = take(2), take(4), take(4)
    ag_sems, back_sems, outs_sems, msg_sems = take(2), take(6), take(4), take(2)
    wqg_sems, wfg_sems, wpg_sems, wog_sems = take(4), take(2), take(2), take(4)

    tokens, width = x_ref.shape
    length = n * tokens
    rows, units = w_fc.shape[0], w_proj.shape[0]
    count = n_dp * n
    d, me = lax.axis_index("dp"), lax.axis_index("ctx")
    flat = d * n + me
    rank, group = group_of(n, flat)
    line = Line(n)
    hello = Greet(n_dp, n)

    xg = LineGather(line, xbuf, line_sems)
    small = ToAll(n_dp, n, lambda f: small_ref, small_all, small_sems)
    wq = ToAll(n_dp, n, lambda f: wqb.at[f], wq_all.at[d], wq_sems[:2], True)
    wf = ToAll(n_dp, n, lambda f: wfb.at[group_of(n, f)[0]], wf_all, wf_sems)
    dyg = Gather(cube, dy_ref, dy_sems)
    wog = Gather(whole, wo_all, wo_sems)
    out = ToAll(n_dp, n, lambda f: packed.at[f], att, att_sems, True)
    g = Gather(cube, sbuf, gather_sems)
    s = Scatter(cube, terms, bufs, scatter_sems)
    dps, wps = [], []
    for i in range(1, n_dp):
        dps.append(remote(wq_all.at[d], wq_all.at[d], wq_sems[2].at[i], wq_sems[3].at[i], {"dp": (d + i) % n_dp}))
        to = wp_ref.at[pl.ds(pl.multiple_of(group * units, units), units)]
        wps.append(remote(w_proj, to, wp_sems[0].at[i], wp_sems[1].at[i], group_peer(n, i, n_dp)[1]))

    low = lax.broadcasted_iota(jnp.int32, (rows, 128), 1) < 64
    for h in range(0, HEADS, 2):
        q, k, v = (w_qkv[:, p * width + h * 64 : p * width + h * 64 + 128].astype(F32) for p in range(3))
        turn = lambda t: pltpu.roll(t, 64, 1)
        wqb[h, :, :128] = jnp.where(low, q, 0.0).astype(BF16)
        wqb[h, :, 128:] = jnp.where(low, k, turn(v)).astype(BF16)
        wqb[h + 1, :, :128] = jnp.where(low, turn(q), 0.0).astype(BF16)
        wqb[h + 1, :, 128:] = jnp.where(low, turn(k), v).astype(BF16)
    xbuf[line.z, line.y, line.c] = x_ref[...]
    put_small(pieces, tile, small_ref)
    small_all[flat] = small_ref[...]
    wq_all[d, me] = wqb[me]
    wo_all[wog.own()] = w_out[...]
    hello.wait()
    xg.start()
    small.start()
    wq.start()
    wog.start()
    for m in range(n):
        for i in range(n_dp):
            at = ((i // 2 * 2 + m // (n // 2)) * n + i % 2 * (n // 2) + m % (n // 2)) * units
            wfb[m, :, i * units : (i + 1) * units] = w_fc[:, at : at + units]
    dy_ref[dyg.own()] = dy_own[...]
    wf_all[flat] = wfb[rank]
    wp_ref[pl.ds(pl.multiple_of(group * units, units), units), :] = w_proj[...]
    xg.z_step(0)
    xg.y_step(3)
    xg.z_step(1)
    xg.y_step(2)
    wq.wait_recv()
    for c in dps:
        c.start()
    small.wait_recv()
    put_params(count, width, small_all, prm, bqv)
    odd = me % 2
    bias[:, :128] = half_row(bqv[pl.ds(me // 2, 1), :], odd, False)
    bias[:, 128:] = half_row(bqv[pl.ds(width // 128 + me // 2, 1), :], odd, True)
    for i in range(n_dp):
        owner = (i // 2 * 2 + d % 2) * n + i % 2 * (n // 2) + me % (n // 2)
        bf_row[:, i * units : (i + 1) * units] = small_all[owner].astype(F32)[BF : BF + 1, :units]
    put_ids(n, small_all, d * n, idrow, idcol)
    per_z = n // 4

    def plane(slot):
        return pl.ds(pl.multiple_of(line.slots[slot] * per_z * tokens, per_z * tokens), per_z * tokens)

    def project(slot):
        z = line.slots[slot]

        def one(i, _):
            at = pl.ds(pl.multiple_of((z * per_z + i) * tokens, tokens), tokens)
            first[at, :] = project_rows(xbuf[z, i // 2, i % 2], prm)
            return 0

        lax.fori_loop(0, per_z, one, 0)
        at = plane(slot)
        qkv = (dot(first[at, :], wq_all[...].reshape(width, 256)) + bias[...]).astype(BF16)
        a_ref[at, :] = qkv[:, :128]
        b_ref[at, :] = qkv[:, 128:]

    wog.step(0)
    xg.z_step(2)
    xg.y_step(1)
    for c in dps:
        c.wait_recv()
    xg.core_wait(3)
    project(3)
    wog.step(1)
    xg.core_wait(2)
    project(2)
    xg.y_step(0)
    dyg.start()
    for c in wps:
        c.start()
    wf.start()
    wog.step(2)
    xg.core_wait(1)
    project(1)
    xg.core_wait(0)
    project(0)
    dyg.step(0)

    kc = min(1024, length)
    half = tokens // 2
    lane = lax.broadcasted_iota(jnp.int32, (half, 128), 1)

    def per_queries(gq, _):
        qs = pl.ds(pl.multiple_of(gq * QB, QB), QB)
        a = a_ref[qs, :] * 0.125
        ids = idcol[qs, :]
        acc[...] = jnp.zeros_like(acc)
        tot[...] = jnp.zeros_like(tot)

        def per_keys(kb, _):
            ks = pl.ds(pl.multiple_of(kb * kc, kc), kc)
            b = b_ref[ks, :]
            w = jnp.where(idrow[:, ks] <= ids, jnp.exp(dot(a, b, NT)), 0.0)
            t = w[:, :128]
            for i in range(1, kc // 128):
                t = t + w[:, i * 128 : (i + 1) * 128]
            tot[...] += t
            acc[...] += dot(w.astype(BF16), b)
            return 0

        lax.fori_loop(0, jnp.minimum(((gq + 2) * QB + kc - 1) // kc, length // kc), per_keys, 0)
        t = jnp.sum(tot[...], axis=-1, keepdims=True)
        o = acc[...] / t
        o_ref[qs, :] = jnp.where(lax.broadcasted_iota(jnp.int32, (QB, 128), 1) < 64, t, o)
        for i in range(QB // tokens):
            lo, hi = o[i * tokens : i * tokens + half], o[i * tokens + half : (i + 1) * tokens]
            packed[gq * (QB // tokens) + i] = jnp.where(lane < 64, pltpu.roll(lo, 64, 1), hi).astype(BF16)
        return 0

    blocks = length // QB
    lax.fori_loop(0, blocks // 2, per_queries, 0)
    dyg.step(1)
    wog.step(3)
    lax.fori_loop(blocks // 2, blocks, per_queries, 0)
    att[me] = packed[me]
    out.start()
    for k in range(4, wog.links):
        wog.step(k)
    wog.core_wait()
    out.wait_recv()

    for h in range(0, HEADS, 2):
        b0, b1 = att[h].astype(F32), att[h + 1].astype(F32)
        at = slice(h * 64, h * 64 + 128)
        low_ref[:half, at] = jnp.where(lane < 64, b0, pltpu.roll(b1, 64, 1)).astype(BF16)
        low_ref[half:, at] = jnp.where(lane < 64, pltpu.roll(b0, 64, 1), b1).astype(BF16)
    middle = x_ref[...].astype(F32) + dot(low_ref[...], wo_all[...].reshape(width, width)) + prm[BO : BO + 1, :]
    middle_ref[...] = middle
    n2, _ = normalize(middle)
    sbuf[g.own()] = (n2 * prm[G2 : G2 + 1, :] + prm[C2 : C2 + 1, :]).astype(BF16)
    g.start()
    for k in range(2, links):
        dyg.step(k)
    for c in wps:
        c.wait_recv()
    dyg.core_wait()

    quarter = (1 << (links - 1)) * tokens
    inner = (slice(None),) * (links - 1)
    block = (2,) * (links - 1) + (tokens, width)
    core = g.mine[-1]

    def span(c, a):
        return pl.ds(pl.multiple_of((2 * c + a) * quarter, quarter), quarter)

    def grad_part(i):
        dy = dy_ref[(i // 2, i % 2) + inner].reshape(quarter, width)
        grads[span(i // 2, i % 2), :] = dot(dy, wp_ref[...], NT)

    for k in range(links):
        grad_part(k)
        g.step(k)
    for k in range(links, 4):
        grad_part(k)
    wf.wait_recv()
    g.core_wait()
    bf_grad[...] = jnp.zeros_like(bf_grad)

    def hidden_part(c, a):
        at = span(c, a)
        weights = wf_all[...].reshape(width, -1)
        active, slope = gelu_both(dot(sbuf[(c, a) + inner].reshape(quarter, width), weights) + bf_row[...])
        act[at, :] = active.astype(BF16)
        h = (slope * grads[at, :]).astype(BF16)
        hid[at, :] = h
        bf_grad[...] += jnp.sum(h.astype(F32), axis=0, keepdims=True)
        terms[(c, a) + inner] = dot(h, weights, NT).astype(BF16).reshape(block)

    for a in range(2):
        hidden_part(1 - core, a)
        s.core(a).start()
    for a in range(2):
        hidden_part(core, a)
        s.add_core(a)
    s.start_links()

    def weight_grads(k):
        at = slice(k * 256, (k + 1) * 256)
        low = sbuf[..., at].reshape(4 * quarter, 256)
        wf_grad[at, :] = jnp.transpose(dot(hid[...], low, TN)).astype(BF16)
        wp_grad[:, at] = dot(act[...], dy_ref[..., at].reshape(4 * quarter, 256), TN).astype(BF16)

    outs = Scatter(cube, terms, out_bufs, outs_sems)
    s.core_sent()
    for i in range(4):
        terms[(i // 2, i % 2) + inner] = dot(act[span(i // 2, i % 2), :], wp_ref[...]).astype(BF16).reshape(block)
    for h in range(2):
        outs.core(h).start()
    for k in range(links):
        s.step(k, sg)
        if k < 2:
            weight_grads(2 * k)
            weight_grads(2 * k + 1)

    for h in range(2):
        outs.add_core(h)
    outs.start_links()
    second_grad = sg[...]
    dy = dy_own[...].astype(F32)
    n2, rstd2 = normalize(middle_ref[...])
    mg = dy + normalize_back(second_grad * prm[G2 : G2 + 1, :], n2, rstd2)
    mg_ref[...] = mg
    branch = mg.astype(BF16)
    branch_ref[...] = branch
    grad = dot(branch, wo_all[...].reshape(width, width), NT)
    for h in range(0, HEADS, 2):
        lo, hi = grad[:half, h * 64 : h * 64 + 128], grad[half:, h * 64 : h * 64 + 128]
        agb[h] = jnp.where(lane < 64, lo, pltpu.roll(hi, 64, 1)).astype(BF16)
        agb[h + 1] = jnp.where(lane < 64, pltpu.roll(lo, 64, 1), hi).astype(BF16)
    heads = ToAll(n_dp, n, lambda f: agb.at[f], ag, ag_sems, True)
    heads.start()
    ag[me] = agb[me]
    column = lambda v: jnp.sum(v, axis=0, keepdims=True)
    sums_ref[0:1, :] = column(branch.astype(F32))
    sums_ref[1:2, :] = column(second_grad * n2)
    sums_ref[2:3, :] = column(second_grad)
    sums_ref[3:4, :] = column(dy)

    block_of = lambda ref, f, size: ref.at[pl.ds(pl.multiple_of(f * size, size), size)]
    wfs = ToAll(n_dp, n, lambda f: block_of(wf_grad, f, rows), wf_got, wfg_sems)
    wqs = ToAll(n_dp, n, lambda f: wq_mine.at[f], wq_got, wqg_sems[:2], True)
    wo = Scatter(whole, wo_all, wo_bufs, wog_sems)
    wf_got[flat] = block_of(wf_grad, flat, rows)[...]
    wp_got[group] = block_of(wp_grad, group, units)[...]
    wpgs, dpgs = [], []
    for i in range(1, n_dp):
        to, peer = group_peer(n, i, n_dp)
        wpgs.append(remote(block_of(wp_grad, to, units), wp_got.at[group], wpg_sems[0].at[i], wpg_sems[1].at[i], peer))
        other = (d + i) % n_dp
        dpgs.append(remote(wq_part.at[other], wq_else.at[i], wqg_sems[2].at[i], wqg_sems[3].at[i], {"dp": other}))
    for c in wpgs:
        c.start()
    heads.wait_recv()
    wfs.start()
    wog.finish()
    for k in range(width // 256):
        part = dot(low_ref[:, k * 256 : (k + 1) * 256], branch, TN).astype(BF16)
        for i in range(256 // rows):
            f = k * (256 // rows) + i
            wo_all[tuple((f >> b) & 1 for b in range(len(whole[0]) - 1, -1, -1))] = part[i * rows : (i + 1) * rows]
    for h in range(2):
        wo.core(h).start()
    mixed, dkv = act, grads
    dkv[:, :128] = jnp.zeros((length, 128), F32)

    def per_queries_back(gq, _):
        qs = pl.ds(pl.multiple_of(gq * QB, QB), QB)
        pieces = []
        for i in range(QB // tokens):
            t = ag[gq * (QB // tokens) + i].astype(F32)
            pieces += [jnp.where(lane >= 64, pltpu.roll(t, 64, 1), 0.0), jnp.where(lane >= 64, t, 0.0)]
        grad = jnp.concatenate(pieces, axis=0)
        o = o_ref[qs, :]
        inverse = 1.0 / o[:, :1]
        upper = lax.broadcasted_iota(jnp.int32, (QB, 128), 1) >= 64
        ratio = jnp.sum(jnp.where(upper, grad * o, 0.0), axis=-1, keepdims=True) * inverse
        ratio = jnp.transpose(jnp.broadcast_to(ratio, (QB, 128)))[:1, :]
        do = (grad * inverse).astype(BF16)
        a = a_ref[qs, :]
        scaled = a * 0.125
        ado = jnp.concatenate([a, do], axis=0)
        ids = idrow[:, qs]
        acc[...] = jnp.zeros_like(acc)

        def per_keys(kb, _):
            ks = pl.ds(pl.multiple_of(kb * kc, kc), kc)
            b = b_ref[ks, :]
            w = jnp.where(idcol[ks, :] <= ids, jnp.exp(dot(b, scaled, NT)), 0.0)
            t = (w * (dot(b, do, NT) - ratio)).astype(BF16)
            dkv[ks, :128] += dot(jnp.concatenate([t, w.astype(BF16)], axis=1), ado)
            acc[...] += dot(t, b, TN)
            return 0

        lax.fori_loop(0, jnp.minimum(((gq + 2) * QB + kc - 1) // kc, length // kc), per_keys, 0)
        mixed[qs, :128] = jnp.where(upper, 0.0, acc[...] * 0.125).astype(BF16)
        return 0

    cuts = [0, blocks // 2, blocks * 3 // 4, blocks]
    for k in range(3):
        lax.fori_loop(cuts[k], cuts[k + 1], per_queries_back, 0)
        if k + 1 < links:
            outs.step(k, osum)
    for h in range(2):
        wo.add_core(h)
    total = dkv[:, :128]
    lower = lax.broadcasted_iota(jnp.int32, (length, 128), 1) < 64
    mixed[:, 128:] = jnp.where(lower, total * 0.125, total).astype(BF16)

    xg.finish()
    rs = LineScatter(line, xbuf, kbuf, ybuf, zbuf, back_sems)

    def first_grad(slot):
        part = dot(mixed[plane(slot), :], wq_all[...].reshape(width, 256), NT).astype(BF16)
        xbuf[line.slots[slot]] = part.reshape(n // 8, 2, tokens, width)
        rs.core_start(slot)

    first_grad(0)
    for slot in range(1, 4):
        first_grad(slot)
        rs.core_step(slot - 1)
    rs.core_step(3)
    for k in range(min(2, links - 1), links):
        outs.step(k, osum)
    wo.start_links()

    def wq_grad(i):
        k = ((d + 1) * (width // 256 // n_dp) + i) % (width // 256)
        part = jnp.transpose(dot(mixed[...], first[:, pl.ds(pl.multiple_of(k * 256, 256), 256)], TN))
        q = 256 // rows
        wq_part[k * q // n, pl.ds(k * q % n, q)] = part.astype(BF16).reshape(q, rows, 256)

    turns = width // 256
    ahead = turns - turns // n_dp
    for i in range(ahead):
        wq_grad(i)
    for c in dpgs:
        c.start()
    rs.z_step(0)
    for i in range(ahead, turns):
        wq_grad(i)
    rs.z_step(1)
    total = wq_part[d].astype(F32)
    for i, c in enumerate(dpgs):
        c.wait_recv()
        total = total + wq_else[i + 1].astype(F32)
    wq_mine[...] = total.astype(BF16)
    wq_got[me] = wq_mine[me]
    wqs.start()
    wo.step(0, wo_own)
    total = jnp.sum(mixed[...].astype(F32), axis=0, keepdims=True)
    q_row = half_row(total[:, :128], 0, False)
    q_row = jnp.where(odd == 1, pltpu.roll(q_row, 64, 1), q_row)
    v_row = half_row(total[:, 128:], 1, True)
    v_row = jnp.where(odd == 1, v_row, pltpu.roll(v_row, 64, 1))
    rs.z_step(2)
    out_ref[...] = (middle_ref[...] + osum[...] + prm[BP : BP + 1, :]).astype(BF16)
    n1, rstd1 = normalize(x_ref[...].astype(F32))
    wo.step(1, wo_own)

    def prepare(f, _):
        at = f * 2 * width // count // 128
        msg[f, 6:7, :] = jnp.where(at == me // 2, q_row, 0.0) + jnp.where(at == width // 128 + me // 2, v_row, 0.0)
        same = group_of(n, f)[0] == rank
        for i in range(bf_grad.shape[1] // 128):
            msg[f, 7 + i : 8 + i, :] = jnp.where(same, bf_grad[:, i * 128 : (i + 1) * 128], 0.0)
        return 0

    msg[...] = jnp.zeros_like(msg)
    lax.fori_loop(0, count, prepare, 0)
    rs.last(sg)

    grad = sg[...]
    gain, shift = column(grad * n1), column(grad)
    per = 128 * count // width
    for k in range(width // 128):
        at = slice(k * 128, (k + 1) * 128)
        lines = jnp.concatenate([gain[:, at], shift[:, at], sums_ref[:, at]], axis=0)
        for i in range(per):
            msg[k * per + i, 0:6, :] = lines
    tell = ToAll(n_dp, n, lambda f: msg.at[f], got, msg_sems)
    tell.start()
    got[flat] = msg[flat]
    ig_ref[...] = (mg_ref[...] + normalize_back(grad * prm[G1 : G1 + 1, :], n1, rstd1)).astype(BF16)
    for k in range(2, wo.links):
        wo.step(k, wo_own)
    wfs.wait_recv()
    wqs.wait_recv()
    for c in wpgs:
        c.wait_recv()
    tell.wait_recv()
    sums[...] = jnp.sum(got[...], axis=0)
    for c in (wq, wf, small, out, heads, wfs, wqs, tell):
        c.wait_send()
    for c in dps + wps + wpgs + dpgs:
        c.wait_send()
    s.links_sent()
    for c in (dyg, g, outs, wo, rs):
        c.finish()


def layer(n_dp, n, x, small, dy, w_qkv, w_fc, w_proj, w_out):
    tokens, width = x.shape
    count, length = n_dp * n, n * tokens
    rows, own = w_fc.shape[0], w_proj.shape[0]
    units = n_dp * own
    cube, whole = cube_plan(n, tokens), all_plan(n_dp, n, rows)
    block = (2,) * len(cube[0]) + (tokens, width)
    shape, v = jax.ShapeDtypeStruct, pltpu.VMEM
    vm = pl.BlockSpec(memory_space=pltpu.VMEM)
    outs = [
        shape((tokens, width), BF16), shape((tokens, width), BF16), shape((16, 128), F32), shape((n, rows, 256), BF16),
        shape((count, rows, units), BF16), shape((n_dp, own, width), BF16), shape((rows, width), F32),
    ]
    heads = (n, tokens // 2, 128)
    all_sems = [DMA((count,))] * 2
    weight_sems = [DMA((n,))] * 2 + [DMA((n_dp,))] * 2
    return pl.pallas_call(
        functools.partial(layer_kernel, n_dp, n, cube, whole),
        out_shape=outs,
        in_specs=[vm] * 15,
        out_specs=[vm] * len(outs),
        scratch_shapes=[
            v((count, 16, 128), BF16), v((length, 128), BF16), v((length, 128), BF16), v((length, 128), F32),
            v((n_dp, n, rows, 256), BF16), v((tokens, width), F32), v((tokens, width), F32), v((tokens, width), BF16),
            v((tokens, width), BF16), v(heads, BF16), v((units, width), BF16), v((width, units), BF16), v((1, units), F32),
            v((4, n // 8, 2, tokens, width), BF16), v((length, width), BF16), v((16, width), F32), v((2 * width // 128, 128), F32),
            v((1, 256), F32), v((1, units), F32), v((1, length), F32), v((length, 1), F32), v(heads, BF16), v((QB, 128), F32),
            v((QB, 128), F32), v(heads, BF16), v((n, rows, 256), BF16), v((n, rows, units), BF16),
            v((count, rows, units), BF16), v((2,) * len(whole[0]) + (rows, width), BF16), v((units, width), BF16), v(block, BF16),
            v(block, BF16), v((length, units), F32), v((length, units), BF16), v((length, units), BF16), v(block, BF16),
            v((tokens, width), F32), v((tokens, width), F32), v((16, 128), F32), v((16, 128), BF16), v((4, width), F32),
            v(heads, BF16),
        ] + LineScatter.scratch(n, tokens, width) + [
            v((count, 16, 128), F32), v((count, 16, 128), F32), v((n_dp, n, rows, 256), BF16), v((n, rows, 256), BF16),
            v((n_dp, n, rows, 256), BF16),
        ] + Scatter.scratch(cube, tokens, width) * 2 + Scatter.scratch(whole, rows, width)
        + LineGather.sems(n) + all_sems + Gather.sems(cube) + [DMA((n,))] * 2 + weight_sems + all_sems + Gather.sems(whole)
        + [DMA((n_dp,))] * 2 + Gather.sems(cube) + Scatter.sems(cube)
        + [DMA((n,))] * 2 + LineScatter.sems(n) + Scatter.sems(cube) + all_sems
        + weight_sems + all_sems + [DMA((n_dp,))] * 2 + Scatter.sems(whole),
        compiler_params=pltpu.CompilerParams(collective_id=4, has_side_effects=True, vmem_limit_bytes=VMEM_MOST),
        name="layer",
    )(x, *small, dy, w_qkv, w_fc, w_proj, w_out)


def back_kernel(n_dp, n, r, spread, cube, whole, *refs):
    refs = list(refs)
    take = lambda k: [refs.pop(0) for _ in range(k)]
    agb, a_ref, b_ref, o_ref, small_all, wq_ref, first, part_out, x_ref, mid_ref, mg_ref, par_ref, sums_in, bf_grad = take(14)
    if spread:
        low_ref, branch_ref, wfg, wpg = take(4)
    out_ref, ig_ref, sums = take(3)
    if spread:
        wq_got, wf_got, wp_got, wo_own = take(4)
    else:
        (wq_sum,) = take(1)
    ag, idrow, idcol, mixed, dqacc, dkv, acc, kbuf, ybuf, zbuf, fg, got, msg, columns, column_sem, own_out, own_sem, osum = take(18)
    links = len(cube[0]) - 1
    out_bufs = take(links + 1)
    if r > 1:
        (dkv_got,) = take(1)
        pair_sems = take(2)
    ag_sems, line_sems, out_sems, msg_sems = take(2), take(6), take(4), take(2)
    if spread:
        wq_part, wq_mine, wq_else, wo_part = take(4)
        wq_sems, wf_sems, wp_sems = take(4), take(2), take(2)
        wo_bufs = take(len(whole[0]))
        wo_sems = take(4)

    tokens, width = x_ref.shape
    length = b_ref.shape[0]
    count = n_dp * n
    d, me = lax.axis_index("dp"), lax.axis_index("ctx")
    flat = d * n + me
    head, part = me // r, me % r
    line = Line(n)
    hello = Greet(n_dp, n)
    kc = min(1024, length)
    half = tokens // 2

    grads = ToAll(n_dp, n, lambda f: agb.at[f], ag, ag_sems, True)
    outs = Scatter(cube, part_out, out_bufs, out_sems, own_out)
    own_copy = outs.fetch_own(own_sem)
    own_copy.start()
    ag[me] = agb[me]
    if spread:
        wf = ToAll(n_dp, n, lambda f: wfg.at[f], wf_got, wf_sems)
        wq = ToAll(n_dp, n, lambda f: wq_mine.at[f], wq_got, wq_sems[:2], True)
        wo = Scatter(whole, wo_part, wo_bufs, wo_sems)
        wf_got[flat] = wfg[flat]
        rank, group = group_of(n, flat)
        wp_got[group] = wpg[group]
        wps, dps = [], []
        for i in range(1, n_dp):
            g, peer = group_peer(n, i, n_dp)
            wps.append(remote(wpg.at[g], wp_got.at[group], wp_sems[0].at[i], wp_sems[1].at[i], peer))
            dps.append(remote(wq_part.at[(d + i) % n_dp], wq_else.at[i], wq_sems[2].at[i], wq_sems[3].at[i], {"dp": (d + i) % n_dp}))
    else:
        rank, group = group_of(n, flat)
    dkv[...] = jnp.zeros_like(dkv)
    if r > 1:
        mixed[...] = jnp.zeros_like(mixed)
    hello.wait()
    grads.start()
    for h in range(2):
        outs.core(h).start()
    if spread:
        for c in wps:
            c.start()
    put_ids(n, small_all, d * n, idrow, idcol)
    if spread:
        rows = width // count
        for k in range(width // 256):
            terms = dot(low_ref[:, k * 256 : (k + 1) * 256], branch_ref[...], TN).astype(BF16)
            for i in range(256 // rows):
                f = k * (256 // rows) + i
                bits = tuple((f >> b) & 1 for b in range(len(whole[0]) - 1, -1, -1))
                wo_part[bits] = terms[i * rows : (i + 1) * rows]
        for h in range(2):
            wo.core(h).start()
    own_copy.wait()
    for h in range(2):
        outs.add_core(h)
    outs.start_links()
    grads.wait_recv()
    if spread:
        wf.start()

    def per_queries(lb, _):
        gq = lb * r + part
        qs = pl.ds(pl.multiple_of(gq * QB, QB), QB)
        at = pl.ds(pl.multiple_of(lb * QB, QB), QB)
        lane = lax.broadcasted_iota(jnp.int32, (half, 128), 1)
        pieces = []
        for i in range(QB // tokens):
            block = ag[gq * (QB // tokens) + i].astype(F32)
            pieces += [jnp.where(lane >= 64, pltpu.roll(block, 64, 1), 0.0), jnp.where(lane >= 64, block, 0.0)]
        grad = jnp.concatenate(pieces, axis=0)
        o = o_ref[at, :]
        inverse = 1.0 / o[:, :1]
        upper = lax.broadcasted_iota(jnp.int32, (QB, 128), 1) >= 64
        ratio = jnp.sum(jnp.where(upper, grad * o, 0.0), axis=-1, keepdims=True) * inverse
        ratio = jnp.transpose(jnp.broadcast_to(ratio, (QB, 128)))[:1, :]
        do = (grad * inverse).astype(BF16)
        a = a_ref[qs, :]
        scaled = a * 0.125
        ado = jnp.concatenate([a, do], axis=0)
        ids = idrow[:, qs]
        dqacc[...] = jnp.zeros_like(dqacc)

        def per_keys(kb, _):
            ks = pl.ds(pl.multiple_of(kb * kc, kc), kc)
            b = b_ref[ks, :]
            w = jnp.where(idcol[ks, :] <= ids, jnp.exp(dot(b, scaled, NT)), 0.0)
            g = (w * (dot(b, do, NT) - ratio)).astype(BF16)
            dkv[ks, :] += dot(jnp.concatenate([g, w.astype(BF16)], axis=1), ado)
            dqacc[...] += dot(g, b, TN)
            return 0

        lax.fori_loop(0, jnp.minimum(((gq + 2) * QB + kc - 1) // kc, length // kc), per_keys, 0)
        mixed[qs, :128] = jnp.where(upper, 0.0, dqacc[...] * 0.125).astype(BF16)
        return 0

    blocks = length // QB // r
    cuts = [0, blocks // 2, blocks * 3 // 4, blocks]
    for k in range(3):
        lax.fori_loop(cuts[k], cuts[k + 1], per_queries, 0)
        if k + 1 < links:
            outs.step(k, osum)
    if spread:
        for h in range(2):
            wo.add_core(h)

    def fetch(k):
        return pltpu.make_async_copy(first.at[:, pl.ds(pl.multiple_of(k * 256, 256), 256)], columns, column_sem)

    turns = [((d + 1) * (width // 256 // n_dp) + i) % (width // 256) if spread else i for i in range(width // 256)]
    fetch(turns[0]).start()
    low = lax.broadcasted_iota(jnp.int32, (length, 128), 1) < 64
    total = dkv[...]
    if r > 1:
        both = remote(dkv, dkv_got, pair_sems[0], pair_sems[1], line.core)
        both.start()
        both.wait()
        total = jnp.where(part == 0, total + dkv_got[...], 0.0)
    mixed[:, 128:] = jnp.where(low, total * 0.125, total).astype(BF16)

    rs = LineScatter(line, acc, kbuf, ybuf, zbuf, line_sems)
    per_z = n // 4 * tokens

    def first_grad(slot):
        z = line.slots[slot]
        at = pl.ds(pl.multiple_of(z * per_z, per_z), per_z)
        acc[z] = dot(mixed[at, :], wq_ref[...], NT).astype(BF16).reshape(n // 8, 2, tokens, width)
        rs.core_start(slot)

    first_grad(0)
    for slot in range(1, 4):
        first_grad(slot)
        rs.core_step(slot - 1)
    rs.core_step(3)
    for k in range(min(2, links - 1), links):
        outs.step(k, osum)
    if spread:
        wo.start_links()

    def wq_grad(i):
        k = turns[i]
        fetch(k).wait()
        g = jnp.transpose(dot(mixed[...], columns[...], TN))
        if i + 1 < len(turns):
            fetch(turns[i + 1]).start()
        if spread:
            per = n_dp * 256 // width
            q = 256 // rows
            at = k * q
            wq_part[at // n, pl.ds(at % n, q)] = g.astype(BF16).reshape(q, rows, 256)
        else:
            wq_sum[pl.ds(pl.multiple_of(k * 256, 256), 256), :] = g

    ahead = len(turns) - len(turns) // n_dp if spread else 2
    for i in range(ahead):
        wq_grad(i)
    if spread:
        for c in dps:
            c.start()
    rs.z_step(0)
    for i in range(ahead, len(turns)):
        wq_grad(i)
    rs.z_step(1)
    if spread:
        total = wq_part[d].astype(F32)
        for i, c in enumerate(dps):
            c.wait_recv()
            total = total + wq_else[i + 1].astype(F32)
        wq_mine[...] = total.astype(BF16)
        wq_got[me] = wq_mine[me]
        wq.start()
        wo.step(0, wo_own)
    column = jnp.sum(mixed[...].astype(F32), axis=0, keepdims=True)
    odd = head % 2
    q_row = half_row(column[:, :128], 0, False)
    q_row = jnp.where(odd == 1, pltpu.roll(q_row, 64, 1), q_row)
    v_row = half_row(column[:, 128:], 1, True)
    v_row = jnp.where(odd == 1, v_row, pltpu.roll(v_row, 64, 1))
    rs.z_step(2)
    out_ref[...] = (mid_ref[...] + osum[...] + par_ref[1:2, :]).astype(BF16)
    n1, rstd1 = normalize(x_ref[...].astype(F32))
    if spread:
        wo.step(1, wo_own)

    wide = bf_grad.shape[1] // 128

    def prepare(f, _):
        tile = f * 2 * width // count // 128
        bqv = jnp.where(tile == head // 2, q_row, 0.0) + jnp.where(tile == width // 128 + head // 2, v_row, 0.0)
        msg[f, 6:7, :] = bqv
        same = group_of(n, f)[0] == rank
        for i in range(wide):
            msg[f, 7 + i : 8 + i, :] = jnp.where(same, bf_grad[:, i * 128 : (i + 1) * 128], 0.0)
        return 0

    msg[...] = jnp.zeros_like(msg)
    lax.fori_loop(0, count, prepare, 0)
    rs.last(fg)

    grad = fg[...]
    gain = jnp.sum(grad * n1, axis=0, keepdims=True)
    shift = jnp.sum(grad, axis=0, keepdims=True)
    per = 128 * count // width
    for k in range(width // 128):
        at = slice(k * 128, (k + 1) * 128)
        lines = jnp.concatenate([gain[:, at], shift[:, at], sums_in[:, at]], axis=0)

        def fill(i, _, k=k, lines=lines):
            msg[k * per + i, 0:6, :] = lines
            return 0

        lax.fori_loop(0, per, fill, 0)
    tell = ToAll(n_dp, n, lambda f: msg.at[f], got, msg_sems)
    tell.start()
    got[flat] = msg[flat]
    ig_ref[...] = (mg_ref[...] + normalize_back(grad * par_ref[0:1, :], n1, rstd1)).astype(BF16)
    if spread:
        for k in range(2, wo.links):
            wo.step(k, wo_own)
        wf.wait_recv()
        wq.wait_recv()
        for c in wps:
            c.wait()
    tell.wait_recv()
    sums[...] = jnp.sum(got[...], axis=0)
    tell.wait_send()
    if spread:
        wf.wait_send()
        wq.wait_send()
        for c in dps:
            c.wait_send()
        wo.finish()
    grads.wait_send()
    outs.finish()
    rs.finish()


def back(n_dp, n, r, agb, a, b, o, small_all, wq, first, part_out, x, middle, mg, params, sums4, bf_grad, grads):
    tokens, width = x.shape
    count, length = n_dp * n, n * tokens
    spread = grads is not None
    cube = cube_plan(n, tokens)
    links = len(cube[0]) - 1
    whole = None
    shape = jax.ShapeDtypeStruct
    ins = [agb, a, b, o, small_all, wq, first, part_out, x, middle, mg, params, sums4, bf_grad]
    outs = [shape((tokens, width), BF16), shape((tokens, width), BF16), shape((16, 128), F32)]
    scratch = [
        pltpu.VMEM((n, tokens // 2, 128), BF16), pltpu.VMEM((1, length), F32), pltpu.VMEM((length, 1), F32),
        pltpu.VMEM((length, 256), BF16), pltpu.VMEM((QB, 128), F32), pltpu.VMEM((length, 128), F32),
        pltpu.VMEM((4, n // 8, 2, tokens, width), BF16),
    ] + LineScatter.scratch(n, tokens, width) + [
        pltpu.VMEM((tokens, width), F32), pltpu.VMEM((count, 16, 128), F32), pltpu.VMEM((count, 16, 128), F32),
        pltpu.VMEM((length, 256), BF16), DMA, pltpu.VMEM((2,) * links + (tokens, width), BF16), DMA,
        pltpu.VMEM((tokens, width), F32),
    ] + Scatter.scratch(cube, tokens, width)
    if r > 1:
        scratch += [pltpu.VMEM((length, 128), F32), DMA, DMA]
    scratch += [DMA((n,))] * 2 + LineScatter.sems(n) + Scatter.sems(cube) + [DMA((count,))] * 2
    if spread:
        low, branch, wfg, wpg = grads
        rows = width // count
        whole = all_plan(n_dp, n, rows)
        ins += [low, branch, wfg, wpg]
        outs += [shape((n, rows, 256), BF16), shape(wfg.shape, BF16), shape(wpg.shape, BF16), shape((rows, width), F32)]
        scratch += [
            pltpu.VMEM((n_dp, n, rows, 256), BF16), pltpu.VMEM((n, rows, 256), BF16), pltpu.VMEM((n_dp, n, rows, 256), BF16),
            pltpu.VMEM((2,) * len(whole[0]) + (rows, width), BF16),
        ]
        scratch += [DMA((n,))] * 2 + [DMA((n_dp,))] * 2 + [DMA((count,))] * 2 + [DMA((n_dp,))] * 2
        scratch += Scatter.scratch(whole, rows, width) + Scatter.sems(whole)
    else:
        outs += [shape((width, 256), F32)]
    vm, hbm = pl.BlockSpec(memory_space=pltpu.VMEM), pl.BlockSpec(memory_space=pl.ANY)
    return pl.pallas_call(
        functools.partial(back_kernel, n_dp, n, r, spread, cube, whole),
        out_shape=outs,
        in_specs=[hbm if v is first or v is part_out else vm for v in ins],
        out_specs=[vm] * len(outs),
        scratch_shapes=scratch,
        compiler_params=pltpu.CompilerParams(collective_id=3, has_side_effects=True, vmem_limit_bytes=VMEM_LIMIT),
        name="back",
    )(*ins)


def own_sums(n_dp, n, piece, sums):
    flat = lax.axis_index("dp") * n + lax.axis_index("ctx")
    wide = pltpu.roll(sums, (128 - flat * piece % 128) % 128, 1)
    return wide, pltpu.roll(sums, (128 - flat * 2 * piece % 128) % 128, 1)[6:7]


def finish_kernel(n_dp, n, out_in, ig_in, sums, wq_got, wf_got, wp_got, wo_in, *outs):
    out, ig, g1, c1, wq_own, bqv, wo_own, bo, g2, c2, wf_own, bf, wp_own, bp = outs
    count = n_dp * n
    rows, width = wo_in.shape
    units = wp_got.shape[1]
    out[0] = out_in[...]
    ig[0] = ig_in[...]
    wo_own[...] = wo_in[...]
    wp_own[...] = jnp.sum(wp_got[...].astype(F32), axis=0)
    for f in range(count):
        m, g = group_of(n, f)
        total = 0.0
        for i in range(n_dp):
            source = (i // 2 * 2 + m // (n // 2)) * n + i % 2 * (n // 2) + m % (n // 2)
            total = total + wf_got[source, :, g * units : (g + 1) * units].astype(F32)
        wf_own[:, f * units : (f + 1) * units] = total
    lower = lax.broadcasted_iota(jnp.int32, (rows, 128), 1) < 64
    turn = lambda t: pltpu.roll(t, 64, 1)
    for h in range(0, HEADS, 2):
        (q0, e0), (q1, e1) = ((wq_got[i, :, :128].astype(F32), wq_got[i, :, 128:].astype(F32)) for i in (h, h + 1))
        for p, v in enumerate((jnp.where(lower, q0, turn(q1)), jnp.where(lower, e0, turn(e1)), jnp.where(lower, turn(e0), e1))):
            wq_own[:, p * width + h * 64 : p * width + h * 64 + 128] = v
    wide, double = own_sums(n_dp, n, rows, sums[...])
    for i, ref in enumerate((g1, c1, bo, g2, c2, bp)):
        ref[...] = wide[i : i + 1, :rows]
    bqv[...] = double[:, : 2 * rows]
    group = group_of(n, lax.axis_index("dp") * n + lax.axis_index("ctx"))[1]
    bf[...] = sums[pl.ds(7 + group, 1), :]


def finish(n_dp, n, out, ig, sums, wq_got, wf_got, wp_got, wo):
    rows, width = wo.shape
    units = wp_got.shape[1]
    shape = jax.ShapeDtypeStruct
    row = shape((1, rows), F32)
    vm = pl.BlockSpec(memory_space=pltpu.VMEM)
    got = pl.pallas_call(
        functools.partial(finish_kernel, n_dp, n),
        out_shape=[
            shape((1,) + out.shape, BF16), shape((1,) + ig.shape, BF16), row, row, shape((rows, 3 * width), F32),
            shape((1, 2 * rows), F32), shape((rows, width), F32), row, row, row, shape((rows, n_dp * n * units), F32),
            shape((1, units), F32), shape((units, width), F32), row,
        ],
        in_specs=[vm] * 7,
        out_specs=[vm] * 14,
        compiler_params=pltpu.CompilerParams(vmem_limit_bytes=VMEM_LIMIT),
        name="finish",
    )(out, ig, sums, wq_got, wf_got, wp_got, wo)
    return tuple(v.reshape(-1) if v.shape[0] == 1 and v.ndim == 2 else v for v in got)


def local(n_dp, n, inputs, cotangent, block_ids, ln1_gain, ln1_bias, w_qkv, b_qkv, w_out, b_out, ln2_gain, ln2_bias, w_fc, b_fc, w_proj, b_proj):
    tokens, width = inputs.shape[1:]
    count = n_dp * n
    rows = w_qkv.shape[0]
    units = w_proj.shape[0]
    r = n // HEADS
    hd = width // HEADS
    d, me = lax.axis_index("dp"), lax.axis_index("ctx")
    flat = d * n + me
    head = me // r
    both = ("dp", "ctx")
    x, dy = inputs[0], cotangent[0]
    halves = (n_dp // 2, 2, 2, n // 2)

    small = (ln1_gain, ln1_bias, b_qkv, block_ids[0], b_out, ln2_gain, ln2_bias, b_fc, b_proj)
    small = [v.reshape(1, -1) for v in small]

    def heads_of(w):
        w = w.reshape(w.shape[0], 3, HEADS, 1, hd)
        w = jnp.stack([w[:, 0], jnp.zeros_like(w[:, 0]), w[:, 1], w[:, 2]], axis=3)
        return w.reshape(w.shape[0], HEADS, 4 * hd)

    spread = rows % 16 == 0 and units == 128 and r == 1
    if spread:
        return finish(n_dp, n, *layer(n_dp, n, x, small, dy, w_qkv, w_fc, w_proj, w_out))
    full = lax.all_gather(w_qkv, both, axis=0, tiled=True)
    wq = lax.dynamic_index_in_dim(heads_of(full), head, 1, keepdims=False)
    wf = lax.all_gather(w_fc, both, axis=0, tiled=True).reshape((width,) + halves + (units,))
    wf = lax.dynamic_index_in_dim(wf, d % 2, 2, keepdims=False)
    wf = lax.dynamic_index_in_dim(wf, me % (n // 2), 3, keepdims=False).reshape(width, n_dp * units)
    wp = lax.all_gather(w_proj, both, axis=0, tiled=True).reshape(halves + (units, width))
    wp = lax.dynamic_index_in_dim(wp, d % 2, 1, keepdims=False)
    wp = lax.dynamic_index_in_dim(wp, me % (n // 2), 2, keepdims=False).reshape(n_dp * units, width)
    wo = lax.all_gather(w_out, both, axis=0, tiled=True)
    small_all, first, a, b, o, att, dy_all = front(n_dp, n, r, x, small, dy, wq)

    def vector(row, size):
        return small_all[:, row, :size].astype(F32).reshape(1, -1)

    params = jnp.concatenate([vector(k, rows) for k in (BO, G2, C2, G1, BP)])
    bf = vector(BF, units).reshape(halves + (units,))
    bf = lax.dynamic_index_in_dim(bf, d % 2, 1, keepdims=False)
    bf = lax.dynamic_index_in_dim(bf, me % (n // 2), 2, keepdims=False).reshape(1, -1)
    got = ffn(n, r, att, x, dy, dy_all, wo, wf, wp, bf, params[:3])
    middle, middle_grad, low, branch, agb, sums4, part_out, wp_grad, wf_grad, bf_grad = got
    got = back(n_dp, n, r, agb, a, b, o, small_all, wq, first, part_out, x, middle, middle_grad, params[3:], sums4, bf_grad, None)
    output, input_grad, sums = got[:3]
    owned = lambda v: lax.psum_scatter(v, both, scatter_dimension=0, tiled=True)
    hot = (jnp.arange(2) == d % 2).reshape(1, 2, 1, 1, 1) & (jnp.arange(n // 2) == me % (n // 2)).reshape(1, 1, 1, -1, 1)
    g = got[3].reshape(width, 4, 1, hd)
    g = jnp.stack([g[:, 0], g[:, 2], g[:, 3]], axis=1)
    wq_own = owned(jnp.where((jnp.arange(HEADS) == head).reshape(1, 1, -1, 1), g, 0.0).reshape(width, 3 * width))
    g = wf_grad.astype(F32).reshape(width, n_dp // 2, 1, 2, 1, units)
    wf_own = owned(jnp.where(hot[None], g, 0.0).reshape(width, -1))
    g = wp_grad.astype(F32).reshape(n_dp // 2, 1, 2, 1, units, width)
    wp_own = owned(jnp.where(hot[..., None], g, 0.0).reshape(-1, width))
    wo_own = owned(dot(low, branch, TN))

    cut = lambda k, size: lax.dynamic_slice(sums[k], (flat * size % 128,), (size,))
    g1g, c1g, bog, g2g, c2g, bpg = (cut(k, rows) for k in range(6))
    bqvg = cut(6, 2 * rows)
    group = d // 2 * 2 + me // (n // 2)
    bfg = lax.dynamic_slice(sums[7 : 7 + n_dp * units // 128].reshape(-1), (group * units,), (units,))
    return (
    output[None], input_grad[None], g1g, c1g, wq_own, bqvg, wo_own, bog, g2g, c2g, wf_own, bfg, wp_own, bpg,
    )


def solution(mesh):
    both = ("dp", "ctx")
    act, vec, mat = P("dp", "ctx", None), P(both), P(both, None)
    return jax.shard_map(
    functools.partial(local, mesh.shape["dp"], mesh.shape["ctx"]),
    mesh=mesh,
    in_specs=(act, act, P("dp", "ctx"), vec, vec, mat, vec, mat, vec, vec, vec, mat, vec, mat, vec),
    out_specs=(act, act, vec, vec, mat, vec, mat, vec, vec, vec, mat, vec, mat, vec),
    check_vma=False,
    )
```

```python
import functools
import math

import jax
import jax.numpy as jnp
from jax import lax
from jax.experimental import pallas as pl
from jax.experimental.pallas import tpu as pltpu
from jax.sharding import PartitionSpec as P

HEADS = 16
EPSILON = 1e-05
QB = 256
F32, BF16 = jnp.float32, jnp.bfloat16
NT = (((1,), (1,)), ((), ()))
TN = (((0,), (0,)), ((), ()))
MESH = pl.DeviceIdType.MESH
DMA = pltpu.SemaphoreType.DMA
VMEM_LIMIT = 60 << 20
VMEM_MOST = 63 << 20


def dot(x, y, dims=(((1,), (0,)), ((), ()))):
    return lax.dot_general(x, y, dims, preferred_element_type=F32)


def remote(src, dst, send, recv, peer):
    return pltpu.make_async_remote_copy(
        src_ref=src, dst_ref=dst, send_sem=send, recv_sem=recv, device_id=peer, device_id_type=MESH
    )


class Greet:
    def __init__(self, n_dp, n, peers=None):
        self.barrier = pltpu.get_barrier_semaphore()
        self.count = n_dp * n - 1 if peers is None else len(peers)
        for peer in peers or ():
            pl.semaphore_signal(self.barrier, inc=1, device_id=peer, device_id_type=MESH)
        if peers is None:
            flat = lax.axis_index("dp") * n + lax.axis_index("ctx")

            def signal(j, _):
                f = lax.rem(flat + j, n_dp * n)
                pl.semaphore_signal(self.barrier, inc=1, device_id={"dp": f // n, "ctx": f % n}, device_id_type=MESH)
                return 0

            lax.fori_loop(1, n_dp * n, signal, 0)

    def wait(self):
        pl.semaphore_wait(self.barrier, self.count)


class ToAll:
    def __init__(self, n_dp, n, block, into, sems, only_ctx=False):
        self.n, self.block, self.into, self.only = n, block, into, only_ctx
        self.send, self.recv = sems
        self.count = n if only_ctx else n_dp * n
        self.me = lax.axis_index("ctx") if only_ctx else lax.axis_index("dp") * n + lax.axis_index("ctx")

    def copy(self, j):
        f = lax.rem(self.me + j, self.count)
        peer = {"ctx": f} if self.only else {"dp": f // self.n, "ctx": f % self.n}
        return remote(self.block(f), self.into.at[self.me], self.send.at[j], self.recv.at[j], peer)

    def each(self, act):
        def step(j, _):
            act(self.copy(j))
            return 0

        lax.fori_loop(1, self.count, step, 0)

    def start(self):
        self.each(lambda c: c.start())

    def wait_recv(self):
        self.each(lambda c: c.wait_recv())

    def wait_send(self):
        self.each(lambda c: c.wait_send())


def own_bit(dim):
    axis, b = dim
    return lax.axis_index(axis) // (1 << b) % 2


def partner(dim):
    axis, b = dim
    return {axis: lax.axis_index(axis) + (1 - 2 * own_bit(dim)) * (1 << b)}


def cube_plan(n, rows):
    top = n.bit_length() - 2
    dims = [("dp", 0)] + [("ctx", b) for b in range(top - 1, 0, -1)] + [("ctx", 0)]
    links = len(dims) - 1
    size = -(-rows // (16 * links)) * 16
    cuts = [min(rows, size * i) for i in range(links)] + [rows]
    return dims, [(cuts[i], cuts[i + 1], [(i + j) % links for j in range(links)]) for i in range(links)], True


def all_plan(n_dp, n, rows):
    dims = [("dp", b) for b in range(n_dp.bit_length() - 2, -1, -1)] + [("ctx", b) for b in range(n.bit_length() - 2, -1, -1)]
    links, own = len(dims) - 1, n_dp.bit_length() - 1
    return dims, [(0, rows, list(range(own, links)) + list(range(own)))], False


class Pairwise:
    def __init__(self, plan, sems):
        self.dims, self.orders, self.core_first = plan
        self.links = len(self.dims) - 1
        self.link_send, self.link_recv, self.core_send, self.core_recv = sems
        self.mine = [own_bit(d) for d in self.dims]

    def index(self, links, core, tail=()):
        links = tuple(links)
        return ((core,) + links if self.core_first else links + (core,)) + tuple(tail)

    def peers(self):
        return [partner(d) for d in self.dims]


class Gather(Pairwise):
    def __init__(self, plan, buf, sems):
        super().__init__(plan, sems)
        self.buf = buf

    @staticmethod
    def sems(plan):
        links, parts = len(plan[0]) - 1, len(plan[1])
        return [DMA((parts, links))] * 2 + [DMA((parts * links + 1,))] * 2

    def own(self):
        return self.index(self.mine[:-1], self.mine[-1])

    def region(self, part, done, flip=None):
        lo, hi, _ = self.orders[part]
        where = [slice(None) if i in done else (1 - m if i == flip else m) for i, m in enumerate(self.mine[:-1])]
        return self.index(where, self.mine[-1], (pl.ds(lo, hi - lo),))

    def copy(self, where, send, recv, dim):
        return remote(self.buf.at[where], self.buf.at[where], send, recv, partner(self.dims[dim]))

    def link(self, part, k):
        order = self.orders[part][2]
        return self.copy(self.region(part, order[:k]), self.link_send.at[part, k], self.link_recv.at[part, k], order[k])

    def core(self, part, k):
        order = self.orders[part][2]
        at = part * self.links + k + 1
        return self.copy(self.region(part, order[:k], order[k]), self.core_send.at[at], self.core_recv.at[at], self.links)

    def core_own(self):
        return self.copy(self.own(), self.core_send.at[0], self.core_recv.at[0], self.links)

    def start(self):
        for part in range(len(self.orders)):
            self.link(part, 0).start()
        self.core_own().start()

    def step(self, k):
        for part in range(len(self.orders)):
            self.link(part, k).wait_recv()
            if k + 1 < self.links:
                self.link(part, k + 1).start()
            self.core(part, k).start()

    def core_wait(self):
        self.core_own().wait_recv()
        for part in range(len(self.orders)):
            for k in range(self.links):
                self.core(part, k).wait_recv()

    def finish(self):
        self.core_own().wait_send()
        for part in range(len(self.orders)):
            for k in range(self.links):
                self.link(part, k).wait_send()
                self.core(part, k).wait_send()


class Scatter(Pairwise):
    def __init__(self, plan, terms, bufs, sems, own=None):
        super().__init__(plan, sems)
        self.terms, self.run, self.bufs, self.own = terms, bufs[0], bufs[1:], own

    def fetch_own(self, sem):
        source = self.terms.at[self.index((slice(None),) * self.links, self.mine[-1])]
        return pltpu.make_async_copy(source, self.own, sem)

    @staticmethod
    def sems(plan):
        links, parts = len(plan[0]) - 1, len(plan[1])
        return [DMA((parts, links))] * 2 + [DMA((2,))] * 2

    @staticmethod
    def scratch(plan, rows, cols):
        links = len(plan[0]) - 1
        return [pltpu.VMEM((2,) * links + (rows, cols), BF16)] + [
            pltpu.VMEM((2,) * (links - 1 - k) + (rows, cols), BF16) for k in range(links)
        ]

    def core(self, half):
        where = (half,) + (slice(None),) * (self.links - 1)
        return remote(
            self.terms.at[self.index(where, 1 - self.mine[-1])], self.run.at[where],
            self.core_send.at[half], self.core_recv.at[half], partner(self.dims[-1]),
        )

    def where(self, part, k, flip):
        lo, hi, order = self.orders[part]
        order = order[::-1]
        d, gone = order[k], order[:k]
        at = []
        for i in range(self.links):
            if i == d:
                at.append(1 - self.mine[i] if flip else self.mine[i])
            else:
                at.append(self.mine[i] if i in gone else slice(None))
        return at, d, (pl.ds(lo, hi - lo),)

    def link(self, part, k):
        at, d, tail = self.where(part, k, True)
        return remote(
            self.run.at[tuple(at) + tail], self.bufs[k].at[(slice(None),) * (self.links - 1 - k) + tail],
            self.link_send.at[part, k], self.link_recv.at[part, k], partner(self.dims[d]),
        )

    def add_core(self, half):
        self.core(half).wait_recv()
        inner = self.links - 1
        for i in range(1 << inner):
            at = (half,) + tuple((i >> (inner - 1 - j)) & 1 for j in range(inner))
            own = self.terms[self.index(at, self.mine[-1])] if self.own is None else self.own[at]
            self.run[at] = (self.run[at].astype(F32) + own.astype(F32)).astype(BF16)

    def start_links(self):
        for part in range(len(self.orders)):
            self.link(part, 0).start()

    def step(self, k, out=None):
        for part in range(len(self.orders)):
            at, _, tail = self.where(part, k, False)
            self.link(part, k).wait_recv()
            free = self.links - 1 - k
            for i in range(1 << free):
                idx = [(i >> (free - 1 - j)) & 1 for j in range(free)]
                rest = iter(idx)
                to = tuple(next(rest) if isinstance(v, slice) else v for v in at) + tail
                total = self.run[to].astype(F32) + self.bufs[k][tuple(idx) + tail].astype(F32)
                if k + 1 < self.links:
                    self.run[to] = total.astype(BF16)
                else:
                    out[tail[0], :] = total
            if k + 1 < self.links:
                self.link(part, k + 1).start()

    def core_sent(self):
        for half in range(2):
            self.core(half).wait_send()

    def links_sent(self):
        for part in range(len(self.orders)):
            for k in range(self.links):
                self.link(part, k).wait_send()

    def finish(self):
        self.core_sent()
        self.links_sent()


class Line:
    def __init__(self, n):
        self.n, self.ys = n, n // 8
        me = lax.axis_index("ctx")
        self.z, self.y, self.c = me // (2 * self.ys), me // 2 % self.ys, me % 2
        high = self.z // 2
        self.slots = [3 - 3 * high, 2 - high, self.z + 1 - 2 * (self.z % 2), self.z]
        self.inner = (self.z == 1) | (self.z == 2)
        self.outer = (self.z == 0) | (self.z == 3)
        self.side = (self.z + 1) // 2 % 2
        self.near = self.at(self.slots[2], self.y, self.c)
        self.far = self.at(self.z + 1 - 2 * high, self.y, self.c)
        self.core = self.at(self.z, self.y, 1 - self.c)

    def at(self, z, y, c):
        return {"ctx": (z * self.ys + y) * 2 + c}

    def others(self):
        return [(self.y + d) % self.ys for d in range(1, self.ys)]


class LineGather:
    def __init__(self, line, buf, sems):
        self.l, self.buf = line, buf
        self.zs, self.zr, self.ys, self.yr, self.ks, self.kr = sems

    @staticmethod
    def sems(n):
        ys = n // 8
        return [DMA((5,)), DMA((3,)), DMA((ys - 1, 4)), DMA((ys - 1, 4)), DMA((ys, 4)), DMA((ys, 4))]

    def move(self, z, y, c, send, recv, peer):
        ref = self.buf.at[z, y, c]
        return remote(ref, ref, send, recv, peer)

    def zcopy(self, i):
        l = self.l
        slot, peer, into = [(3, l.near, 0), (3, l.far, 1), (2, l.far, 2), (1, l.near, 1), (0, l.near, 2)][i]
        return self.move(l.slots[slot], l.y, l.c, self.zs.at[i], self.zr.at[into], peer)

    def ycopy(self, d, slot):
        l = self.l
        return self.move(l.slots[slot], l.y, l.c, self.ys.at[d, slot], self.yr.at[d, slot], l.at(l.z, l.others()[d], l.c))

    def kcopy(self, d, slot):
        l = self.l
        y = l.y if d == 0 else (l.y + l.ys - d) % l.ys
        return self.move(l.slots[slot], y, l.c, self.ks.at[d, slot], self.kr.at[d, slot], l.core)

    def spread(self, slot):
        for d in range(self.l.ys - 1):
            self.ycopy(d, slot).start()
        self.kcopy(0, slot).start()

    def start(self):
        self.zcopy(0).start()

        @pl.when(self.l.inner)
        def _():
            self.zcopy(1).start()

        self.spread(3)

    def z_step(self, r):
        self.zcopy((0, 3, 4)[r]).wait_recv()

        @pl.when(self.l.inner)
        def _():
            self.zcopy(2 + r).start()

        self.spread(2 - r)

    def y_step(self, slot):
        for d in range(self.l.ys - 1):
            self.ycopy(d, slot).wait_recv()
            self.kcopy(d + 1, slot).start()

    def run(self):
        self.start()
        for r in range(3):
            self.z_step(r)
            self.y_step(3 - r)
        self.y_step(0)

    def core_wait(self, slot):
        for d in range(self.l.ys):
            self.kcopy(d, slot).wait_recv()

    def finish(self):
        self.zcopy(0).wait_send()

        @pl.when(self.l.inner)
        def _():
            for i in range(1, 5):
                self.zcopy(i).wait_send()

        for slot in range(4):
            for d in range(self.l.ys - 1):
                self.ycopy(d, slot).wait_send()
            for d in range(self.l.ys):
                self.kcopy(d, slot).wait_send()


class LineScatter:
    def __init__(self, line, acc, kbuf, ybuf, zbuf, sems):
        self.l, self.acc, self.kbuf, self.ybuf, self.zbuf = line, acc, kbuf, ybuf, zbuf
        self.zs, self.zr, self.ys, self.yr, self.ks, self.kr = sems

    @staticmethod
    def sems(n):
        ys = n // 8
        return [DMA((3,)), DMA((2, 3)), DMA((ys - 1, 4)), DMA((ys - 1, 4)), DMA((ys, 4)), DMA((ys, 4))]

    @staticmethod
    def scratch(n, rows, cols):
        ys = n // 8
        return [pltpu.VMEM((4, ys, rows, cols), BF16), pltpu.VMEM((ys - 1, 4, rows, cols), BF16), pltpu.VMEM((2, 3, rows, cols), BF16)]

    def y_of(self, d):
        return self.l.y if d == 0 else self.l.others()[d - 1]

    def kcopy(self, d, slot):
        l = self.l
        z, y = l.slots[slot], self.y_of(d)
        return remote(self.acc.at[z, y, 1 - l.c], self.kbuf.at[z, y], self.ks.at[d, slot], self.kr.at[d, slot], l.core)

    def ycopy(self, d, slot):
        l = self.l
        z, y = l.slots[slot], self.y_of(d + 1)
        return remote(self.acc.at[z, y, l.c], self.ybuf.at[d, slot], self.ys.at[d, slot], self.yr.at[d, slot], l.at(l.z, y, l.c))

    def zcopy(self, slot):
        l = self.l
        return remote(self.acc.at[l.slots[slot], l.y, l.c], self.zbuf.at[l.side, slot], self.zs.at[slot], self.zr.at[l.side, slot], l.far if slot < 2 else l.near)

    def zwait(self, side, slot):
        buf = self.zbuf.at[side, slot]
        remote(buf, buf, self.zs.at[slot], self.zr.at[side, slot], self.l.near).wait_recv()
        return self.zbuf[side, slot].astype(F32)

    def own(self, slot):
        return (self.l.slots[slot], self.l.y, self.l.c)

    def core_start(self, slot):
        for d in range(self.l.ys - 1, -1, -1):
            self.kcopy(d, slot).start()

    def core_step(self, slot):
        l = self.l
        for d in list(range(1, l.ys)) + [0]:
            z, y = l.slots[slot], self.y_of(d)
            self.kcopy(d, slot).wait_recv()
            self.acc[z, y, l.c] = (self.acc[z, y, l.c].astype(F32) + self.kbuf[z, y].astype(F32)).astype(BF16)
            if d > 0:
                self.ycopy(d - 1, slot).start()

    def y_sum(self, slot):
        total = self.acc[self.own(slot)].astype(F32)
        for d in range(self.l.ys - 1):
            self.ycopy(d, slot).wait_recv()
            total = total + self.ybuf[d, slot].astype(F32)
        return total

    def z_step(self, slot):
        l, own = self.l, self.own(slot)
        total = self.y_sum(slot)
        self.acc[own] = total.astype(BF16)
        @pl.when(l.inner)
        def _():
            self.acc[own] = (self.acc[own].astype(F32) + self.zwait(*((0, slot) if slot < 2 else (1, 0)))).astype(BF16)

        self.zcopy(slot).start()

    def last(self, out):
        l = self.l
        out[...] = self.y_sum(3)

        @pl.when(l.inner)
        def _():
            out[...] += self.zwait(0, 2) + self.zwait(1, 1)

        @pl.when(l.outer)
        def _():
            out[...] += self.zwait(1, 2)

    def finish(self):
        for slot in range(4):
            for d in range(self.l.ys):
                self.kcopy(d, slot).wait_send()
            for d in range(self.l.ys - 1):
                self.ycopy(d, slot).wait_send()
        for slot in range(3):
            self.zcopy(slot).wait_send()


G1, C1, BQV, IDS, BO, G2, C2, BF, BP = range(9)


def put_ids(n, small_all, first, row, col):
    tokens = small_all.shape[2]
    for j in range(n):
        ids = small_all[first + j].astype(F32)[IDS : IDS + 1, :]
        row[:, j * tokens : (j + 1) * tokens] = ids
        col[j * tokens : (j + 1) * tokens, :] = jnp.transpose(jnp.broadcast_to(ids, (tokens, tokens)))[:, :1]


def half_row(tile_row, odd, high):
    lane = lax.broadcasted_iota(jnp.int32, tile_row.shape, 1)
    turned = pltpu.roll(tile_row, 64, 1)
    moved = jnp.where((odd == 1) == high, tile_row, turned)
    return jnp.where((lane >= 64) == high, moved, 0.0)


def normalize(rows):
    centred = rows - jnp.mean(rows, axis=-1, keepdims=True)
    rstd = lax.rsqrt(jnp.mean(centred * centred, axis=-1, keepdims=True) + EPSILON)
    return centred * rstd, rstd


def group_of(n, f):
    d, j = f // n, f % n
    return d % 2 * (n // 2) + j % (n // 2), d // 2 * 2 + j // (n // 2)


def group_peer(n, i, count):
    d, j = lax.axis_index("dp"), lax.axis_index("ctx")
    g = lax.rem(d // 2 * 2 + j // (n // 2) + i, count)
    return g, {"dp": g // 2 * 2 + d % 2, "ctx": g % 2 * (n // 2) + j % (n // 2)}


def put_small(pieces, tile, small_ref):
    tile[...] = jnp.zeros_like(tile)
    for k, piece in enumerate(pieces):
        tile[k : k + 1, : piece.shape[1]] = piece[...].astype(F32)
    small_ref[...] = tile[...].astype(BF16)


def put_params(count, width, small_all, prm, bqv):
    for size, ref in ((width // count, prm), (2 * width // count, bqv)):
        per = 128 // size
        for k in range(count // per):
            tile = small_all[k * per].astype(F32)
            for i in range(1, per):
                tile = tile + pltpu.roll(small_all[k * per + i].astype(F32), i * size, 1)
            if ref is prm:
                prm[:, k * 128 : (k + 1) * 128] = tile
            else:
                bqv[k : k + 1, :] = tile[BQV : BQV + 1]


def front_kernel(n_dp, n, r, cube, *refs):
    refs = list(refs)
    take = lambda k: [refs.pop(0) for _ in range(k)]
    x_ref, pieces, dy_ref = refs.pop(0), take(9), refs.pop(0)
    (wq_all,) = take(1)
    small_all, first_out, a_ref, b_ref, o_ref, att, dy_all = take(7)
    xbuf, first, prm, bqv, bias, idrow, idcol, packed, acc, tot, own_sems, first_sems, tile, small_ref = take(14)
    line_sems, small_sems, dy_sems, att_sems = take(6), take(2), take(4), take(2)
    tokens, width = x_ref.shape
    count = n_dp * n
    d, me = lax.axis_index("dp"), lax.axis_index("ctx")
    flat = d * n + me
    head, part = me // r, me % r
    line = Line(n)
    hello = Greet(n_dp, n)

    xg = LineGather(line, xbuf, line_sems)
    small = ToAll(n_dp, n, lambda f: small_ref, small_all, small_sems)
    dyg = Gather(cube, dy_all, dy_sems)
    own_copies = [pltpu.make_async_copy(dy_ref, dy_all.at[dyg.own()], own_sems.at[0])]
    for c in own_copies:
        c.start()
    xbuf[line.z, line.y, line.c] = x_ref[...]
    put_small(pieces, tile, small_ref)
    small_all[flat] = small_ref[...]
    hello.wait()
    xg.start()
    small.start()
    for c in own_copies:
        c.wait()
    xg.z_step(0)
    xg.y_step(3)
    small.wait_recv()
    put_params(count, width, small_all, prm, bqv)
    odd = head % 2
    bias[:, :128] = half_row(bqv[pl.ds(head // 2, 1), :], odd, False)
    bias[:, 128:] = half_row(bqv[pl.ds(width // 128 + head // 2, 1), :], odd, True)
    put_ids(n, small_all, d * n, idrow, idcol)
    per_z = n // 4

    def plane(slot):
        return pl.ds(pl.multiple_of(line.slots[slot] * per_z * tokens, per_z * tokens), per_z * tokens)

    def save(slot):
        return pltpu.make_async_copy(first.at[plane(slot)], first_out.at[plane(slot)], first_sems.at[slot])

    def project(slot):
        z = line.slots[slot]

        def one(i, _):
            normed, _ = normalize(xbuf[z, i // 2, i % 2].astype(F32))
            low = (normed * prm[G1 : G1 + 1, :] + prm[C1 : C1 + 1, :]).astype(BF16)
            first[pl.ds(pl.multiple_of((z * per_z + i) * tokens, tokens), tokens), :] = low
            return 0

        lax.fori_loop(0, per_z, one, 0)
        at = plane(slot)
        weights = wq_all[...]
        qkv = (dot(first[at, :], weights) + bias[...]).astype(BF16)
        a_ref[at, :] = qkv[:, :128]
        b_ref[at, :] = qkv[:, 128:]
        save(slot).start()

    xg.z_step(1)
    xg.y_step(2)
    xg.core_wait(3)
    project(3)
    xg.z_step(2)
    xg.y_step(1)
    xg.core_wait(2)
    project(2)
    xg.y_step(0)
    dyg.start()
    xg.core_wait(1)
    project(1)
    xg.core_wait(0)
    project(0)
    dyg.step(0)

    length = b_ref.shape[0]
    kc = min(1024, length)
    half = tokens // 2
    if r > 1:
        packed[...] = jnp.zeros_like(packed)

    def per_queries(lb, _):
        gq = lb * r + part
        qs = pl.ds(pl.multiple_of(gq * QB, QB), QB)
        a = a_ref[qs, :] * 0.125
        ids = idcol[qs, :]
        acc[...] = jnp.zeros_like(acc)
        tot[...] = jnp.zeros_like(tot)

        def per_keys(kb, _):
            ks = pl.ds(pl.multiple_of(kb * kc, kc), kc)
            b = b_ref[ks, :]
            s = dot(a, b, NT)
            w = jnp.where(idrow[:, ks] <= ids, jnp.exp(s), 0.0)
            t = w[:, :128]
            for i in range(1, kc // 128):
                t = t + w[:, i * 128 : (i + 1) * 128]
            tot[...] += t
            acc[...] += dot(w.astype(BF16), b)
            return 0

        lax.fori_loop(0, jnp.minimum(((gq + 2) * QB + kc - 1) // kc, length // kc), per_keys, 0)
        t = jnp.sum(tot[...], axis=-1, keepdims=True)
        o = acc[...] / t
        lane = lax.broadcasted_iota(jnp.int32, (QB, 128), 1)
        o_ref[pl.ds(pl.multiple_of(lb * QB, QB), QB), :] = jnp.where(lane < 64, t, o)
        lane = lax.broadcasted_iota(jnp.int32, (half, 128), 1)
        for i in range(QB // tokens):
            lo, hi = o[i * tokens : i * tokens + half], o[i * tokens + half : (i + 1) * tokens]
            packed[gq * (QB // tokens) + i] = jnp.where(lane < 64, pltpu.roll(lo, 64, 1), hi).astype(BF16)
        return 0

    blocks = length // QB // r
    cuts = [0, blocks // 2, blocks * 3 // 4, blocks]
    for k in range(3):
        lax.fori_loop(cuts[k], cuts[k + 1], per_queries, 0)
        if k + 1 < dyg.links:
            dyg.step(k + 1)
    out = ToAll(n_dp, n, lambda f: packed.at[f], att, att_sems, True)
    att[me] = packed[me]
    out.start()
    for k in range(3, dyg.links):
        dyg.step(k)
    out.wait_recv()
    dyg.core_wait()
    for slot in range(4):
        save(slot).wait()
    small.wait_send()
    out.wait_send()
    xg.finish()
    dyg.finish()


def front(n_dp, n, r, x, small, dy, weights):
    tokens, width = x.shape
    count, length = n_dp * n, n * tokens
    cube = cube_plan(n, tokens)
    shape = jax.ShapeDtypeStruct
    vm, hbm = pl.BlockSpec(memory_space=pltpu.VMEM), pl.BlockSpec(memory_space=pl.ANY)
    outs = [
        (shape((count, 16, 128), BF16), vm), (shape((length, width), BF16), hbm), (shape((length, 128), BF16), vm),
        (shape((length, 128), BF16), vm), (shape((length // r, 128), F32), vm), (shape((n, tokens // 2, 128), BF16), vm),
        (shape((2,) * len(cube[0]) + (tokens, width), BF16), hbm),
    ]
    sems = LineGather.sems(n) + [DMA((count,))] * 2 + Gather.sems(cube) + [DMA((n,))] * 2
    ins = [x, *small, dy]
    ins += [weights]
    return pl.pallas_call(
        functools.partial(front_kernel, n_dp, n, r, cube),
        out_shape=[o for o, _ in outs],
        in_specs=[vm] * len(ins),
        out_specs=[s for _, s in outs],
        scratch_shapes=[
            pltpu.VMEM((4, n // 8, 2, tokens, width), BF16), pltpu.VMEM((length, width), BF16), pltpu.VMEM((16, width), F32),
            pltpu.VMEM((2 * width // 128, 128), F32), pltpu.VMEM((1, 256), F32), pltpu.VMEM((1, length), F32),
            pltpu.VMEM((length, 1), F32), pltpu.VMEM((n, tokens // 2, 128), BF16), pltpu.VMEM((QB, 128), F32),
            pltpu.VMEM((QB, 128), F32), DMA((3,)), DMA((4,)),
            pltpu.VMEM((16, 128), F32), pltpu.VMEM((16, 128), BF16),
        ] + sems,
        compiler_params=pltpu.CompilerParams(collective_id=1, has_side_effects=True, vmem_limit_bytes=VMEM_LIMIT),
        name="front",
    )(*ins)


def gelu_both(u):
    c = math.sqrt(2.0 / math.pi)
    t = jnp.tanh(c * (u + 0.044715 * (u * u * u)))
    half = 0.5 * (1.0 + t)
    return u * half, half + 0.5 * u * (1.0 - t * t) * (c * (1.0 + 3.0 * 0.044715 * (u * u)))


def normalize_back(grad, normed, rstd):
    return rstd * (
        grad
        - jnp.mean(grad, axis=-1, keepdims=True)
        - normed * jnp.mean(grad * normed, axis=-1, keepdims=True)
    )


def ffn_kernel(n, r, plan, *refs):
    refs = list(refs)
    take = lambda k: [refs.pop(0) for _ in range(k)]
    att, x_ref, dy_own, dy_hbm, wo_ref, wf_ref, wp_in, bf_ref, par_ref = take(9)
    middle_ref, mg_ref, low_ref, branch_ref, agb, sums_ref, out_hbm, wp_grad, wf_grad, bf_grad = take(10)
    links = len(plan[0]) - 1
    sbuf, dy_ref, grads, act, hid, acc, out_ref, sg, copy_sems, out_sems = take(10)
    bufs, gather_sems, scatter_sems = take(links + 1), take(4), take(4)
    g = Gather(plan, sbuf, gather_sems)
    s = Scatter(plan, acc, bufs, scatter_sems)
    peers = g.peers()
    hello = Greet(1, n, peers)
    wp_ref = wp_in
    dy_copy = pltpu.make_async_copy(dy_hbm, dy_ref, copy_sems)
    dy_copy.start()
    tokens, width = x_ref.shape
    half = tokens // 2
    quarter = (1 << (links - 1)) * tokens
    inner = (slice(None),) * (links - 1)
    core = g.mine[-1]

    lane = lax.broadcasted_iota(jnp.int32, (half, 128), 1)

    def block(h):
        total = att[h * r].astype(F32)
        for i in range(1, r):
            total = total + att[h * r + i].astype(F32)
        return total

    for h in range(0, HEADS, 2):
        b0, b1 = block(h), block(h + 1)
        at = slice(h * 64, h * 64 + 128)
        low_ref[:half, at] = jnp.where(lane < 64, b0, pltpu.roll(b1, 64, 1)).astype(BF16)
        low_ref[half:, at] = jnp.where(lane < 64, pltpu.roll(b0, 64, 1), b1).astype(BF16)
    middle = x_ref[...].astype(F32) + dot(low_ref[...], wo_ref[...]) + par_ref[0:1, :]
    middle_ref[...] = middle
    n2, _ = normalize(middle)
    sbuf[g.own()] = (n2 * par_ref[1:2, :] + par_ref[2:3, :]).astype(BF16)
    hello.wait()
    g.start()
    dy_copy.wait()
    def rows(c, a):
        return pl.ds(pl.multiple_of((2 * c + a) * quarter, quarter), quarter)

    def grad_part(i):
        dy = dy_ref[(i // 2, i % 2) + inner].reshape(quarter, width)
        grads[rows(i // 2, i % 2), :] = dot(dy, wp_ref[...], NT)

    for k in range(links):
        g.step(k)
        if k == 1:
            for i in range(4):
                grad_part(i)
    g.core_wait()
    bf_grad[...] = jnp.zeros_like(bf_grad)

    def hidden_part(c, a):
        at = rows(c, a)
        low = sbuf[(c, a) + inner].reshape(quarter, width)
        active, slope = gelu_both(dot(low, wf_ref[...]) + bf_ref[...])
        act[at, :] = active.astype(BF16)
        h = (slope * grads[at, :]).astype(BF16)
        hid[at, :] = h
        bf_grad[...] += jnp.sum(h.astype(F32), axis=0, keepdims=True)
        acc[(c, a) + inner] = dot(h, wf_ref[...], NT).astype(BF16).reshape((2,) * (links - 1) + (tokens, width))

    for a in range(2):
        hidden_part(1 - core, a)
        s.core(a).start()
    for a in range(2):
        hidden_part(core, a)
        s.add_core(a)
    s.start_links()

    def weight_grads(k):
        at = slice(k * 256, (k + 1) * 256)
        low = sbuf[..., at].reshape(4 * quarter, 256)
        wf_grad[at, :] = jnp.transpose(dot(hid[...], low, TN)).astype(BF16)
        dy = dy_ref[..., at].reshape(4 * quarter, 256)
        wp_grad[:, at] = dot(act[...], dy, TN).astype(BF16)

    def out_part(i):
        at = (i // 2, i % 2) + inner
        if i >= out_ref.shape[0]:
            out_copy(i - out_ref.shape[0]).wait()
        terms = dot(act[rows(i // 2, i % 2), :], wp_ref[...]).astype(BF16)
        out_ref[i % out_ref.shape[0]] = terms.reshape((2,) * (links - 1) + (tokens, width))
        out_copy(i).start()

    def out_copy(i):
        slot = i % out_ref.shape[0]
        return pltpu.make_async_copy(out_ref.at[slot], out_hbm.at[(i // 2, i % 2) + inner], out_sems.at[slot])

    for i in range(4):
        out_part(i)
    for k in range(links):
        s.step(k, sg)
        if k < 2:
            weight_grads(2 * k)
            weight_grads(2 * k + 1)

    second_grad = sg[...]
    dy = dy_own[...].astype(F32)
    n2, rstd2 = normalize(middle_ref[...])
    mg = dy + normalize_back(second_grad * par_ref[1:2, :], n2, rstd2)
    mg_ref[...] = mg
    branch = mg.astype(BF16)
    branch_ref[...] = branch
    grad = dot(branch, wo_ref[...], NT)
    for h in range(0, HEADS, 2):
        lo, hi = grad[:half, h * 64 : h * 64 + 128], grad[half:, h * 64 : h * 64 + 128]
        b0 = jnp.where(lane < 64, lo, pltpu.roll(hi, 64, 1)).astype(BF16)
        b1 = jnp.where(lane < 64, pltpu.roll(lo, 64, 1), hi).astype(BF16)
        for i in range(r):
            agb[h * r + i] = b0
            agb[(h + 1) * r + i] = b1
    column = lambda v: jnp.sum(v, axis=0, keepdims=True)
    sums_ref[0:1, :] = column(branch.astype(F32))
    sums_ref[1:2, :] = column(second_grad * n2)
    sums_ref[2:3, :] = column(second_grad)
    sums_ref[3:4, :] = column(dy)
    for i in range(4 - out_ref.shape[0], 4):
        out_copy(i).wait()
    s.finish()
    g.finish()


def ffn(n, r, att, x, dy, dy_all, wo, wf, wp, bf, params):
    tokens, width = x.shape
    units = wf.shape[1]
    plan = cube_plan(n, tokens)
    block = (2,) * len(plan[0])
    length = n * tokens
    shape = jax.ShapeDtypeStruct
    vm, hbm = pl.BlockSpec(memory_space=pltpu.VMEM), pl.BlockSpec(memory_space=pl.ANY)
    return pl.pallas_call(
        functools.partial(ffn_kernel, n, r, plan),
        out_shape=[
            shape((tokens, width), F32), shape((tokens, width), F32), shape((tokens, width), BF16), shape((tokens, width), BF16),
            shape((n, tokens // 2, 128), BF16), shape((4, width), F32), shape(block + (tokens, width), BF16),
            shape((units, width), BF16), shape((width, units), BF16), shape((1, units), F32),
        ],
        in_specs=[vm, vm, vm, hbm, vm, vm, vm, vm, vm],
        out_specs=[vm, vm, vm, vm, vm, vm, hbm, vm, vm, vm],
        scratch_shapes=[
            pltpu.VMEM(block + (tokens, width), BF16), pltpu.VMEM(block + (tokens, width), BF16), pltpu.VMEM((length, units), F32),
            pltpu.VMEM((length, units), BF16), pltpu.VMEM((length, units), BF16), pltpu.VMEM(block + (tokens, width), BF16),
            pltpu.VMEM((2,) + block[2:] + (tokens, width), BF16), pltpu.VMEM((tokens, width), F32), DMA, DMA((2,)),
        ] + Scatter.scratch(plan, tokens, width) + Gather.sems(plan) + Scatter.sems(plan),
        compiler_params=pltpu.CompilerParams(collective_id=2, has_side_effects=True, vmem_limit_bytes=VMEM_LIMIT),
        name="ffn",
    )(att, x, dy, dy_all, wo, wf, wp, bf, params)


def project_rows(rows, prm):
    normed, _ = normalize(rows.astype(F32))
    return (normed * prm[G1 : G1 + 1, :] + prm[C1 : C1 + 1, :]).astype(BF16)


def layer_kernel(n_dp, n, cube, whole, *refs):
    refs = list(refs)
    take = lambda k: [refs.pop(0) for _ in range(k)]
    x_ref, pieces, (dy_own, w_qkv, w_fc, w_proj, w_out) = refs.pop(0), take(9), take(5)
    out_ref, ig_ref, sums, wq_got, wf_got, wp_got, wo_own = take(7)
    small_all, a_ref, b_ref, o_ref, wq_all, middle_ref, mg_ref, low_ref, branch_ref, agb, wp_grad, wf_grad, bf_grad = take(13)
    xbuf, first, prm, bqv, bias, bf_row, idrow, idcol, packed, acc, tot, att, wqb, wfb = take(14)
    wf_all, wo_all, wp_ref, dy_ref, sbuf, grads, act, hid, terms, sg, osum, tile, small_ref, sums_ref = take(14)
    ag, kbuf, ybuf, zbuf, got, msg, wq_part, wq_mine, wq_else = take(9)
    links = len(cube[0]) - 1
    bufs, out_bufs = take(links + 1), take(links + 1)
    wo_bufs = take(len(whole[0]))
    line_sems, small_sems, dy_sems, att_sems, wq_sems, wf_sems, wo_sems = take(6), take(2), take(4), take(2), take(4), take(2), take(4)
    wp_sems, gather_sems, scatter_sems = take(2), take(4), take(4)
    ag_sems, back_sems, outs_sems, msg_sems = take(2), take(6), take(4), take(2)
    wqg_sems, wfg_sems, wpg_sems, wog_sems = take(4), take(2), take(2), take(4)

    tokens, width = x_ref.shape
    length = n * tokens
    rows, units = w_fc.shape[0], w_proj.shape[0]
    count = n_dp * n
    d, me = lax.axis_index("dp"), lax.axis_index("ctx")
    flat = d * n + me
    rank, group = group_of(n, flat)
    line = Line(n)
    hello = Greet(n_dp, n)

    xg = LineGather(line, xbuf, line_sems)
    small = ToAll(n_dp, n, lambda f: small_ref, small_all, small_sems)
    wq = ToAll(n_dp, n, lambda f: wqb.at[f], wq_all.at[d], wq_sems[:2], True)
    wf = ToAll(n_dp, n, lambda f: wfb.at[group_of(n, f)[0]], wf_all, wf_sems)
    dyg = Gather(cube, dy_ref, dy_sems)
    wog = Gather(whole, wo_all, wo_sems)
    out = ToAll(n_dp, n, lambda f: packed.at[f], att, att_sems, True)
    g = Gather(cube, sbuf, gather_sems)
    s = Scatter(cube, terms, bufs, scatter_sems)
    dps, wps = [], []
    for i in range(1, n_dp):
        dps.append(remote(wq_all.at[d], wq_all.at[d], wq_sems[2].at[i], wq_sems[3].at[i], {"dp": (d + i) % n_dp}))
        to = wp_ref.at[pl.ds(pl.multiple_of(group * units, units), units)]
        wps.append(remote(w_proj, to, wp_sems[0].at[i], wp_sems[1].at[i], group_peer(n, i, n_dp)[1]))

    low = lax.broadcasted_iota(jnp.int32, (rows, 128), 1) < 64
    for h in range(0, HEADS, 2):
        q, k, v = (w_qkv[:, p * width + h * 64 : p * width + h * 64 + 128].astype(F32) for p in range(3))
        turn = lambda t: pltpu.roll(t, 64, 1)
        wqb[h, :, :128] = jnp.where(low, q, 0.0).astype(BF16)
        wqb[h, :, 128:] = jnp.where(low, k, turn(v)).astype(BF16)
        wqb[h + 1, :, :128] = jnp.where(low, turn(q), 0.0).astype(BF16)
        wqb[h + 1, :, 128:] = jnp.where(low, turn(k), v).astype(BF16)
    xbuf[line.z, line.y, line.c] = x_ref[...]
    put_small(pieces, tile, small_ref)
    small_all[flat] = small_ref[...]
    wq_all[d, me] = wqb[me]
    wo_all[wog.own()] = w_out[...]
    hello.wait()
    xg.start()
    small.start()
    wq.start()
    wog.start()
    for m in range(n):
        for i in range(n_dp):
            at = ((i // 2 * 2 + m // (n // 2)) * n + i % 2 * (n // 2) + m % (n // 2)) * units
            wfb[m, :, i * units : (i + 1) * units] = w_fc[:, at : at + units]
    dy_ref[dyg.own()] = dy_own[...]
    wf_all[flat] = wfb[rank]
    wp_ref[pl.ds(pl.multiple_of(group * units, units), units), :] = w_proj[...]
    xg.z_step(0)
    xg.y_step(3)
    xg.z_step(1)
    xg.y_step(2)
    wq.wait_recv()
    for c in dps:
        c.start()
    small.wait_recv()
    put_params(count, width, small_all, prm, bqv)
    odd = me % 2
    bias[:, :128] = half_row(bqv[pl.ds(me // 2, 1), :], odd, False)
    bias[:, 128:] = half_row(bqv[pl.ds(width // 128 + me // 2, 1), :], odd, True)
    for i in range(n_dp):
        owner = (i // 2 * 2 + d % 2) * n + i % 2 * (n // 2) + me % (n // 2)
        bf_row[:, i * units : (i + 1) * units] = small_all[owner].astype(F32)[BF : BF + 1, :units]
    put_ids(n, small_all, d * n, idrow, idcol)
    per_z = n // 4

    def plane(slot):
        return pl.ds(pl.multiple_of(line.slots[slot] * per_z * tokens, per_z * tokens), per_z * tokens)

    def project(slot):
        z = line.slots[slot]

        def one(i, _):
            at = pl.ds(pl.multiple_of((z * per_z + i) * tokens, tokens), tokens)
            first[at, :] = project_rows(xbuf[z, i // 2, i % 2], prm)
            return 0

        lax.fori_loop(0, per_z, one, 0)
        at = plane(slot)
        qkv = (dot(first[at, :], wq_all[...].reshape(width, 256)) + bias[...]).astype(BF16)
        a_ref[at, :] = qkv[:, :128]
        b_ref[at, :] = qkv[:, 128:]

    wog.step(0)
    xg.z_step(2)
    xg.y_step(1)
    for c in dps:
        c.wait_recv()
    xg.core_wait(3)
    project(3)
    wog.step(1)
    xg.core_wait(2)
    project(2)
    xg.y_step(0)
    dyg.start()
    for c in wps:
        c.start()
    wog.step(2)
    xg.core_wait(1)
    project(1)
    xg.core_wait(0)
    project(0)
    dyg.step(0)

    kc = min(1024, length)
    half = tokens // 2
    lane = lax.broadcasted_iota(jnp.int32, (half, 128), 1)

    def per_queries(gq, _):
        qs = pl.ds(pl.multiple_of(gq * QB, QB), QB)
        a = a_ref[qs, :] * 0.125
        ids = idcol[qs, :]
        acc[...] = jnp.zeros_like(acc)
        tot[...] = jnp.zeros_like(tot)

        def per_keys(kb, _):
            ks = pl.ds(pl.multiple_of(kb * kc, kc), kc)
            b = b_ref[ks, :]
            w = jnp.where(idrow[:, ks] <= ids, jnp.exp(dot(a, b, NT)), 0.0)
            t = w[:, :128]
            for i in range(1, kc // 128):
                t = t + w[:, i * 128 : (i + 1) * 128]
            tot[...] += t
            acc[...] += dot(w.astype(BF16), b)
            return 0

        lax.fori_loop(0, jnp.minimum(((gq + 2) * QB + kc - 1) // kc, length // kc), per_keys, 0)
        t = jnp.sum(tot[...], axis=-1, keepdims=True)
        o = acc[...] / t
        o_ref[qs, :] = jnp.where(lax.broadcasted_iota(jnp.int32, (QB, 128), 1) < 64, t, o)
        for i in range(QB // tokens):
            lo, hi = o[i * tokens : i * tokens + half], o[i * tokens + half : (i + 1) * tokens]
            packed[gq * (QB // tokens) + i] = jnp.where(lane < 64, pltpu.roll(lo, 64, 1), hi).astype(BF16)
        return 0

    blocks = length // QB
    lax.fori_loop(0, blocks // 2, per_queries, 0)
    dyg.step(1)
    wog.step(3)
    lax.fori_loop(blocks // 2, blocks, per_queries, 0)
    att[me] = packed[me]
    out.start()
    wf.start()
    for k in range(4, wog.links):
        wog.step(k)
    wog.core_wait()
    out.wait_recv()

    for h in range(0, HEADS, 2):
        b0, b1 = att[h].astype(F32), att[h + 1].astype(F32)
        at = slice(h * 64, h * 64 + 128)
        low_ref[:half, at] = jnp.where(lane < 64, b0, pltpu.roll(b1, 64, 1)).astype(BF16)
        low_ref[half:, at] = jnp.where(lane < 64, pltpu.roll(b0, 64, 1), b1).astype(BF16)
    middle = x_ref[...].astype(F32) + dot(low_ref[...], wo_all[...].reshape(width, width)) + prm[BO : BO + 1, :]
    middle_ref[...] = middle
    n2, _ = normalize(middle)
    sbuf[g.own()] = (n2 * prm[G2 : G2 + 1, :] + prm[C2 : C2 + 1, :]).astype(BF16)
    g.start()
    for k in range(2, links):
        dyg.step(k)
    for c in wps:
        c.wait_recv()
    dyg.core_wait()

    quarter = (1 << (links - 1)) * tokens
    inner = (slice(None),) * (links - 1)
    block = (2,) * (links - 1) + (tokens, width)
    core = g.mine[-1]

    def span(c, a):
        return pl.ds(pl.multiple_of((2 * c + a) * quarter, quarter), quarter)

    def grad_part(i):
        dy = dy_ref[(i // 2, i % 2) + inner].reshape(quarter, width)
        grads[span(i // 2, i % 2), :] = dot(dy, wp_ref[...], NT)

    for k in range(links):
        grad_part(k)
        g.step(k)
    for k in range(links, 4):
        grad_part(k)
    wf.wait_recv()
    g.core_wait()
    bf_grad[...] = jnp.zeros_like(bf_grad)

    def hidden_part(c, a):
        at = span(c, a)
        weights = wf_all[...].reshape(width, -1)
        active, slope = gelu_both(dot(sbuf[(c, a) + inner].reshape(quarter, width), weights) + bf_row[...])
        act[at, :] = active.astype(BF16)
        h = (slope * grads[at, :]).astype(BF16)
        hid[at, :] = h
        bf_grad[...] += jnp.sum(h.astype(F32), axis=0, keepdims=True)
        terms[(c, a) + inner] = dot(h, weights, NT).astype(BF16).reshape(block)

    for a in range(2):
        hidden_part(1 - core, a)
        s.core(a).start()
    for a in range(2):
        hidden_part(core, a)
        s.add_core(a)
    s.start_links()

    def weight_grads(k):
        at = slice(k * 256, (k + 1) * 256)
        low = sbuf[..., at].reshape(4 * quarter, 256)
        wf_grad[at, :] = jnp.transpose(dot(hid[...], low, TN)).astype(BF16)
        wp_grad[:, at] = dot(act[...], dy_ref[..., at].reshape(4 * quarter, 256), TN).astype(BF16)

    outs = Scatter(cube, terms, out_bufs, outs_sems)
    s.core_sent()
    for i in range(4):
        terms[(i // 2, i % 2) + inner] = dot(act[span(i // 2, i % 2), :], wp_ref[...]).astype(BF16).reshape(block)
    for h in range(2):
        outs.core(h).start()
    for k in range(links):
        s.step(k, sg)
        if k < 2:
            weight_grads(2 * k)
            weight_grads(2 * k + 1)

    for h in range(2):
        outs.add_core(h)
    outs.start_links()
    second_grad = sg[...]
    dy = dy_own[...].astype(F32)
    n2, rstd2 = normalize(middle_ref[...])
    mg = dy + normalize_back(second_grad * prm[G2 : G2 + 1, :], n2, rstd2)
    mg_ref[...] = mg
    branch = mg.astype(BF16)
    branch_ref[...] = branch
    grad = dot(branch, wo_all[...].reshape(width, width), NT)
    for h in range(0, HEADS, 2):
        lo, hi = grad[:half, h * 64 : h * 64 + 128], grad[half:, h * 64 : h * 64 + 128]
        agb[h] = jnp.where(lane < 64, lo, pltpu.roll(hi, 64, 1)).astype(BF16)
        agb[h + 1] = jnp.where(lane < 64, pltpu.roll(lo, 64, 1), hi).astype(BF16)
    heads = ToAll(n_dp, n, lambda f: agb.at[f], ag, ag_sems, True)
    heads.start()
    ag[me] = agb[me]
    column = lambda v: jnp.sum(v, axis=0, keepdims=True)
    sums_ref[0:1, :] = column(branch.astype(F32))
    sums_ref[1:2, :] = column(second_grad * n2)
    sums_ref[2:3, :] = column(second_grad)
    sums_ref[3:4, :] = column(dy)

    block_of = lambda ref, f, size: ref.at[pl.ds(pl.multiple_of(f * size, size), size)]
    wfs = ToAll(n_dp, n, lambda f: block_of(wf_grad, f, rows), wf_got, wfg_sems)
    wqs = ToAll(n_dp, n, lambda f: wq_mine.at[f], wq_got, wqg_sems[:2], True)
    wo = Scatter(whole, wo_all, wo_bufs, wog_sems)
    wf_got[flat] = block_of(wf_grad, flat, rows)[...]
    wp_got[group] = block_of(wp_grad, group, units)[...]
    wpgs, dpgs = [], []
    for i in range(1, n_dp):
        to, peer = group_peer(n, i, n_dp)
        wpgs.append(remote(block_of(wp_grad, to, units), wp_got.at[group], wpg_sems[0].at[i], wpg_sems[1].at[i], peer))
        other = (d + i) % n_dp
        dpgs.append(remote(wq_part.at[other], wq_else.at[i], wqg_sems[2].at[i], wqg_sems[3].at[i], {"dp": other}))
    for c in wpgs:
        c.start()
    heads.wait_recv()
    wfs.start()
    wog.finish()
    for k in range(width // 256):
        part = dot(low_ref[:, k * 256 : (k + 1) * 256], branch, TN).astype(BF16)
        for i in range(256 // rows):
            f = k * (256 // rows) + i
            wo_all[tuple((f >> b) & 1 for b in range(len(whole[0]) - 1, -1, -1))] = part[i * rows : (i + 1) * rows]
    for h in range(2):
        wo.core(h).start()
    mixed, dkv = act, grads
    dkv[:, :128] = jnp.zeros((length, 128), F32)

    def per_queries_back(gq, _):
        qs = pl.ds(pl.multiple_of(gq * QB, QB), QB)
        pieces = []
        for i in range(QB // tokens):
            t = ag[gq * (QB // tokens) + i].astype(F32)
            pieces += [jnp.where(lane >= 64, pltpu.roll(t, 64, 1), 0.0), jnp.where(lane >= 64, t, 0.0)]
        grad = jnp.concatenate(pieces, axis=0)
        o = o_ref[qs, :]
        inverse = 1.0 / o[:, :1]
        upper = lax.broadcasted_iota(jnp.int32, (QB, 128), 1) >= 64
        ratio = jnp.sum(jnp.where(upper, grad * o, 0.0), axis=-1, keepdims=True) * inverse
        ratio = jnp.transpose(jnp.broadcast_to(ratio, (QB, 128)))[:1, :]
        do = (grad * inverse).astype(BF16)
        a = a_ref[qs, :]
        scaled = a * 0.125
        ado = jnp.concatenate([a, do], axis=0)
        ids = idrow[:, qs]
        acc[...] = jnp.zeros_like(acc)

        def per_keys(kb, _):
            ks = pl.ds(pl.multiple_of(kb * kc, kc), kc)
            b = b_ref[ks, :]
            w = jnp.where(idcol[ks, :] <= ids, jnp.exp(dot(b, scaled, NT)), 0.0)
            t = (w * (dot(b, do, NT) - ratio)).astype(BF16)
            dkv[ks, :128] += dot(jnp.concatenate([t, w.astype(BF16)], axis=1), ado)
            acc[...] += dot(t, b, TN)
            return 0

        lax.fori_loop(0, jnp.minimum(((gq + 2) * QB + kc - 1) // kc, length // kc), per_keys, 0)
        mixed[qs, :128] = jnp.where(upper, 0.0, acc[...] * 0.125).astype(BF16)
        return 0

    cuts = [0, blocks // 2, blocks * 3 // 4, blocks]
    for k in range(3):
        lax.fori_loop(cuts[k], cuts[k + 1], per_queries_back, 0)
        if k + 1 < links:
            outs.step(k, osum)
    for h in range(2):
        wo.add_core(h)
    total = dkv[:, :128]
    lower = lax.broadcasted_iota(jnp.int32, (length, 128), 1) < 64
    mixed[:, 128:] = jnp.where(lower, total * 0.125, total).astype(BF16)

    xg.finish()
    rs = LineScatter(line, xbuf, kbuf, ybuf, zbuf, back_sems)

    def first_grad(slot):
        part = dot(mixed[plane(slot), :], wq_all[...].reshape(width, 256), NT).astype(BF16)
        xbuf[line.slots[slot]] = part.reshape(n // 8, 2, tokens, width)
        rs.core_start(slot)

    first_grad(0)
    for slot in range(1, 4):
        first_grad(slot)
        rs.core_step(slot - 1)
    rs.core_step(3)
    for k in range(min(2, links - 1), links):
        outs.step(k, osum)
    wo.start_links()

    def wq_grad(i):
        k = ((d + 1) * (width // 256 // n_dp) + i) % (width // 256)
        part = jnp.transpose(dot(mixed[...], first[:, pl.ds(pl.multiple_of(k * 256, 256), 256)], TN))
        q = 256 // rows
        wq_part[k * q // n, pl.ds(k * q % n, q)] = part.astype(BF16).reshape(q, rows, 256)

    turns = width // 256
    ahead = turns - turns // n_dp
    for i in range(ahead):
        wq_grad(i)
    for c in dpgs:
        c.start()
    rs.z_step(0)
    for i in range(ahead, turns):
        wq_grad(i)
    rs.z_step(1)
    total = wq_part[d].astype(F32)
    for i, c in enumerate(dpgs):
        c.wait_recv()
        total = total + wq_else[i + 1].astype(F32)
    wq_mine[...] = total.astype(BF16)
    wq_got[me] = wq_mine[me]
    wqs.start()
    wo.step(0, wo_own)
    total = jnp.sum(mixed[...].astype(F32), axis=0, keepdims=True)
    q_row = half_row(total[:, :128], 0, False)
    q_row = jnp.where(odd == 1, pltpu.roll(q_row, 64, 1), q_row)
    v_row = half_row(total[:, 128:], 1, True)
    v_row = jnp.where(odd == 1, v_row, pltpu.roll(v_row, 64, 1))
    rs.z_step(2)
    out_ref[...] = (middle_ref[...] + osum[...] + prm[BP : BP + 1, :]).astype(BF16)
    n1, rstd1 = normalize(x_ref[...].astype(F32))
    wo.step(1, wo_own)

    def prepare(f, _):
        at = f * 2 * width // count // 128
        msg[f, 6:7, :] = jnp.where(at == me // 2, q_row, 0.0) + jnp.where(at == width // 128 + me // 2, v_row, 0.0)
        same = group_of(n, f)[0] == rank
        for i in range(bf_grad.shape[1] // 128):
            msg[f, 7 + i : 8 + i, :] = jnp.where(same, bf_grad[:, i * 128 : (i + 1) * 128], 0.0)
        return 0

    msg[...] = jnp.zeros_like(msg)
    lax.fori_loop(0, count, prepare, 0)
    rs.last(sg)

    grad = sg[...]
    gain, shift = column(grad * n1), column(grad)
    per = 128 * count // width
    for k in range(width // 128):
        at = slice(k * 128, (k + 1) * 128)
        lines = jnp.concatenate([gain[:, at], shift[:, at], sums_ref[:, at]], axis=0)
        for i in range(per):
            msg[k * per + i, 0:6, :] = lines
    tell = ToAll(n_dp, n, lambda f: msg.at[f], got, msg_sems)
    tell.start()
    got[flat] = msg[flat]
    ig_ref[...] = (mg_ref[...] + normalize_back(grad * prm[G1 : G1 + 1, :], n1, rstd1)).astype(BF16)
    for k in range(2, wo.links):
        wo.step(k, wo_own)
    wfs.wait_recv()
    wqs.wait_recv()
    for c in wpgs:
        c.wait_recv()
    tell.wait_recv()
    sums[...] = jnp.sum(got[...], axis=0)
    for c in (wq, wf, small, out, heads, wfs, wqs, tell):
        c.wait_send()
    for c in dps + wps + wpgs + dpgs:
        c.wait_send()
    s.links_sent()
    for c in (dyg, g, outs, wo, rs):
        c.finish()


def layer(n_dp, n, x, small, dy, w_qkv, w_fc, w_proj, w_out):
    tokens, width = x.shape
    count, length = n_dp * n, n * tokens
    rows, own = w_fc.shape[0], w_proj.shape[0]
    units = n_dp * own
    cube, whole = cube_plan(n, tokens), all_plan(n_dp, n, rows)
    block = (2,) * len(cube[0]) + (tokens, width)
    shape, v = jax.ShapeDtypeStruct, pltpu.VMEM
    vm = pl.BlockSpec(memory_space=pltpu.VMEM)
    outs = [
        shape((tokens, width), BF16), shape((tokens, width), BF16), shape((16, 128), F32), shape((n, rows, 256), BF16),
        shape((count, rows, units), BF16), shape((n_dp, own, width), BF16), shape((rows, width), F32),
    ]
    heads = (n, tokens // 2, 128)
    all_sems = [DMA((count,))] * 2
    weight_sems = [DMA((n,))] * 2 + [DMA((n_dp,))] * 2
    return pl.pallas_call(
        functools.partial(layer_kernel, n_dp, n, cube, whole),
        out_shape=outs,
        in_specs=[vm] * 15,
        out_specs=[vm] * len(outs),
        scratch_shapes=[
            v((count, 16, 128), BF16), v((length, 128), BF16), v((length, 128), BF16), v((length, 128), F32),
            v((n_dp, n, rows, 256), BF16), v((tokens, width), F32), v((tokens, width), F32), v((tokens, width), BF16),
            v((tokens, width), BF16), v(heads, BF16), v((units, width), BF16), v((width, units), BF16), v((1, units), F32),
            v((4, n // 8, 2, tokens, width), BF16), v((length, width), BF16), v((16, width), F32), v((2 * width // 128, 128), F32),
            v((1, 256), F32), v((1, units), F32), v((1, length), F32), v((length, 1), F32), v(heads, BF16), v((QB, 128), F32),
            v((QB, 128), F32), v(heads, BF16), v((n, rows, 256), BF16), v((n, rows, units), BF16),
            v((count, rows, units), BF16), v((2,) * len(whole[0]) + (rows, width), BF16), v((units, width), BF16), v(block, BF16),
            v(block, BF16), v((length, units), F32), v((length, units), BF16), v((length, units), BF16), v(block, BF16),
            v((tokens, width), F32), v((tokens, width), F32), v((16, 128), F32), v((16, 128), BF16), v((4, width), F32),
            v(heads, BF16),
        ] + LineScatter.scratch(n, tokens, width) + [
            v((count, 16, 128), F32), v((count, 16, 128), F32), v((n_dp, n, rows, 256), BF16), v((n, rows, 256), BF16),
            v((n_dp, n, rows, 256), BF16),
        ] + Scatter.scratch(cube, tokens, width) * 2 + Scatter.scratch(whole, rows, width)
        + LineGather.sems(n) + all_sems + Gather.sems(cube) + [DMA((n,))] * 2 + weight_sems + all_sems + Gather.sems(whole)
        + [DMA((n_dp,))] * 2 + Gather.sems(cube) + Scatter.sems(cube)
        + [DMA((n,))] * 2 + LineScatter.sems(n) + Scatter.sems(cube) + all_sems
        + weight_sems + all_sems + [DMA((n_dp,))] * 2 + Scatter.sems(whole),
        compiler_params=pltpu.CompilerParams(collective_id=4, has_side_effects=True, vmem_limit_bytes=VMEM_MOST),
        name="layer",
    )(x, *small, dy, w_qkv, w_fc, w_proj, w_out)


def back_kernel(n_dp, n, r, spread, cube, whole, *refs):
    refs = list(refs)
    take = lambda k: [refs.pop(0) for _ in range(k)]
    agb, a_ref, b_ref, o_ref, small_all, wq_ref, first, part_out, x_ref, mid_ref, mg_ref, par_ref, sums_in, bf_grad = take(14)
    if spread:
        low_ref, branch_ref, wfg, wpg = take(4)
    out_ref, ig_ref, sums = take(3)
    if spread:
        wq_got, wf_got, wp_got, wo_own = take(4)
    else:
        (wq_sum,) = take(1)
    ag, idrow, idcol, mixed, dqacc, dkv, acc, kbuf, ybuf, zbuf, fg, got, msg, columns, column_sem, own_out, own_sem, osum = take(18)
    links = len(cube[0]) - 1
    out_bufs = take(links + 1)
    if r > 1:
        (dkv_got,) = take(1)
        pair_sems = take(2)
    ag_sems, line_sems, out_sems, msg_sems = take(2), take(6), take(4), take(2)
    if spread:
        wq_part, wq_mine, wq_else, wo_part = take(4)
        wq_sems, wf_sems, wp_sems = take(4), take(2), take(2)
        wo_bufs = take(len(whole[0]))
        wo_sems = take(4)

    tokens, width = x_ref.shape
    length = b_ref.shape[0]
    count = n_dp * n
    d, me = lax.axis_index("dp"), lax.axis_index("ctx")
    flat = d * n + me
    head, part = me // r, me % r
    line = Line(n)
    hello = Greet(n_dp, n)
    kc = min(1024, length)
    half = tokens // 2

    grads = ToAll(n_dp, n, lambda f: agb.at[f], ag, ag_sems, True)
    outs = Scatter(cube, part_out, out_bufs, out_sems, own_out)
    own_copy = outs.fetch_own(own_sem)
    own_copy.start()
    ag[me] = agb[me]
    if spread:
        wf = ToAll(n_dp, n, lambda f: wfg.at[f], wf_got, wf_sems)
        wq = ToAll(n_dp, n, lambda f: wq_mine.at[f], wq_got, wq_sems[:2], True)
        wo = Scatter(whole, wo_part, wo_bufs, wo_sems)
        wf_got[flat] = wfg[flat]
        rank, group = group_of(n, flat)
        wp_got[group] = wpg[group]
        wps, dps = [], []
        for i in range(1, n_dp):
            g, peer = group_peer(n, i, n_dp)
            wps.append(remote(wpg.at[g], wp_got.at[group], wp_sems[0].at[i], wp_sems[1].at[i], peer))
            dps.append(remote(wq_part.at[(d + i) % n_dp], wq_else.at[i], wq_sems[2].at[i], wq_sems[3].at[i], {"dp": (d + i) % n_dp}))
    else:
        rank, group = group_of(n, flat)
    dkv[...] = jnp.zeros_like(dkv)
    if r > 1:
        mixed[...] = jnp.zeros_like(mixed)
    hello.wait()
    grads.start()
    for h in range(2):
        outs.core(h).start()
    if spread:
        for c in wps:
            c.start()
    put_ids(n, small_all, d * n, idrow, idcol)
    if spread:
        rows = width // count
        for k in range(width // 256):
            terms = dot(low_ref[:, k * 256 : (k + 1) * 256], branch_ref[...], TN).astype(BF16)
            for i in range(256 // rows):
                f = k * (256 // rows) + i
                bits = tuple((f >> b) & 1 for b in range(len(whole[0]) - 1, -1, -1))
                wo_part[bits] = terms[i * rows : (i + 1) * rows]
        for h in range(2):
            wo.core(h).start()
    own_copy.wait()
    for h in range(2):
        outs.add_core(h)
    outs.start_links()
    grads.wait_recv()
    if spread:
        wf.start()

    def per_queries(lb, _):
        gq = lb * r + part
        qs = pl.ds(pl.multiple_of(gq * QB, QB), QB)
        at = pl.ds(pl.multiple_of(lb * QB, QB), QB)
        lane = lax.broadcasted_iota(jnp.int32, (half, 128), 1)
        pieces = []
        for i in range(QB // tokens):
            block = ag[gq * (QB // tokens) + i].astype(F32)
            pieces += [jnp.where(lane >= 64, pltpu.roll(block, 64, 1), 0.0), jnp.where(lane >= 64, block, 0.0)]
        grad = jnp.concatenate(pieces, axis=0)
        o = o_ref[at, :]
        inverse = 1.0 / o[:, :1]
        upper = lax.broadcasted_iota(jnp.int32, (QB, 128), 1) >= 64
        ratio = jnp.sum(jnp.where(upper, grad * o, 0.0), axis=-1, keepdims=True) * inverse
        ratio = jnp.transpose(jnp.broadcast_to(ratio, (QB, 128)))[:1, :]
        do = (grad * inverse).astype(BF16)
        a = a_ref[qs, :]
        scaled = a * 0.125
        ado = jnp.concatenate([a, do], axis=0)
        ids = idrow[:, qs]
        dqacc[...] = jnp.zeros_like(dqacc)

        def per_keys(kb, _):
            ks = pl.ds(pl.multiple_of(kb * kc, kc), kc)
            b = b_ref[ks, :]
            w = jnp.where(idcol[ks, :] <= ids, jnp.exp(dot(b, scaled, NT)), 0.0)
            g = (w * (dot(b, do, NT) - ratio)).astype(BF16)
            dkv[ks, :] += dot(jnp.concatenate([g, w.astype(BF16)], axis=1), ado)
            dqacc[...] += dot(g, b, TN)
            return 0

        lax.fori_loop(0, jnp.minimum(((gq + 2) * QB + kc - 1) // kc, length // kc), per_keys, 0)
        mixed[qs, :128] = jnp.where(upper, 0.0, dqacc[...] * 0.125).astype(BF16)
        return 0

    blocks = length // QB // r
    cuts = [0, blocks // 2, blocks * 3 // 4, blocks]
    for k in range(3):
        lax.fori_loop(cuts[k], cuts[k + 1], per_queries, 0)
        if k + 1 < links:
            outs.step(k, osum)
    if spread:
        for h in range(2):
            wo.add_core(h)

    def fetch(k):
        return pltpu.make_async_copy(first.at[:, pl.ds(pl.multiple_of(k * 256, 256), 256)], columns, column_sem)

    turns = [((d + 1) * (width // 256 // n_dp) + i) % (width // 256) if spread else i for i in range(width // 256)]
    fetch(turns[0]).start()
    low = lax.broadcasted_iota(jnp.int32, (length, 128), 1) < 64
    total = dkv[...]
    if r > 1:
        both = remote(dkv, dkv_got, pair_sems[0], pair_sems[1], line.core)
        both.start()
        both.wait()
        total = jnp.where(part == 0, total + dkv_got[...], 0.0)
    mixed[:, 128:] = jnp.where(low, total * 0.125, total).astype(BF16)

    rs = LineScatter(line, acc, kbuf, ybuf, zbuf, line_sems)
    per_z = n // 4 * tokens

    def first_grad(slot):
        z = line.slots[slot]
        at = pl.ds(pl.multiple_of(z * per_z, per_z), per_z)
        acc[z] = dot(mixed[at, :], wq_ref[...], NT).astype(BF16).reshape(n // 8, 2, tokens, width)
        rs.core_start(slot)

    first_grad(0)
    for slot in range(1, 4):
        first_grad(slot)
        rs.core_step(slot - 1)
    rs.core_step(3)
    for k in range(min(2, links - 1), links):
        outs.step(k, osum)
    if spread:
        wo.start_links()

    def wq_grad(i):
        k = turns[i]
        fetch(k).wait()
        g = jnp.transpose(dot(mixed[...], columns[...], TN))
        if i + 1 < len(turns):
            fetch(turns[i + 1]).start()
        if spread:
            per = n_dp * 256 // width
            q = 256 // rows
            at = k * q
            wq_part[at // n, pl.ds(at % n, q)] = g.astype(BF16).reshape(q, rows, 256)
        else:
            wq_sum[pl.ds(pl.multiple_of(k * 256, 256), 256), :] = g

    ahead = len(turns) - len(turns) // n_dp if spread else 2
    for i in range(ahead):
        wq_grad(i)
    if spread:
        for c in dps:
            c.start()
    rs.z_step(0)
    for i in range(ahead, len(turns)):
        wq_grad(i)
    rs.z_step(1)
    if spread:
        total = wq_part[d].astype(F32)
        for i, c in enumerate(dps):
            c.wait_recv()
            total = total + wq_else[i + 1].astype(F32)
        wq_mine[...] = total.astype(BF16)
        wq_got[me] = wq_mine[me]
        wq.start()
        wo.step(0, wo_own)
    column = jnp.sum(mixed[...].astype(F32), axis=0, keepdims=True)
    odd = head % 2
    q_row = half_row(column[:, :128], 0, False)
    q_row = jnp.where(odd == 1, pltpu.roll(q_row, 64, 1), q_row)
    v_row = half_row(column[:, 128:], 1, True)
    v_row = jnp.where(odd == 1, v_row, pltpu.roll(v_row, 64, 1))
    rs.z_step(2)
    out_ref[...] = (mid_ref[...] + osum[...] + par_ref[1:2, :]).astype(BF16)
    n1, rstd1 = normalize(x_ref[...].astype(F32))
    if spread:
        wo.step(1, wo_own)

    wide = bf_grad.shape[1] // 128

    def prepare(f, _):
        tile = f * 2 * width // count // 128
        bqv = jnp.where(tile == head // 2, q_row, 0.0) + jnp.where(tile == width // 128 + head // 2, v_row, 0.0)
        msg[f, 6:7, :] = bqv
        same = group_of(n, f)[0] == rank
        for i in range(wide):
            msg[f, 7 + i : 8 + i, :] = jnp.where(same, bf_grad[:, i * 128 : (i + 1) * 128], 0.0)
        return 0

    msg[...] = jnp.zeros_like(msg)
    lax.fori_loop(0, count, prepare, 0)
    rs.last(fg)

    grad = fg[...]
    gain = jnp.sum(grad * n1, axis=0, keepdims=True)
    shift = jnp.sum(grad, axis=0, keepdims=True)
    per = 128 * count // width
    for k in range(width // 128):
        at = slice(k * 128, (k + 1) * 128)
        lines = jnp.concatenate([gain[:, at], shift[:, at], sums_in[:, at]], axis=0)

        def fill(i, _, k=k, lines=lines):
            msg[k * per + i, 0:6, :] = lines
            return 0

        lax.fori_loop(0, per, fill, 0)
    tell = ToAll(n_dp, n, lambda f: msg.at[f], got, msg_sems)
    tell.start()
    got[flat] = msg[flat]
    ig_ref[...] = (mg_ref[...] + normalize_back(grad * par_ref[0:1, :], n1, rstd1)).astype(BF16)
    if spread:
        for k in range(2, wo.links):
            wo.step(k, wo_own)
        wf.wait_recv()
        wq.wait_recv()
        for c in wps:
            c.wait()
    tell.wait_recv()
    sums[...] = jnp.sum(got[...], axis=0)
    tell.wait_send()
    if spread:
        wf.wait_send()
        wq.wait_send()
        for c in dps:
            c.wait_send()
        wo.finish()
    grads.wait_send()
    outs.finish()
    rs.finish()


def back(n_dp, n, r, agb, a, b, o, small_all, wq, first, part_out, x, middle, mg, params, sums4, bf_grad, grads):
    tokens, width = x.shape
    count, length = n_dp * n, n * tokens
    spread = grads is not None
    cube = cube_plan(n, tokens)
    links = len(cube[0]) - 1
    whole = None
    shape = jax.ShapeDtypeStruct
    ins = [agb, a, b, o, small_all, wq, first, part_out, x, middle, mg, params, sums4, bf_grad]
    outs = [shape((tokens, width), BF16), shape((tokens, width), BF16), shape((16, 128), F32)]
    scratch = [
        pltpu.VMEM((n, tokens // 2, 128), BF16), pltpu.VMEM((1, length), F32), pltpu.VMEM((length, 1), F32),
        pltpu.VMEM((length, 256), BF16), pltpu.VMEM((QB, 128), F32), pltpu.VMEM((length, 128), F32),
        pltpu.VMEM((4, n // 8, 2, tokens, width), BF16),
    ] + LineScatter.scratch(n, tokens, width) + [
        pltpu.VMEM((tokens, width), F32), pltpu.VMEM((count, 16, 128), F32), pltpu.VMEM((count, 16, 128), F32),
        pltpu.VMEM((length, 256), BF16), DMA, pltpu.VMEM((2,) * links + (tokens, width), BF16), DMA,
        pltpu.VMEM((tokens, width), F32),
    ] + Scatter.scratch(cube, tokens, width)
    if r > 1:
        scratch += [pltpu.VMEM((length, 128), F32), DMA, DMA]
    scratch += [DMA((n,))] * 2 + LineScatter.sems(n) + Scatter.sems(cube) + [DMA((count,))] * 2
    if spread:
        low, branch, wfg, wpg = grads
        rows = width // count
        whole = all_plan(n_dp, n, rows)
        ins += [low, branch, wfg, wpg]
        outs += [shape((n, rows, 256), BF16), shape(wfg.shape, BF16), shape(wpg.shape, BF16), shape((rows, width), F32)]
        scratch += [
            pltpu.VMEM((n_dp, n, rows, 256), BF16), pltpu.VMEM((n, rows, 256), BF16), pltpu.VMEM((n_dp, n, rows, 256), BF16),
            pltpu.VMEM((2,) * len(whole[0]) + (rows, width), BF16),
        ]
        scratch += [DMA((n,))] * 2 + [DMA((n_dp,))] * 2 + [DMA((count,))] * 2 + [DMA((n_dp,))] * 2
        scratch += Scatter.scratch(whole, rows, width) + Scatter.sems(whole)
    else:
        outs += [shape((width, 256), F32)]
    vm, hbm = pl.BlockSpec(memory_space=pltpu.VMEM), pl.BlockSpec(memory_space=pl.ANY)
    return pl.pallas_call(
        functools.partial(back_kernel, n_dp, n, r, spread, cube, whole),
        out_shape=outs,
        in_specs=[hbm if v is first or v is part_out else vm for v in ins],
        out_specs=[vm] * len(outs),
        scratch_shapes=scratch,
        compiler_params=pltpu.CompilerParams(collective_id=3, has_side_effects=True, vmem_limit_bytes=VMEM_LIMIT),
        name="back",
    )(*ins)


def own_sums(n_dp, n, piece, sums):
    flat = lax.axis_index("dp") * n + lax.axis_index("ctx")
    wide = pltpu.roll(sums, (128 - flat * piece % 128) % 128, 1)
    return wide, pltpu.roll(sums, (128 - flat * 2 * piece % 128) % 128, 1)[6:7]


def finish_kernel(n_dp, n, out_in, ig_in, sums, wq_got, wf_got, wp_got, wo_in, *outs):
    out, ig, g1, c1, wq_own, bqv, wo_own, bo, g2, c2, wf_own, bf, wp_own, bp = outs
    count = n_dp * n
    rows, width = wo_in.shape
    units = wp_got.shape[1]
    out[0] = out_in[...]
    ig[0] = ig_in[...]
    wo_own[...] = wo_in[...]
    wp_own[...] = jnp.sum(wp_got[...].astype(F32), axis=0)
    for f in range(count):
        m, g = group_of(n, f)
        total = 0.0
        for i in range(n_dp):
            source = (i // 2 * 2 + m // (n // 2)) * n + i % 2 * (n // 2) + m % (n // 2)
            total = total + wf_got[source, :, g * units : (g + 1) * units].astype(F32)
        wf_own[:, f * units : (f + 1) * units] = total
    lower = lax.broadcasted_iota(jnp.int32, (rows, 128), 1) < 64
    turn = lambda t: pltpu.roll(t, 64, 1)
    for h in range(0, HEADS, 2):
        (q0, e0), (q1, e1) = ((wq_got[i, :, :128].astype(F32), wq_got[i, :, 128:].astype(F32)) for i in (h, h + 1))
        for p, v in enumerate((jnp.where(lower, q0, turn(q1)), jnp.where(lower, e0, turn(e1)), jnp.where(lower, turn(e0), e1))):
            wq_own[:, p * width + h * 64 : p * width + h * 64 + 128] = v
    wide, double = own_sums(n_dp, n, rows, sums[...])
    for i, ref in enumerate((g1, c1, bo, g2, c2, bp)):
        ref[...] = wide[i : i + 1, :rows]
    bqv[...] = double[:, : 2 * rows]
    group = group_of(n, lax.axis_index("dp") * n + lax.axis_index("ctx"))[1]
    bf[...] = sums[pl.ds(7 + group, 1), :]


def finish(n_dp, n, out, ig, sums, wq_got, wf_got, wp_got, wo):
    rows, width = wo.shape
    units = wp_got.shape[1]
    shape = jax.ShapeDtypeStruct
    row = shape((1, rows), F32)
    vm = pl.BlockSpec(memory_space=pltpu.VMEM)
    got = pl.pallas_call(
        functools.partial(finish_kernel, n_dp, n),
        out_shape=[
            shape((1,) + out.shape, BF16), shape((1,) + ig.shape, BF16), row, row, shape((rows, 3 * width), F32),
            shape((1, 2 * rows), F32), shape((rows, width), F32), row, row, row, shape((rows, n_dp * n * units), F32),
            shape((1, units), F32), shape((units, width), F32), row,
        ],
        in_specs=[vm] * 7,
        out_specs=[vm] * 14,
        compiler_params=pltpu.CompilerParams(vmem_limit_bytes=VMEM_LIMIT),
        name="finish",
    )(out, ig, sums, wq_got, wf_got, wp_got, wo)
    return tuple(v.reshape(-1) if v.shape[0] == 1 and v.ndim == 2 else v for v in got)


def local(n_dp, n, inputs, cotangent, block_ids, ln1_gain, ln1_bias, w_qkv, b_qkv, w_out, b_out, ln2_gain, ln2_bias, w_fc, b_fc, w_proj, b_proj):
    tokens, width = inputs.shape[1:]
    count = n_dp * n
    rows = w_qkv.shape[0]
    units = w_proj.shape[0]
    r = n // HEADS
    hd = width // HEADS
    d, me = lax.axis_index("dp"), lax.axis_index("ctx")
    flat = d * n + me
    head = me // r
    both = ("dp", "ctx")
    x, dy = inputs[0], cotangent[0]
    halves = (n_dp // 2, 2, 2, n // 2)

    small = (ln1_gain, ln1_bias, b_qkv, block_ids[0], b_out, ln2_gain, ln2_bias, b_fc, b_proj)
    small = [v.reshape(1, -1) for v in small]

    def heads_of(w):
        w = w.reshape(w.shape[0], 3, HEADS, 1, hd)
        w = jnp.stack([w[:, 0], jnp.zeros_like(w[:, 0]), w[:, 1], w[:, 2]], axis=3)
        return w.reshape(w.shape[0], HEADS, 4 * hd)

    spread = rows % 16 == 0 and units == 128 and r == 1
    if spread:
        return finish(n_dp, n, *layer(n_dp, n, x, small, dy, w_qkv, w_fc, w_proj, w_out))
    full = lax.all_gather(w_qkv, both, axis=0, tiled=True)
    wq = lax.dynamic_index_in_dim(heads_of(full), head, 1, keepdims=False)
    wf = lax.all_gather(w_fc, both, axis=0, tiled=True).reshape((width,) + halves + (units,))
    wf = lax.dynamic_index_in_dim(wf, d % 2, 2, keepdims=False)
    wf = lax.dynamic_index_in_dim(wf, me % (n // 2), 3, keepdims=False).reshape(width, n_dp * units)
    wp = lax.all_gather(w_proj, both, axis=0, tiled=True).reshape(halves + (units, width))
    wp = lax.dynamic_index_in_dim(wp, d % 2, 1, keepdims=False)
    wp = lax.dynamic_index_in_dim(wp, me % (n // 2), 2, keepdims=False).reshape(n_dp * units, width)
    wo = lax.all_gather(w_out, both, axis=0, tiled=True)
    small_all, first, a, b, o, att, dy_all = front(n_dp, n, r, x, small, dy, wq)

    def vector(row, size):
        return small_all[:, row, :size].astype(F32).reshape(1, -1)

    params = jnp.concatenate([vector(k, rows) for k in (BO, G2, C2, G1, BP)])
    bf = vector(BF, units).reshape(halves + (units,))
    bf = lax.dynamic_index_in_dim(bf, d % 2, 1, keepdims=False)
    bf = lax.dynamic_index_in_dim(bf, me % (n // 2), 2, keepdims=False).reshape(1, -1)
    got = ffn(n, r, att, x, dy, dy_all, wo, wf, wp, bf, params[:3])
    middle, middle_grad, low, branch, agb, sums4, part_out, wp_grad, wf_grad, bf_grad = got
    got = back(n_dp, n, r, agb, a, b, o, small_all, wq, first, part_out, x, middle, middle_grad, params[3:], sums4, bf_grad, None)
    output, input_grad, sums = got[:3]
    owned = lambda v: lax.psum_scatter(v, both, scatter_dimension=0, tiled=True)
    hot = (jnp.arange(2) == d % 2).reshape(1, 2, 1, 1, 1) & (jnp.arange(n // 2) == me % (n // 2)).reshape(1, 1, 1, -1, 1)
    g = got[3].reshape(width, 4, 1, hd)
    g = jnp.stack([g[:, 0], g[:, 2], g[:, 3]], axis=1)
    wq_own = owned(jnp.where((jnp.arange(HEADS) == head).reshape(1, 1, -1, 1), g, 0.0).reshape(width, 3 * width))
    g = wf_grad.astype(F32).reshape(width, n_dp // 2, 1, 2, 1, units)
    wf_own = owned(jnp.where(hot[None], g, 0.0).reshape(width, -1))
    g = wp_grad.astype(F32).reshape(n_dp // 2, 1, 2, 1, units, width)
    wp_own = owned(jnp.where(hot[..., None], g, 0.0).reshape(-1, width))
    wo_own = owned(dot(low, branch, TN))

    cut = lambda k, size: lax.dynamic_slice(sums[k], (flat * size % 128,), (size,))
    g1g, c1g, bog, g2g, c2g, bpg = (cut(k, rows) for k in range(6))
    bqvg = cut(6, 2 * rows)
    group = d // 2 * 2 + me // (n // 2)
    bfg = lax.dynamic_slice(sums[7 : 7 + n_dp * units // 128].reshape(-1), (group * units,), (units,))
    return (
    output[None], input_grad[None], g1g, c1g, wq_own, bqvg, wo_own, bog, g2g, c2g, wf_own, bfg, wp_own, bpg,
    )


def solution(mesh):
    both = ("dp", "ctx")
    act, vec, mat = P("dp", "ctx", None), P(both), P(both, None)
    return jax.shard_map(
    functools.partial(local, mesh.shape["dp"], mesh.shape["ctx"]),
    mesh=mesh,
    in_specs=(act, act, P("dp", "ctx"), vec, vec, mat, vec, mat, vec, vec, vec, mat, vec, mat, vec),
    out_specs=(act, act, vec, vec, mat, vec, mat, vec, vec, vec, mat, vec, mat, vec),
    check_vma=False,
    )
```
